32 devices in a mesh: group: 4 (over y, x), fsdp: 8 (over z, core).
Axes of the slice: x: 2, y: 2, z: 4, core: 2. Of those that a mesh axis runs over, the one named last changes fastest.
Arguments:
- tokens: bfloat16 [16, 1024, 1536], P('group', 'fsdp'), may hold values from -6 to 6
- item_bucket: int32 [11], replicated, may hold values from 0 to 999, as said below
- slot_item: int32 [16], P('group'), may hold values from 0 to 10, as said below
- slot_live: int32 [16], P('group'), may hold values from 0 to 1, as said below
- slot_tokens: int32 [16], P('group'), may hold values from 512 to 1024, as said below
- ada_weight: bfloat16 [1536, 4608], P(None, 'fsdp'), may hold values from -0.15625 to 0.15625
- ada_bias: bfloat16 [4608], P('fsdp'), may hold values from -3 to 3
- in_weight: bfloat16 [1536, 6144], P('fsdp'), may hold values from -0.15625 to 0.15625
- conv_weight: bfloat16 [2, 4, 3072], P(None, None, 'fsdp'), may hold values from -3 to 3
- conv_bias: bfloat16 [2, 3072], P(None, 'fsdp'), may hold values from -0.5 to 0.5
- xproj_weight: bfloat16 [2, 3072, 128], P(None, 'fsdp'), may hold values from -0.109375 to 0.109375
- dt_weight: bfloat16 [2, 96, 3072], P(None, None, 'fsdp'), may hold values from -0.625 to 0.625
- dt_bias: bfloat16 [2, 3072], P(None, 'fsdp'), may hold values from -6.5 to -2.5
- a_log: bfloat16 [2, 16, 3072], P(None, None, 'fsdp'), may hold values from 0 to 2.796875
- skip_gain: bfloat16 [2, 3072], P(None, 'fsdp'), may hold values from 0.5 to 1.5
- out_weight: bfloat16 [3072, 1536], P('fsdp'), may hold values from -0.109375 to 0.109375
- cotangent: bfloat16 [16, 1024, 1536], P('group', 'fsdp'), may hold values from -6 to 6
Outputs:
- layer_out: bfloat16 [16, 1024, 1536], P('group', 'fsdp')
- tokens_grad: float32 [16, 1024, 1536], P('group', 'fsdp')
- ada_weight_grad: float32 [1536, 4608], P(None, 'fsdp')
- ada_bias_grad: float32 [4608], P('fsdp')
- in_weight_grad: float32 [1536, 6144], P('fsdp')
- conv_weight_grad: float32 [2, 4, 3072], P(None, None, 'fsdp')
- conv_bias_grad: float32 [2, 3072], P(None, 'fsdp')
- xproj_weight_grad: float32 [2, 3072, 128], P(None, 'fsdp')
- dt_weight_grad: float32 [2, 96, 3072], P(None, None, 'fsdp')
- dt_bias_grad: float32 [2, 3072], P(None, 'fsdp')
- a_log_grad: float32 [2, 16, 3072], P(None, None, 'fsdp')
- skip_gain_grad: float32 [2, 3072], P(None, 'fsdp')
- out_weight_grad: float32 [3072, 1536], P('fsdp')
The draws below stay inside these ranges and needn't reach their ends.
Inputs may be any that keep to these rules, and one draw needn't show every extreme that they name: `slot_live`: exactly 11 slots are live, and every slot of at least one group is live. `slot_item`: A live slot names its item; each item sits in exactly one live slot; a slot that is not live names item 0. `slot_tokens`: the item's real tokens are the first ones of its slot; some live slot holds 1024 and some live slot 512. `item_bucket`: an item in a slot of group g has a bucket from g * (250) to (g + 1) * 250 - 1.
All inputs are finite; a program needn't handle non-finite values.
Results may differ from the reference program's by a relative error of at most 0.014.
Values may be sent and summed in bfloat16 or wider, within the bound.
A program may use at most 448 MiB of HBM per device.

```python
import math
import jax
import jax.numpy as jnp
from jax import lax

D = 1536
E = 3072
N = 16
R = 96
CONV = 4
XW = 128
LEN = 1024
SLOT_G = 4
TSTEPS = 1000
GROUPS = 4
SLOTS = 16
ITEMS = 11
N_FSDP = 8


def plan_layout(key):
    favour_key = jax.random.fold_in(key, 101)
    full_key = jax.random.fold_in(key, 102)
    order_key = jax.random.fold_in(key, 103)
    bucket_key = jax.random.fold_in(key, 104)
    length_key = jax.random.fold_in(key, 105)
    group_ids = jnp.arange(GROUPS, dtype=jnp.int32)
    favour = jax.random.randint(favour_key, (GROUPS,), 0, 3, dtype=jnp.int32)
    full_group = jax.random.randint(full_key, (), 0, GROUPS, dtype=jnp.int32)
    favour = jnp.where(group_ids == full_group, 8, favour)
    slot_ids = jnp.arange(SLOTS, dtype=jnp.int32)
    slot_group = slot_ids // SLOT_G
    scores = (favour[slot_group] * 65536 + jax.random.randint(order_key, (SLOTS,), 0, 65536, dtype=jnp.int32)) * SLOTS + slot_ids
    _, chosen = lax.top_k(scores, ITEMS)
    chosen = chosen.astype(jnp.int32)
    item_ids = jnp.arange(ITEMS, dtype=jnp.int32)
    slot_item = jnp.zeros((SLOTS,), jnp.int32).at[chosen].set(item_ids)
    slot_live = jnp.zeros((SLOTS,), jnp.int32).at[chosen].set(1)
    bucket_width = TSTEPS // GROUPS
    item_bucket = slot_group[chosen] * bucket_width + jax.random.randint(bucket_key, (ITEMS,), 0, bucket_width, dtype=jnp.int32)
    lengths = jax.random.randint(length_key, (SLOTS,), LEN // 2, LEN + 1, dtype=jnp.int32)
    first_full = full_group * SLOT_G
    lengths = jnp.where(slot_ids == first_full, LEN, lengths)
    lengths = jnp.where(slot_ids == first_full + 1, LEN // 2, lengths)
    return (slot_item, slot_live, item_bucket, lengths)


def draw_item_bucket(key, part):
    return plan_layout(key)[2]


def draw_slot_item(key, part):
    return plan_layout(key)[0]


def draw_slot_live(key, part):
    return plan_layout(key)[1]


def draw_slot_tokens(key, part):
    return plan_layout(key)[3]


def level_of(own_key, dims, shards, smallest, largest):
    gain = 1.0
    for axis_at, shards_of in shards:
        heights = jax.random.uniform(jax.random.fold_in(jax.random.fold_in(own_key, 6), axis_at), (shards_of,), jnp.float32, smallest / len(shards), largest / len(shards))
        gain = gain * jnp.repeat(jnp.exp(heights), dims[axis_at] // shards_of).reshape((-1,) + (1,) * (len(dims) - 1 - axis_at))
    return gain


def scatter_about(own_key, dims, spread, limit, shards=(), held_as=jnp.bfloat16):
    values = spread * jax.random.normal(own_key, dims, jnp.float32)
    if shards:
        values = values * level_of(own_key, dims, shards, -0.22, 0.18)
    return jnp.clip(values, -limit, limit).astype(held_as)


def setup_inputs(seed: int = 0) -> dict:
    streams_of = jax.random.split(jax.random.key(seed), 18)
    return {
        "tokens": scatter_about(streams_of[0], (SLOTS, LEN, D), 1.0, 6.0, ((0, 4), (1, 8))),
        "item_bucket": draw_item_bucket(jax.random.fold_in(streams_of[17], 71), 0),
        "slot_item": draw_slot_item(jax.random.fold_in(streams_of[17], 71), 0),
        "slot_live": draw_slot_live(jax.random.fold_in(streams_of[17], 71), 0),
        "slot_tokens": draw_slot_tokens(jax.random.fold_in(streams_of[17], 71), 0),
        "ada_weight": scatter_about(streams_of[5], (D, 3 * D), D ** -0.5, 0.15625, ((1, 8),)),
        "ada_bias": scatter_about(streams_of[6], (3 * D,), 0.5, 3.0, ((0, 8),)),
        "in_weight": scatter_about(streams_of[7], (D, 2 * E), D ** -0.5, 0.15625, ((0, 8),)),
        "conv_weight": scatter_about(streams_of[8], (2, CONV, E), CONV ** -0.5, 3.0, ((2, 8),)),
        "conv_bias": jnp.clip(jax.random.uniform(streams_of[9], (2, E), jnp.float32, -0.5, 0.5) * level_of(streams_of[9], (2, E), ((1, 8),), -0.4, 0.0), -0.5, 0.5).astype(jnp.bfloat16),
        "xproj_weight": scatter_about(streams_of[10], (2, E, XW), E ** -0.5, 0.109375, ((1, 8),)),
        "dt_weight": scatter_about(streams_of[11], (2, R, E), R ** -0.5, 0.625, ((2, 8),)),
        "dt_bias": jnp.clip(-6.5 + 4.0 * jax.random.uniform(streams_of[12], (2, E), jnp.float32) ** level_of(streams_of[12], (2, E), ((1, 8),), -0.2, 0.2), -6.5, -2.5).astype(jnp.bfloat16),
        "a_log": jnp.clip(2.796875 * jax.random.uniform(streams_of[13], (2, N, E), jnp.float32) ** level_of(streams_of[13], (2, N, E), ((2, 8),), -0.2, 0.2), 0.0, 2.796875).astype(jnp.bfloat16),
        "skip_gain": jnp.clip(0.5 + 1.0 * jax.random.uniform(streams_of[14], (2, E), jnp.float32) ** level_of(streams_of[14], (2, E), ((1, 8),), -0.2, 0.2), 0.5, 1.5).astype(jnp.bfloat16),
        "out_weight": scatter_about(streams_of[15], (E, D), E ** -0.5, 0.109375, ((0, 8),)),
        "cotangent": scatter_about(streams_of[16], (SLOTS, LEN, D), 1.0, 6.0, ((0, 4), (1, 8))),
    }


@jax.custom_vjp
def low(v):
    return lax.optimization_barrier(v.astype(jnp.bfloat16)).astype(jnp.float32)

@jax.custom_vjp
def low_back(v):
    return v

def low_keep(v):
    return (low(v), None)

def low_pass(kept, grad):
    return (grad,)

def back_keep(v):
    return (v, None)

def back_low(kept, grad):
    return (low(grad),)
low.defvjp(low_keep, low_pass)
low_back.defvjp(back_keep, back_low)
EPSILON = 1e-06

def matmul_high(left_side, right_side):
    return jnp.dot(left_side, right_side, precision=lax.Precision.HIGHEST, preferred_element_type=jnp.float32)

def time_embed(buckets, model_width):
    half_width = model_width // 2
    frequency = jnp.exp(-math.log(10000.0) * jnp.arange(half_width, dtype=jnp.float32) / half_width)
    angles = buckets.astype(jnp.float32)[:, None] * frequency[None, :]
    return jnp.concatenate([jnp.cos(angles), jnp.sin(angles)], axis=1)

def selective_scan(step_size, driving, input_mix, output_mix, decay_rate):
    block_len = LEN // N_FSDP

    def block_run(hidden, pieces):

        def token_run(inner_state, row_values):
            step_row, drive_row, input_row, output_row = row_values
            inner_state = jnp.exp(step_row[None, :] * decay_rate) * inner_state + drive_row[None, :] * input_row[:, None]
            return (inner_state, lax.optimization_barrier(jnp.sum(output_row[:, None] * inner_state, axis=0)))
        return lax.scan(token_run, hidden, pieces)
    pieces = tuple((values.reshape((LEN // block_len, block_len) + values.shape[1:]) for values in (step_size, driving, input_mix, output_mix)))
    initial = jnp.zeros(decay_rate.shape, jnp.float32)
    _, outputs = lax.scan(jax.checkpoint(block_run), initial, pieces)
    return outputs.reshape(LEN, decay_rate.shape[1])

def direction_output(inner_x, mask_row, conv_taps, conv_shift, xproj, dt_matrix, dt_shift, log_rate, skip_row):
    kernel = conv_taps.shape[0]
    padded = jnp.concatenate([jnp.zeros((kernel - 1, inner_x.shape[1]), jnp.float32), inner_x], axis=0)
    pre_conv = conv_shift + sum((conv_taps[tap_index] * padded[tap_index:tap_index + LEN] for tap_index in range(kernel)))
    conv_out = low(jax.nn.silu(pre_conv) * mask_row[:, None])
    projected = low_back(matmul_high(conv_out, xproj))
    rank_part = low(projected[:, :R])
    input_mix = projected[:, R:R + N]
    output_mix = projected[:, R + N:]
    step_size = jax.nn.softplus(low_back(matmul_high(rank_part, dt_matrix)) + dt_shift)
    decay_rate = -jnp.exp(log_rate)
    return selective_scan(step_size, step_size * conv_out, input_mix, output_mix, decay_rate) + skip_row * conv_out

def slot_forward(params, row_tokens, mask_row, embed_row):
    ada_matrix, ada_shift, input_matrix, conv_taps, conv_shift, xproj, dt_matrix, dt_shift, log_rate, skip_rows, output_matrix = params
    condition = low(jax.nn.silu(embed_row))
    modulation = low_back(matmul_high(condition[None, :], ada_matrix)[0]) + ada_shift
    shift_mod = modulation[:D]
    scale_mod = modulation[D:2 * D]
    gate_mod = modulation[2 * D:]
    centered = row_tokens - lax.optimization_barrier(jnp.mean(row_tokens, axis=1, keepdims=True))
    normed = centered * lax.rsqrt(lax.optimization_barrier(jnp.mean(centered * centered, axis=1, keepdims=True)) + EPSILON)
    modulated_input = low((normed * (1.0 + scale_mod) + shift_mod) * mask_row[:, None])
    inner_projection = low_back(matmul_high(modulated_input, input_matrix))
    inner_x = inner_projection[:, :E]
    gate_z = inner_projection[:, E:]
    forward_y = direction_output(inner_x, mask_row, conv_taps[0], conv_shift[0], xproj[0], dt_matrix[0], dt_shift[0], log_rate[0], skip_rows[0])
    reverse_y = direction_output(inner_x[::-1], mask_row[::-1], conv_taps[1], conv_shift[1], xproj[1], dt_matrix[1], dt_shift[1], log_rate[1], skip_rows[1])[::-1]
    gated_output = low((forward_y + reverse_y) * jax.nn.silu(gate_z))
    branch_output = low_back(matmul_high(gated_output, output_matrix))
    return (row_tokens + gate_mod * branch_output) * mask_row[:, None]

def reference(tokens, item_bucket, slot_item, slot_live, slot_tokens, ada_weight, ada_bias, in_weight, conv_weight, conv_bias, xproj_weight, dt_weight, dt_bias, a_log, skip_gain, out_weight, cotangent):
    params = tuple((weight_arg.astype(jnp.float32) for weight_arg in (ada_weight, ada_bias, in_weight, conv_weight, conv_bias, xproj_weight, dt_weight, dt_bias, a_log, skip_gain, out_weight)))
    counts = slot_tokens * slot_live
    group_count = lax.optimization_barrier(jnp.sum(counts.reshape(GROUPS, SLOT_G), axis=1)).astype(jnp.float32)
    slot_share = jnp.repeat(group_count / jnp.sum(group_count), SLOT_G)
    masks = (jnp.arange(LEN, dtype=jnp.int32)[None, :] < counts[:, None]).astype(jnp.float32)
    embeds = time_embed(item_bucket[slot_item], D)
    zero_grads = tuple((jnp.zeros(weight_arg.shape, jnp.float32) for weight_arg in params))

    def one_slot(totals, pieces):
        row_tokens, row_cot, mask_row, embed_row, share_row = pieces
        result, pullback = jax.vjp(lambda weights, inputs: slot_forward(weights, inputs, mask_row, embed_row), params, row_tokens.astype(jnp.float32))
        weight_grads, input_grad = pullback(row_cot.astype(jnp.float32))
        totals = tuple((total_grad + share_row * new_grad for total_grad, new_grad in zip(totals, weight_grads)))
        return (totals, (result.astype(jnp.bfloat16), share_row * input_grad))
    grads, (layer_out, tokens_grad) = lax.scan(one_slot, zero_grads, (tokens, cotangent, masks, embeds, slot_share))
    return (layer_out, tokens_grad, grads[0], grads[1], grads[2], grads[3], grads[4], grads[5], grads[6], grads[7], grads[8], grads[9], grads[10])
```

```python
import functools
import math

import jax
import jax.numpy as jnp
from jax import lax
from jax.experimental import pallas as pl
from jax.experimental.pallas import tpu as pltpu
from jax.sharding import PartitionSpec as P

EPSILON = 1e-06
LANES = 128
ROWS = 8
BLOCK = 16
LOG2E = math.log2(math.e)
LN2 = math.log(2.0)
F32 = jnp.float32
BF16 = jnp.bfloat16
MIB = 1 << 20


def time_embed(buckets, model_width):
    half_width = model_width // 2
    frequency = jnp.exp(-math.log(10000.0) * jnp.arange(half_width, dtype=F32) / half_width)
    angles = buckets.astype(F32)[:, None] * frequency[None, :]
    return jnp.concatenate([jnp.cos(angles), jnp.sin(angles)], axis=1)


def silu_slope(values):
    sigmoid = jax.nn.sigmoid(values)
    return sigmoid * (1.0 + values * (1.0 - sigmoid))


def dot32(left, right, dims):
    return lax.dot_general(left, right, (dims, ((), ())), preferred_element_type=F32)


def spread_columns(proj_ref, first, count, out_ref):
    rows = proj_ref.shape[0]

    def block(i, carry):
        start = pl.multiple_of(i * ROWS, ROWS)
        turned = jnp.transpose(proj_ref[pl.ds(start, ROWS), :])
        for j in range(ROWS):
            column = turned[first : first + count, j : j + 1]
            out_ref[start + j] = jnp.broadcast_to(column, (count, LANES)).reshape(
                count // ROWS, ROWS, LANES
            )
        return carry

    lax.fori_loop(0, rows // ROWS, block, 0, unroll=True)


def sweep(length, backward, body, start):
    def block(i, carry):
        at = length // ROWS - 1 - i if backward else i
        first = pl.multiple_of(at * ROWS, ROWS)
        blocks = {}

        def row(ref, j):
            if id(ref) not in blocks:
                blocks[id(ref)] = ref[pl.ds(first, ROWS), :]
            rows = blocks[id(ref)]
            return [
                jnp.broadcast_to(rows[j : j + 1, k : k + LANES], (ROWS, LANES))[None]
                for k in range(0, rows.shape[1], LANES)
            ]

        for j in reversed(range(ROWS)) if backward else range(ROWS):
            carry = body(first + j, functools.partial(row, j=j), carry)
        return carry

    return lax.fori_loop(0, length // ROWS, block, start)


def pass_one(
    states, active, conv, proj, grad_y, dt_w, dt_b, decay, step, end, pull, total, drive, mix_b, mix_c
):
    slot, direction = pl.program_id(0), pl.program_id(1)
    length, channels = drive.shape
    chunks = channels // LANES
    halves = states // ROWS
    rank = proj.shape[1] - 2 * states

    @pl.when(active[slot] == 0)
    def _():
        step[...] = jnp.zeros_like(step)
        end[...] = jnp.zeros_like(end)
        pull[...] = jnp.zeros_like(pull)
        total[...] = jnp.zeros_like(total)

    @pl.when(active[slot] != 0)
    def _():
        pre = dot32(proj[...].astype(BF16), dt_w[direction], ((1,), (0,))) + dt_b[direction]
        steps = jnp.maximum(pre, 0.0) + jnp.log1p(jnp.exp(-jnp.abs(pre)))
        step[...] = steps
        drive[...] = steps * conv[...].astype(F32)
        total[...] = jnp.broadcast_to(jnp.sum(steps, axis=0, keepdims=True), total.shape)
        spread_columns(proj, rank, states, mix_b)
        spread_columns(proj, rank + states, states, mix_c)

        def token(t, row, carry):
            hidden, running, pulled = carry
            b, c = mix_b[t], mix_c[t]
            step_row, drive_row, grad_row = row(step), row(drive), row(grad_y)
            new = ([], [], [])
            for k in range(chunks):
                lanes = slice(k * LANES, (k + 1) * LANES)
                factor = jnp.exp2(step_row[k] * decay[direction, :, :, lanes])
                new[0].append(factor * hidden[k] + drive_row[k] * b)
                runs = running[k] * factor
                new[1].append(runs)
                new[2].append(pulled[k] + runs * (grad_row[k] * c))
            return tuple(tuple(part) for part in new)

        zero = jnp.zeros((halves, ROWS, LANES), F32)
        start = ((zero,) * chunks, (zero + 1.0,) * chunks, (zero,) * chunks)
        for backward in range(2):

            @pl.when(direction == backward)
            def _():
                hidden, _, pulled = sweep(length, backward, token, start)
                for k in range(chunks):
                    lanes = slice(k * LANES, (k + 1) * LANES)
                    end[:, :, lanes] = hidden[k]
                    pull[:, :, lanes] = pulled[k]


def pass_two(
    states,
    active,
    conv,
    proj,
    grad_y,
    step,
    entry,
    arrive,
    dt_w,
    decay,
    skip,
    tile_b,
    tile_c,
    sel,
    take_b,
    take_c,
    y,
    conv_grad,
    proj_grad,
    dtw_grad,
    dtb_grad,
    alog_grad,
    skip_grad,
    drive,
    mix,
    hid,
    gst,
    thd,
    mixed,
    sdec,
):
    slot, direction = pl.program_id(0), pl.program_id(1)
    length, channels = drive.shape
    chunks = channels // LANES
    halves = states // ROWS
    rank = proj.shape[1] - 2 * states
    wide = BLOCK * states

    @pl.when((slot == 0) & (direction == 0))
    def _():
        dtw_grad[...] = jnp.zeros_like(dtw_grad)
        dtb_grad[...] = jnp.zeros_like(dtb_grad)
        alog_grad[...] = jnp.zeros_like(alog_grad)
        skip_grad[...] = jnp.zeros_like(skip_grad)

    @pl.when(direction == 0)
    def _():
        y[...] = jnp.zeros_like(y)

    @pl.when(active[slot] == 0)
    def _():
        conv_grad[...] = jnp.zeros_like(conv_grad)
        proj_grad[...] = jnp.zeros_like(proj_grad)

    @pl.when(active[slot] != 0)
    def _():
        drive[...] = step[...] * conv[...].astype(F32)
        spread_columns(proj, rank, states, mix)
        forward = direction == 0
        first = jnp.where(forward, 0, length + 1)
        back = jnp.where(forward, 0, 2)
        start = []
        for k in range(chunks):
            lanes = slice(k * LANES, (k + 1) * LANES)
            value = entry[:, :, lanes]
            start.append(value)
            hid[first, :, lanes] = value.reshape(states, LANES).astype(BF16)

        def token(t, row, hidden):
            b = mix[t]
            step_row, drive_row = row(step), row(drive)
            new = []
            for k in range(chunks):
                lanes = slice(k * LANES, (k + 1) * LANES)
                factor = jnp.exp2(step_row[k] * decay[direction, :, :, lanes])
                value = factor * hidden[k] + drive_row[k] * b
                hid[t + 1, :, lanes] = value.reshape(states, LANES).astype(BF16)
                new.append(value)
            return tuple(new)

        def token_back(t, row, carry):
            carried, total = carry
            c = mix[t]
            step_row, grad_row = row(step), row(grad_y)
            news, sums = [], []
            for k in range(chunks):
                lanes = slice(k * LANES, (k + 1) * LANES)
                rate = decay[direction, :, :, lanes]
                factor = jnp.exp2(step_row[k] * rate)
                grad_state = grad_row[k] * c + carried[k]
                gst[t, :, lanes] = grad_state.reshape(states, LANES).astype(BF16)
                onward = factor * grad_state
                before = hid[t + back, :, lanes].astype(F32).reshape(halves, ROWS, LANES)
                through = onward * before
                sums.append(total[k] + through * step_row[k])
                thd[t, :, lanes] = (through * rate).reshape(states, LANES).astype(BF16)
                news.append(onward)
            return (tuple(news), tuple(sums))

        for backward in range(2):

            @pl.when(direction == backward)
            def _():
                sweep(length, backward, token, tuple(start))

        spread_columns(proj, rank + states, states, mix)
        zero = jnp.zeros((halves, ROWS, LANES), F32)
        begin = tuple(arrive[:, :, k * LANES : (k + 1) * LANES] for k in range(chunks))
        for backward in range(2):

            @pl.when(direction == backward)
            def _():
                _, sums = sweep(length, 1 - backward, token_back, (begin, (zero,) * chunks))
                for k in range(chunks):
                    lanes = slice(k * LANES, (k + 1) * LANES)
                    alog_grad[direction, :, :, lanes] += sums[k]

        proj_low = proj[...].astype(BF16)
        picked = sel[...]
        mix_b_rows = (dot32(proj_low, tile_b[...], ((1,), (0,))) * picked).astype(BF16)
        mix_c_rows = (dot32(proj_low, tile_c[...], ((1,), (0,))) * picked).astype(BF16)
        picked_low = picked.astype(BF16)
        for i in range(length // BLOCK):
            rows = slice(i * BLOCK, (i + 1) * BLOCK)
            after = slice(i * BLOCK + 1, (i + 1) * BLOCK + 1)
            h_rows = hid[after].reshape(wide, channels)
            g_rows = gst[rows].reshape(wide, channels)
            t_rows = thd[rows].reshape(wide, channels)
            y[rows, :] += dot32(mix_c_rows[rows], h_rows, ((1,), (0,)))
            mixed[rows, :] = dot32(mix_b_rows[rows], g_rows, ((1,), (0,)))
            sdec[rows, :] = dot32(picked_low[rows], t_rows, ((1,), (0,)))
            in_grad = dot32(drive[rows, :].astype(BF16), g_rows, ((1,), (1,)))
            out_grad = dot32(grad_y[rows, :].astype(BF16), h_rows, ((1,), (1,)))
            in_grad = (in_grad * picked[rows]).astype(BF16)
            out_grad = (out_grad * picked[rows]).astype(BF16)
            proj_grad[rows, :] = dot32(in_grad, take_b[...], ((1,), (0,))) + dot32(
                out_grad, take_c[...], ((1,), (0,))
            )

        conv_values = conv[...].astype(F32)
        steps = step[...]
        grads = grad_y[...]
        step_grad = conv_values * mixed[...] + LN2 * sdec[...]
        pre_grad = step_grad * (1.0 - jnp.exp(-steps))
        dtb_grad[direction] += jnp.sum(pre_grad, axis=0, keepdims=True)
        low = pre_grad.astype(BF16)
        proj_grad[...] += dot32(low, dt_w[direction], ((1,), (1,)))
        dtw_grad[direction] += dot32(jnp.transpose(proj[...]).astype(BF16), low, ((1,), (0,)))
        y[...] += skip[direction] * conv_values
        skip_grad[direction] += jnp.sum(grads * conv_values, axis=0, keepdims=True)
        conv_grad[...] = grads * skip[direction] + steps * mixed[...]


def whole(array):
    zeros = (0,) * array.ndim
    return pl.BlockSpec(array.shape, lambda s, d, a: zeros)


def scan_ends(active, conv, proj, grad_y, dt_w, dt_b, decay):
    slots, length, channels = grad_y.shape
    halves = decay.shape[1]
    width = proj.shape[3]
    states = halves * ROWS
    pair = lambda *tail: pl.BlockSpec((None, None) + tail, lambda s, d, a: (d, s) + (0,) * len(tail))
    state = (2, slots, halves, ROWS, channels)
    return pl.pallas_call(
        functools.partial(pass_one, states),
        grid_spec=pltpu.PrefetchScalarGridSpec(
            num_scalar_prefetch=1,
            grid=(slots, 2),
            in_specs=[
                pair(length, channels),
                pair(length, width),
                pl.BlockSpec((None, length, channels), lambda s, d, a: (s, 0, 0)),
                whole(dt_w),
                whole(dt_b),
                whole(decay),
            ],
            out_specs=[
                pair(length, channels),
                pair(halves, ROWS, channels),
                pair(halves, ROWS, channels),
                pair(ROWS, channels),
            ],
            scratch_shapes=[
                pltpu.VMEM((length, channels), F32),
                pltpu.VMEM((length, halves, ROWS, LANES), F32),
                pltpu.VMEM((length, halves, ROWS, LANES), F32),
            ],
        ),
        out_shape=[
            jax.ShapeDtypeStruct((2, slots, length, channels), F32),
            jax.ShapeDtypeStruct(state, F32),
            jax.ShapeDtypeStruct(state, F32),
            jax.ShapeDtypeStruct((2, slots, ROWS, channels), F32),
        ],
        compiler_params=pltpu.CompilerParams(vmem_limit_bytes=24 * MIB),
        name="scan_ends",
    )(active, conv, proj, grad_y, dt_w, dt_b, decay)


def scan_all(active, conv, proj, grad_y, step, entry, arrive, dt_w, decay, skip):
    slots, length, channels = grad_y.shape
    halves = decay.shape[1]
    width = proj.shape[3]
    states = halves * ROWS
    wide = BLOCK * states
    rank = width - 2 * states
    column = jnp.arange(width)[:, None]
    lane = jnp.arange(wide)[None, :]
    tile_b = (column == rank + lane % states).astype(BF16)
    tile_c = (column == rank + states + lane % states).astype(BF16)
    sel = (jnp.arange(length)[:, None] % BLOCK == lane // states).astype(F32)
    pair = lambda *tail: pl.BlockSpec((None, None) + tail, lambda s, d, a: (d, s) + (0,) * len(tail))
    one = pl.BlockSpec((None, length, channels), lambda s, d, a: (s, 0, 0))
    constants = (dt_w, decay, skip, tile_b, tile_c, sel, tile_b.T, tile_c.T)
    sums = (
        jax.ShapeDtypeStruct((2, width, channels), F32),
        jax.ShapeDtypeStruct((2, 1, channels), F32),
        jax.ShapeDtypeStruct((2, halves, ROWS, channels), F32),
        jax.ShapeDtypeStruct((2, 1, channels), F32),
    )
    return pl.pallas_call(
        functools.partial(pass_two, states),
        grid_spec=pltpu.PrefetchScalarGridSpec(
            num_scalar_prefetch=1,
            grid=(slots, 2),
            in_specs=[
                pair(length, channels),
                pair(length, width),
                one,
                pair(length, channels),
                pair(halves, ROWS, channels),
                pair(halves, ROWS, channels),
            ]
            + [whole(c) for c in constants],
            out_specs=[one, pair(length, channels), pair(length, width)] + [whole(c) for c in sums],
            scratch_shapes=[
                pltpu.VMEM((length, channels), F32),
                pltpu.VMEM((length, halves, ROWS, LANES), F32),
                pltpu.VMEM((length + 2, states, channels), BF16),
                pltpu.VMEM((length, states, channels), BF16),
                pltpu.VMEM((length, states, channels), BF16),
                pltpu.VMEM((length, channels), F32),
                pltpu.VMEM((length, channels), F32),
            ],
        ),
        out_shape=[
            jax.ShapeDtypeStruct((slots, length, channels), F32),
            jax.ShapeDtypeStruct((2, slots, length, channels), F32),
            jax.ShapeDtypeStruct((2, slots, length, width), F32),
        ]
        + list(sums),
        compiler_params=pltpu.CompilerParams(vmem_limit_bytes=40 * MIB),
        name="scan_all",
    )(active, conv, proj, grad_y, step, entry, arrive, *constants)


def chain(count, end, pull, total, decay, entry, arrive, held, send_sem, recv_sem):
    mine = lax.axis_index("fsdp")
    slots = end.shape[1]
    mesh_id = pl.DeviceIdType.MESH
    after, before = lax.rem(mine + 1, count), lax.rem(mine + count - 1, count)
    barrier = pltpu.get_barrier_semaphore()
    for other in (after, before):
        pl.semaphore_signal(barrier, inc=1, device_id={"fsdp": other}, device_id_type=mesh_id)
    pl.semaphore_wait(barrier, 2)
    kinds = (
        ((entry, end, 0), (arrive, pull, 1), mine > 0, mine < count - 1, after),
        ((entry, end, 1), (arrive, pull, 0), mine < count - 1, mine > 0, before),
    )

    def copies(which, s):
        first, second, _, _, target = kinds[which]
        made = []
        for j, (landing, _, d) in enumerate((first, second)):
            made.append(
                pltpu.make_async_remote_copy(
                    src_ref=held.at[which, j, s],
                    dst_ref=landing.at[d, s],
                    send_sem=send_sem.at[which, j, s],
                    recv_sem=recv_sem.at[which, j, s],
                    device_id={"fsdp": target},
                    device_id_type=mesh_id,
                )
            )
        return made

    lags = (mine, count - 1 - mine)

    def wave(turn, carry):
        for which in range(2):
            first, second, gets, sends, _ = kinds[which]
            s = turn - lags[which]
            here = (s >= 0) & (s < slots)

            @pl.when(here & gets)
            def _():
                for copy in copies(which, s):
                    copy.wait_recv()

            @pl.when(here & jnp.logical_not(gets))
            def _():
                for landing, _, d in (first, second):
                    landing[d, s] = jnp.zeros(landing.shape[2:], F32)

            @pl.when(here & sends)
            def _():
                for j, (landing, local, d) in enumerate((first, second)):
                    through = jnp.exp2(decay[d] * total[d, s][None])
                    held[which, j, s] = through * landing[d, s] + local[d, s]
                for copy in copies(which, s):
                    copy.start()

        return carry

    lax.fori_loop(0, slots + count - 1, wave, 0)

    def drain(s, carry):
        for which in range(2):

            @pl.when(kinds[which][3])
            def _():
                for copy in copies(which, s):
                    copy.wait_send()

        return carry

    lax.fori_loop(0, slots, drain, 0)


def pass_states(end, pull, total, decay):
    _, slots, halves, rows, channels = end.shape
    return pl.pallas_call(
        functools.partial(chain, lax.axis_size("fsdp")),
        in_specs=[pl.BlockSpec(memory_space=pltpu.VMEM)] * 4,
        out_specs=[pl.BlockSpec(memory_space=pltpu.VMEM)] * 2,
        out_shape=[jax.ShapeDtypeStruct(end.shape, F32)] * 2,
        scratch_shapes=[
            pltpu.VMEM((2, 2, slots, halves, rows, channels), F32),
            pltpu.SemaphoreType.DMA((2, 2, slots)),
            pltpu.SemaphoreType.DMA((2, 2, slots)),
        ],
        compiler_params=pltpu.CompilerParams(
            collective_id=0, has_side_effects=True, vmem_limit_bytes=40 * MIB
        ),
        name="pass_states",
    )(end, pull, total, decay)


def to_owner(groups, parts):
    ratio = parts // groups
    pairs = []
    for g in range(groups):
        for f in range(parts):
            pairs.append((g * parts + f, (f // ratio) * parts + groups * (f % ratio) + g))
    return pairs


def on_device(
    tokens,
    item_bucket,
    slot_item,
    slot_live,
    slot_tokens,
    ada_weight,
    ada_bias,
    in_weight,
    conv_weight,
    conv_bias,
    xproj_weight,
    dt_weight,
    dt_bias,
    a_log,
    skip_gain,
    out_weight,
    cotangent,
):
    own_slots, length, model_width = tokens.shape
    groups, parts = lax.axis_size("group"), lax.axis_size("fsdp")
    g, f = lax.axis_index("group"), lax.axis_index("fsdp")
    slots = own_slots * groups
    inner_width = in_weight.shape[1] // 2
    channels = inner_width // groups
    kernel = conv_weight.shape[1]
    halo = kernel - 1
    rank_width = dt_weight.shape[1]
    width = xproj_weight.shape[2]
    states = (width - rank_width) // 2

    matches = slot_item[:, None] == jnp.arange(item_bucket.shape[0], dtype=jnp.int32)[None, :]
    own_buckets = jnp.sum(jnp.where(matches, item_bucket[None, :], 0), axis=1)
    facts = lax.all_gather(jnp.stack([slot_tokens * slot_live, own_buckets]), "group", axis=1, tiled=True)
    counts, buckets = facts[0], facts[1]
    group_counts = jnp.sum(counts.reshape(groups, own_slots), axis=1).astype(F32)
    share = jnp.repeat(group_counts / jnp.sum(group_counts), own_slots)
    positions = f * length + jnp.concatenate(
        [jnp.arange(length), jnp.arange(-halo, 0), length + jnp.arange(halo), jnp.full((ROWS - 2 * halo,), -length * parts)]
    ).astype(jnp.int32)
    mask_all = ((positions[None, :] >= 0) & (positions[None, :] < counts[:, None])).astype(F32)
    mask = mask_all[:, :length]
    active = (counts > f * length).astype(jnp.int32)
    own_mask = lax.dynamic_slice_in_dim(mask, g * own_slots, own_slots, 0)[:, :, None]
    own_share = lax.dynamic_slice_in_dim(share, g * own_slots, own_slots, 0)[:, None, None]

    edges = [(i, i + 1) for i in range(parts - 1)]
    before = lax.ppermute(tokens[:, length - halo :], "fsdp", edges)
    after = lax.ppermute(tokens[:, :halo], "fsdp", [(j, i) for i, j in edges])
    padding = jnp.zeros((own_slots, ROWS - 2 * halo, model_width), tokens.dtype)
    extended_tokens = jnp.concatenate([tokens, before, after, padding], axis=1)
    all_tokens = lax.all_gather(extended_tokens, "group", axis=0, tiled=True)
    all_cotangent = lax.all_gather(cotangent, "group", axis=0, tiled=True)

    in_own = lax.dynamic_slice_in_dim(
        in_weight.reshape(in_weight.shape[0], 2, groups, channels), g, 1, 2
    ).reshape(in_weight.shape[0], 2 * channels)
    in_matrix = lax.all_gather(in_own, "fsdp", axis=0, tiled=True)
    shard = out_weight.shape[0]
    small = jnp.concatenate(
        [
            dt_weight.reshape(2 * rank_width, shard),
            a_log.reshape(2 * states, shard),
            conv_weight.reshape(2 * kernel, shard),
            conv_bias,
            dt_bias,
            skip_gain,
        ],
        axis=0,
    )
    small_rows = small.shape[0]
    small_pad = -small_rows % LANES
    packed = jnp.concatenate(
        [
            out_weight,
            xproj_weight[0],
            xproj_weight[1],
            jnp.pad(small.T, ((0, 0), (0, small_pad))),
        ],
        axis=1,
    )
    piece = shard // groups
    sent = lax.ppermute(
        lax.dynamic_slice_in_dim(packed, g * piece, piece, 0),
        ("group", "fsdp"),
        to_owner(groups, parts),
    )
    mine = lax.all_gather(sent, "fsdp", axis=0, tiled=True)
    out_matrix = mine[:, :model_width]
    xproj = [mine[:, model_width + d * width : model_width + (d + 1) * width] for d in range(2)]
    rest = mine[:, model_width + 2 * width :].T
    edge = 0

    def take(rows):
        nonlocal edge
        edge += rows
        return rest[edge - rows : edge]

    dt_matrix = jnp.pad(
        take(2 * rank_width).reshape(2, rank_width, channels), ((0, 0), (0, width - rank_width), (0, 0))
    )
    rate = -jnp.exp(take(2 * states).astype(F32)).reshape(2, states // ROWS, ROWS, channels)
    taps = take(2 * kernel).reshape(2, kernel, channels).astype(F32)
    conv_shift = take(2).astype(F32)
    dt_shift = take(2).astype(F32).reshape(2, 1, channels)
    skip = take(2).astype(F32).reshape(2, 1, channels)
    decay = rate * LOG2E

    condition = jax.nn.silu(time_embed(buckets, model_width)).astype(BF16)
    modulation = lax.all_gather(
        jnp.dot(condition, ada_weight, preferred_element_type=F32) + ada_bias.astype(F32),
        "fsdp",
        axis=1,
        tiled=True,
    )
    shift_mod = modulation[:, None, :model_width]
    scale_mod = modulation[:, None, model_width : 2 * model_width]
    gate_mod = modulation[:, None, 2 * model_width :]

    def normalise(values):
        inputs = values.astype(F32)
        centered = inputs - jnp.mean(inputs, axis=2, keepdims=True)
        inv_std = lax.rsqrt(jnp.mean(centered * centered, axis=2, keepdims=True) + EPSILON)
        return (inputs, centered * inv_std, inv_std)

    normed = normalise(all_tokens)[1]
    modulated_all = ((normed * (1.0 + scale_mod) + shift_mod) * mask_all[:, :, None]).astype(BF16)
    modulated = modulated_all[:, :length]
    inner_all = jnp.einsum("sld,dc->slc", modulated_all, in_matrix, preferred_element_type=F32)
    inner_x = inner_all[:, :, :channels]
    gate_z = inner_all[:, :length, channels:]
    extended = jnp.concatenate(
        [inner_x[:, length : length + halo], inner_x[:, :length], inner_x[:, length + halo : length + 2 * halo]],
        axis=1,
    )
    pre, conv_out, projected = [], [], []
    for d in range(2):
        value = conv_shift[d]
        for k in range(kernel):
            row = k if d == 0 else 2 * halo - k
            value = value + taps[d, k] * extended[:, row : row + length]
        pre.append(value)
        conv_out.append((jax.nn.silu(value) * mask[:, :, None]).astype(BF16))
        projected.append(
            jnp.einsum("slc,ck->slk", conv_out[d], xproj[d], preferred_element_type=F32)
        )
    conv_out = jnp.stack(conv_out)
    proj = lax.psum(jnp.stack(projected), "group")

    grad_in_all = all_cotangent.astype(F32) * (mask * share[:, None])[:, :, None]
    branch_gradient = (grad_in_all * gate_mod).astype(BF16)
    grad_gated = jnp.einsum("sld,cd->slc", branch_gradient, out_matrix, preferred_element_type=F32)
    grad_y = grad_gated * jax.nn.silu(gate_z)

    step, end, pull, total = scan_ends(active, conv_out, proj, grad_y, dt_matrix, dt_shift, decay)
    entry, arrive = pass_states(end, pull, total, decay)
    y, conv_grad, proj_part, dtw_grad, dtb_grad, decay_grad, skip_grad = scan_all(
        active, conv_out, proj, grad_y, step, entry, arrive, dt_matrix, decay, skip
    )
    proj_grad = lax.psum(proj_part, "group").astype(BF16)
    alog_grad = (decay_grad * rate).reshape(2 * states, channels)

    gated_output = (y * jax.nn.silu(gate_z)).astype(BF16)
    branch_part = jnp.einsum("slc,cd->sld", gated_output, out_matrix, preferred_element_type=F32)
    branch = lax.psum_scatter(
        branch_part.astype(BF16), "group", scatter_dimension=0, tiled=True
    ).astype(F32)
    own_gate = lax.dynamic_slice_in_dim(gate_mod, g * own_slots, own_slots, 0)
    own_scale = lax.dynamic_slice_in_dim(scale_mod, g * own_slots, own_slots, 0)
    own_inputs, own_normed, own_inv = normalise(tokens)
    layer_out = ((own_inputs + own_gate * branch) * own_mask).astype(BF16)
    grad_in = cotangent.astype(F32) * own_mask * own_share
    grad_gate = jnp.sum(grad_in * branch, axis=1)
    outward = jnp.einsum("slc,sld->cd", gated_output, branch_gradient, preferred_element_type=F32)
    grad_z = grad_gated * y * silu_slope(gate_z)

    pre_grads, conv_grads, convb_grads, xproj_grads = [], [], [], []
    for d in range(2):
        into = conv_grad[d] + jnp.einsum(
            "slk,ck->slc", proj_grad[d], xproj[d], preferred_element_type=F32
        )
        pre_grad = into * mask[:, :, None] * silu_slope(pre[d])
        xproj_grads.append(
            jnp.einsum("slc,slk->ck", conv_out[d], proj_grad[d], preferred_element_type=F32)
        )
        convb_grads.append(jnp.sum(pre_grad, axis=(0, 1)))
        for k in range(kernel):
            row = k if d == 0 else 2 * halo - k
            conv_grads.append(jnp.sum(pre_grad * extended[:, row : row + length], axis=(0, 1)))
        pre_grads.append(pre_grad)
    ahead = lax.ppermute(pre_grads[0][:, :halo], "fsdp", [(j, i) for i, j in edges])
    behind = lax.ppermute(pre_grads[1][:, length - halo :], "fsdp", edges)
    ahead_rows = jnp.concatenate([pre_grads[0], ahead], axis=1)
    behind_rows = jnp.concatenate([behind, pre_grads[1]], axis=1)
    grad_x = jnp.zeros(gate_z.shape, F32)
    for k in range(kernel):
        grad_x = grad_x + taps[0, k] * ahead_rows[:, halo - k : halo - k + length]
        grad_x = grad_x + taps[1, k] * behind_rows[:, k : k + length]
    inner_gradient = jnp.concatenate([grad_x, grad_z], axis=2).astype(BF16)
    grad_mod_part = jnp.einsum(
        "slc,dc->sld", inner_gradient, in_matrix, preferred_element_type=F32
    )
    grad_mod = (
        lax.psum_scatter(grad_mod_part.astype(BF16), "group", scatter_dimension=0, tiled=True).astype(F32)
        * own_mask
    )
    inward = jnp.einsum("sld,slc->dc", modulated, inner_gradient, preferred_element_type=F32)

    grad_shift = jnp.sum(grad_mod, axis=1)
    grad_scale = jnp.sum(grad_mod * own_normed, axis=1)
    grad_normed = grad_mod * (1.0 + own_scale)
    grad_ln = own_inv * (
        grad_normed
        - jnp.mean(grad_normed, axis=2, keepdims=True)
        - own_normed * jnp.mean(grad_normed * own_normed, axis=2, keepdims=True)
    )
    tokens_grad = grad_in + grad_ln

    mod_part = jnp.concatenate([grad_shift, grad_scale, grad_gate], axis=1)
    mod_slice = lax.psum_scatter(mod_part, "fsdp", scatter_dimension=1, tiled=True)
    mod_all = lax.all_gather(mod_slice, "group", axis=0, tiled=True)
    ada_grad = jnp.einsum("sd,sk->dk", condition, mod_all.astype(BF16), preferred_element_type=F32)
    adab_grad = jnp.sum(mod_all, axis=0)

    small_grads = jnp.concatenate(
        [
            dtw_grad[:, :rank_width].reshape(2 * rank_width, channels),
            alog_grad,
            jnp.stack(conv_grads),
            jnp.stack(convb_grads),
            dtb_grad.reshape(2, channels),
            skip_grad.reshape(2, channels),
        ],
        axis=0,
    )
    packed_grads = jnp.concatenate(
        [outward, xproj_grads[0], xproj_grads[1], jnp.pad(small_grads.T, ((0, 0), (0, small_pad)))],
        axis=1,
    ).astype(BF16)
    packed_piece = lax.psum_scatter(packed_grads, "fsdp", scatter_dimension=0, tiled=True)
    packed_piece = lax.ppermute(
        packed_piece, ("group", "fsdp"), [(j, i) for i, j in to_owner(groups, parts)]
    )
    packed_own = lax.all_gather(packed_piece, "group", axis=0, tiled=True).astype(F32)
    out_grad = packed_own[:, :model_width]
    xproj_grad = jnp.stack(
        [packed_own[:, model_width + d * width : model_width + (d + 1) * width] for d in range(2)]
    )
    rest_grads = packed_own[:, model_width + 2 * width :].T
    sizes = [2 * rank_width, 2 * states, 2 * kernel, 2, 2, 2]
    cuts = [sum(sizes[:i]) for i in range(len(sizes) + 1)]
    dtw_out, alog_out, conv_w_out, conv_b_out, dtb_out, skip_out = [
        rest_grads[cuts[i] : cuts[i + 1]] for i in range(len(sizes))
    ]
    inward_piece = lax.psum_scatter(inward.astype(BF16), "fsdp", scatter_dimension=0, tiled=True)
    inward_all = lax.all_gather(inward_piece, "group", axis=0)
    in_grad = (
        inward_all.reshape(groups, in_weight.shape[0], 2, channels)
        .transpose(1, 2, 0, 3)
        .reshape(in_weight.shape)
        .astype(F32)
    )
    return (
        layer_out,
        tokens_grad,
        ada_grad,
        adab_grad,
        in_grad,
        conv_w_out.reshape(2, kernel, shard),
        conv_b_out,
        xproj_grad,
        dtw_out.reshape(2, rank_width, shard),
        dtb_out,
        alog_out.reshape(2, states, shard),
        skip_out,
        out_grad,
    )


def solution(mesh):
    in_specs = (
        P("group", "fsdp", None),
        P(),
        P("group"),
        P("group"),
        P("group"),
        P(None, "fsdp"),
        P("fsdp"),
        P("fsdp", None),
        P(None, None, "fsdp"),
        P(None, "fsdp"),
        P(None, "fsdp", None),
        P(None, None, "fsdp"),
        P(None, "fsdp"),
        P(None, None, "fsdp"),
        P(None, "fsdp"),
        P("fsdp", None),
        P("group", "fsdp", None),
    )
    out_specs = (
        P("group", "fsdp", None),
        P("group", "fsdp", None),
        P(None, "fsdp"),
        P("fsdp"),
        P("fsdp", None),
        P(None, None, "fsdp"),
        P(None, "fsdp"),
        P(None, "fsdp", None),
        P(None, None, "fsdp"),
        P(None, "fsdp"),
        P(None, None, "fsdp"),
        P(None, "fsdp"),
        P("fsdp", None),
    )
    return jax.shard_map(
        on_device, mesh=mesh, in_specs=in_specs, out_specs=out_specs, check_vma=False
    )
```

```python
import functools
import math

import jax
import jax.numpy as jnp
from jax import lax
from jax.experimental import pallas as pl
from jax.experimental.pallas import tpu as pltpu
from jax.sharding import PartitionSpec as P

EPSILON = 1e-06
LANES = 128
ROWS = 8
BLOCK = 16
LOG2E = math.log2(math.e)
LN2 = math.log(2.0)
F32 = jnp.float32
BF16 = jnp.bfloat16
MIB = 1 << 20


def time_embed(buckets, model_width):
    half_width = model_width // 2
    frequency = jnp.exp(-math.log(10000.0) * jnp.arange(half_width, dtype=F32) / half_width)
    angles = buckets.astype(F32)[:, None] * frequency[None, :]
    return jnp.concatenate([jnp.cos(angles), jnp.sin(angles)], axis=1)


def silu_slope(values):
    sigmoid = jax.nn.sigmoid(values)
    return sigmoid * (1.0 + values * (1.0 - sigmoid))


def dot32(left, right, dims):
    return lax.dot_general(left, right, (dims, ((), ())), preferred_element_type=F32)


def spread_columns(proj_ref, first, count, out_ref):
    rows = proj_ref.shape[0]

    def block(i, carry):
        start = pl.multiple_of(i * ROWS, ROWS)
        turned = jnp.transpose(proj_ref[pl.ds(start, ROWS), :])
        for j in range(ROWS):
            column = turned[first : first + count, j : j + 1]
            out_ref[start + j] = jnp.broadcast_to(column, (count, LANES)).reshape(
                count // ROWS, ROWS, LANES
            )
        return carry

    lax.fori_loop(0, rows // ROWS, block, 0, unroll=True)


def sweep(length, backward, body, start):
    def block(i, carry):
        at = length // ROWS - 1 - i if backward else i
        first = pl.multiple_of(at * ROWS, ROWS)
        blocks = {}

        def row(ref, j):
            if id(ref) not in blocks:
                blocks[id(ref)] = ref[pl.ds(first, ROWS), :]
            rows = blocks[id(ref)]
            return [
                jnp.broadcast_to(rows[j : j + 1, k : k + LANES], (ROWS, LANES))[None]
                for k in range(0, rows.shape[1], LANES)
            ]

        for j in reversed(range(ROWS)) if backward else range(ROWS):
            carry = body(first + j, functools.partial(row, j=j), carry)
        return carry

    return lax.fori_loop(0, length // ROWS, block, start)


def pass_one(
    states, active, conv, proj, grad_y, dt_w, dt_b, decay, step, end, pull, total, drive, mix_b, mix_c
):
    slot, direction = pl.program_id(0), pl.program_id(1)
    length, channels = drive.shape
    chunks = channels // LANES
    halves = states // ROWS
    rank = proj.shape[1] - 2 * states

    @pl.when(active[slot] == 0)
    def _():
        step[...] = jnp.zeros_like(step)
        end[...] = jnp.zeros_like(end)
        pull[...] = jnp.zeros_like(pull)
        total[...] = jnp.zeros_like(total)

    @pl.when(active[slot] != 0)
    def _():
        pre = dot32(proj[...].astype(BF16), dt_w[direction], ((1,), (0,))) + dt_b[direction]
        steps = jnp.maximum(pre, 0.0) + jnp.log1p(jnp.exp(-jnp.abs(pre)))
        step[...] = steps
        drive[...] = steps * conv[...].astype(F32)
        total[...] = jnp.broadcast_to(jnp.sum(steps, axis=0, keepdims=True), total.shape)
        spread_columns(proj, rank, states, mix_b)
        spread_columns(proj, rank + states, states, mix_c)

        def token(t, row, carry):
            hidden, running, pulled = carry
            b, c = mix_b[t], mix_c[t]
            step_row, drive_row, grad_row = row(step), row(drive), row(grad_y)
            new = ([], [], [])
            for k in range(chunks):
                lanes = slice(k * LANES, (k + 1) * LANES)
                factor = jnp.exp2(step_row[k] * decay[direction, :, :, lanes])
                new[0].append(factor * hidden[k] + drive_row[k] * b)
                runs = running[k] * factor
                new[1].append(runs)
                new[2].append(pulled[k] + runs * (grad_row[k] * c))
            return tuple(tuple(part) for part in new)

        zero = jnp.zeros((halves, ROWS, LANES), F32)
        start = ((zero,) * chunks, (zero + 1.0,) * chunks, (zero,) * chunks)
        for backward in range(2):

            @pl.when(direction == backward)
            def _():
                hidden, _, pulled = sweep(length, backward, token, start)
                for k in range(chunks):
                    lanes = slice(k * LANES, (k + 1) * LANES)
                    end[:, :, lanes] = hidden[k]
                    pull[:, :, lanes] = pulled[k]


def pass_two(
    states,
    active,
    conv,
    proj,
    grad_y,
    step,
    entry,
    arrive,
    dt_w,
    decay,
    skip,
    tile_b,
    tile_c,
    sel,
    take_b,
    take_c,
    y,
    conv_grad,
    proj_grad,
    dtw_grad,
    dtb_grad,
    alog_grad,
    skip_grad,
    drive,
    mix,
    hid,
    gst,
    thd,
    mixed,
    sdec,
):
    slot, direction = pl.program_id(0), pl.program_id(1)
    length, channels = drive.shape
    chunks = channels // LANES
    halves = states // ROWS
    rank = proj.shape[1] - 2 * states
    wide = BLOCK * states

    @pl.when((slot == 0) & (direction == 0))
    def _():
        dtw_grad[...] = jnp.zeros_like(dtw_grad)
        dtb_grad[...] = jnp.zeros_like(dtb_grad)
        alog_grad[...] = jnp.zeros_like(alog_grad)
        skip_grad[...] = jnp.zeros_like(skip_grad)

    @pl.when(direction == 0)
    def _():
        y[...] = jnp.zeros_like(y)

    @pl.when(active[slot] == 0)
    def _():
        conv_grad[...] = jnp.zeros_like(conv_grad)
        proj_grad[...] = jnp.zeros_like(proj_grad)

    @pl.when(active[slot] != 0)
    def _():
        drive[...] = step[...] * conv[...].astype(F32)
        spread_columns(proj, rank, states, mix)
        forward = direction == 0
        first = jnp.where(forward, 0, length + 1)
        back = jnp.where(forward, 0, 2)
        start = []
        for k in range(chunks):
            lanes = slice(k * LANES, (k + 1) * LANES)
            value = entry[:, :, lanes]
            start.append(value)
            hid[first, :, lanes] = value.reshape(states, LANES).astype(BF16)

        def token(t, row, hidden):
            b = mix[t]
            step_row, drive_row = row(step), row(drive)
            new = []
            for k in range(chunks):
                lanes = slice(k * LANES, (k + 1) * LANES)
                factor = jnp.exp2(step_row[k] * decay[direction, :, :, lanes])
                value = factor * hidden[k] + drive_row[k] * b
                hid[t + 1, :, lanes] = value.reshape(states, LANES).astype(BF16)
                new.append(value)
            return tuple(new)

        def token_back(t, row, carry):
            carried, total = carry
            c = mix[t]
            step_row, grad_row = row(step), row(grad_y)
            news, sums = [], []
            for k in range(chunks):
                lanes = slice(k * LANES, (k + 1) * LANES)
                rate = decay[direction, :, :, lanes]
                factor = jnp.exp2(step_row[k] * rate)
                grad_state = grad_row[k] * c + carried[k]
                gst[t, :, lanes] = grad_state.reshape(states, LANES).astype(BF16)
                onward = factor * grad_state
                before = hid[t + back, :, lanes].astype(F32).reshape(halves, ROWS, LANES)
                through = onward * before
                sums.append(total[k] + through * step_row[k])
                thd[t, :, lanes] = (through * rate).reshape(states, LANES).astype(BF16)
                news.append(onward)
            return (tuple(news), tuple(sums))

        for backward in range(2):

            @pl.when(direction == backward)
            def _():
                sweep(length, backward, token, tuple(start))

        spread_columns(proj, rank + states, states, mix)
        zero = jnp.zeros((halves, ROWS, LANES), F32)
        begin = tuple(arrive[:, :, k * LANES : (k + 1) * LANES] for k in range(chunks))
        for backward in range(2):

            @pl.when(direction == backward)
            def _():
                _, sums = sweep(length, 1 - backward, token_back, (begin, (zero,) * chunks))
                for k in range(chunks):
                    lanes = slice(k * LANES, (k + 1) * LANES)
                    alog_grad[direction, :, :, lanes] += sums[k]

        proj_low = proj[...].astype(BF16)
        picked = sel[...]
        mix_b_rows = (dot32(proj_low, tile_b[...], ((1,), (0,))) * picked).astype(BF16)
        mix_c_rows = (dot32(proj_low, tile_c[...], ((1,), (0,))) * picked).astype(BF16)
        picked_low = picked.astype(BF16)
        for i in range(length // BLOCK):
            rows = slice(i * BLOCK, (i + 1) * BLOCK)
            after = slice(i * BLOCK + 1, (i + 1) * BLOCK + 1)
            h_rows = hid[after].reshape(wide, channels)
            g_rows = gst[rows].reshape(wide, channels)
            t_rows = thd[rows].reshape(wide, channels)
            y[rows, :] += dot32(mix_c_rows[rows], h_rows, ((1,), (0,)))
            mixed[rows, :] = dot32(mix_b_rows[rows], g_rows, ((1,), (0,)))
            sdec[rows, :] = dot32(picked_low[rows], t_rows, ((1,), (0,)))
            in_grad = dot32(drive[rows, :].astype(BF16), g_rows, ((1,), (1,)))
            out_grad = dot32(grad_y[rows, :].astype(BF16), h_rows, ((1,), (1,)))
            in_grad = (in_grad * picked[rows]).astype(BF16)
            out_grad = (out_grad * picked[rows]).astype(BF16)
            proj_grad[rows, :] = dot32(in_grad, take_b[...], ((1,), (0,))) + dot32(
                out_grad, take_c[...], ((1,), (0,))
            )

        conv_values = conv[...].astype(F32)
        steps = step[...]
        grads = grad_y[...]
        step_grad = conv_values * mixed[...] + LN2 * sdec[...]
        pre_grad = step_grad * (1.0 - jnp.exp(-steps))
        dtb_grad[direction] += jnp.sum(pre_grad, axis=0, keepdims=True)
        low = pre_grad.astype(BF16)
        proj_grad[...] += dot32(low, dt_w[direction], ((1,), (1,)))
        dtw_grad[direction] += dot32(jnp.transpose(proj[...]).astype(BF16), low, ((1,), (0,)))
        y[...] += skip[direction] * conv_values
        skip_grad[direction] += jnp.sum(grads * conv_values, axis=0, keepdims=True)
        conv_grad[...] = grads * skip[direction] + steps * mixed[...]


def whole(array):
    zeros = (0,) * array.ndim
    return pl.BlockSpec(array.shape, lambda s, d, a: zeros)


def scan_ends(active, conv, proj, grad_y, dt_w, dt_b, decay):
    slots, length, channels = grad_y.shape
    halves = decay.shape[1]
    width = proj.shape[3]
    states = halves * ROWS
    turn = lambda *tail: pl.BlockSpec((None, None) + tail, lambda s, d, a: (s, d) + (0,) * len(tail))
    pair = lambda *tail: pl.BlockSpec((None, None) + tail, lambda s, d, a: (d, s) + (0,) * len(tail))
    state = (2, slots, halves, ROWS, channels)
    return pl.pallas_call(
        functools.partial(pass_one, states),
        grid_spec=pltpu.PrefetchScalarGridSpec(
            num_scalar_prefetch=1,
            grid=(slots, 2),
            in_specs=[
                pair(length, channels),
                turn(length, width),
                pl.BlockSpec((None, length, channels), lambda s, d, a: (s, 0, 0)),
                whole(dt_w),
                whole(dt_b),
                whole(decay),
            ],
            out_specs=[
                pair(length, channels),
                pair(halves, ROWS, channels),
                pair(halves, ROWS, channels),
                pair(ROWS, channels),
            ],
            scratch_shapes=[
                pltpu.VMEM((length, channels), F32),
                pltpu.VMEM((length, halves, ROWS, LANES), F32),
                pltpu.VMEM((length, halves, ROWS, LANES), F32),
            ],
        ),
        out_shape=[
            jax.ShapeDtypeStruct((2, slots, length, channels), F32),
            jax.ShapeDtypeStruct(state, F32),
            jax.ShapeDtypeStruct(state, F32),
            jax.ShapeDtypeStruct((2, slots, ROWS, channels), F32),
        ],
        compiler_params=pltpu.CompilerParams(vmem_limit_bytes=24 * MIB),
        name="scan_ends",
    )(active, conv, proj, grad_y, dt_w, dt_b, decay)


def scan_all(active, conv, proj, grad_y, step, entry, arrive, dt_w, decay, skip):
    slots, length, channels = grad_y.shape
    halves = decay.shape[1]
    width = proj.shape[3]
    states = halves * ROWS
    turn = lambda *tail: pl.BlockSpec((None, None) + tail, lambda s, d, a: (s, d) + (0,) * len(tail))
    wide = BLOCK * states
    rank = width - 2 * states
    column = jnp.arange(width)[:, None]
    lane = jnp.arange(wide)[None, :]
    tile_b = (column == rank + lane % states).astype(BF16)
    tile_c = (column == rank + states + lane % states).astype(BF16)
    sel = (jnp.arange(length)[:, None] % BLOCK == lane // states).astype(F32)
    pair = lambda *tail: pl.BlockSpec((None, None) + tail, lambda s, d, a: (d, s) + (0,) * len(tail))
    one = pl.BlockSpec((None, length, channels), lambda s, d, a: (s, 0, 0))
    constants = (dt_w, decay, skip, tile_b, tile_c, sel, tile_b.T, tile_c.T)
    sums = (
        jax.ShapeDtypeStruct((2, width, channels), F32),
        jax.ShapeDtypeStruct((2, 1, channels), F32),
        jax.ShapeDtypeStruct((2, halves, ROWS, channels), F32),
        jax.ShapeDtypeStruct((2, 1, channels), F32),
    )
    return pl.pallas_call(
        functools.partial(pass_two, states),
        grid_spec=pltpu.PrefetchScalarGridSpec(
            num_scalar_prefetch=1,
            grid=(slots, 2),
            in_specs=[
                pair(length, channels),
                turn(length, width),
                one,
                pair(length, channels),
                pair(halves, ROWS, channels),
                pair(halves, ROWS, channels),
            ]
            + [whole(c) for c in constants],
            out_specs=[one, pair(length, channels), turn(length, width)] + [whole(c) for c in sums],
            scratch_shapes=[
                pltpu.VMEM((length, channels), F32),
                pltpu.VMEM((length, halves, ROWS, LANES), F32),
                pltpu.VMEM((length + 2, states, channels), BF16),
                pltpu.VMEM((length, states, channels), BF16),
                pltpu.VMEM((length, states, channels), BF16),
                pltpu.VMEM((length, channels), F32),
                pltpu.VMEM((length, channels), F32),
            ],
        ),
        out_shape=[
            jax.ShapeDtypeStruct((slots, length, channels), F32),
            jax.ShapeDtypeStruct((2, slots, length, channels), F32),
            jax.ShapeDtypeStruct((slots, 2, length, width), F32),
        ]
        + list(sums),
        compiler_params=pltpu.CompilerParams(vmem_limit_bytes=40 * MIB),
        name="scan_all",
    )(active, conv, proj, grad_y, step, entry, arrive, *constants)


def chain(count, end, pull, total, decay, entry, arrive, held, send_sem, recv_sem):
    mine = lax.axis_index("fsdp")
    slots = end.shape[1]
    mesh_id = pl.DeviceIdType.MESH
    after, before = lax.rem(mine + 1, count), lax.rem(mine + count - 1, count)
    barrier = pltpu.get_barrier_semaphore()
    for other in (after, before):
        pl.semaphore_signal(barrier, inc=1, device_id={"fsdp": other}, device_id_type=mesh_id)
    pl.semaphore_wait(barrier, 2)
    kinds = (
        ((entry, end, 0), (arrive, pull, 1), mine > 0, mine < count - 1, after),
        ((entry, end, 1), (arrive, pull, 0), mine < count - 1, mine > 0, before),
    )

    def copies(which, s):
        first, second, _, _, target = kinds[which]
        made = []
        for j, (landing, _, d) in enumerate((first, second)):
            made.append(
                pltpu.make_async_remote_copy(
                    src_ref=held.at[which, j, s],
                    dst_ref=landing.at[d, s],
                    send_sem=send_sem.at[which, j, s],
                    recv_sem=recv_sem.at[which, j, s],
                    device_id={"fsdp": target},
                    device_id_type=mesh_id,
                )
            )
        return made

    lags = (mine, count - 1 - mine)

    def wave(turn, carry):
        for which in range(2):
            first, second, gets, sends, _ = kinds[which]
            s = turn - lags[which]
            here = (s >= 0) & (s < slots)

            @pl.when(here & gets)
            def _():
                for copy in copies(which, s):
                    copy.wait_recv()

            @pl.when(here & jnp.logical_not(gets))
            def _():
                for landing, _, d in (first, second):
                    landing[d, s] = jnp.zeros(landing.shape[2:], F32)

            @pl.when(here & sends)
            def _():
                for j, (landing, local, d) in enumerate((first, second)):
                    through = jnp.exp2(decay[d] * total[d, s][None])
                    held[which, j, s] = through * landing[d, s] + local[d, s]
                for copy in copies(which, s):
                    copy.start()

        return carry

    lax.fori_loop(0, slots + count - 1, wave, 0)

    def drain(s, carry):
        for which in range(2):

            @pl.when(kinds[which][3])
            def _():
                for copy in copies(which, s):
                    copy.wait_send()

        return carry

    lax.fori_loop(0, slots, drain, 0)


def pass_states(end, pull, total, decay):
    _, slots, halves, rows, channels = end.shape
    return pl.pallas_call(
        functools.partial(chain, lax.axis_size("fsdp")),
        in_specs=[pl.BlockSpec(memory_space=pltpu.VMEM)] * 4,
        out_specs=[pl.BlockSpec(memory_space=pltpu.VMEM)] * 2,
        out_shape=[jax.ShapeDtypeStruct(end.shape, F32)] * 2,
        scratch_shapes=[
            pltpu.VMEM((2, 2, slots, halves, rows, channels), F32),
            pltpu.SemaphoreType.DMA((2, 2, slots)),
            pltpu.SemaphoreType.DMA((2, 2, slots)),
        ],
        compiler_params=pltpu.CompilerParams(
            collective_id=0, has_side_effects=True, vmem_limit_bytes=40 * MIB
        ),
        name="pass_states",
    )(end, pull, total, decay)


def to_owner(groups, parts):
    ratio = parts // groups
    pairs = []
    for g in range(groups):
        for f in range(parts):
            pairs.append((g * parts + f, (f // ratio) * parts + groups * (f % ratio) + g))
    return pairs


def cut(array, pieces):
    slots = array.shape[0]
    edges = [slots * i // pieces for i in range(pieces + 1)]
    return [array[lo:hi] for lo, hi in zip(edges[:-1], edges[1:])]


def flip(array, groups, bit):
    return lax.ppermute(array, "group", [(i, i ^ bit) for i in range(groups)])


def bits_of(groups, first):
    count = groups.bit_length() - 1
    return [1 << ((first + i) % count) for i in range(count)]


def gather_relative(array):
    groups = lax.axis_size("group")
    ways = groups.bit_length() - 1
    found = [[None] * ways for _ in range(groups)]
    for p, part in enumerate(cut(array, ways)):
        held = {0: part}
        for bit in bits_of(groups, p):
            held |= {r ^ bit: flip(value, groups, bit) for r, value in held.items()}
        for r, value in held.items():
            found[r][p] = value
    return jnp.concatenate([part for block in found for part in block], axis=0)


def scatter_relative(array, low):
    groups = lax.axis_size("group")
    ways = groups.bit_length() - 1
    blocks = jnp.split(array, groups, axis=0)
    pieces = [cut(block, ways) for block in blocks]
    sums = []
    for p in range(ways):
        held = {r: pieces[r][p].astype(F32) for r in range(groups)}
        for bit in bits_of(groups, p):
            for r in [r for r in held if r & bit]:
                held[r ^ bit] = held[r ^ bit] + flip(held[r].astype(low), groups, bit).astype(F32)
                del held[r]
        sums.append(held[0])
    return jnp.concatenate(sums, axis=0)


def sum_relative(array, low):
    return gather_relative(scatter_relative(array, F32).astype(low))


def gather_line(array):
    parts, mine = lax.axis_size("fsdp"), lax.axis_index("fsdp")
    chips = parts // 2
    rows = array.shape[0]
    lower, upper = [array], [array]
    for _ in range(chips - 1):
        lower.append(lax.ppermute(lower[-1], "fsdp", [(i, i + 2) for i in range(parts - 2)]))
        upper.append(lax.ppermute(upper[-1], "fsdp", [(i + 2, i) for i in range(parts - 2)]))
    line = jnp.stack(lower[:0:-1] + upper)
    own = lax.dynamic_slice_in_dim(line, chips - 1 - mine // 2, chips, 0)
    other = lax.ppermute(own, "fsdp", [(i, i ^ 1) for i in range(parts)])
    odd = mine % 2 == 1
    pair = jnp.stack([jnp.where(odd, other, own), jnp.where(odd, own, other)], axis=1)
    return pair.reshape(parts * rows, array.shape[1])


def on_device(
    tokens,
    item_bucket,
    slot_item,
    slot_live,
    slot_tokens,
    ada_weight,
    ada_bias,
    in_weight,
    conv_weight,
    conv_bias,
    xproj_weight,
    dt_weight,
    dt_bias,
    a_log,
    skip_gain,
    out_weight,
    cotangent,
):
    own_slots, length, model_width = tokens.shape
    groups, parts = lax.axis_size("group"), lax.axis_size("fsdp")
    g, f = lax.axis_index("group"), lax.axis_index("fsdp")
    slots = own_slots * groups
    inner_width = in_weight.shape[1] // 2
    channels = inner_width // groups
    kernel = conv_weight.shape[1]
    halo = kernel - 1
    rank_width = dt_weight.shape[1]
    width = xproj_weight.shape[2]
    states = (width - rank_width) // 2

    matches = slot_item[:, None] == jnp.arange(item_bucket.shape[0], dtype=jnp.int32)[None, :]
    own_buckets = jnp.sum(jnp.where(matches, item_bucket[None, :], 0), axis=1)
    facts = jnp.stack([slot_tokens * slot_live, own_buckets], axis=1)
    facts = jnp.concatenate([facts] + [flip(facts, groups, r) for r in range(1, groups)], axis=0)
    counts, buckets = facts[:, 0], facts[:, 1]
    group_counts = jnp.sum(counts.reshape(groups, own_slots), axis=1).astype(F32)
    share = jnp.repeat(group_counts / jnp.sum(group_counts), own_slots)
    positions = f * length + jnp.concatenate(
        [jnp.arange(length), jnp.arange(-halo, 0), length + jnp.arange(halo), jnp.full((ROWS - 2 * halo,), -length * parts)]
    ).astype(jnp.int32)
    mask_all = ((positions[None, :] >= 0) & (positions[None, :] < counts[:, None])).astype(F32)
    mask = mask_all[:, :length]
    active = (counts > f * length).astype(jnp.int32)
    own_mask = mask[:own_slots, :, None]
    own_share = share[:own_slots, None, None]

    edges = [(i, i + 1) for i in range(parts - 1)]
    before = lax.ppermute(tokens[:, length - halo :], "fsdp", edges)
    after = lax.ppermute(tokens[:, :halo], "fsdp", [(j, i) for i, j in edges])
    padding = jnp.zeros((own_slots, ROWS - 2 * halo, model_width), tokens.dtype)
    extended_tokens = jnp.concatenate([tokens, before, after, padding], axis=1)
    all_tokens = gather_relative(extended_tokens)
    late_cotangent, all_tokens = lax.optimization_barrier((cotangent, all_tokens))
    all_cotangent = gather_relative(late_cotangent)

    in_own = lax.dynamic_slice_in_dim(
        in_weight.reshape(in_weight.shape[0], 2, groups, channels), g, 1, 2
    ).reshape(in_weight.shape[0], 2 * channels)
    in_matrix = gather_line(in_own)
    shard = out_weight.shape[0]
    small = jnp.concatenate(
        [
            dt_weight.reshape(2 * rank_width, shard),
            a_log.reshape(2 * states, shard),
            conv_weight.reshape(2 * kernel, shard),
            conv_bias,
            dt_bias,
            skip_gain,
        ],
        axis=0,
    )
    small_rows = small.shape[0]
    small_pad = -small_rows % LANES
    packed = jnp.concatenate(
        [
            out_weight,
            xproj_weight[0],
            xproj_weight[1],
            jnp.pad(small.T, ((0, 0), (0, small_pad))),
        ],
        axis=1,
    )
    piece = shard // groups
    sent = lax.ppermute(
        lax.dynamic_slice_in_dim(packed, g * piece, piece, 0),
        ("group", "fsdp"),
        to_owner(groups, parts),
    )
    mine = lax.all_gather(sent, "fsdp", axis=0, tiled=True)
    out_matrix = mine[:, :model_width]
    xproj = [mine[:, model_width + d * width : model_width + (d + 1) * width] for d in range(2)]
    rest = mine[:, model_width + 2 * width :].T
    edge = 0

    def take(rows):
        nonlocal edge
        edge += rows
        return rest[edge - rows : edge]

    dt_matrix = jnp.pad(
        take(2 * rank_width).reshape(2, rank_width, channels), ((0, 0), (0, width - rank_width), (0, 0))
    )
    rate = -jnp.exp(take(2 * states).astype(F32)).reshape(2, states // ROWS, ROWS, channels)
    taps = take(2 * kernel).reshape(2, kernel, channels).astype(F32)
    conv_shift = take(2).astype(F32)
    dt_shift = take(2).astype(F32).reshape(2, 1, channels)
    skip = take(2).astype(F32).reshape(2, 1, channels)
    decay = rate * LOG2E

    condition = jax.nn.silu(time_embed(buckets, model_width)).astype(BF16)
    modulation = lax.all_gather(
        jnp.dot(condition, ada_weight, preferred_element_type=F32) + ada_bias.astype(F32),
        "fsdp",
        axis=1,
        tiled=True,
    )
    shift_mod = modulation[:, None, :model_width]
    scale_mod = modulation[:, None, model_width : 2 * model_width]
    gate_mod = modulation[:, None, 2 * model_width :]

    def normalise(values):
        inputs = values.astype(F32)
        centered = inputs - jnp.mean(inputs, axis=2, keepdims=True)
        inv_std = lax.rsqrt(jnp.mean(centered * centered, axis=2, keepdims=True) + EPSILON)
        return (inputs, centered * inv_std, inv_std)

    normed = normalise(all_tokens)[1]
    modulated_all = ((normed * (1.0 + scale_mod) + shift_mod) * mask_all[:, :, None]).astype(BF16)
    modulated = modulated_all[:, :length]
    inner_all = jnp.einsum("sld,dc->slc", modulated_all, in_matrix, preferred_element_type=F32)
    inner_x = inner_all[:, :, :channels]
    gate_z = inner_all[:, :length, channels:]
    extended = jnp.concatenate(
        [inner_x[:, length : length + halo], inner_x[:, :length], inner_x[:, length + halo : length + 2 * halo]],
        axis=1,
    )
    pre, conv_out, projected = [], [], []
    for d in range(2):
        value = conv_shift[d]
        for k in range(kernel):
            row = k if d == 0 else 2 * halo - k
            value = value + taps[d, k] * extended[:, row : row + length]
        pre.append(value)
        conv_out.append((jax.nn.silu(value) * mask[:, :, None]).astype(BF16))
        projected.append(
            jnp.einsum("slc,ck->slk", conv_out[d], xproj[d], preferred_element_type=F32)
        )
    conv_out = jnp.stack(conv_out)
    proj = sum_relative(jnp.stack(projected, axis=1), F32)

    grad_in_all = all_cotangent.astype(F32) * (mask * share[:, None])[:, :, None]
    branch_gradient = (grad_in_all * gate_mod).astype(BF16)
    grad_gated = jnp.einsum("sld,cd->slc", branch_gradient, out_matrix, preferred_element_type=F32)
    grad_y = grad_gated * jax.nn.silu(gate_z)

    step, end, pull, total = scan_ends(active, conv_out, proj, grad_y, dt_matrix, dt_shift, decay)
    entry, arrive = pass_states(end, pull, total, decay)
    y, conv_grad, proj_part, dtw_grad, dtb_grad, decay_grad, skip_grad = scan_all(
        active, conv_out, proj, grad_y, step, entry, arrive, dt_matrix, decay, skip
    )
    proj_grad = sum_relative(proj_part, BF16)
    alog_grad = (decay_grad * rate).reshape(2 * states, channels)

    gated_output = (y * jax.nn.silu(gate_z)).astype(BF16)
    branch_part = jnp.einsum("slc,cd->sld", gated_output, out_matrix, preferred_element_type=F32)
    branch = scatter_relative(branch_part, BF16)
    own_gate = gate_mod[:own_slots]
    own_scale = scale_mod[:own_slots]
    own_inputs, own_normed, own_inv = normalise(tokens)
    layer_out = ((own_inputs + own_gate * branch) * own_mask).astype(BF16)
    grad_in = cotangent.astype(F32) * own_mask * own_share
    grad_gate = jnp.sum(grad_in * branch, axis=1)
    outward = jnp.einsum("slc,sld->cd", gated_output, branch_gradient, preferred_element_type=F32)
    grad_z = grad_gated * y * silu_slope(gate_z)

    pre_grads, conv_grads, convb_grads, xproj_grads = [], [], [], []
    for d in range(2):
        into = conv_grad[d] + jnp.einsum(
            "slk,ck->slc", proj_grad[:, d], xproj[d], preferred_element_type=F32
        )
        pre_grad = into * mask[:, :, None] * silu_slope(pre[d])
        xproj_grads.append(
            jnp.einsum("slc,slk->ck", conv_out[d], proj_grad[:, d], preferred_element_type=F32)
        )
        convb_grads.append(jnp.sum(pre_grad, axis=(0, 1)))
        for k in range(kernel):
            row = k if d == 0 else 2 * halo - k
            conv_grads.append(jnp.sum(pre_grad * extended[:, row : row + length], axis=(0, 1)))
        pre_grads.append(pre_grad)
    ahead = lax.ppermute(pre_grads[0][:, :halo], "fsdp", [(j, i) for i, j in edges])
    behind = lax.ppermute(pre_grads[1][:, length - halo :], "fsdp", edges)
    ahead_rows = jnp.concatenate([pre_grads[0], ahead], axis=1)
    behind_rows = jnp.concatenate([behind, pre_grads[1]], axis=1)
    grad_x = jnp.zeros(gate_z.shape, F32)
    for k in range(kernel):
        grad_x = grad_x + taps[0, k] * ahead_rows[:, halo - k : halo - k + length]
        grad_x = grad_x + taps[1, k] * behind_rows[:, k : k + length]
    inner_gradient = jnp.concatenate([grad_x, grad_z], axis=2).astype(BF16)
    grad_mod_part = jnp.einsum(
        "slc,dc->sld", inner_gradient, in_matrix, preferred_element_type=F32
    )
    grad_mod = scatter_relative(grad_mod_part, BF16) * own_mask
    inward = jnp.einsum("sld,slc->dc", modulated, inner_gradient, preferred_element_type=F32)

    grad_shift = jnp.sum(grad_mod, axis=1)
    grad_scale = jnp.sum(grad_mod * own_normed, axis=1)
    grad_normed = grad_mod * (1.0 + own_scale)
    grad_ln = own_inv * (
        grad_normed
        - jnp.mean(grad_normed, axis=2, keepdims=True)
        - own_normed * jnp.mean(grad_normed * own_normed, axis=2, keepdims=True)
    )
    tokens_grad = grad_in + grad_ln

    mod_part = jnp.concatenate([grad_shift, grad_scale, grad_gate], axis=1)
    mod_slice = lax.psum_scatter(mod_part, "fsdp", scatter_dimension=1, tiled=True)
    mod_all = jnp.concatenate(
        [mod_slice] + [flip(mod_slice, groups, r) for r in range(1, groups)], axis=0
    )
    ada_grad = jnp.einsum("sd,sk->dk", condition, mod_all.astype(BF16), preferred_element_type=F32)
    adab_grad = jnp.sum(mod_all, axis=0)

    small_grads = jnp.concatenate(
        [
            dtw_grad[:, :rank_width].reshape(2 * rank_width, channels),
            alog_grad,
            jnp.stack(conv_grads),
            jnp.stack(convb_grads),
            dtb_grad.reshape(2, channels),
            skip_grad.reshape(2, channels),
        ],
        axis=0,
    )
    packed_grads = jnp.concatenate(
        [outward, xproj_grads[0], xproj_grads[1], jnp.pad(small_grads.T, ((0, 0), (0, small_pad)))],
        axis=1,
    ).astype(BF16)
    packed_piece = lax.psum_scatter(packed_grads, "fsdp", scatter_dimension=0, tiled=True)
    packed_piece = lax.ppermute(
        packed_piece, ("group", "fsdp"), [(j, i) for i, j in to_owner(groups, parts)]
    )
    packed_own = lax.all_gather(packed_piece, "group", axis=0, tiled=True).astype(F32)
    out_grad = packed_own[:, :model_width]
    xproj_grad = jnp.stack(
        [packed_own[:, model_width + d * width : model_width + (d + 1) * width] for d in range(2)]
    )
    rest_grads = packed_own[:, model_width + 2 * width :].T
    sizes = [2 * rank_width, 2 * states, 2 * kernel, 2, 2, 2]
    cuts = [sum(sizes[:i]) for i in range(len(sizes) + 1)]
    dtw_out, alog_out, conv_w_out, conv_b_out, dtb_out, skip_out = [
        rest_grads[cuts[i] : cuts[i + 1]] for i in range(len(sizes))
    ]
    inward_piece = lax.psum_scatter(inward.astype(BF16), "fsdp", scatter_dimension=0, tiled=True)
    inward_all = lax.all_gather(inward_piece, "group", axis=0)
    in_grad = (
        inward_all.reshape(groups, in_weight.shape[0], 2, channels)
        .transpose(1, 2, 0, 3)
        .reshape(in_weight.shape)
        .astype(F32)
    )
    return (
        layer_out,
        tokens_grad,
        ada_grad,
        adab_grad,
        in_grad,
        conv_w_out.reshape(2, kernel, shard),
        conv_b_out,
        xproj_grad,
        dtw_out.reshape(2, rank_width, shard),
        dtb_out,
        alog_out.reshape(2, states, shard),
        skip_out,
        out_grad,
    )


def solution(mesh):
    in_specs = (
        P("group", "fsdp", None),
        P(),
        P("group"),
        P("group"),
        P("group"),
        P(None, "fsdp"),
        P("fsdp"),
        P("fsdp", None),
        P(None, None, "fsdp"),
        P(None, "fsdp"),
        P(None, "fsdp", None),
        P(None, None, "fsdp"),
        P(None, "fsdp"),
        P(None, None, "fsdp"),
        P(None, "fsdp"),
        P("fsdp", None),
        P("group", "fsdp", None),
    )
    out_specs = (
        P("group", "fsdp", None),
        P("group", "fsdp", None),
        P(None, "fsdp"),
        P("fsdp"),
        P("fsdp", None),
        P(None, None, "fsdp"),
        P(None, "fsdp"),
        P(None, "fsdp", None),
        P(None, None, "fsdp"),
        P(None, "fsdp"),
        P(None, None, "fsdp"),
        P(None, "fsdp"),
        P("fsdp", None),
    )
    return jax.shard_map(
        on_device, mesh=mesh, in_specs=in_specs, out_specs=out_specs, check_vma=False
    )
```

```python
import functools
import math

import jax
import jax.numpy as jnp
from jax import lax
from jax.experimental import pallas as pl
from jax.experimental.pallas import tpu as pltpu
from jax.sharding import PartitionSpec as P

EPSILON = 1e-06
LANES = 128
ROWS = 8
BLOCK = 16
WIDE = 256
LAG = 3
LOG2E = math.log2(math.e)
LN2 = math.log(2.0)
F32 = jnp.float32
BF16 = jnp.bfloat16
MIB = 1 << 20


def time_embed(buckets, model_width):
    half_width = model_width // 2
    frequency = jnp.exp(-math.log(10000.0) * jnp.arange(half_width, dtype=F32) / half_width)
    angles = buckets.astype(F32)[:, None] * frequency[None, :]
    return jnp.concatenate([jnp.cos(angles), jnp.sin(angles)], axis=1)


def silu_slope(values):
    sigmoid = jax.nn.sigmoid(values)
    return sigmoid * (1.0 + values * (1.0 - sigmoid))


def dot32(left, right, dims):
    return lax.dot_general(left, right, (dims, ((), ())), preferred_element_type=F32)


def spread_columns(proj_ref, first, count, out_ref):
    rows = proj_ref.shape[0]

    def block(i, carry):
        start = pl.multiple_of(i * ROWS, ROWS)
        turned = jnp.transpose(proj_ref[pl.ds(start, ROWS), :])
        for j in range(ROWS):
            column = turned[first : first + count, j : j + 1]
            out_ref[start + j] = jnp.broadcast_to(column, (count, LANES)).reshape(
                count // ROWS, ROWS, LANES
            )
        return carry

    lax.fori_loop(0, rows // ROWS, block, 0, unroll=True)


def sweep(length, backward, body, start):
    def block(i, carry):
        at = length // ROWS - 1 - i if backward else i
        first = pl.multiple_of(at * ROWS, ROWS)
        blocks = {}

        def row(ref, j):
            if id(ref) not in blocks:
                blocks[id(ref)] = ref[pl.ds(first, ROWS), :]
            rows = blocks[id(ref)]
            return [
                jnp.broadcast_to(rows[j : j + 1, k : k + LANES], (ROWS, LANES))[None]
                for k in range(0, rows.shape[1], LANES)
            ]

        for j in reversed(range(ROWS)) if backward else range(ROWS):
            carry = body(first + j, functools.partial(row, j=j), carry)
        return carry

    return lax.fori_loop(0, length // ROWS, block, start)


def pass_one(
    states, active, conv, proj, grad_y, dt_w, dt_b, decay, step, end, pull, total, mix_b, mix_c, drive
):
    slot, direction = pl.program_id(0), pl.program_id(1)
    length, channels = drive.shape
    chunks = channels // LANES
    halves = states // ROWS
    rank = proj.shape[1] - 2 * states

    @pl.when(active[slot] == 0)
    def _():
        step[...] = jnp.zeros_like(step)
        end[...] = jnp.zeros_like(end)
        pull[...] = jnp.zeros_like(pull)
        total[...] = jnp.zeros_like(total)

    @pl.when(active[slot] != 0)
    def _():
        pre = dot32(proj[...].astype(BF16), dt_w[direction], ((1,), (0,))) + dt_b[direction]
        steps = jnp.maximum(pre, 0.0) + jnp.log1p(jnp.exp(-jnp.abs(pre)))
        step[...] = steps
        drive[...] = steps * conv[...].astype(F32)
        total[...] = jnp.broadcast_to(jnp.sum(steps, axis=0, keepdims=True), total.shape)
        spread_columns(proj, rank, states, mix_b)
        spread_columns(proj, rank + states, states, mix_c)

        def token(t, row, carry):
            hidden, running, pulled = carry
            b, c = mix_b[t], mix_c[t]
            step_row, drive_row, grad_row = row(step), row(drive), row(grad_y)
            new = ([], [], [])
            for k in range(chunks):
                lanes = slice(k * LANES, (k + 1) * LANES)
                factor = jnp.exp2(step_row[k] * decay[direction, :, :, lanes])
                new[0].append(factor * hidden[k] + drive_row[k] * b)
                runs = running[k] * factor
                new[1].append(runs)
                new[2].append(pulled[k] + runs * (grad_row[k] * c))
            return tuple(tuple(part) for part in new)

        zero = jnp.zeros((halves, ROWS, LANES), F32)
        start = ((zero,) * chunks, (zero + 1.0,) * chunks, (zero,) * chunks)
        for backward in range(2):

            @pl.when(direction == backward)
            def _():
                hidden, _, pulled = sweep(length, backward, token, start)
                for k in range(chunks):
                    lanes = slice(k * LANES, (k + 1) * LANES)
                    end[:, :, lanes] = hidden[k]
                    pull[:, :, lanes] = pulled[k]


def pass_two(
    states,
    active,
    conv,
    proj,
    grad_y,
    step,
    mix_b,
    mix_c,
    entry,
    arrive,
    dt_w,
    decay,
    skip,
    tile_b,
    tile_c,
    sel,
    take_b,
    take_c,
    y,
    conv_grad,
    proj_grad,
    dtw_grad,
    dtb_grad,
    alog_grad,
    skip_grad,
    drive,
    hid_even,
    hid_odd,
    edge,
    gst_even,
    gst_odd,
    thd_even,
    thd_odd,
    mixed,
    sdec,
    scan_y,
    in_part,
    out_part,
    rows_b,
    rows_c,
    drive_low,
    grad_low,
):
    slot, direction = pl.program_id(0), pl.program_id(1)
    length, channels = drive.shape
    chunks = channels // LANES
    halves = states // ROWS
    wide = BLOCK * states
    pairs = length // (2 * BLOCK)
    hid, gst, thd = (hid_even, hid_odd), (gst_even, gst_odd), (thd_even, thd_odd)
    lanes = [slice(k * LANES, (k + 1) * LANES) for k in range(chunks)]

    @pl.when((slot == 0) & (direction == 0))
    def _():
        dtw_grad[...] = jnp.zeros_like(dtw_grad)
        dtb_grad[...] = jnp.zeros_like(dtb_grad)
        alog_grad[...] = jnp.zeros_like(alog_grad)
        skip_grad[...] = jnp.zeros_like(skip_grad)

    @pl.when(direction == 0)
    def _():
        y[...] = jnp.zeros_like(y)

    @pl.when(active[slot] == 0)
    def _():
        conv_grad[...] = jnp.zeros_like(conv_grad)
        proj_grad[...] = jnp.zeros_like(proj_grad)

    def low(value):
        return value.reshape(states, LANES).astype(BF16)

    def block_range(pair, odd):
        return pl.ds(pl.multiple_of((2 * pair + odd) * BLOCK, BLOCK), BLOCK)

    def sweep_blocks(backward, tokens, matmuls, start):
        first, second = (1, 0) if backward else (0, 1)

        def two(i, carry):
            pair = pairs - 1 - i if backward else i
            before = lax.rem(pair + (1 if backward else pairs - 1), pairs)
            carry = tokens(pair, first, backward, matmuls(before, second), carry)
            return tokens(pair, second, backward, matmuls(pair, first), carry)

        carry = lax.fori_loop(0, pairs, two, start)
        for issue, keep in matmuls(0 if backward else pairs - 1, second):
            keep(issue())
        return carry

    def pieces(out, rows, left, right, dims, width):
        made = []
        for n in range(0, width, WIDE):
            cols = slice(n, min(n + WIDE, width))
            picked = right[:, cols] if dims[1] == (0,) else right

            def issue(left=left, picked=picked):
                return dot32(left, picked, dims)

            def keep(product, cols=cols):
                out[rows, cols] = product

            made.append((issue, keep))
        return made

    def scan_rows(pair, odd, backward, refs, body, beside, carry):
        order = list(range(BLOCK))[:: -1 if backward else 1]
        waiting = []
        for at_step, j in enumerate(order):
            if j % ROWS == (ROWS - 1 if backward else 0):
                at = pl.multiple_of((2 * pair + odd) * BLOCK + j // ROWS * ROWS, ROWS)
                held = [ref[pl.ds(at, ROWS), :] for ref in refs]
            i = j % ROWS
            rows = [
                [jnp.broadcast_to(h[i : i + 1, c], (ROWS, LANES))[None] for c in lanes] for h in held
            ]
            for issue, keep in beside[at_step * len(beside) // BLOCK : (at_step + 1) * len(beside) // BLOCK]:
                waiting.append((at_step + LAG, keep, issue()))
            carry = body(j, rows, carry)
            while waiting and waiting[0][0] <= at_step:
                _, keep, product = waiting.pop(0)
                keep(product)
        for _, keep, product in waiting:
            keep(product)
        return carry

    def forward_tokens(pair, odd, backward, beside, hidden):
        for k in range(chunks):
            edge[2 * pair + odd, :, lanes[k]] = low(hidden[k])

        def token(j, rows, hidden):
            b = mix_b[(2 * pair + odd) * BLOCK + j]
            new = []
            for k in range(chunks):
                factor = jnp.exp2(rows[0][k] * decay[direction, :, :, lanes[k]])
                value = factor * hidden[k] + rows[1][k] * b
                hid[odd][pair, j, :, lanes[k]] = low(value)
                new.append(value)
            return tuple(new)

        return scan_rows(pair, odd, backward, (step, drive), token, beside, hidden)

    def forward_matmuls(pair, odd):
        rows = block_range(pair, odd)
        h_rows = hid[odd][pair].reshape(wide, channels)
        return pieces(scan_y, rows, rows_c[rows, :], h_rows, ((1,), (0,)), channels) + pieces(
            out_part, rows, grad_low[rows, :], h_rows, ((1,), (1,)), wide
        )

    def backward_tokens(pair, odd, backward, beside, carry):
        earlier = -1 if backward else 1

        def token(j, rows, carry):
            carried, total = carry
            c = mix_c[(2 * pair + odd) * BLOCK + j]
            news, sums = [], []
            p = j + earlier
            for k in range(chunks):
                rate = decay[direction, :, :, lanes[k]]
                factor = jnp.exp2(rows[0][k] * rate)
                grad_state = rows[1][k] * c + carried[k]
                gst[odd][j, :, lanes[k]] = low(grad_state)
                onward = factor * grad_state
                if 0 <= p < BLOCK:
                    before = hid[odd][pair, p, :, lanes[k]]
                else:
                    before = edge[2 * pair + odd, :, lanes[k]]
                through = onward * before.astype(F32).reshape(halves, ROWS, LANES)
                sums.append(total[k] + through * rows[0][k])
                thd[odd][j, :, lanes[k]] = low(through * rate)
                news.append(onward)
            return (tuple(news), tuple(sums))

        return scan_rows(pair, odd, backward, (step, grad_y), token, beside, carry)

    def backward_matmuls(pair, odd):
        rows = block_range(pair, odd)
        g_rows = gst[odd][...].reshape(wide, channels)
        t_rows = thd[odd][...].reshape(wide, channels)
        return (
            pieces(mixed, rows, rows_b[rows, :], g_rows, ((1,), (0,)), channels)
            + pieces(sdec, rows, sel[...].astype(BF16), t_rows, ((1,), (0,)), channels)
            + pieces(in_part, rows, drive_low[rows, :], g_rows, ((1,), (1,)), wide)
        )

    @pl.when(active[slot] != 0)
    def _():
        drive[...] = step[...] * conv[...].astype(F32)
        drive_low[...] = drive[...].astype(BF16)
        grad_low[...] = grad_y[...].astype(BF16)
        proj_low = proj[...].astype(BF16)
        picked = jnp.concatenate([sel[...]] * (length // BLOCK), axis=0)
        rows_b[...] = (dot32(proj_low, tile_b[...], ((1,), (0,))) * picked).astype(BF16)
        rows_c[...] = (dot32(proj_low, tile_c[...], ((1,), (0,))) * picked).astype(BF16)
        zero = jnp.zeros((halves, ROWS, LANES), F32)
        for reverse in (False, True):

            @pl.when(direction == int(reverse))
            def _():
                start = tuple(entry[:, :, c] for c in lanes)
                sweep_blocks(reverse, forward_tokens, forward_matmuls, start)
                start = (tuple(arrive[:, :, c] for c in lanes), (zero,) * chunks)
                _, sums = sweep_blocks(not reverse, backward_tokens, backward_matmuls, start)
                for k in range(chunks):
                    alog_grad[direction, :, :, lanes[k]] += sums[k]

        conv_values = conv[...].astype(F32)
        steps = step[...]
        grads = grad_y[...]
        step_grad = conv_values * mixed[...] + LN2 * sdec[...]
        pre_grad = step_grad * (1.0 - jnp.exp(-steps))
        dtb_grad[direction] += jnp.sum(pre_grad, axis=0, keepdims=True)
        pre_low = pre_grad.astype(BF16)
        proj_grad[...] = (
            dot32((in_part[...] * picked).astype(BF16), take_b[...], ((1,), (0,)))
            + dot32((out_part[...] * picked).astype(BF16), take_c[...], ((1,), (0,)))
            + dot32(pre_low, dt_w[direction], ((1,), (1,)))
        )
        dtw_grad[direction] += dot32(jnp.transpose(proj[...]).astype(BF16), pre_low, ((1,), (0,)))
        y[...] += scan_y[...] + skip[direction] * conv_values
        skip_grad[direction] += jnp.sum(grads * conv_values, axis=0, keepdims=True)
        conv_grad[...] = grads * skip[direction] + steps * mixed[...]


def whole(array):
    zeros = (0,) * array.ndim
    return pl.BlockSpec(array.shape, lambda s, d, a: zeros)


def scan_ends(active, conv, proj, grad_y, dt_w, dt_b, decay):
    slots, length, channels = grad_y.shape
    halves = decay.shape[1]
    width = proj.shape[3]
    states = halves * ROWS
    turn = lambda *tail: pl.BlockSpec((None, None) + tail, lambda s, d, a: (s, d) + (0,) * len(tail))
    pair = lambda *tail: pl.BlockSpec((None, None) + tail, lambda s, d, a: (d, s) + (0,) * len(tail))
    state = (2, slots, halves, ROWS, channels)
    mixes = (length, halves, ROWS, LANES)
    return pl.pallas_call(
        functools.partial(pass_one, states),
        grid_spec=pltpu.PrefetchScalarGridSpec(
            num_scalar_prefetch=1,
            grid=(slots, 2),
            in_specs=[
                pair(length, channels),
                turn(length, width),
                pl.BlockSpec((None, length, channels), lambda s, d, a: (s, 0, 0)),
                whole(dt_w),
                whole(dt_b),
                whole(decay),
            ],
            out_specs=[
                pair(length, channels),
                pair(halves, ROWS, channels),
                pair(halves, ROWS, channels),
                pair(ROWS, channels),
                turn(*mixes),
                turn(*mixes),
            ],
            scratch_shapes=[pltpu.VMEM((length, channels), F32)],
        ),
        out_shape=[
            jax.ShapeDtypeStruct((2, slots, length, channels), F32),
            jax.ShapeDtypeStruct(state, F32),
            jax.ShapeDtypeStruct(state, F32),
            jax.ShapeDtypeStruct((2, slots, ROWS, channels), F32),
            jax.ShapeDtypeStruct((slots, 2) + mixes, F32),
            jax.ShapeDtypeStruct((slots, 2) + mixes, F32),
        ],
        compiler_params=pltpu.CompilerParams(vmem_limit_bytes=24 * MIB),
        name="scan_ends",
    )(active, conv, proj, grad_y, dt_w, dt_b, decay)


def scan_all(active, conv, proj, grad_y, step, mix_b, mix_c, entry, arrive, dt_w, decay, skip):
    slots, length, channels = grad_y.shape
    halves = decay.shape[1]
    width = proj.shape[3]
    states = halves * ROWS
    wide = BLOCK * states
    rank = width - 2 * states
    column = jnp.arange(width)[:, None]
    lane = jnp.arange(wide)[None, :]
    tile_b = (column == rank + lane % states).astype(BF16)
    tile_c = (column == rank + states + lane % states).astype(BF16)
    sel = (jnp.arange(BLOCK)[:, None] == lane // states).astype(F32)
    turn = lambda *tail: pl.BlockSpec((None, None) + tail, lambda s, d, a: (s, d) + (0,) * len(tail))
    pair = lambda *tail: pl.BlockSpec((None, None) + tail, lambda s, d, a: (d, s) + (0,) * len(tail))
    one = pl.BlockSpec((None, length, channels), lambda s, d, a: (s, 0, 0))
    constants = (dt_w, decay, skip, tile_b, tile_c, sel, tile_b.T, tile_c.T)
    sums = (
        jax.ShapeDtypeStruct((2, width, channels), F32),
        jax.ShapeDtypeStruct((2, 1, channels), F32),
        jax.ShapeDtypeStruct((2, halves, ROWS, channels), F32),
        jax.ShapeDtypeStruct((2, 1, channels), F32),
    )
    pairs = length // (2 * BLOCK)
    return pl.pallas_call(
        functools.partial(pass_two, states),
        grid_spec=pltpu.PrefetchScalarGridSpec(
            num_scalar_prefetch=1,
            grid=(slots, 2),
            in_specs=[
                pair(length, channels),
                turn(length, width),
                one,
                pair(length, channels),
                turn(length, halves, ROWS, LANES),
                turn(length, halves, ROWS, LANES),
                pair(halves, ROWS, channels),
                pair(halves, ROWS, channels),
            ]
            + [whole(c) for c in constants],
            out_specs=[one, pair(length, channels), turn(length, width)] + [whole(c) for c in sums],
            scratch_shapes=[pltpu.VMEM((length, channels), F32)]
            + [pltpu.VMEM((pairs, BLOCK, states, channels), BF16)] * 2
            + [pltpu.VMEM((2 * pairs, states, channels), BF16)]
            + [pltpu.VMEM((BLOCK, states, channels), BF16)] * 4
            + [pltpu.VMEM((length, channels), F32)] * 3
            + [pltpu.VMEM((length, wide), F32)] * 2
            + [pltpu.VMEM((length, wide), BF16)] * 2
            + [pltpu.VMEM((length, channels), BF16)] * 2,
        ),
        out_shape=[
            jax.ShapeDtypeStruct((slots, length, channels), F32),
            jax.ShapeDtypeStruct((2, slots, length, channels), F32),
            jax.ShapeDtypeStruct((slots, 2, length, width), F32),
        ]
        + list(sums),
        compiler_params=pltpu.CompilerParams(vmem_limit_bytes=44 * MIB),
        name="scan_all",
    )(active, conv, proj, grad_y, step, mix_b, mix_c, entry, arrive, *constants)


def chain(count, end, pull, total, decay, entry, arrive, held, send_sem, recv_sem):
    mine = lax.axis_index("fsdp")
    slots = end.shape[1]
    mesh_id = pl.DeviceIdType.MESH
    after, before = lax.rem(mine + 1, count), lax.rem(mine + count - 1, count)
    barrier = pltpu.get_barrier_semaphore()
    for other in (after, before):
        pl.semaphore_signal(barrier, inc=1, device_id={"fsdp": other}, device_id_type=mesh_id)
    pl.semaphore_wait(barrier, 2)
    kinds = (
        ((entry, end, 0), (arrive, pull, 1), mine > 0, mine < count - 1, after),
        ((entry, end, 1), (arrive, pull, 0), mine < count - 1, mine > 0, before),
    )

    def copies(which, s):
        first, second, _, _, target = kinds[which]
        made = []
        for j, (landing, _, d) in enumerate((first, second)):
            made.append(
                pltpu.make_async_remote_copy(
                    src_ref=held.at[which, j, s],
                    dst_ref=landing.at[d, s],
                    send_sem=send_sem.at[which, j, s],
                    recv_sem=recv_sem.at[which, j, s],
                    device_id={"fsdp": target},
                    device_id_type=mesh_id,
                )
            )
        return made

    lags = (mine, count - 1 - mine)

    def wave(turn, carry):
        for which in range(2):
            first, second, gets, sends, _ = kinds[which]
            s = turn - lags[which]
            here = (s >= 0) & (s < slots)

            @pl.when(here & gets)
            def _():
                for copy in copies(which, s):
                    copy.wait_recv()

            @pl.when(here & jnp.logical_not(gets))
            def _():
                for landing, _, d in (first, second):
                    landing[d, s] = jnp.zeros(landing.shape[2:], F32)

            @pl.when(here & sends)
            def _():
                for j, (landing, local, d) in enumerate((first, second)):
                    through = jnp.exp2(decay[d] * total[d, s][None])
                    held[which, j, s] = through * landing[d, s] + local[d, s]
                for copy in copies(which, s):
                    copy.start()

        return carry

    lax.fori_loop(0, slots + count - 1, wave, 0)

    def drain(s, carry):
        for which in range(2):

            @pl.when(kinds[which][3])
            def _():
                for copy in copies(which, s):
                    copy.wait_send()

        return carry

    lax.fori_loop(0, slots, drain, 0)


def pass_states(end, pull, total, decay):
    _, slots, halves, rows, channels = end.shape
    return pl.pallas_call(
        functools.partial(chain, lax.axis_size("fsdp")),
        in_specs=[pl.BlockSpec(memory_space=pltpu.VMEM)] * 4,
        out_specs=[pl.BlockSpec(memory_space=pltpu.VMEM)] * 2,
        out_shape=[jax.ShapeDtypeStruct(end.shape, F32)] * 2,
        scratch_shapes=[
            pltpu.VMEM((2, 2, slots, halves, rows, channels), F32),
            pltpu.SemaphoreType.DMA((2, 2, slots)),
            pltpu.SemaphoreType.DMA((2, 2, slots)),
        ],
        compiler_params=pltpu.CompilerParams(
            collective_id=0, has_side_effects=True, vmem_limit_bytes=40 * MIB
        ),
        name="pass_states",
    )(end, pull, total, decay)


def partner(g, bit):
    return g + bit * (1 - 2 * lax.rem(g // bit, 2))


class Mail:
    def __init__(self, send_sem, recv_sem):
        self.send_sem, self.recv_sem, self.made = send_sem, recv_sem, []

    def post(self, src, dst, target, here=None, there=None, landing=None):
        n = len(self.made)
        copy = lambda into: pltpu.make_async_remote_copy(
            src_ref=src,
            dst_ref=into,
            send_sem=self.send_sem.at[n],
            recv_sem=self.recv_sem.at[n],
            device_id=target,
            device_id_type=pl.DeviceIdType.MESH,
        )
        when = lambda cond: (lambda body: body()) if cond is None else pl.when(cond)
        landing = dst if landing is None else landing
        entry = dict(got=False)

        @when(here)
        def _():
            copy(dst).start()

        def take():
            if not entry["got"]:
                entry["got"] = True

                @when(there)
                def _():
                    copy(landing).wait_recv()

        def sent():
            @when(here)
            def _():
                copy(dst).wait_send()

        self.made.append((take, sent))
        return take

    def finish(self):
        for take, _ in self.made:
            take()
        for _, sent in self.made:
            sent()


def collect(
    groups,
    parts,
    tokens,
    halo,
    in_own,
    xproj,
    small,
    facts,
    cotangent,
    all_tokens,
    all_halo,
    in_matrix,
    all_xproj,
    all_small,
    all_facts,
    all_cotangent,
    send_sem,
    recv_sem,
    own_sem,
):
    g, f = lax.axis_index("group"), lax.axis_index("fsdp")
    chips = parts // 2
    z, core = f // 2, lax.rem(f, 2)
    ways = groups.bit_length() - 1
    bits = [1 << i for i in range(ways)]
    barrier = pltpu.get_barrier_semaphore()
    for bit in bits:
        pl.semaphore_signal(
            barrier, inc=1, device_id={"group": partner(g, bit)}, device_id_type=pl.DeviceIdType.MESH
        )
    for k in range(1, parts):
        pl.semaphore_signal(
            barrier,
            inc=1,
            device_id={"fsdp": lax.rem(f + k, parts)},
            device_id_type=pl.DeviceIdType.MESH,
        )
    pl.semaphore_wait(barrier, ways + parts - 1)
    mail = Mail(send_sem, recv_sem)
    place = lambda part: lax.rem(part + 2 * parts, parts)
    sibling = {"fsdp": f + 1 - 2 * core}
    up, down = {"fsdp": f + 2}, {"fsdp": f - 2}

    fact_takes = []
    for k in range(1, parts):
        fact_takes.append(
            mail.post(
                facts,
                all_facts.at[0, f],
                {"fsdp": lax.rem(f + k, parts)},
                landing=all_facts.at[0, lax.rem(f + parts - k, parts)],
            )
        )

    def cuts(count):
        edges = [count * i // ways for i in range(ways + 1)]
        return [pl.ds(lo, hi - lo) for lo, hi in zip(edges[:-1], edges[1:])]

    def relative(own, every, count):
        pieces = cuts(count)
        held = [{0: None} for _ in range(ways)]
        steps = [[] for _ in range(ways)]
        for t in range(ways):
            for p in range(ways):
                bit = bits[(p + t) % ways]
                for r in list(held[p]):
                    held[p][r ^ bit] = None
                    steps[t].append((p, r, bit))
        takes = {}

        def run(chosen):
            for p, r, bit in chosen:
                if r:
                    takes[p, r]()
                src = own.at[pieces[p]] if r == 0 else every.at[r, pieces[p]]
                takes[p, r ^ bit] = mail.post(
                    src, every.at[r ^ bit, pieces[p]], {"group": partner(g, bit)}
                )

        run([move for step in steps for move in step if move[1] == 0])
        return [functools.partial(run, [move for move in step if move[1]]) for step in steps[1:]]

    token_steps = relative(tokens, all_tokens, tokens.shape[0])
    halo_steps = relative(halo, all_halo, halo.shape[0])

    line = []

    def hop(h):
        for sign, target, inside in ((1, up, z < chips - 1), (-1, down, z > 0)):
            shard = f - sign * 2 * (h - 1)
            src = in_own if h == 1 else in_matrix.at[place(shard)]
            far = z - sign * (h - 1)
            come = z - sign * h
            line.append(
                mail.post(
                    src,
                    in_matrix.at[place(shard)],
                    target,
                    here=inside & (far >= 0) & (far < chips),
                    there=(come >= 0) & (come < chips),
                    landing=in_matrix.at[place(f - sign * 2 * h)],
                )
            )

    def share(h):
        for sign in (1, -1):
            shard = place(f - sign * 2 * h)
            come = z - sign * h
            known = (come >= 0) & (come < chips)
            mail.post(
                in_own if h == 0 else in_matrix.at[shard],
                in_matrix.at[shard],
                sibling,
                here=known,
                there=known,
                landing=in_matrix.at[place(f + 1 - 2 * core - sign * 2 * h)],
            )
            if h == 0:
                break

    hop(1)
    share(0)

    own_fact = pltpu.make_async_copy(facts, all_facts.at[0, f], own_sem.at[0])
    own_fact.start()
    held_copies = [
        pltpu.make_async_copy(xproj, all_xproj.at[core], own_sem.at[1]),
        pltpu.make_async_copy(small, all_small.at[core], own_sem.at[2]),
    ]

    @pl.when(z == g)
    def _():
        for copy in held_copies:
            copy.start()

    own_fact.wait()
    for take in fact_takes:
        take()
    fact_steps = relative(all_facts.at[0], all_facts, parts)

    pairs = ((xproj, all_xproj), (small, all_small))
    for distance in range(1, chips):
        for sign, target in ((1, up), (-1, down)):
            source = g + sign * (distance - 1)
            here = (z == source) & (source + sign >= 0) & (source + sign < chips)
            there = z == source + sign
            for own, every in pairs:
                src = own if distance == 1 else every.at[core]
                take = mail.post(src, every.at[core], target, here=here, there=there)
                take()
        if distance == 1:
            for step in fact_steps:
                step()
    for own, every in pairs:
        for src, where in ((own, z == g), (every.at[core], z != g)):
            mail.post(
                src, every.at[core], sibling, here=where, there=where, landing=every.at[1 - core]
            )

    for h in range(1, chips):
        for take in line[-2:]:
            take()
        if h < chips - 1:
            hop(h + 1)
        share(h)
        if h == 1 or chips == 2:
            for step in halo_steps:
                step()
            for step in token_steps:
                step()
            cotangent_steps = relative(cotangent, all_cotangent, cotangent.shape[0])

    for step in cotangent_steps:
        step()

    @pl.when(z == g)
    def _():
        for copy in held_copies:
            copy.wait()

    mail.finish()


def collect_inputs(tokens, halo, in_own, xproj, small, facts, cotangent):
    groups, parts = lax.axis_size("group"), lax.axis_size("fsdp")
    ins = (tokens, halo, in_own, xproj, small, facts, cotangent)
    outs = [
        jax.ShapeDtypeStruct((groups,) + tokens.shape, tokens.dtype),
        jax.ShapeDtypeStruct((groups,) + halo.shape, halo.dtype),
        jax.ShapeDtypeStruct((parts,) + in_own.shape, in_own.dtype),
        jax.ShapeDtypeStruct((2,) + xproj.shape, xproj.dtype),
        jax.ShapeDtypeStruct((2,) + small.shape, small.dtype),
        jax.ShapeDtypeStruct((groups, parts) + facts.shape, facts.dtype),
        jax.ShapeDtypeStruct((groups,) + cotangent.shape, cotangent.dtype),
    ]
    ways = groups.bit_length() - 1
    copies = 4 * ways * (groups - 1) + (parts - 1) + 4 * (parts // 2 - 1) + 1 + 4 * (parts // 2 - 1) + 4
    outs = pl.pallas_call(
        functools.partial(collect, groups, parts),
        in_specs=[pl.BlockSpec(memory_space=pl.ANY)] * len(ins),
        out_specs=[pl.BlockSpec(memory_space=pl.ANY)] * len(outs),
        out_shape=outs,
        scratch_shapes=[
            pltpu.SemaphoreType.DMA((copies,)),
            pltpu.SemaphoreType.DMA((copies,)),
            pltpu.SemaphoreType.DMA((3,)),
        ],
        compiler_params=pltpu.CompilerParams(collective_id=1, has_side_effects=True),
        name="collect_inputs",
    )(*ins)
    all_tokens, all_halo, in_matrix, all_xproj, all_small, all_facts, all_cotangent = outs
    return (
        all_tokens.at[0].set(tokens),
        all_halo.at[0].set(halo),
        lax.dynamic_update_index_in_dim(in_matrix, in_own, lax.axis_index("fsdp"), 0),
        all_xproj,
        all_small,
        all_facts,
        all_cotangent.at[0].set(cotangent),
    )


def runs(count, ways):
    edges = [count * i // ways for i in range(ways + 1)]
    return [pl.ds(lo, hi - lo) for lo, hi in zip(edges[:-1], edges[1:])]


def greet(groups):
    g = lax.axis_index("group")
    bits = [1 << i for i in range(groups.bit_length() - 1)]
    barrier = pltpu.get_barrier_semaphore()
    for bit in bits:
        pl.semaphore_signal(
            barrier, inc=1, device_id={"group": partner(g, bit)}, device_id_type=pl.DeviceIdType.MESH
        )
    pl.semaphore_wait(barrier, len(bits))
    return g, bits


def total_blocks(groups, terms, out, sums, parcel, landed, gathered, send_sem, recv_sem):
    g, bits = greet(groups)
    ways = len(bits)
    pieces = runs(terms.shape[1], ways)
    mail = Mail(send_sem, recv_sem)
    sums[...] = terms[...]
    held = [set(range(groups)) for _ in range(ways)]
    for t in range(ways):
        coming = []
        for p in range(ways):
            bit = bits[(p + t) % ways]
            for r in sorted(r for r in held[p] if r & bit):
                parcel[r, pieces[p]] = sums[r, pieces[p]].astype(parcel.dtype)
                take = mail.post(
                    parcel.at[r, pieces[p]],
                    landed.at[t, r ^ bit, pieces[p]],
                    {"group": partner(g, bit)},
                )
                coming.append((take, p, r ^ bit))
                held[p].remove(r)
        for take, p, r in coming:
            take()
            sums[r, pieces[p]] = sums[r, pieces[p]] + landed[t, r, pieces[p]].astype(F32)
    gathered[0] = sums[0].astype(gathered.dtype)
    known = [{0: None} for _ in range(ways)]
    for t in range(ways):
        for p in range(ways):
            bit = bits[(p + t) % ways]
            for r, take in list(known[p].items()):
                if take is not None:
                    take()
                known[p][r ^ bit] = mail.post(
                    gathered.at[r, pieces[p]],
                    gathered.at[r ^ bit, pieces[p]],
                    {"group": partner(g, bit)},
                )
    mail.finish()
    out[...] = gathered[...].astype(out.dtype)


def sum_blocks(terms, sent, result, number):
    groups = lax.axis_size("group")
    ways = groups.bit_length() - 1
    shape = (groups, terms.shape[0] // groups, terms.shape[1] * terms.shape[2], terms.shape[3])
    copies = 2 * ways * (groups - 1)
    return pl.pallas_call(
        functools.partial(total_blocks, groups),
        in_specs=[pl.BlockSpec(memory_space=pltpu.VMEM)],
        out_specs=pl.BlockSpec(memory_space=pltpu.VMEM),
        out_shape=jax.ShapeDtypeStruct(shape, result),
        scratch_shapes=[
            pltpu.VMEM(shape, F32),
            pltpu.VMEM(shape, sent),
            pltpu.VMEM((ways,) + shape, sent),
            pltpu.VMEM(shape, BF16),
            pltpu.SemaphoreType.DMA((copies,)),
            pltpu.SemaphoreType.DMA((copies,)),
        ],
        compiler_params=pltpu.CompilerParams(
            collective_id=number, has_side_effects=True, vmem_limit_bytes=32 * MIB
        ),
        name="sum_blocks",
    )(terms.reshape(shape)).reshape(terms.shape)


def front(
    halo_rows,
    info,
    tokens,
    halo,
    modulation,
    in_matrix,
    taps,
    conv_shift,
    xproj,
    modulated,
    extended,
    gate_z,
    conv_out,
    projected,
):
    slot = pl.program_id(0)
    length, model_width = tokens.shape
    channels = gate_z.shape[1]
    count, base = info[slot], info[pl.num_programs(0)]
    outs = (modulated, extended, gate_z, conv_out, projected)

    @pl.when(count <= base)
    def _():
        for out in outs:
            out[...] = jnp.zeros_like(out)

    @pl.when(count > base)
    def _():
        values = jnp.concatenate([tokens[...].astype(F32), halo[...].astype(F32)], axis=0)
        row = lax.broadcasted_iota(jnp.int32, (length + ROWS, 1), 0)
        behind, ahead = row - length - halo_rows, row - halo_rows
        at = jnp.where(row < length, row, jnp.where(behind < 0, behind, ahead))
        at = at + base
        known = (row < length + 2 * halo_rows) & (at >= 0) & (at < count)
        mask = known.astype(F32)
        centered = values - jnp.mean(values, axis=1, keepdims=True)
        normed = centered * lax.rsqrt(
            jnp.mean(centered * centered, axis=1, keepdims=True) + EPSILON
        )
        shift = modulation[:, :model_width]
        scale = modulation[:, model_width : 2 * model_width]
        low = ((normed * (1.0 + scale) + shift) * mask).astype(BF16)
        modulated[...] = low[:length]
        inner = dot32(low, in_matrix[...], ((1,), (0,)))
        gate_z[...] = inner[:length, channels:]
        extended[...] = jnp.zeros_like(extended)
        extended[ROWS : ROWS + length, :] = inner[:length, :channels]
        extended[ROWS - halo_rows : ROWS, :] = inner[length : length + halo_rows, :channels]
        extended[ROWS + length : ROWS + length + halo_rows, :] = inner[
            length + halo_rows : length + 2 * halo_rows, :channels
        ]
        for d in range(2):
            pre = conv_rows(extended, taps, conv_shift, d, length)
            value = (pre * jax.nn.sigmoid(pre) * mask[:length]).astype(BF16)
            conv_out[d] = value
            projected[d] = dot32(value, xproj[d], ((1,), (0,)))


def tap_row(d, k, kernel):
    return ROWS - (kernel - 1) + k if d == 0 else ROWS + (kernel - 1) - k


def conv_rows(extended, taps, conv_shift, d, length):
    kernel = taps.shape[1]
    pre = conv_shift[d : d + 1, :]
    for k in range(kernel):
        row = tap_row(d, k, kernel)
        pre = pre + taps[d, k : k + 1, :] * extended[row : row + length, :]
    return pre


def project(info, tokens, halo, modulation, in_matrix, taps, conv_shift, xproj):
    slots, length, model_width = tokens.shape
    channels = taps.shape[2]
    width = xproj.shape[2]
    fixed = lambda array: pl.BlockSpec(array.shape, lambda s, i: (0,) * array.ndim)
    one = lambda *tail: pl.BlockSpec((None,) + tail, lambda s, i: (s,) + (0,) * len(tail))
    return pl.pallas_call(
        functools.partial(front, taps.shape[1] - 1),
        grid_spec=pltpu.PrefetchScalarGridSpec(
            num_scalar_prefetch=1,
            grid=(slots,),
            in_specs=[
                one(length, model_width),
                one(ROWS, model_width),
                one(1, modulation.shape[2]),
                fixed(in_matrix),
                fixed(taps),
                fixed(conv_shift),
                fixed(xproj),
            ],
            out_specs=[
                one(length, model_width),
                one(length + 2 * ROWS, channels),
                one(length, channels),
                pl.BlockSpec((2, None, length, channels), lambda s, i: (0, s, 0, 0)),
                one(2, length, width),
            ],
        ),
        out_shape=[
            jax.ShapeDtypeStruct((slots, length, model_width), BF16),
            jax.ShapeDtypeStruct((slots, length + 2 * ROWS, channels), F32),
            jax.ShapeDtypeStruct((slots, length, channels), F32),
            jax.ShapeDtypeStruct((2, slots, length, channels), BF16),
            jax.ShapeDtypeStruct((slots, 2, length, width), F32),
        ],
        compiler_params=pltpu.CompilerParams(vmem_limit_bytes=40 * MIB),
        name="project",
    )(info, tokens, halo, modulation, in_matrix, taps, conv_shift, xproj)


def to_owner(groups, parts):
    ratio = parts // groups
    pairs = []
    for g in range(groups):
        for f in range(parts):
            pairs.append((g * parts + f, (f // ratio) * parts + groups * (f % ratio) + g))
    return pairs


def cut(array, pieces):
    slots = array.shape[0]
    edges = [slots * i // pieces for i in range(pieces + 1)]
    return [array[lo:hi] for lo, hi in zip(edges[:-1], edges[1:])]


def flip(array, groups, bit):
    return lax.ppermute(array, "group", [(i, i ^ bit) for i in range(groups)])


def bits_of(groups, first):
    count = groups.bit_length() - 1
    return [1 << ((first + i) % count) for i in range(count)]


def gather_relative(array):
    groups = lax.axis_size("group")
    ways = groups.bit_length() - 1
    found = [[None] * ways for _ in range(groups)]
    for p, part in enumerate(cut(array, ways)):
        held = {0: part}
        for bit in bits_of(groups, p):
            held |= {r ^ bit: flip(value, groups, bit) for r, value in held.items()}
        for r, value in held.items():
            found[r][p] = value
    return jnp.concatenate([part for block in found for part in block], axis=0)


def scatter_relative(array, low):
    groups = lax.axis_size("group")
    ways = groups.bit_length() - 1
    blocks = jnp.split(array, groups, axis=0)
    pieces = [cut(block, ways) for block in blocks]
    sums = []
    for p in range(ways):
        held = {r: pieces[r][p].astype(F32) for r in range(groups)}
        for bit in bits_of(groups, p):
            for r in [r for r in held if r & bit]:
                held[r ^ bit] = held[r ^ bit] + flip(held[r].astype(low), groups, bit).astype(F32)
                del held[r]
        sums.append(held[0])
    return jnp.concatenate(sums, axis=0)


def sum_relative(array, low):
    return gather_relative(scatter_relative(array, F32).astype(low))


def gather_line(array):
    parts, mine = lax.axis_size("fsdp"), lax.axis_index("fsdp")
    chips = parts // 2
    rows = array.shape[0]
    lower, upper = [array], [array]
    for _ in range(chips - 1):
        lower.append(lax.ppermute(lower[-1], "fsdp", [(i, i + 2) for i in range(parts - 2)]))
        upper.append(lax.ppermute(upper[-1], "fsdp", [(i + 2, i) for i in range(parts - 2)]))
    line = jnp.stack(lower[:0:-1] + upper)
    own = lax.dynamic_slice_in_dim(line, chips - 1 - mine // 2, chips, 0)
    other = lax.ppermute(own, "fsdp", [(i, i ^ 1) for i in range(parts)])
    odd = mine % 2 == 1
    pair = jnp.stack([jnp.where(odd, other, own), jnp.where(odd, own, other)], axis=1)
    return pair.reshape(parts * rows, array.shape[1])


def on_device(
    tokens,
    item_bucket,
    slot_item,
    slot_live,
    slot_tokens,
    ada_weight,
    ada_bias,
    in_weight,
    conv_weight,
    conv_bias,
    xproj_weight,
    dt_weight,
    dt_bias,
    a_log,
    skip_gain,
    out_weight,
    cotangent,
):
    own_slots, length, model_width = tokens.shape
    groups, parts = lax.axis_size("group"), lax.axis_size("fsdp")
    g, f = lax.axis_index("group"), lax.axis_index("fsdp")
    slots = own_slots * groups
    inner_width = in_weight.shape[1] // 2
    channels = inner_width // groups
    kernel = conv_weight.shape[1]
    halo = kernel - 1
    rank_width = dt_weight.shape[1]
    width = xproj_weight.shape[2]
    states = (width - rank_width) // 2

    matches = slot_item[:, None] == jnp.arange(item_bucket.shape[0], dtype=jnp.int32)[None, :]
    own_buckets = jnp.sum(jnp.where(matches, item_bucket[None, :], 0), axis=1)
    own_condition = jax.nn.silu(time_embed(own_buckets, model_width)).astype(BF16)
    own_modulation = jnp.dot(own_condition, ada_weight, preferred_element_type=F32)
    own_modulation = own_modulation + ada_bias.astype(F32)
    plain = jnp.stack([slot_tokens * slot_live, own_buckets], axis=1).astype(F32)
    facts = jnp.concatenate([own_modulation, jnp.repeat(plain, LANES // 2, axis=1)], axis=1)

    edges = [(i, i + 1) for i in range(parts - 1)]
    before = lax.ppermute(tokens[:, length - halo :], "fsdp", edges)
    after = lax.ppermute(tokens[:, :halo], "fsdp", [(j, i) for i, j in edges])
    padding = jnp.zeros((own_slots, ROWS - 2 * halo, model_width), tokens.dtype)
    in_own = lax.dynamic_slice_in_dim(
        in_weight.reshape(in_weight.shape[0], 2, groups, channels), g, 1, 2
    ).reshape(in_weight.shape[0], 2 * channels)
    shard = out_weight.shape[0]
    small = jnp.concatenate(
        [
            dt_weight.reshape(2 * rank_width, shard),
            a_log.reshape(2 * states, shard),
            conv_weight.reshape(2 * kernel, shard),
            conv_bias,
            dt_bias,
            skip_gain,
        ],
        axis=0,
    )
    small_rows = small.shape[0]
    small_pad = -small_rows % LANES
    small = jnp.pad(small, ((0, -small_rows % BLOCK), (0, 0)))
    all_tokens, all_halo, in_matrix, all_xproj, all_small, all_facts, all_cotangent = collect_inputs(
        tokens,
        jnp.concatenate([before, after, padding], axis=1),
        in_own,
        xproj_weight,
        small,
        facts,
        cotangent,
    )
    all_cotangent = all_cotangent.reshape(slots, length, model_width)
    all_tokens = all_tokens.reshape(slots, length, model_width)
    all_halo = all_halo.reshape(slots, ROWS, model_width)
    in_matrix = in_matrix.reshape(model_width, 2 * channels)

    piece = shard // groups
    sent = lax.ppermute(
        lax.dynamic_slice_in_dim(out_weight, g * piece, piece, 0),
        ("group", "fsdp"),
        to_owner(groups, parts),
    )
    out_matrix = lax.all_gather(sent, "fsdp", axis=0, tiled=True)
    xproj = jnp.concatenate([all_xproj[0], all_xproj[1]], axis=1)
    rest = jnp.concatenate([all_small[0], all_small[1]], axis=1)
    edge = 0

    def take(rows):
        nonlocal edge
        edge += rows
        return rest[edge - rows : edge]

    dt_matrix = jnp.pad(
        take(2 * rank_width).reshape(2, rank_width, channels), ((0, 0), (0, width - rank_width), (0, 0))
    )
    rate = -jnp.exp(take(2 * states).astype(F32)).reshape(2, states // ROWS, ROWS, channels)
    taps = take(2 * kernel).reshape(2, kernel, channels).astype(F32)
    conv_shift = take(2).astype(F32)
    dt_shift = take(2).astype(F32).reshape(2, 1, channels)
    skip = take(2).astype(F32).reshape(2, 1, channels)
    decay = rate * LOG2E

    columns = facts.shape[1] - LANES
    plain = all_facts[:, 0, :, columns:].reshape(slots, LANES).astype(jnp.int32)
    counts, buckets = plain[:, 0], plain[:, LANES // 2]
    modulation = all_facts[:, :, :, :columns].transpose(0, 2, 1, 3).reshape(slots, parts * columns)
    group_counts = jnp.sum(counts.reshape(groups, own_slots), axis=1).astype(F32)
    share = jnp.repeat(group_counts / jnp.sum(group_counts), own_slots)
    positions = f * length + jnp.arange(length, dtype=jnp.int32)
    mask = (positions[None, :] < counts[:, None]).astype(F32)
    active = (counts > f * length).astype(jnp.int32)
    own_mask = mask[:own_slots, :, None]
    own_share = share[:own_slots, None, None]
    condition = jax.nn.silu(time_embed(buckets, model_width)).astype(BF16)
    shift_mod = modulation[:, None, :model_width]
    scale_mod = modulation[:, None, model_width : 2 * model_width]
    gate_mod = modulation[:, None, 2 * model_width :]

    info = jnp.concatenate([counts, (f * length)[None]]).astype(jnp.int32)
    modulated, wide_x, gate_z, conv_out, projected = project(
        info, all_tokens, all_halo, modulation[:, None, :], in_matrix, taps, conv_shift, xproj
    )
    proj = sum_blocks(projected, F32, F32, 2)
    extended = wide_x[:, ROWS - halo : ROWS + length + halo]
    pre = []
    for d in range(2):
        value = conv_shift[d]
        for k in range(kernel):
            row = k if d == 0 else 2 * halo - k
            value = value + taps[d, k] * extended[:, row : row + length]
        pre.append(value)

    def normalise(values):
        inputs = values.astype(F32)
        centered = inputs - jnp.mean(inputs, axis=2, keepdims=True)
        inv_std = lax.rsqrt(jnp.mean(centered * centered, axis=2, keepdims=True) + EPSILON)
        return (inputs, centered * inv_std, inv_std)

    grad_in_all = all_cotangent.astype(F32) * (mask * share[:, None])[:, :, None]
    branch_gradient = (grad_in_all * gate_mod).astype(BF16)
    grad_gated = jnp.einsum("sld,cd->slc", branch_gradient, out_matrix, preferred_element_type=F32)
    grad_y = grad_gated * jax.nn.silu(gate_z)

    step, end, pull, total, mix_b, mix_c = scan_ends(active, conv_out, proj, grad_y, dt_matrix, dt_shift, decay)
    entry, arrive = pass_states(end, pull, total, decay)
    y, conv_grad, proj_part, dtw_grad, dtb_grad, decay_grad, skip_grad = scan_all(
        active, conv_out, proj, grad_y, step, mix_b, mix_c, entry, arrive, dt_matrix, decay, skip
    )
    proj_grad = sum_blocks(proj_part, BF16, BF16, 3)
    alog_grad = (decay_grad * rate).reshape(2 * states, channels)

    gated_output = (y * jax.nn.silu(gate_z)).astype(BF16)
    branch_part = jnp.einsum("slc,cd->sld", gated_output, out_matrix, preferred_element_type=F32)
    branch = scatter_relative(branch_part, BF16)
    own_gate = gate_mod[:own_slots]
    own_scale = scale_mod[:own_slots]
    own_inputs, own_normed, own_inv = normalise(tokens)
    layer_out = ((own_inputs + own_gate * branch) * own_mask).astype(BF16)
    grad_in = cotangent.astype(F32) * own_mask * own_share
    grad_gate = jnp.sum(grad_in * branch, axis=1)
    outward = jnp.einsum("slc,sld->cd", gated_output, branch_gradient, preferred_element_type=F32)
    grad_z = grad_gated * y * silu_slope(gate_z)

    pre_grads, conv_grads, convb_grads, xproj_grads = [], [], [], []
    for d in range(2):
        into = conv_grad[d] + jnp.einsum(
            "slk,ck->slc", proj_grad[:, d], xproj[d], preferred_element_type=F32
        )
        pre_grad = into * mask[:, :, None] * silu_slope(pre[d])
        xproj_grads.append(
            jnp.einsum("slc,slk->ck", conv_out[d], proj_grad[:, d], preferred_element_type=F32)
        )
        convb_grads.append(jnp.sum(pre_grad, axis=(0, 1)))
        for k in range(kernel):
            row = k if d == 0 else 2 * halo - k
            conv_grads.append(jnp.sum(pre_grad * extended[:, row : row + length], axis=(0, 1)))
        pre_grads.append(pre_grad)
    ahead = lax.ppermute(pre_grads[0][:, :halo], "fsdp", [(j, i) for i, j in edges])
    behind = lax.ppermute(pre_grads[1][:, length - halo :], "fsdp", edges)
    ahead_rows = jnp.concatenate([pre_grads[0], ahead], axis=1)
    behind_rows = jnp.concatenate([behind, pre_grads[1]], axis=1)
    grad_x = jnp.zeros(gate_z.shape, F32)
    for k in range(kernel):
        grad_x = grad_x + taps[0, k] * ahead_rows[:, halo - k : halo - k + length]
        grad_x = grad_x + taps[1, k] * behind_rows[:, k : k + length]
    inner_gradient = jnp.concatenate([grad_x, grad_z], axis=2).astype(BF16)
    grad_mod_part = jnp.einsum(
        "slc,dc->sld", inner_gradient, in_matrix, preferred_element_type=F32
    )
    grad_mod = scatter_relative(grad_mod_part, BF16) * own_mask
    inward = jnp.einsum("sld,slc->dc", modulated, inner_gradient, preferred_element_type=F32)

    grad_shift = jnp.sum(grad_mod, axis=1)
    grad_scale = jnp.sum(grad_mod * own_normed, axis=1)
    grad_normed = grad_mod * (1.0 + own_scale)
    grad_ln = own_inv * (
        grad_normed
        - jnp.mean(grad_normed, axis=2, keepdims=True)
        - own_normed * jnp.mean(grad_normed * own_normed, axis=2, keepdims=True)
    )
    tokens_grad = grad_in + grad_ln

    mod_part = jnp.concatenate([grad_shift, grad_scale, grad_gate], axis=1)
    mod_slice = lax.psum_scatter(mod_part, "fsdp", scatter_dimension=1, tiled=True)
    mod_all = jnp.concatenate(
        [mod_slice] + [flip(mod_slice, groups, r) for r in range(1, groups)], axis=0
    )
    ada_grad = jnp.einsum("sd,sk->dk", condition, mod_all.astype(BF16), preferred_element_type=F32)
    adab_grad = jnp.sum(mod_all, axis=0)

    small_grads = jnp.concatenate(
        [
            dtw_grad[:, :rank_width].reshape(2 * rank_width, channels),
            alog_grad,
            jnp.stack(conv_grads),
            jnp.stack(convb_grads),
            dtb_grad.reshape(2, channels),
            skip_grad.reshape(2, channels),
        ],
        axis=0,
    )
    packed_grads = jnp.concatenate(
        [outward, xproj_grads[0], xproj_grads[1], jnp.pad(small_grads.T, ((0, 0), (0, small_pad)))],
        axis=1,
    ).astype(BF16)
    packed_piece = lax.psum_scatter(packed_grads, "fsdp", scatter_dimension=0, tiled=True)
    packed_piece = lax.ppermute(
        packed_piece, ("group", "fsdp"), [(j, i) for i, j in to_owner(groups, parts)]
    )
    packed_own = lax.all_gather(packed_piece, "group", axis=0, tiled=True).astype(F32)
    out_grad = packed_own[:, :model_width]
    xproj_grad = jnp.stack(
        [packed_own[:, model_width + d * width : model_width + (d + 1) * width] for d in range(2)]
    )
    rest_grads = packed_own[:, model_width + 2 * width :].T
    sizes = [2 * rank_width, 2 * states, 2 * kernel, 2, 2, 2]
    cuts = [sum(sizes[:i]) for i in range(len(sizes) + 1)]
    dtw_out, alog_out, conv_w_out, conv_b_out, dtb_out, skip_out = [
        rest_grads[cuts[i] : cuts[i + 1]] for i in range(len(sizes))
    ]
    inward_piece = lax.psum_scatter(inward.astype(BF16), "fsdp", scatter_dimension=0, tiled=True)
    inward_all = lax.all_gather(inward_piece, "group", axis=0)
    in_grad = (
        inward_all.reshape(groups, in_weight.shape[0], 2, channels)
        .transpose(1, 2, 0, 3)
        .reshape(in_weight.shape)
        .astype(F32)
    )
    return (
        layer_out,
        tokens_grad,
        ada_grad,
        adab_grad,
        in_grad,
        conv_w_out.reshape(2, kernel, shard),
        conv_b_out,
        xproj_grad,
        dtw_out.reshape(2, rank_width, shard),
        dtb_out,
        alog_out.reshape(2, states, shard),
        skip_out,
        out_grad,
    )


def solution(mesh):
    in_specs = (
        P("group", "fsdp", None),
        P(),
        P("group"),
        P("group"),
        P("group"),
        P(None, "fsdp"),
        P("fsdp"),
        P("fsdp", None),
        P(None, None, "fsdp"),
        P(None, "fsdp"),
        P(None, "fsdp", None),
        P(None, None, "fsdp"),
        P(None, "fsdp"),
        P(None, None, "fsdp"),
        P(None, "fsdp"),
        P("fsdp", None),
        P("group", "fsdp", None),
    )
    out_specs = (
        P("group", "fsdp", None),
        P("group", "fsdp", None),
        P(None, "fsdp"),
        P("fsdp"),
        P("fsdp", None),
        P(None, None, "fsdp"),
        P(None, "fsdp"),
        P(None, "fsdp", None),
        P(None, None, "fsdp"),
        P(None, "fsdp"),
        P(None, None, "fsdp"),
        P(None, "fsdp"),
        P("fsdp", None),
    )
    return jax.shard_map(
        on_device, mesh=mesh, in_specs=in_specs, out_specs=out_specs, check_vma=False
    )
```

```python
import functools
import math

import jax
import jax.numpy as jnp
from jax import lax
from jax.experimental import pallas as pl
from jax.experimental.pallas import tpu as pltpu
from jax.sharding import PartitionSpec as P

EPSILON = 1e-06
LANES = 128
ROWS = 8
BLOCK = 16
WIDE = 256
LAG = 3
RUN = 2
LOG2E = math.log2(math.e)
LN2 = math.log(2.0)
F32 = jnp.float32
BF16 = jnp.bfloat16
MIB = 1 << 20


def time_embed(buckets, model_width):
    half_width = model_width // 2
    frequency = jnp.exp(-math.log(10000.0) * jnp.arange(half_width, dtype=F32) / half_width)
    angles = buckets.astype(F32)[:, None] * frequency[None, :]
    return jnp.concatenate([jnp.cos(angles), jnp.sin(angles)], axis=1)


def silu_slope(values):
    sigmoid = jax.nn.sigmoid(values)
    return sigmoid * (1.0 + values * (1.0 - sigmoid))


def dot32(left, right, dims):
    return lax.dot_general(left, right, (dims, ((), ())), preferred_element_type=F32)


def spread_columns(proj_ref, first, count, out_ref):
    rows = proj_ref.shape[0]

    def block(i, carry):
        start = pl.multiple_of(i * ROWS, ROWS)
        turned = jnp.transpose(proj_ref[pl.ds(start, ROWS), :])
        for j in range(ROWS):
            column = turned[first : first + count, j : j + 1]
            out_ref[start + j] = jnp.broadcast_to(column, (count, LANES)).reshape(
                count // ROWS, ROWS, LANES
            )
        return carry

    lax.fori_loop(0, rows // ROWS, block, 0, unroll=True)


def sweep(length, backward, body, start):
    def block(i, carry):
        at = length // ROWS - 1 - i if backward else i
        first = pl.multiple_of(at * ROWS, ROWS)
        blocks = {}

        def row(ref, j):
            if id(ref) not in blocks:
                blocks[id(ref)] = ref[pl.ds(first, ROWS), :]
            rows = blocks[id(ref)]
            return [
                jnp.broadcast_to(rows[j : j + 1, k : k + LANES], (ROWS, LANES))[None]
                for k in range(0, rows.shape[1], LANES)
            ]

        for j in reversed(range(ROWS)) if backward else range(ROWS):
            carry = body(first + j, functools.partial(row, j=j), carry)
        return carry

    return lax.fori_loop(0, length // ROWS, block, start)


def pass_one(
    states, active, conv, proj, grad_y, dt_w, dt_b, decay, step, end, pull, total, mix_b, mix_c, drive
):
    slot, direction = pl.program_id(0), pl.program_id(1)
    length, channels = drive.shape
    chunks = channels // LANES
    halves = states // ROWS
    rank = proj.shape[1] - 2 * states

    @pl.when(active[slot] == 0)
    def _():
        end[...] = jnp.zeros_like(end)
        pull[...] = jnp.zeros_like(pull)
        total[...] = jnp.zeros_like(total)

    @pl.when(active[slot] != 0)
    def _():
        pre = dot32(proj[...].astype(BF16), dt_w[direction], ((1,), (0,))) + dt_b[direction]
        steps = jnp.maximum(pre, 0.0) + jnp.log1p(jnp.exp(-jnp.abs(pre)))
        step[...] = steps
        drive[...] = steps * conv[...].astype(F32)
        total[...] = jnp.broadcast_to(jnp.sum(steps, axis=0, keepdims=True), total.shape)
        spread_columns(proj, rank, states, mix_b)
        spread_columns(proj, rank + states, states, mix_c)

        def token(t, row, carry):
            hidden, running, pulled = carry
            b, c = mix_b[t], mix_c[t]
            step_row, drive_row, grad_row = row(step), row(drive), row(grad_y)
            new = ([], [], [])
            for k in range(chunks):
                lanes = slice(k * LANES, (k + 1) * LANES)
                factor = jnp.exp2(step_row[k] * decay[direction, :, :, lanes])
                new[0].append(factor * hidden[k] + drive_row[k] * b)
                runs = running[k] * factor
                new[1].append(runs)
                new[2].append(pulled[k] + runs * (grad_row[k] * c))
            return tuple(tuple(part) for part in new)

        zero = jnp.zeros((halves, ROWS, LANES), F32)
        start = ((zero,) * chunks, (zero + 1.0,) * chunks, (zero,) * chunks)
        for backward in range(2):

            @pl.when(direction == backward)
            def _():
                hidden, _, pulled = sweep(length, backward, token, start)
                for k in range(chunks):
                    lanes = slice(k * LANES, (k + 1) * LANES)
                    end[:, :, lanes] = hidden[k]
                    pull[:, :, lanes] = pulled[k]


def pass_two(
    states,
    active,
    conv,
    proj,
    grad_y,
    step,
    mix_b,
    mix_c,
    entry,
    arrive,
    gate_z,
    grad_gated,
    dt_w,
    decay,
    skip,
    tile_b,
    tile_c,
    sel,
    take_b,
    take_c,
    gated,
    grad_z,
    conv_grad,
    proj_grad,
    dtw_grad,
    dtb_grad,
    alog_grad,
    skip_grad,
    drive,
    hid_even,
    hid_odd,
    edge,
    gst_even,
    gst_odd,
    thd_even,
    thd_odd,
    mixed,
    sdec,
    scan_y,
    in_part,
    out_part,
    rows_b,
    rows_c,
    drive_low,
    grad_low,
    y,
):
    slot, direction = pl.program_id(0), pl.program_id(1)
    length, channels = drive.shape
    chunks = channels // LANES
    halves = states // ROWS
    wide = BLOCK * states
    pairs = length // (2 * BLOCK)
    hid, gst, thd = (hid_even, hid_odd), (gst_even, gst_odd), (thd_even, thd_odd)
    lanes = [slice(k * LANES, (k + 1) * LANES) for k in range(chunks)]

    @pl.when((slot == 0) & (direction == 0))
    def _():
        dtw_grad[...] = jnp.zeros_like(dtw_grad)
        dtb_grad[...] = jnp.zeros_like(dtb_grad)
        alog_grad[...] = jnp.zeros_like(alog_grad)
        skip_grad[...] = jnp.zeros_like(skip_grad)

    @pl.when(direction == 0)
    def _():
        y[...] = jnp.zeros_like(y)

    @pl.when(active[slot] == 0)
    def _():
        conv_grad[...] = jnp.zeros_like(conv_grad)
        proj_grad[...] = jnp.zeros_like(proj_grad)
        gated[...] = jnp.zeros_like(gated)
        grad_z[...] = jnp.zeros_like(grad_z)

    def low(value):
        return value.reshape(states, LANES).astype(BF16)

    def block_range(pair, odd):
        return pl.ds(pl.multiple_of((2 * pair + odd) * BLOCK, BLOCK), BLOCK)

    def sweep_blocks(backward, tokens, matmuls, start):
        first, second = (1, 0) if backward else (0, 1)

        def two(i, carry):
            pair = pairs - 1 - i if backward else i
            before = lax.rem(pair + (1 if backward else pairs - 1), pairs)
            carry = tokens(pair, first, backward, matmuls(before, second), carry)
            return tokens(pair, second, backward, matmuls(pair, first), carry)

        carry = lax.fori_loop(0, pairs, two, start)
        for issue, keep in matmuls(0 if backward else pairs - 1, second):
            keep(issue())
        return carry

    def pieces(out, rows, left, right, dims, width):
        made = []
        for n in range(0, width, WIDE):
            cols = slice(n, min(n + WIDE, width))
            picked = right[:, cols] if dims[1] == (0,) else right

            def issue(left=left, picked=picked):
                return dot32(left, picked, dims)

            def keep(product, cols=cols):
                out[rows, cols] = product

            made.append((issue, keep))
        return made

    def scan_rows(pair, odd, backward, refs, body, beside, carry):
        order = list(range(BLOCK))[:: -1 if backward else 1]
        waiting = []
        for at_step, j in enumerate(order):
            if j % ROWS == (ROWS - 1 if backward else 0):
                at = pl.multiple_of((2 * pair + odd) * BLOCK + j // ROWS * ROWS, ROWS)
                held = [ref[pl.ds(at, ROWS), :] for ref in refs]
            i = j % ROWS
            rows = [
                [jnp.broadcast_to(h[i : i + 1, c], (ROWS, LANES))[None] for c in lanes] for h in held
            ]
            for issue, keep in beside[at_step * len(beside) // BLOCK : (at_step + 1) * len(beside) // BLOCK]:
                waiting.append((at_step + LAG, keep, issue()))
            carry = body(j, rows, carry)
            while waiting and waiting[0][0] <= at_step:
                _, keep, product = waiting.pop(0)
                keep(product)
        for _, keep, product in waiting:
            keep(product)
        return carry

    def forward_tokens(pair, odd, backward, beside, hidden):
        for k in range(chunks):
            edge[2 * pair + odd, :, lanes[k]] = low(hidden[k])

        def token(j, rows, hidden):
            b = mix_b[(2 * pair + odd) * BLOCK + j]
            new = []
            for k in range(chunks):
                factor = jnp.exp2(rows[0][k] * decay[direction, :, :, lanes[k]])
                value = factor * hidden[k] + rows[1][k] * b
                hid[odd][pair, j, :, lanes[k]] = low(value)
                new.append(value)
            return tuple(new)

        return scan_rows(pair, odd, backward, (step, drive), token, beside, hidden)

    def forward_matmuls(pair, odd):
        rows = block_range(pair, odd)
        h_rows = hid[odd][pair].reshape(wide, channels)
        return pieces(scan_y, rows, rows_c[rows, :], h_rows, ((1,), (0,)), channels) + pieces(
            out_part, rows, grad_low[rows, :], h_rows, ((1,), (1,)), wide
        )

    def backward_tokens(pair, odd, backward, beside, carry):
        earlier = -1 if backward else 1

        def token(j, rows, carry):
            carried, total = carry
            c = mix_c[(2 * pair + odd) * BLOCK + j]
            news, sums = [], []
            p = j + earlier
            for k in range(chunks):
                rate = decay[direction, :, :, lanes[k]]
                factor = jnp.exp2(rows[0][k] * rate)
                grad_state = rows[1][k] * c + carried[k]
                gst[odd][j, :, lanes[k]] = low(grad_state)
                onward = factor * grad_state
                if 0 <= p < BLOCK:
                    before = hid[odd][pair, p, :, lanes[k]]
                else:
                    before = edge[2 * pair + odd, :, lanes[k]]
                through = onward * before.astype(F32).reshape(halves, ROWS, LANES)
                sums.append(total[k] + through * rows[0][k])
                thd[odd][j, :, lanes[k]] = low(through * rate)
                news.append(onward)
            return (tuple(news), tuple(sums))

        return scan_rows(pair, odd, backward, (step, grad_y), token, beside, carry)

    def backward_matmuls(pair, odd):
        rows = block_range(pair, odd)
        g_rows = gst[odd][...].reshape(wide, channels)
        t_rows = thd[odd][...].reshape(wide, channels)
        return (
            pieces(mixed, rows, rows_b[rows, :], g_rows, ((1,), (0,)), channels)
            + pieces(sdec, rows, sel[...].astype(BF16), t_rows, ((1,), (0,)), channels)
            + pieces(in_part, rows, drive_low[rows, :], g_rows, ((1,), (1,)), wide)
        )

    @pl.when(active[slot] != 0)
    def _():
        drive[...] = step[...] * conv[...].astype(F32)
        drive_low[...] = drive[...].astype(BF16)
        grad_low[...] = grad_y[...].astype(BF16)
        proj_low = proj[...].astype(BF16)
        picked = jnp.concatenate([sel[...]] * (length // BLOCK), axis=0)
        rows_b[...] = (dot32(proj_low, tile_b[...], ((1,), (0,))) * picked).astype(BF16)
        rows_c[...] = (dot32(proj_low, tile_c[...], ((1,), (0,))) * picked).astype(BF16)
        zero = jnp.zeros((halves, ROWS, LANES), F32)
        for reverse in (False, True):

            @pl.when(direction == int(reverse))
            def _():
                start = tuple(entry[:, :, c].astype(F32) for c in lanes)
                sweep_blocks(reverse, forward_tokens, forward_matmuls, start)
                start = (tuple(arrive[:, :, c].astype(F32) for c in lanes), (zero,) * chunks)
                _, sums = sweep_blocks(not reverse, backward_tokens, backward_matmuls, start)
                for k in range(chunks):
                    alog_grad[direction, :, :, lanes[k]] += sums[k]

        conv_values = conv[...].astype(F32)
        steps = step[...]
        grads = grad_y[...]
        step_grad = conv_values * mixed[...] + LN2 * sdec[...]
        pre_grad = step_grad * (1.0 - jnp.exp(-steps))
        dtb_grad[direction] += jnp.sum(pre_grad, axis=0, keepdims=True)
        pre_low = pre_grad.astype(BF16)
        proj_grad[...] = (
            dot32((in_part[...] * picked).astype(BF16), take_b[...], ((1,), (0,)))
            + dot32((out_part[...] * picked).astype(BF16), take_c[...], ((1,), (0,)))
            + dot32(pre_low, dt_w[direction], ((1,), (1,)))
        )
        dtw_grad[direction] += dot32(jnp.transpose(proj[...]).astype(BF16), pre_low, ((1,), (0,)))
        y[...] += scan_y[...] + skip[direction] * conv_values
        skip_grad[direction] += jnp.sum(grads * conv_values, axis=0, keepdims=True)
        conv_grad[...] = grads * skip[direction] + steps * mixed[...]

        @pl.when(direction == 1)
        def _():
            total = y[...]
            value = gate_z[...]
            sigmoid = jax.nn.sigmoid(value)
            gated[...] = (total * (value * sigmoid)).astype(BF16)
            slope = sigmoid * (1.0 + value * (1.0 - sigmoid))
            grad_z[...] = (grad_gated[...] * total * slope).astype(BF16)


def whole(array):
    zeros = (0,) * array.ndim
    return pl.BlockSpec(array.shape, lambda s, d, a: zeros)


def scan_ends(active, conv, proj, grad_y, dt_w, dt_b, decay):
    slots, length, channels = grad_y.shape
    halves = decay.shape[1]
    width = proj.shape[3]
    states = halves * ROWS
    turn = lambda *tail: pl.BlockSpec((None, None) + tail, lambda s, d, a: (s, d) + (0,) * len(tail))
    pair = lambda *tail: pl.BlockSpec((None, None) + tail, lambda s, d, a: (d, s) + (0,) * len(tail))
    state = (2, slots, halves, ROWS, channels)
    mixes = (length, halves, ROWS, LANES)
    spare = lambda s, a: jnp.where(a[s] != 0, s, slots)
    kept_pair = pl.BlockSpec(
        (None, None, length, channels), lambda s, d, a: (jnp.where(a[s] != 0, d, 0), spare(s, a), 0, 0)
    )
    kept_mix = pl.BlockSpec(
        (None, None) + mixes, lambda s, d, a: (spare(s, a), jnp.where(a[s] != 0, d, 0), 0, 0, 0, 0)
    )
    return pl.pallas_call(
        functools.partial(pass_one, states),
        grid_spec=pltpu.PrefetchScalarGridSpec(
            num_scalar_prefetch=1,
            grid=(slots, 2),
            in_specs=[
                pair(length, channels),
                turn(length, width),
                pl.BlockSpec((None, length, channels), lambda s, d, a: (s, 0, 0)),
                whole(dt_w),
                whole(dt_b),
                whole(decay),
            ],
            out_specs=[
                kept_pair,
                pair(halves, ROWS, channels),
                pair(halves, ROWS, channels),
                pair(ROWS, channels),
                kept_mix,
                kept_mix,
            ],
            scratch_shapes=[pltpu.VMEM((length, channels), F32)],
        ),
        out_shape=[
            jax.ShapeDtypeStruct((2, slots + 1, length, channels), F32),
            jax.ShapeDtypeStruct(state, F32),
            jax.ShapeDtypeStruct(state, F32),
            jax.ShapeDtypeStruct((2, slots, ROWS, channels), F32),
            jax.ShapeDtypeStruct((slots + 1, 2) + mixes, F32),
            jax.ShapeDtypeStruct((slots + 1, 2) + mixes, F32),
        ],
        compiler_params=pltpu.CompilerParams(vmem_limit_bytes=24 * MIB),
        name="scan_ends",
    )(active, conv, proj, grad_y, dt_w, dt_b, decay)


def scan_all(
    active, conv, proj, grad_y, step, mix_b, mix_c, entering, gate_z, grad_gated, dt_w, decay, skip
):
    slots, length, channels = grad_y.shape
    halves = decay.shape[1]
    width = proj.shape[3]
    states = halves * ROWS
    wide = BLOCK * states
    rank = width - 2 * states
    column = jnp.arange(width)[:, None]
    lane = jnp.arange(wide)[None, :]
    tile_b = (column == rank + lane % states).astype(BF16)
    tile_c = (column == rank + states + lane % states).astype(BF16)
    sel = (jnp.arange(BLOCK)[:, None] == lane // states).astype(F32)
    turn = lambda *tail: pl.BlockSpec((None, None) + tail, lambda s, d, a: (s, d) + (0,) * len(tail))
    pair = lambda *tail: pl.BlockSpec((None, None) + tail, lambda s, d, a: (d, s) + (0,) * len(tail))
    one = pl.BlockSpec((None, length, channels), lambda s, d, a: (s, 0, 0))
    constants = (dt_w, decay, skip, tile_b, tile_c, sel, tile_b.T, tile_c.T)
    sums = (
        jax.ShapeDtypeStruct((2, width, channels), F32),
        jax.ShapeDtypeStruct((2, 1, channels), F32),
        jax.ShapeDtypeStruct((2, halves, ROWS, channels), F32),
        jax.ShapeDtypeStruct((2, 1, channels), F32),
    )
    pairs = length // (2 * BLOCK)
    read_s = lambda s, a: jnp.where(a[s] != 0, s, 0)
    read_d = lambda s, d, a: jnp.where(a[s] != 0, d, 0)
    got_one = pl.BlockSpec((None, length, channels), lambda s, d, a: (read_s(s, a), 0, 0))

    def got_pair(*tail):
        return pl.BlockSpec(
            (None, None) + tail, lambda s, d, a: (read_d(s, d, a), read_s(s, a)) + (0,) * len(tail)
        )

    def got_turn(*tail):
        return pl.BlockSpec(
            (None, None) + tail, lambda s, d, a: (read_s(s, a), read_d(s, d, a)) + (0,) * len(tail)
        )

    def got_state(kind):
        def place(s, d, a):
            way = read_d(s, d, a)
            return (way + kind * (1 - 2 * way), read_s(s, a), kind, 0, 0, 0)

        return pl.BlockSpec((None, None, None, halves, ROWS, channels), place)

    return pl.pallas_call(
        functools.partial(pass_two, states),
        grid_spec=pltpu.PrefetchScalarGridSpec(
            num_scalar_prefetch=1,
            grid=(slots, 2),
            in_specs=[
                got_pair(length, channels),
                got_turn(length, width),
                got_one,
                got_pair(length, channels),
                got_turn(length, halves, ROWS, LANES),
                got_turn(length, halves, ROWS, LANES),
                got_state(0),
                got_state(1),
                got_one,
                got_one,
            ]
            + [whole(c) for c in constants],
            out_specs=[one, one, pair(length, channels), turn(length, width)] + [whole(c) for c in sums],
            scratch_shapes=[pltpu.VMEM((length, channels), F32)]
            + [pltpu.VMEM((pairs, BLOCK, states, channels), BF16)] * 2
            + [pltpu.VMEM((2 * pairs, states, channels), BF16)]
            + [pltpu.VMEM((BLOCK, states, channels), BF16)] * 4
            + [pltpu.VMEM((length, channels), F32)] * 3
            + [pltpu.VMEM((length, wide), F32)] * 2
            + [pltpu.VMEM((length, wide), BF16)] * 2
            + [pltpu.VMEM((length, channels), BF16)] * 2
            + [pltpu.VMEM((length, channels), F32)],
        ),
        out_shape=[
            jax.ShapeDtypeStruct((slots, length, channels), BF16),
            jax.ShapeDtypeStruct((slots, length, channels), BF16),
            jax.ShapeDtypeStruct((2, slots, length, channels), F32),
            jax.ShapeDtypeStruct((slots, 2, length, width), F32),
        ]
        + list(sums),
        compiler_params=pltpu.CompilerParams(vmem_limit_bytes=44 * MIB),
        name="scan_all",
    )(active, conv, proj, grad_y, step, mix_b, mix_c, entering, entering, gate_z, grad_gated, *constants)


def chain(count, run, end, pull, total, decay, entering, held, send_sem, recv_sem):
    mine = lax.axis_index("fsdp")
    waves = end.shape[1] // run
    mesh_id = pl.DeviceIdType.MESH
    after, before = lax.rem(mine + 1, count), lax.rem(mine + count - 1, count)
    barrier = pltpu.get_barrier_semaphore()
    for other in (after, before):
        pl.semaphore_signal(barrier, inc=1, device_id={"fsdp": other}, device_id_type=mesh_id)
    pl.semaphore_wait(barrier, 2)
    ways = ((mine > 0, mine < count - 1, after), (mine < count - 1, mine > 0, before))

    def copy(way, s):
        slots = pl.ds(s * run, run)
        return pltpu.make_async_remote_copy(
            src_ref=held.at[way, slots],
            dst_ref=entering.at[way, slots],
            send_sem=send_sem.at[way, s],
            recv_sem=recv_sem.at[way, s],
            device_id={"fsdp": ways[way][2]},
            device_id_type=mesh_id,
        )

    lags = (mine, count - 1 - mine)

    def wave(turn, carry):
        for way in range(2):
            gets, sends, _ = ways[way]
            s = turn - lags[way]
            here = (s >= 0) & (s < waves)

            @pl.when(here & gets)
            def _():
                copy(way, s).wait_recv()

            @pl.when(here & jnp.logical_not(gets))
            def _():
                entering[way, pl.ds(s * run, run)] = jnp.zeros((run,) + entering.shape[2:], entering.dtype)

            @pl.when(here & sends)
            def _():
                for i in range(run):
                    slot = s * run + i
                    for kind, local in enumerate((end, pull)):
                        d = (way + kind) % 2
                        through = jnp.exp2(decay[d] * total[d, slot][None])
                        value = through * entering[way, slot, kind].astype(F32) + local[d, slot]
                        held[way, slot, kind] = value.astype(held.dtype)
                copy(way, s).start()

        return carry

    lax.fori_loop(0, waves + count - 1, wave, 0)

    def drain(s, carry):
        for way in range(2):

            @pl.when(ways[way][1])
            def _():
                copy(way, s).wait_send()

        return carry

    lax.fori_loop(0, waves, drain, 0)


def pass_states(end, pull, total, decay):
    _, slots, halves, rows, channels = end.shape
    run = RUN
    shape = (2, slots, 2, halves, rows, channels)
    return pl.pallas_call(
        functools.partial(chain, lax.axis_size("fsdp"), run),
        in_specs=[pl.BlockSpec(memory_space=pltpu.VMEM)] * 4,
        out_specs=pl.BlockSpec(memory_space=pltpu.VMEM),
        out_shape=jax.ShapeDtypeStruct(shape, BF16),
        scratch_shapes=[
            pltpu.VMEM(shape, BF16),
            pltpu.SemaphoreType.DMA((2, slots // run)),
            pltpu.SemaphoreType.DMA((2, slots // run)),
        ],
        compiler_params=pltpu.CompilerParams(
            collective_id=0, has_side_effects=True, vmem_limit_bytes=40 * MIB
        ),
        name="pass_states",
    )(end, pull, total, decay)


def partner(g, bit):
    return g + bit * (1 - 2 * lax.rem(g // bit, 2))


class Mail:
    def __init__(self, send_sem, recv_sem):
        self.send_sem, self.recv_sem, self.made = send_sem, recv_sem, []

    def post(self, src, dst, target, here=None, there=None, landing=None):
        n = len(self.made)
        copy = lambda into: pltpu.make_async_remote_copy(
            src_ref=src,
            dst_ref=into,
            send_sem=self.send_sem.at[n],
            recv_sem=self.recv_sem.at[n],
            device_id=target,
            device_id_type=pl.DeviceIdType.MESH,
        )
        when = lambda cond: (lambda body: body()) if cond is None else pl.when(cond)
        landing = dst if landing is None else landing
        entry = dict(got=False)

        @when(here)
        def _():
            copy(dst).start()

        def take():
            if not entry["got"]:
                entry["got"] = True

                @when(there)
                def _():
                    copy(landing).wait_recv()

        def sent():
            @when(here)
            def _():
                copy(dst).wait_send()

        self.made.append((take, sent))
        return take

    def finish(self):
        for take, _ in self.made:
            take()
        for _, sent in self.made:
            sent()


def collect(
    groups,
    parts,
    tokens,
    halo,
    in_own,
    xproj,
    small,
    facts,
    cotangent,
    all_tokens,
    all_halo,
    in_matrix,
    all_xproj,
    all_small,
    all_facts,
    all_cotangent,
    send_sem,
    recv_sem,
    own_sem,
):
    g, f = lax.axis_index("group"), lax.axis_index("fsdp")
    chips = parts // 2
    z, core = f // 2, lax.rem(f, 2)
    ways = groups.bit_length() - 1
    bits = [1 << i for i in range(ways)]
    barrier = pltpu.get_barrier_semaphore()
    for bit in bits:
        pl.semaphore_signal(
            barrier, inc=1, device_id={"group": partner(g, bit)}, device_id_type=pl.DeviceIdType.MESH
        )
    for k in range(1, parts):
        pl.semaphore_signal(
            barrier,
            inc=1,
            device_id={"fsdp": lax.rem(f + k, parts)},
            device_id_type=pl.DeviceIdType.MESH,
        )
    pl.semaphore_wait(barrier, ways + parts - 1)
    mail = Mail(send_sem, recv_sem)
    place = lambda part: lax.rem(part + 2 * parts, parts)
    sibling = {"fsdp": f + 1 - 2 * core}
    up, down = {"fsdp": f + 2}, {"fsdp": f - 2}

    fact_takes = []
    for k in range(1, parts):
        fact_takes.append(
            mail.post(
                facts,
                all_facts.at[0, f],
                {"fsdp": lax.rem(f + k, parts)},
                landing=all_facts.at[0, lax.rem(f + parts - k, parts)],
            )
        )

    def cuts(count):
        edges = [count * i // ways for i in range(ways + 1)]
        return [pl.ds(lo, hi - lo) for lo, hi in zip(edges[:-1], edges[1:])]

    def relative(own, every, count):
        pieces = cuts(count)
        held = [{0: None} for _ in range(ways)]
        steps = [[] for _ in range(ways)]
        for t in range(ways):
            for p in range(ways):
                bit = bits[(p + t) % ways]
                for r in list(held[p]):
                    held[p][r ^ bit] = None
                    steps[t].append((p, r, bit))
        takes = {}

        def run(chosen):
            for p, r, bit in chosen:
                if r:
                    takes[p, r]()
                src = own.at[pieces[p]] if r == 0 else every.at[r, pieces[p]]
                takes[p, r ^ bit] = mail.post(
                    src, every.at[r ^ bit, pieces[p]], {"group": partner(g, bit)}
                )

        run([move for step in steps for move in step if move[1] == 0])
        return [functools.partial(run, [move for move in step if move[1]]) for step in steps[1:]]

    token_steps = relative(tokens, all_tokens, tokens.shape[0])
    halo_steps = relative(halo, all_halo, halo.shape[0])

    line = []

    def hop(h):
        for sign, target, inside in ((1, up, z < chips - 1), (-1, down, z > 0)):
            shard = f - sign * 2 * (h - 1)
            src = in_own if h == 1 else in_matrix.at[place(shard)]
            far = z - sign * (h - 1)
            come = z - sign * h
            line.append(
                mail.post(
                    src,
                    in_matrix.at[place(shard)],
                    target,
                    here=inside & (far >= 0) & (far < chips),
                    there=(come >= 0) & (come < chips),
                    landing=in_matrix.at[place(f - sign * 2 * h)],
                )
            )

    def share(h):
        for sign in (1, -1):
            shard = place(f - sign * 2 * h)
            come = z - sign * h
            known = (come >= 0) & (come < chips)
            mail.post(
                in_own if h == 0 else in_matrix.at[shard],
                in_matrix.at[shard],
                sibling,
                here=known,
                there=known,
                landing=in_matrix.at[place(f + 1 - 2 * core - sign * 2 * h)],
            )
            if h == 0:
                break

    hop(1)
    share(0)

    own_fact = pltpu.make_async_copy(facts, all_facts.at[0, f], own_sem.at[0])
    own_fact.start()
    held_copies = [
        pltpu.make_async_copy(xproj, all_xproj.at[core], own_sem.at[1]),
        pltpu.make_async_copy(small, all_small.at[core], own_sem.at[2]),
    ]

    @pl.when(z == g)
    def _():
        for copy in held_copies:
            copy.start()

    own_fact.wait()
    for take in fact_takes:
        take()
    fact_steps = relative(all_facts.at[0], all_facts, parts)

    pairs = ((xproj, all_xproj), (small, all_small))
    for distance in range(1, chips):
        for sign, target in ((1, up), (-1, down)):
            source = g + sign * (distance - 1)
            here = (z == source) & (source + sign >= 0) & (source + sign < chips)
            there = z == source + sign
            for own, every in pairs:
                src = own if distance == 1 else every.at[core]
                take = mail.post(src, every.at[core], target, here=here, there=there)
                take()
        if distance == 1:
            for step in fact_steps:
                step()
    for own, every in pairs:
        for src, where in ((own, z == g), (every.at[core], z != g)):
            mail.post(
                src, every.at[core], sibling, here=where, there=where, landing=every.at[1 - core]
            )

    for h in range(1, chips):
        for take in line[-2:]:
            take()
        if h < chips - 1:
            hop(h + 1)
        share(h)
        if h == 1 or chips == 2:
            for step in halo_steps:
                step()
            for step in token_steps:
                step()
            cotangent_steps = relative(cotangent, all_cotangent, cotangent.shape[0])

    for step in cotangent_steps:
        step()

    @pl.when(z == g)
    def _():
        for copy in held_copies:
            copy.wait()

    mail.finish()


def collect_inputs(tokens, halo, in_own, xproj, small, facts, cotangent):
    groups, parts = lax.axis_size("group"), lax.axis_size("fsdp")
    ins = (tokens, halo, in_own, xproj, small, facts, cotangent)
    outs = [
        jax.ShapeDtypeStruct((groups,) + tokens.shape, tokens.dtype),
        jax.ShapeDtypeStruct((groups,) + halo.shape, halo.dtype),
        jax.ShapeDtypeStruct((parts,) + in_own.shape, in_own.dtype),
        jax.ShapeDtypeStruct((2,) + xproj.shape, xproj.dtype),
        jax.ShapeDtypeStruct((2,) + small.shape, small.dtype),
        jax.ShapeDtypeStruct((groups, parts) + facts.shape, facts.dtype),
        jax.ShapeDtypeStruct((groups,) + cotangent.shape, cotangent.dtype),
    ]
    ways = groups.bit_length() - 1
    copies = 4 * ways * (groups - 1) + (parts - 1) + 4 * (parts // 2 - 1) + 1 + 4 * (parts // 2 - 1) + 4
    outs = pl.pallas_call(
        functools.partial(collect, groups, parts),
        in_specs=[pl.BlockSpec(memory_space=pl.ANY)] * len(ins),
        out_specs=[pl.BlockSpec(memory_space=pl.ANY)] * len(outs),
        out_shape=outs,
        scratch_shapes=[
            pltpu.SemaphoreType.DMA((copies,)),
            pltpu.SemaphoreType.DMA((copies,)),
            pltpu.SemaphoreType.DMA((3,)),
        ],
        compiler_params=pltpu.CompilerParams(collective_id=1, has_side_effects=True),
        name="collect_inputs",
    )(*ins)
    all_tokens, all_halo, in_matrix, all_xproj, all_small, all_facts, all_cotangent = outs
    return (
        all_tokens.at[0].set(tokens),
        all_halo.at[0].set(halo),
        lax.dynamic_update_index_in_dim(in_matrix, in_own, lax.axis_index("fsdp"), 0),
        all_xproj,
        all_small,
        all_facts,
        all_cotangent.at[0].set(cotangent),
    )


def runs(count, ways):
    edges = [count * i // ways for i in range(ways + 1)]
    return [pl.ds(lo, hi - lo) for lo, hi in zip(edges[:-1], edges[1:])]


def greet(groups):
    g = lax.axis_index("group")
    bits = [1 << i for i in range(groups.bit_length() - 1)]
    barrier = pltpu.get_barrier_semaphore()
    for bit in bits:
        pl.semaphore_signal(
            barrier, inc=1, device_id={"group": partner(g, bit)}, device_id_type=pl.DeviceIdType.MESH
        )
    pl.semaphore_wait(barrier, len(bits))
    return g, bits


def total_blocks(groups, terms, out, sums, parcel, landed, gathered, send_sem, recv_sem):
    g, bits = greet(groups)
    ways = len(bits)
    pieces = runs(terms.shape[1], ways)
    mail = Mail(send_sem, recv_sem)
    sums[...] = terms[...]
    held = [set(range(groups)) for _ in range(ways)]
    for t in range(ways):
        coming = []
        for p in range(ways):
            bit = bits[(p + t) % ways]
            for r in sorted(r for r in held[p] if r & bit):
                parcel[r, pieces[p]] = sums[r, pieces[p]].astype(parcel.dtype)
                take = mail.post(
                    parcel.at[r, pieces[p]],
                    landed.at[t, r ^ bit, pieces[p]],
                    {"group": partner(g, bit)},
                )
                coming.append((take, p, r ^ bit))
                held[p].remove(r)
        for take, p, r in coming:
            take()
            sums[r, pieces[p]] = sums[r, pieces[p]] + landed[t, r, pieces[p]].astype(F32)
    gathered[0] = sums[0].astype(gathered.dtype)
    known = [{0: None} for _ in range(ways)]
    for t in range(ways):
        for p in range(ways):
            bit = bits[(p + t) % ways]
            for r, take in list(known[p].items()):
                if take is not None:
                    take()
                known[p][r ^ bit] = mail.post(
                    gathered.at[r, pieces[p]],
                    gathered.at[r ^ bit, pieces[p]],
                    {"group": partner(g, bit)},
                )
    mail.finish()
    out[...] = gathered[...].astype(out.dtype)


def sum_blocks(terms, sent, result, number):
    groups = lax.axis_size("group")
    ways = groups.bit_length() - 1
    shape = (groups, terms.shape[0] // groups, terms.shape[1] * terms.shape[2], terms.shape[3])
    copies = 2 * ways * (groups - 1)
    return pl.pallas_call(
        functools.partial(total_blocks, groups),
        in_specs=[pl.BlockSpec(memory_space=pltpu.VMEM)],
        out_specs=pl.BlockSpec(memory_space=pltpu.VMEM),
        out_shape=jax.ShapeDtypeStruct(shape, result),
        scratch_shapes=[
            pltpu.VMEM(shape, F32),
            pltpu.VMEM(shape, sent),
            pltpu.VMEM((ways,) + shape, sent),
            pltpu.VMEM(shape, BF16),
            pltpu.SemaphoreType.DMA((copies,)),
            pltpu.SemaphoreType.DMA((copies,)),
        ],
        compiler_params=pltpu.CompilerParams(
            collective_id=number, has_side_effects=True, vmem_limit_bytes=32 * MIB
        ),
        name="sum_blocks",
    )(terms.reshape(shape)).reshape(terms.shape)


def front(
    halo_rows,
    info,
    tokens,
    halo,
    modulation,
    in_matrix,
    taps,
    conv_shift,
    xproj,
    modulated,
    extended,
    gate_z,
    conv_out,
    projected,
):
    slot = pl.program_id(0)
    length, model_width = tokens.shape
    channels = gate_z.shape[1]
    count, base = info[slot], info[pl.num_programs(0)]
    outs = (modulated, extended, gate_z, conv_out, projected)

    @pl.when(count <= base)
    def _():
        for out in outs:
            out[...] = jnp.zeros_like(out)

    @pl.when(count > base)
    def _():
        values = jnp.concatenate([tokens[...].astype(F32), halo[...].astype(F32)], axis=0)
        row = lax.broadcasted_iota(jnp.int32, (length + ROWS, 1), 0)
        behind, ahead = row - length - halo_rows, row - halo_rows
        at = jnp.where(row < length, row, jnp.where(behind < 0, behind, ahead))
        at = at + base
        known = (row < length + 2 * halo_rows) & (at >= 0) & (at < count)
        mask = known.astype(F32)
        centered = values - jnp.mean(values, axis=1, keepdims=True)
        normed = centered * lax.rsqrt(
            jnp.mean(centered * centered, axis=1, keepdims=True) + EPSILON
        )
        shift = modulation[:, :model_width]
        scale = modulation[:, model_width : 2 * model_width]
        low = ((normed * (1.0 + scale) + shift) * mask).astype(BF16)
        modulated[...] = low[:length]
        inner = dot32(low, in_matrix[...], ((1,), (0,)))
        gate_z[...] = inner[:length, channels:]
        extended[...] = jnp.zeros_like(extended)
        extended[ROWS : ROWS + length, :] = inner[:length, :channels]
        extended[ROWS - halo_rows : ROWS, :] = inner[length : length + halo_rows, :channels]
        extended[ROWS + length : ROWS + length + halo_rows, :] = inner[
            length + halo_rows : length + 2 * halo_rows, :channels
        ]
        for d in range(2):
            pre = conv_rows(extended, taps, conv_shift, d, length)
            value = (pre * jax.nn.sigmoid(pre) * mask[:length]).astype(BF16)
            conv_out[d] = value
            projected[d] = dot32(value, xproj[d], ((1,), (0,)))


def tap_row(d, k, kernel):
    return ROWS - (kernel - 1) + k if d == 0 else ROWS + (kernel - 1) - k


def conv_rows(extended, taps, conv_shift, d, length):
    kernel = taps.shape[1]
    pre = conv_shift[d : d + 1, :]
    for k in range(kernel):
        row = tap_row(d, k, kernel)
        pre = pre + taps[d, k : k + 1, :] * extended[row : row + length, :]
    return pre


def project(info, tokens, halo, modulation, in_matrix, taps, conv_shift, xproj):
    slots, length, model_width = tokens.shape
    channels = taps.shape[2]
    width = xproj.shape[2]
    fixed = lambda array: pl.BlockSpec(array.shape, lambda s, i: (0,) * array.ndim)
    one = lambda *tail: pl.BlockSpec((None,) + tail, lambda s, i: (s,) + (0,) * len(tail))
    return pl.pallas_call(
        functools.partial(front, taps.shape[1] - 1),
        grid_spec=pltpu.PrefetchScalarGridSpec(
            num_scalar_prefetch=1,
            grid=(slots,),
            in_specs=[
                one(length, model_width),
                one(ROWS, model_width),
                one(1, modulation.shape[2]),
                fixed(in_matrix),
                fixed(taps),
                fixed(conv_shift),
                fixed(xproj),
            ],
            out_specs=[
                one(length, model_width),
                one(length + 2 * ROWS, channels),
                one(length, channels),
                pl.BlockSpec((2, None, length, channels), lambda s, i: (0, s, 0, 0)),
                one(2, length, width),
            ],
        ),
        out_shape=[
            jax.ShapeDtypeStruct((slots, length, model_width), BF16),
            jax.ShapeDtypeStruct((slots, length + 2 * ROWS, channels), F32),
            jax.ShapeDtypeStruct((slots, length, channels), F32),
            jax.ShapeDtypeStruct((2, slots, length, channels), BF16),
            jax.ShapeDtypeStruct((slots, 2, length, width), F32),
        ],
        compiler_params=pltpu.CompilerParams(vmem_limit_bytes=40 * MIB),
        name="project",
    )(info, tokens, halo, modulation, in_matrix, taps, conv_shift, xproj)


def back(
    info,
    extended,
    conv_grad,
    proj_grad,
    conv_out,
    taps,
    conv_shift,
    xproj,
    grad_x,
    rim,
    sums,
    xproj_grad,
    rows,
):
    slot = pl.program_id(0)
    length, channels = grad_x.shape
    kernel = taps.shape[1]
    halo = kernel - 1
    count, base = info[slot], info[pl.num_programs(0)]

    @pl.when(slot == 0)
    def _():
        sums[...] = jnp.zeros_like(sums)
        xproj_grad[...] = jnp.zeros_like(xproj_grad)
        rows[...] = jnp.zeros_like(rows)

    @pl.when(count <= base)
    def _():
        grad_x[...] = jnp.zeros_like(grad_x)
        rim[...] = jnp.zeros_like(rim)

    @pl.when(count > base)
    def _():
        row = lax.broadcasted_iota(jnp.int32, (length, 1), 0)
        mask = (base + row < count).astype(F32)
        for d in range(2):
            pre = conv_rows(extended, taps, conv_shift, d, length)
            sigmoid = jax.nn.sigmoid(pre)
            slope = sigmoid * (1.0 + pre * (1.0 - sigmoid))
            into = conv_grad[d] + dot32(proj_grad[d], xproj[d], ((1,), (1,)))
            value = into * mask * slope
            rows[d, ROWS : ROWS + length, :] = value
            turned = jnp.transpose(proj_grad[d].astype(F32)).astype(BF16)
            xproj_grad[d] += dot32(turned, conv_out[d], ((1,), (0,)))
            for k in range(kernel):
                first = tap_row(d, k, kernel)
                at = d * kernel + k
                sums[at : at + 1, :] += jnp.sum(
                    value * extended[first : first + length, :], axis=0, keepdims=True
                )
            at = 2 * kernel + d
            sums[at : at + 1, :] += jnp.sum(value, axis=0, keepdims=True)
        total = jnp.zeros((length, channels), F32)
        for k in range(kernel):
            ahead, behind = ROWS + halo - k, ROWS - halo + k
            total = total + taps[0, k : k + 1, :] * rows[0, ahead : ahead + length, :]
            total = total + taps[1, k : k + 1, :] * rows[1, behind : behind + length, :]
        grad_x[...] = total
        rim[0] = rows[0, ROWS : 2 * ROWS, :]
        rim[1] = rows[1, length : length + ROWS, :]


def back_through(info, extended, conv_grad, proj_grad, conv_out, taps, conv_shift, xproj):
    slots = extended.shape[0]
    length, channels = conv_out.shape[2:]
    width = xproj.shape[2]
    kernel = taps.shape[1]
    sum_rows = 2 * ROWS * ((2 * kernel + 2 + 2 * ROWS - 1) // (2 * ROWS))
    fixed = lambda array: pl.BlockSpec(array.shape, lambda s, i: (0,) * len(array.shape))
    one = lambda *tail: pl.BlockSpec((None,) + tail, lambda s, i: (s,) + (0,) * len(tail))
    both = pl.BlockSpec((2, None, length, channels), lambda s, i: (0, s, 0, 0))
    sums = jax.ShapeDtypeStruct((sum_rows, channels), F32)
    xproj_grad = jax.ShapeDtypeStruct((2, width, channels), F32)
    return pl.pallas_call(
        back,
        grid_spec=pltpu.PrefetchScalarGridSpec(
            num_scalar_prefetch=1,
            grid=(slots,),
            in_specs=[
                one(length + 2 * ROWS, channels),
                both,
                one(2, length, width),
                both,
                fixed(taps),
                fixed(conv_shift),
                fixed(xproj),
            ],
            out_specs=[one(length, channels), one(2, ROWS, channels), fixed(sums), fixed(xproj_grad)],
            scratch_shapes=[pltpu.VMEM((2, length + 2 * ROWS, channels), F32)],
        ),
        out_shape=[
            jax.ShapeDtypeStruct((slots, length, channels), F32),
            jax.ShapeDtypeStruct((slots, 2, ROWS, channels), F32),
            sums,
            xproj_grad,
        ],
        compiler_params=pltpu.CompilerParams(vmem_limit_bytes=32 * MIB),
        cost_estimate=pl.CostEstimate(
            flops=24000 * slots * length * channels,
            bytes_accessed=30 * slots * length * channels,
            transcendentals=0,
        ),
        name="back_through",
    )(info, extended, conv_grad, proj_grad, conv_out, taps, conv_shift, xproj)


def scatter(groups, terms, out, parcel, landed, send_sem, recv_sem):
    g, bits = greet(groups)
    ways = len(bits)
    pieces = runs(terms.shape[1], ways)
    mail = Mail(send_sem, recv_sem)
    held = [set(range(groups)) for _ in range(ways)]
    came = [{r: [] for r in range(groups)} for _ in range(ways)]

    def summed(p, r):
        value = terms[r, pieces[p]].astype(F32)
        for t, take in came[p][r]:
            take()
            value = value + landed[t, r, pieces[p]].astype(F32)
        return value

    for t in range(ways):
        for p in range(ways):
            bit = bits[(p + t) % ways]
            for r in sorted(r for r in held[p] if r & bit):
                src = terms
                if t:
                    parcel[r, pieces[p]] = summed(p, r).astype(parcel.dtype)
                    src = parcel
                take = mail.post(
                    src.at[r, pieces[p]],
                    landed.at[t, r ^ bit, pieces[p]],
                    {"group": partner(g, bit)},
                )
                came[p][r ^ bit].append((t, take))
                held[p].remove(r)
    for p in range(ways):
        out[pieces[p]] = summed(p, 0)
    mail.finish()


def scatter_blocks(terms, number):
    groups = lax.axis_size("group")
    ways = groups.bit_length() - 1
    slots, length, model_width = terms.shape
    block = (slots // groups, length, model_width)
    copies = ways * (groups - 1)
    return pl.pallas_call(
        functools.partial(scatter, groups),
        in_specs=[pl.BlockSpec(memory_space=pltpu.VMEM)],
        out_specs=pl.BlockSpec(memory_space=pltpu.VMEM),
        out_shape=jax.ShapeDtypeStruct(block, F32),
        scratch_shapes=[
            pltpu.VMEM((groups,) + block, terms.dtype),
            pltpu.VMEM((ways, groups) + block, terms.dtype),
            pltpu.SemaphoreType.DMA((copies,)),
            pltpu.SemaphoreType.DMA((copies,)),
        ],
        compiler_params=pltpu.CompilerParams(
            collective_id=number, has_side_effects=True, vmem_limit_bytes=48 * MIB
        ),
        name="scatter_blocks",
    )(terms.reshape((groups,) + block))


def modulation_total(groups, parts, terms, out, landed, send_sem, recv_sem):
    g, f = lax.axis_index("group"), lax.axis_index("fsdp")
    bits = [1 << i for i in range(groups.bit_length() - 1)]
    ways = len(bits)
    barrier = pltpu.get_barrier_semaphore()
    others = [{"group": partner(g, bit)} for bit in bits]
    others += [{"fsdp": lax.rem(f + k, parts)} for k in range(1, parts)]
    for other in others:
        pl.semaphore_signal(barrier, inc=1, device_id=other, device_id_type=pl.DeviceIdType.MESH)
    pl.semaphore_wait(barrier, len(others))
    mail = Mail(send_sem, recv_sem)
    takes = []
    for k in range(1, parts):
        there = lax.rem(f + k, parts)
        takes.append(mail.post(terms.at[there], landed.at[k - 1], {"fsdp": there}))
    total = terms[f]
    for k, take in enumerate(takes):
        take()
        total = total + landed[k]
    out[0] = total
    known = {0: None}
    for bit in bits:
        for r, take in list(known.items()):
            if take is not None:
                take()
            known[r ^ bit] = mail.post(out.at[r], out.at[r ^ bit], {"group": partner(g, bit)})
    mail.finish()


def sum_modulation(terms, number):
    groups, parts = lax.axis_size("group"), lax.axis_size("fsdp")
    block = terms.shape[1:]
    copies = parts - 1 + groups - 1
    return pl.pallas_call(
        functools.partial(modulation_total, groups, parts),
        in_specs=[pl.BlockSpec(memory_space=pltpu.VMEM)],
        out_specs=pl.BlockSpec(memory_space=pltpu.VMEM),
        out_shape=jax.ShapeDtypeStruct((groups,) + block, F32),
        scratch_shapes=[
            pltpu.VMEM((parts - 1,) + block, F32),
            pltpu.SemaphoreType.DMA((copies,)),
            pltpu.SemaphoreType.DMA((copies,)),
        ],
        compiler_params=pltpu.CompilerParams(collective_id=number, has_side_effects=True),
        name="sum_modulation",
    )(terms)


def to_owner(groups, parts):
    ratio = parts // groups
    pairs = []
    for g in range(groups):
        for f in range(parts):
            pairs.append((g * parts + f, (f // ratio) * parts + groups * (f % ratio) + g))
    return pairs


def cut(array, pieces):
    slots = array.shape[0]
    edges = [slots * i // pieces for i in range(pieces + 1)]
    return [array[lo:hi] for lo, hi in zip(edges[:-1], edges[1:])]


def flip(array, groups, bit):
    return lax.ppermute(array, "group", [(i, i ^ bit) for i in range(groups)])


def bits_of(groups, first):
    count = groups.bit_length() - 1
    return [1 << ((first + i) % count) for i in range(count)]


def gather_relative(array):
    groups = lax.axis_size("group")
    ways = groups.bit_length() - 1
    found = [[None] * ways for _ in range(groups)]
    for p, part in enumerate(cut(array, ways)):
        held = {0: part}
        for bit in bits_of(groups, p):
            held |= {r ^ bit: flip(value, groups, bit) for r, value in held.items()}
        for r, value in held.items():
            found[r][p] = value
    return jnp.concatenate([part for block in found for part in block], axis=0)


def scatter_stage(pieces, groups, t):
    nexts = []
    for p, held in enumerate(pieces):
        bit = bits_of(groups, p)[t]
        sums = {r: value for r, value in held.items() if not r & bit}
        for r in [r for r in held if r & bit]:
            came = flip(held[r], groups, bit).astype(F32)
            sums[r ^ bit] = (sums[r ^ bit].astype(F32) + came).astype(BF16)
        nexts.append(sums)
    return nexts


def on_device(
    tokens,
    item_bucket,
    slot_item,
    slot_live,
    slot_tokens,
    ada_weight,
    ada_bias,
    in_weight,
    conv_weight,
    conv_bias,
    xproj_weight,
    dt_weight,
    dt_bias,
    a_log,
    skip_gain,
    out_weight,
    cotangent,
):
    own_slots, length, model_width = tokens.shape
    groups, parts = lax.axis_size("group"), lax.axis_size("fsdp")
    g, f = lax.axis_index("group"), lax.axis_index("fsdp")
    slots = own_slots * groups
    inner_width = in_weight.shape[1] // 2
    channels = inner_width // groups
    kernel = conv_weight.shape[1]
    halo = kernel - 1
    rank_width = dt_weight.shape[1]
    width = xproj_weight.shape[2]
    states = (width - rank_width) // 2

    matches = slot_item[:, None] == jnp.arange(item_bucket.shape[0], dtype=jnp.int32)[None, :]
    own_buckets = jnp.sum(jnp.where(matches, item_bucket[None, :], 0), axis=1)
    own_condition = jax.nn.silu(time_embed(own_buckets, model_width)).astype(BF16)
    own_modulation = jnp.dot(own_condition, ada_weight, preferred_element_type=F32)
    own_modulation = own_modulation + ada_bias.astype(F32)
    plain = jnp.stack([slot_tokens * slot_live, own_buckets], axis=1).astype(F32)
    facts = jnp.concatenate([own_modulation, jnp.repeat(plain, LANES // 2, axis=1)], axis=1)

    edges = [(i, i + 1) for i in range(parts - 1)]
    before = lax.ppermute(tokens[:, length - halo :], "fsdp", edges)
    after = lax.ppermute(tokens[:, :halo], "fsdp", [(j, i) for i, j in edges])
    padding = jnp.zeros((own_slots, ROWS - 2 * halo, model_width), tokens.dtype)
    in_own = jnp.concatenate(
        [
            lax.dynamic_slice_in_dim(in_weight, h * inner_width + g * channels, channels, 1)
            for h in range(2)
        ],
        axis=1,
    )
    shard = out_weight.shape[0]
    small = jnp.concatenate(
        [
            dt_weight.reshape(2 * rank_width, shard),
            a_log.reshape(2 * states, shard),
            conv_weight.reshape(2 * kernel, shard),
            conv_bias,
            dt_bias,
            skip_gain,
        ],
        axis=0,
    )
    small_rows = small.shape[0]
    small_pad = -small_rows % LANES
    small = jnp.pad(small, ((0, -small_rows % BLOCK), (0, 0)))
    all_tokens, all_halo, in_matrix, all_xproj, all_small, all_facts, all_cotangent = collect_inputs(
        tokens,
        jnp.concatenate([before, after, padding], axis=1),
        in_own,
        xproj_weight,
        small,
        facts,
        cotangent,
    )
    all_cotangent = all_cotangent.reshape(slots, length, model_width)
    all_tokens = all_tokens.reshape(slots, length, model_width)
    all_halo = all_halo.reshape(slots, ROWS, model_width)
    in_matrix = in_matrix.reshape(model_width, 2 * channels)

    piece = shard // groups
    sent = lax.ppermute(
        lax.dynamic_slice_in_dim(out_weight, g * piece, piece, 0),
        ("group", "fsdp"),
        to_owner(groups, parts),
    )
    out_matrix = lax.all_gather(sent, "fsdp", axis=0, tiled=True)
    xproj = jnp.concatenate([all_xproj[0], all_xproj[1]], axis=1)
    rest = jnp.concatenate([all_small[0], all_small[1]], axis=1)
    edge = 0

    def take(rows):
        nonlocal edge
        edge += rows
        return rest[edge - rows : edge]

    dt_matrix = jnp.pad(
        take(2 * rank_width).reshape(2, rank_width, channels), ((0, 0), (0, width - rank_width), (0, 0))
    )
    rate = -jnp.exp(take(2 * states).astype(F32)).reshape(2, states // ROWS, ROWS, channels)
    taps = take(2 * kernel).reshape(2, kernel, channels).astype(F32)
    conv_shift = take(2).astype(F32)
    dt_shift = take(2).astype(F32).reshape(2, 1, channels)
    skip = take(2).astype(F32).reshape(2, 1, channels)
    decay = rate * LOG2E

    columns = facts.shape[1] - LANES
    plain = all_facts[:, 0, :, columns:].reshape(slots, LANES).astype(jnp.int32)
    counts, buckets = plain[:, 0], plain[:, LANES // 2]
    modulation = all_facts[:, :, :, :columns].transpose(0, 2, 1, 3).reshape(slots, parts * columns)
    group_counts = jnp.sum(counts.reshape(groups, own_slots), axis=1).astype(F32)
    share = jnp.repeat(group_counts / jnp.sum(group_counts), own_slots)
    positions = f * length + jnp.arange(length, dtype=jnp.int32)
    mask = (positions[None, :] < counts[:, None]).astype(F32)
    active = (counts > f * length).astype(jnp.int32)
    own_mask = mask[:own_slots, :, None]
    own_share = share[:own_slots, None, None]
    condition = jax.nn.silu(time_embed(buckets, model_width)).astype(BF16)
    shift_mod = modulation[:, None, :model_width]
    scale_mod = modulation[:, None, model_width : 2 * model_width]
    gate_mod = modulation[:, None, 2 * model_width :]

    info = jnp.concatenate([counts, (f * length)[None]]).astype(jnp.int32)
    modulated, wide_x, gate_z, conv_out, projected = project(
        info, all_tokens, all_halo, modulation[:, None, :], in_matrix, taps, conv_shift, xproj
    )
    proj = sum_blocks(projected, F32, F32, 2)

    def normalise(values):
        inputs = values.astype(F32)
        centered = inputs - jnp.mean(inputs, axis=2, keepdims=True)
        inv_std = lax.rsqrt(jnp.mean(centered * centered, axis=2, keepdims=True) + EPSILON)
        return (inputs, centered * inv_std, inv_std)

    grad_in_all = all_cotangent.astype(F32) * (mask * share[:, None])[:, :, None]
    branch_gradient = (grad_in_all * gate_mod).astype(BF16)
    grad_gated = jnp.einsum("sld,cd->slc", branch_gradient, out_matrix, preferred_element_type=F32)
    grad_y = grad_gated * jax.nn.silu(gate_z)

    step, end, pull, total, mix_b, mix_c = scan_ends(active, conv_out, proj, grad_y, dt_matrix, dt_shift, decay)
    entering = pass_states(end, pull, total, decay)
    gated_output, grad_z, conv_grad, proj_part, dtw_grad, dtb_grad, decay_grad, skip_grad = scan_all(
        active,
        conv_out,
        proj,
        grad_y,
        step,
        mix_b,
        mix_c,
        entering,
        gate_z,
        grad_gated,
        dt_matrix,
        decay,
        skip,
    )
    proj_grad = sum_blocks(proj_part, BF16, BF16, 3)
    alog_grad = (decay_grad * rate).reshape(2 * states, channels)

    branch_part = jnp.einsum("slc,cd->sld", gated_output, out_matrix, preferred_element_type=F32)
    branch_part, proj_grad = lax.optimization_barrier((branch_part.astype(BF16), proj_grad))
    ways = groups.bit_length() - 1
    cut_blocks = [cut(block, ways) for block in jnp.split(branch_part, groups, axis=0)]
    moving = [{r: cut_blocks[r][p] for r in range(groups)} for p in range(ways)]
    moving = scatter_stage(moving, groups, 0)
    outward = jnp.einsum("slc,sld->cd", gated_output, branch_gradient, preferred_element_type=F32)

    grad_x, rim, conv_sums, xproj_grads = back_through(
        info, wide_x, conv_grad, proj_grad, conv_out, taps, conv_shift, xproj
    )
    moving, rim = lax.optimization_barrier((moving, rim))
    ahead = lax.ppermute(rim[:, 0, :halo], "fsdp", [(j, i) for i, j in edges])
    behind = lax.ppermute(rim[:, 1, ROWS - halo :], "fsdp", edges)
    zeros = jnp.zeros_like(ahead)
    ahead, behind = jnp.concatenate([zeros, ahead], 1), jnp.concatenate([behind, zeros], 1)
    last = sum(taps[0, k] * ahead[:, halo - k : 2 * halo - k] for k in range(kernel))
    first = sum(taps[1, k] * behind[:, k : k + halo] for k in range(kernel))
    grad_x = grad_x + jnp.concatenate(
        [first, jnp.zeros((slots, length - 2 * halo, channels), F32), last], axis=1
    )
    inner_gradient = jnp.concatenate([grad_x.astype(BF16), grad_z], axis=2)
    inward = jnp.einsum("sld,slc->dc", modulated, inner_gradient, preferred_element_type=F32)
    grad_mod_part = jnp.einsum(
        "slc,dc->sld", inner_gradient, in_matrix, preferred_element_type=F32
    ).astype(BF16)
    for t in range(1, ways):
        moving = scatter_stage(moving, groups, t)
    branch = jnp.concatenate([held[0] for held in moving], axis=0)
    inward, grad_mod_part, branch = lax.optimization_barrier(
        (inward.astype(BF16), grad_mod_part, branch)
    )
    branch = branch.astype(F32)
    grad_mod = scatter_blocks(grad_mod_part, 4) * own_mask

    own_gate = gate_mod[:own_slots]
    own_scale = scale_mod[:own_slots]
    own_inputs, own_normed, own_inv = normalise(tokens)
    layer_out = ((own_inputs + own_gate * branch) * own_mask).astype(BF16)
    grad_in = cotangent.astype(F32) * own_mask * own_share
    grad_gate = jnp.sum(grad_in * branch, axis=1)

    grad_shift = jnp.sum(grad_mod, axis=1)
    grad_scale = jnp.sum(grad_mod * own_normed, axis=1)
    grad_normed = grad_mod * (1.0 + own_scale)
    grad_ln = own_inv * (
        grad_normed
        - jnp.mean(grad_normed, axis=2, keepdims=True)
        - own_normed * jnp.mean(grad_normed * own_normed, axis=2, keepdims=True)
    )
    tokens_grad = grad_in + grad_ln

    mod_part = jnp.concatenate([grad_shift, grad_scale, grad_gate], axis=1)
    mod_terms = mod_part.reshape(own_slots, parts, -1).transpose(1, 0, 2)
    mod_all = sum_modulation(mod_terms, 5).reshape(slots, -1)
    ada_grad = jnp.einsum("sd,sk->dk", condition, mod_all.astype(BF16), preferred_element_type=F32)
    adab_grad = jnp.sum(mod_all, axis=0)

    small_grads = jnp.concatenate(
        [
            xproj_grads.reshape(2 * width, channels),
            dtw_grad[:, :rank_width].reshape(2 * rank_width, channels),
            alog_grad,
            conv_sums[: 2 * kernel + 2],
            dtb_grad.reshape(2, channels),
            skip_grad.reshape(2, channels),
            jnp.zeros((small_pad, channels), F32),
        ],
        axis=0,
    ).astype(BF16)
    packed_grads = jnp.concatenate([outward.astype(BF16), small_grads.T], axis=1)
    packed_piece = lax.psum_scatter(packed_grads, "fsdp", scatter_dimension=0, tiled=True)
    packed_piece = lax.ppermute(
        packed_piece, ("group", "fsdp"), [(j, i) for i, j in to_owner(groups, parts)]
    )
    packed_own = lax.all_gather(packed_piece, "group", axis=0, tiled=True).astype(F32)
    out_grad = packed_own[:, :model_width]
    xproj_grad = jnp.stack(
        [packed_own[:, model_width + d * width : model_width + (d + 1) * width] for d in range(2)]
    )
    rest_grads = packed_own[:, model_width + 2 * width :].T
    sizes = [2 * rank_width, 2 * states, 2 * kernel, 2, 2, 2]
    cuts = [sum(sizes[:i]) for i in range(len(sizes) + 1)]
    dtw_out, alog_out, conv_w_out, conv_b_out, dtb_out, skip_out = [
        rest_grads[cuts[i] : cuts[i + 1]] for i in range(len(sizes))
    ]
    inward_piece = lax.psum_scatter(inward, "fsdp", scatter_dimension=0, tiled=True)
    inward_all = lax.all_gather(inward_piece, "group", axis=0)
    in_grad = jnp.concatenate(
        [inward_all[j, :, h * channels : (h + 1) * channels] for h in range(2) for j in range(groups)],
        axis=1,
    ).astype(F32)
    return (
        layer_out,
        tokens_grad,
        ada_grad,
        adab_grad,
        in_grad,
        conv_w_out.reshape(2, kernel, shard),
        conv_b_out,
        xproj_grad,
        dtw_out.reshape(2, rank_width, shard),
        dtb_out,
        alog_out.reshape(2, states, shard),
        skip_out,
        out_grad,
    )


def solution(mesh):
    in_specs = (
        P("group", "fsdp", None),
        P(),
        P("group"),
        P("group"),
        P("group"),
        P(None, "fsdp"),
        P("fsdp"),
        P("fsdp", None),
        P(None, None, "fsdp"),
        P(None, "fsdp"),
        P(None, "fsdp", None),
        P(None, None, "fsdp"),
        P(None, "fsdp"),
        P(None, None, "fsdp"),
        P(None, "fsdp"),
        P("fsdp", None),
        P("group", "fsdp", None),
    )
    out_specs = (
        P("group", "fsdp", None),
        P("group", "fsdp", None),
        P(None, "fsdp"),
        P("fsdp"),
        P("fsdp", None),
        P(None, None, "fsdp"),
        P(None, "fsdp"),
        P(None, "fsdp", None),
        P(None, None, "fsdp"),
        P(None, "fsdp"),
        P(None, None, "fsdp"),
        P(None, "fsdp"),
        P("fsdp", None),
    )
    return jax.shard_map(
        on_device, mesh=mesh, in_specs=in_specs, out_specs=out_specs, check_vma=False
    )
```

```python
import functools
import math

import jax
import jax.numpy as jnp
from jax import lax
from jax.experimental import pallas as pl
from jax.experimental.pallas import tpu as pltpu
from jax.sharding import PartitionSpec as P

EPSILON = 1e-06
LANES = 128
ROWS = 8
BLOCK = 16
WIDE = 256
LAG = 3
RUN = 2
LOG2E = math.log2(math.e)
LN2 = math.log(2.0)
F32 = jnp.float32
BF16 = jnp.bfloat16
MIB = 1 << 20


def time_embed(buckets, model_width):
    half_width = model_width // 2
    frequency = jnp.exp(-math.log(10000.0) * jnp.arange(half_width, dtype=F32) / half_width)
    angles = buckets.astype(F32)[:, None] * frequency[None, :]
    return jnp.concatenate([jnp.cos(angles), jnp.sin(angles)], axis=1)


def silu_slope(values):
    sigmoid = jax.nn.sigmoid(values)
    return sigmoid * (1.0 + values * (1.0 - sigmoid))


def dot32(left, right, dims):
    return lax.dot_general(left, right, (dims, ((), ())), preferred_element_type=F32)


def pass_one(
    states, active, conv, proj, grad_y, dt_w, dt_b, decay, step, end, pull, total, mix_b, mix_c, drive, turned
):
    slot, direction = pl.program_id(0), pl.program_id(1)
    length, channels = drive.shape
    chunks = channels // LANES
    halves = states // ROWS
    rank = proj.shape[1] - 2 * states

    @pl.when(active[slot] == 0)
    def _():
        end[...] = jnp.zeros_like(end)
        pull[...] = jnp.zeros_like(pull)
        total[...] = jnp.zeros_like(total)

    @pl.when(active[slot] != 0)
    def _():
        pre = dot32(proj[...].astype(BF16), dt_w[direction], ((1,), (0,))) + dt_b[direction]
        steps = jnp.maximum(pre, 0.0) + jnp.log(1.0 + jnp.exp(-jnp.abs(pre)))
        step[...] = steps
        drive[...] = steps * conv[...].astype(F32)
        total[...] = jnp.broadcast_to(jnp.sum(steps, axis=0, keepdims=True), total.shape)

        def turn(i, carry):
            at = pl.multiple_of(i * ROWS, ROWS)
            turned[i] = jnp.transpose(proj[pl.ds(at, ROWS), :])[rank : rank + 2 * states]
            return carry

        lax.fori_loop(0, length // ROWS, turn, 0, unroll=True)
        zero = jnp.zeros((halves, ROWS, LANES), F32)
        for backward in range(2):

            @pl.when(direction == backward)
            def _():
                carry = ((zero,) * chunks, (zero + 1.0,) * chunks, (zero,) * chunks)
                rates = [decay[direction, :, :, k : k + LANES] for k in range(0, channels, LANES)]

                def block(i, carry):
                    at = length // ROWS - 1 - i if backward else i
                    rows = pl.ds(pl.multiple_of(at * ROWS, ROWS), ROWS)
                    held = [ref[rows, :] for ref in (step, drive, grad_y)]
                    hidden, running, pulled = carry
                    columns = turned[at]
                    for j in list(range(ROWS))[:: -1 if backward else 1]:
                        t = at * ROWS + j
                        wide = jnp.broadcast_to(columns[:, j : j + 1], (2 * states, LANES))
                        b = wide[:states].reshape(halves, ROWS, LANES)
                        c = wide[states:].reshape(halves, ROWS, LANES)
                        mix_b[t] = b
                        mix_c[t] = c
                        rowed = [
                            [
                                jnp.broadcast_to(h[j : j + 1, k : k + LANES], (ROWS, LANES))[None]
                                for k in range(0, channels, LANES)
                            ]
                            for h in held
                        ]
                        new = ([], [], [])
                        for k in range(chunks):
                            factor = jnp.exp2(rowed[0][k] * rates[k])
                            new[0].append(factor * hidden[k] + rowed[1][k] * b)
                            run = running[k] * factor
                            new[1].append(run)
                            new[2].append(pulled[k] + run * (rowed[2][k] * c))
                        hidden, running, pulled = new
                    return (tuple(hidden), tuple(running), tuple(pulled))

                hidden, _, pulled = lax.fori_loop(0, length // ROWS, block, carry)
                for k in range(chunks):
                    lanes = slice(k * LANES, (k + 1) * LANES)
                    end[:, :, lanes] = hidden[k]
                    pull[:, :, lanes] = pulled[k]


def pass_two(
    states,
    active,
    conv,
    proj,
    grad_y,
    step,
    mix_b,
    mix_c,
    entry,
    arrive,
    gate_z,
    grad_gated,
    dt_w,
    decay,
    skip,
    tile_b,
    tile_c,
    sel,
    take_b,
    take_c,
    gated,
    grad_z,
    conv_grad,
    proj_grad,
    dtw_grad,
    dtb_grad,
    alog_grad,
    skip_grad,
    drive,
    hid_even,
    hid_odd,
    edge,
    gst_even,
    gst_odd,
    thd_even,
    thd_odd,
    mixed,
    sdec,
    scan_y,
    in_part,
    out_part,
    rows_b,
    rows_c,
    drive_low,
    grad_low,
    y,
):
    slot, direction = pl.program_id(0), pl.program_id(1)
    length, channels = drive.shape
    chunks = channels // LANES
    halves = states // ROWS
    wide = BLOCK * states
    pairs = length // (2 * BLOCK)
    hid, gst, thd = (hid_even, hid_odd), (gst_even, gst_odd), (thd_even, thd_odd)
    lanes = [slice(k * LANES, (k + 1) * LANES) for k in range(chunks)]

    @pl.when((slot == 0) & (direction == 0))
    def _():
        dtw_grad[...] = jnp.zeros_like(dtw_grad)
        dtb_grad[...] = jnp.zeros_like(dtb_grad)
        alog_grad[...] = jnp.zeros_like(alog_grad)
        skip_grad[...] = jnp.zeros_like(skip_grad)

    @pl.when(direction == 0)
    def _():
        y[...] = jnp.zeros_like(y)

    @pl.when(active[slot] == 0)
    def _():
        conv_grad[...] = jnp.zeros_like(conv_grad)
        proj_grad[...] = jnp.zeros_like(proj_grad)
        gated[...] = jnp.zeros_like(gated)
        grad_z[...] = jnp.zeros_like(grad_z)

    def low(value):
        return value.reshape(states, LANES).astype(BF16)

    def block_range(pair, odd):
        return pl.ds(pl.multiple_of((2 * pair + odd) * BLOCK, BLOCK), BLOCK)

    def sweep_blocks(backward, tokens, matmuls, start):
        first, second = (1, 0) if backward else (0, 1)

        def two(i, carry):
            pair = pairs - 1 - i if backward else i
            before = lax.rem(pair + (1 if backward else pairs - 1), pairs)
            carry = tokens(pair, first, backward, matmuls(before, second), carry)
            return tokens(pair, second, backward, matmuls(pair, first), carry)

        carry = lax.fori_loop(0, pairs, two, start)
        for issue, keep in matmuls(0 if backward else pairs - 1, second):
            keep(issue())
        return carry

    def pieces(out, rows, left, right, dims, width):
        made = []
        for n in range(0, width, WIDE):
            cols = slice(n, min(n + WIDE, width))
            picked = right[:, cols] if dims[1] == (0,) else right

            def issue(left=left, picked=picked):
                return dot32(left, picked, dims)

            def keep(product, cols=cols):
                out[rows, cols] = product

            made.append((issue, keep))
        return made

    def scan_rows(pair, odd, backward, refs, body, beside, carry):
        order = list(range(BLOCK))[:: -1 if backward else 1]
        waiting = []
        for at_step, j in enumerate(order):
            if j % ROWS == (ROWS - 1 if backward else 0):
                at = pl.multiple_of((2 * pair + odd) * BLOCK + j // ROWS * ROWS, ROWS)
                held = [ref[pl.ds(at, ROWS), :] for ref in refs]
            i = j % ROWS
            rows = [
                [jnp.broadcast_to(h[i : i + 1, c], (ROWS, LANES))[None] for c in lanes] for h in held
            ]
            for issue, keep in beside[at_step * len(beside) // BLOCK : (at_step + 1) * len(beside) // BLOCK]:
                waiting.append((at_step + LAG, keep, issue()))
            carry = body(j, rows, carry)
            while waiting and waiting[0][0] <= at_step:
                _, keep, product = waiting.pop(0)
                keep(product)
        for _, keep, product in waiting:
            keep(product)
        return carry

    def forward_tokens(pair, odd, backward, beside, hidden):
        for k in range(chunks):
            edge[2 * pair + odd, :, lanes[k]] = low(hidden[k])

        def token(j, rows, hidden):
            b = mix_b[(2 * pair + odd) * BLOCK + j]
            new = []
            for k in range(chunks):
                factor = jnp.exp2(rows[0][k] * decay[direction, :, :, lanes[k]])
                value = factor * hidden[k] + rows[1][k] * b
                hid[odd][pair, j, :, lanes[k]] = low(value)
                new.append(value)
            return tuple(new)

        return scan_rows(pair, odd, backward, (step, drive), token, beside, hidden)

    def forward_matmuls(pair, odd):
        rows = block_range(pair, odd)
        h_rows = hid[odd][pair].reshape(wide, channels)
        return pieces(scan_y, rows, rows_c[rows, :], h_rows, ((1,), (0,)), channels) + pieces(
            out_part, rows, grad_low[rows, :], h_rows, ((1,), (1,)), wide
        )

    def backward_tokens(pair, odd, backward, beside, carry):
        earlier = -1 if backward else 1

        def token(j, rows, carry):
            carried, total = carry
            c = mix_c[(2 * pair + odd) * BLOCK + j]
            news, sums = [], []
            p = j + earlier
            for k in range(chunks):
                rate = decay[direction, :, :, lanes[k]]
                factor = jnp.exp2(rows[0][k] * rate)
                grad_state = rows[1][k] * c + carried[k]
                gst[odd][j, :, lanes[k]] = low(grad_state)
                onward = factor * grad_state
                if 0 <= p < BLOCK:
                    before = hid[odd][pair, p, :, lanes[k]]
                else:
                    before = edge[2 * pair + odd, :, lanes[k]]
                through = onward * before.astype(F32).reshape(halves, ROWS, LANES)
                sums.append(total[k] + through * rows[0][k])
                thd[odd][j, :, lanes[k]] = low(through * rate)
                news.append(onward)
            return (tuple(news), tuple(sums))

        return scan_rows(pair, odd, backward, (step, grad_y), token, beside, carry)

    def backward_matmuls(pair, odd):
        rows = block_range(pair, odd)
        g_rows = gst[odd][...].reshape(wide, channels)
        t_rows = thd[odd][...].reshape(wide, channels)
        return (
            pieces(mixed, rows, rows_b[rows, :], g_rows, ((1,), (0,)), channels)
            + pieces(sdec, rows, sel[...].astype(BF16), t_rows, ((1,), (0,)), channels)
            + pieces(in_part, rows, drive_low[rows, :], g_rows, ((1,), (1,)), wide)
        )

    @pl.when(active[slot] != 0)
    def _():
        drive[...] = step[...] * conv[...].astype(F32)
        drive_low[...] = drive[...].astype(BF16)
        grad_low[...] = grad_y[...].astype(BF16)
        proj_low = proj[...].astype(BF16)
        picked = jnp.concatenate([sel[...]] * (length // BLOCK), axis=0)
        rows_b[...] = (dot32(proj_low, tile_b[...], ((1,), (0,))) * picked).astype(BF16)
        rows_c[...] = (dot32(proj_low, tile_c[...], ((1,), (0,))) * picked).astype(BF16)
        zero = jnp.zeros((halves, ROWS, LANES), F32)
        for reverse in (False, True):

            @pl.when(direction == int(reverse))
            def _():
                start = tuple(entry[:, :, c].astype(F32) for c in lanes)
                sweep_blocks(reverse, forward_tokens, forward_matmuls, start)
                start = (tuple(arrive[:, :, c].astype(F32) for c in lanes), (zero,) * chunks)
                _, sums = sweep_blocks(not reverse, backward_tokens, backward_matmuls, start)
                for k in range(chunks):
                    alog_grad[direction, :, :, lanes[k]] += sums[k]

        conv_values = conv[...].astype(F32)
        steps = step[...]
        grads = grad_y[...]
        step_grad = conv_values * mixed[...] + LN2 * sdec[...]
        pre_grad = step_grad * (1.0 - jnp.exp(-steps))
        dtb_grad[direction] += jnp.sum(pre_grad, axis=0, keepdims=True)
        pre_low = pre_grad.astype(BF16)
        proj_grad[...] = (
            dot32((in_part[...] * picked).astype(BF16), take_b[...], ((1,), (0,)))
            + dot32((out_part[...] * picked).astype(BF16), take_c[...], ((1,), (0,)))
            + dot32(pre_low, dt_w[direction], ((1,), (1,)))
        )
        dtw_grad[direction] += dot32(jnp.transpose(proj[...]).astype(BF16), pre_low, ((1,), (0,)))
        y[...] += scan_y[...] + skip[direction] * conv_values
        skip_grad[direction] += jnp.sum(grads * conv_values, axis=0, keepdims=True)
        conv_grad[...] = grads * skip[direction] + steps * mixed[...]

        @pl.when(direction == 1)
        def _():
            total = y[...]
            value = gate_z[...]
            sigmoid = jax.nn.sigmoid(value)
            gated[...] = (total * (value * sigmoid)).astype(BF16)
            slope = sigmoid * (1.0 + value * (1.0 - sigmoid))
            grad_z[...] = (grad_gated[...] * total * slope).astype(BF16)


def whole(array):
    zeros = (0,) * array.ndim
    return pl.BlockSpec(array.shape, lambda s, d, a: zeros)


def scan_ends(active, conv, proj, grad_y, dt_w, dt_b, decay):
    slots, length, channels = grad_y.shape
    halves = decay.shape[1]
    width = proj.shape[3]
    states = halves * ROWS
    turn = lambda *tail: pl.BlockSpec((None, None) + tail, lambda s, d, a: (s, d) + (0,) * len(tail))
    pair = lambda *tail: pl.BlockSpec((None, None) + tail, lambda s, d, a: (d, s) + (0,) * len(tail))
    state = (2, slots, halves, ROWS, channels)
    mixes = (length, halves, ROWS, LANES)
    spare = lambda s, a: jnp.where(a[s] != 0, s, slots)
    kept_pair = pl.BlockSpec(
        (None, None, length, channels), lambda s, d, a: (jnp.where(a[s] != 0, d, 0), spare(s, a), 0, 0)
    )
    kept_mix = pl.BlockSpec(
        (None, None) + mixes, lambda s, d, a: (spare(s, a), jnp.where(a[s] != 0, d, 0), 0, 0, 0, 0)
    )
    return pl.pallas_call(
        functools.partial(pass_one, states),
        grid_spec=pltpu.PrefetchScalarGridSpec(
            num_scalar_prefetch=1,
            grid=(slots, 2),
            in_specs=[
                pair(length, channels),
                turn(length, width),
                pl.BlockSpec((None, length, channels), lambda s, d, a: (s, 0, 0)),
                whole(dt_w),
                whole(dt_b),
                whole(decay),
            ],
            out_specs=[
                kept_pair,
                pair(halves, ROWS, channels),
                pair(halves, ROWS, channels),
                pair(ROWS, channels),
                kept_mix,
                kept_mix,
            ],
            scratch_shapes=[
                pltpu.VMEM((length, channels), F32),
                pltpu.VMEM((length // ROWS, 2 * states, ROWS), F32),
            ],
        ),
        out_shape=[
            jax.ShapeDtypeStruct((2, slots + 1, length, channels), F32),
            jax.ShapeDtypeStruct(state, F32),
            jax.ShapeDtypeStruct(state, F32),
            jax.ShapeDtypeStruct((2, slots, ROWS, channels), F32),
            jax.ShapeDtypeStruct((slots + 1, 2) + mixes, F32),
            jax.ShapeDtypeStruct((slots + 1, 2) + mixes, F32),
        ],
        compiler_params=pltpu.CompilerParams(vmem_limit_bytes=24 * MIB),
        name="scan_ends",
    )(active, conv, proj, grad_y, dt_w, dt_b, decay)


def scan_all(
    active, conv, proj, grad_y, step, mix_b, mix_c, entering, gate_z, grad_gated, dt_w, decay, skip
):
    slots, length, channels = grad_y.shape
    halves = decay.shape[1]
    width = proj.shape[3]
    states = halves * ROWS
    wide = BLOCK * states
    rank = width - 2 * states
    column = jnp.arange(width)[:, None]
    lane = jnp.arange(wide)[None, :]
    tile_b = (column == rank + lane % states).astype(BF16)
    tile_c = (column == rank + states + lane % states).astype(BF16)
    sel = (jnp.arange(BLOCK)[:, None] == lane // states).astype(F32)
    turn = lambda *tail: pl.BlockSpec((None, None) + tail, lambda s, d, a: (s, d) + (0,) * len(tail))
    pair = lambda *tail: pl.BlockSpec((None, None) + tail, lambda s, d, a: (d, s) + (0,) * len(tail))
    one = pl.BlockSpec((None, length, channels), lambda s, d, a: (s, 0, 0))
    constants = (dt_w, decay, skip, tile_b, tile_c, sel, tile_b.T, tile_c.T)
    sums = (
        jax.ShapeDtypeStruct((2, width, channels), F32),
        jax.ShapeDtypeStruct((2, 1, channels), F32),
        jax.ShapeDtypeStruct((2, halves, ROWS, channels), F32),
        jax.ShapeDtypeStruct((2, 1, channels), F32),
    )
    pairs = length // (2 * BLOCK)
    read_s = lambda s, a: jnp.where(a[s] != 0, s, 0)
    read_d = lambda s, d, a: jnp.where(a[s] != 0, d, 0)
    got_one = pl.BlockSpec((None, length, channels), lambda s, d, a: (read_s(s, a), 0, 0))

    def got_pair(*tail):
        return pl.BlockSpec(
            (None, None) + tail, lambda s, d, a: (read_d(s, d, a), read_s(s, a)) + (0,) * len(tail)
        )

    def got_turn(*tail):
        return pl.BlockSpec(
            (None, None) + tail, lambda s, d, a: (read_s(s, a), read_d(s, d, a)) + (0,) * len(tail)
        )

    def got_state(kind):
        def place(s, d, a):
            way = read_d(s, d, a)
            return (way + kind * (1 - 2 * way), read_s(s, a), kind, 0, 0, 0)

        return pl.BlockSpec((None, None, None, halves, ROWS, channels), place)

    return pl.pallas_call(
        functools.partial(pass_two, states),
        grid_spec=pltpu.PrefetchScalarGridSpec(
            num_scalar_prefetch=1,
            grid=(slots, 2),
            in_specs=[
                got_pair(length, channels),
                got_turn(length, width),
                got_one,
                got_pair(length, channels),
                got_turn(length, halves, ROWS, LANES),
                got_turn(length, halves, ROWS, LANES),
                got_state(0),
                got_state(1),
                got_one,
                got_one,
            ]
            + [whole(c) for c in constants],
            out_specs=[one, one, pair(length, channels), turn(length, width)] + [whole(c) for c in sums],
            scratch_shapes=[pltpu.VMEM((length, channels), F32)]
            + [pltpu.VMEM((pairs, BLOCK, states, channels), BF16)] * 2
            + [pltpu.VMEM((2 * pairs, states, channels), BF16)]
            + [pltpu.VMEM((BLOCK, states, channels), BF16)] * 4
            + [pltpu.VMEM((length, channels), F32)] * 3
            + [pltpu.VMEM((length, wide), F32)] * 2
            + [pltpu.VMEM((length, wide), BF16)] * 2
            + [pltpu.VMEM((length, channels), BF16)] * 2
            + [pltpu.VMEM((length, channels), F32)],
        ),
        out_shape=[
            jax.ShapeDtypeStruct((slots, length, channels), BF16),
            jax.ShapeDtypeStruct((slots, length, channels), BF16),
            jax.ShapeDtypeStruct((2, slots, length, channels), F32),
            jax.ShapeDtypeStruct((slots, 2, length, width), F32),
        ]
        + list(sums),
        compiler_params=pltpu.CompilerParams(vmem_limit_bytes=44 * MIB),
        name="scan_all",
    )(active, conv, proj, grad_y, step, mix_b, mix_c, entering, entering, gate_z, grad_gated, *constants)


def chain(count, run, end, pull, total, decay, entering, held, send_sem, recv_sem):
    mine = lax.axis_index("fsdp")
    waves = end.shape[1] // run
    mesh_id = pl.DeviceIdType.MESH
    after, before = lax.rem(mine + 1, count), lax.rem(mine + count - 1, count)
    barrier = pltpu.get_barrier_semaphore()
    for other in (after, before):
        pl.semaphore_signal(barrier, inc=1, device_id={"fsdp": other}, device_id_type=mesh_id)
    pl.semaphore_wait(barrier, 2)
    ways = ((mine > 0, mine < count - 1, after), (mine < count - 1, mine > 0, before))

    def copy(way, s):
        slots = pl.ds(s * run, run)
        return pltpu.make_async_remote_copy(
            src_ref=held.at[way, slots],
            dst_ref=entering.at[way, slots],
            send_sem=send_sem.at[way, s],
            recv_sem=recv_sem.at[way, s],
            device_id={"fsdp": ways[way][2]},
            device_id_type=mesh_id,
        )

    lags = (mine, count - 1 - mine)

    def wave(turn, carry):
        for way in range(2):
            gets, sends, _ = ways[way]
            s = turn - lags[way]
            here = (s >= 0) & (s < waves)

            @pl.when(here & gets)
            def _():
                copy(way, s).wait_recv()

            @pl.when(here & jnp.logical_not(gets))
            def _():
                entering[way, pl.ds(s * run, run)] = jnp.zeros((run,) + entering.shape[2:], entering.dtype)

            @pl.when(here & sends)
            def _():
                for i in range(run):
                    slot = s * run + i
                    for kind, local in enumerate((end, pull)):
                        d = (way + kind) % 2
                        through = jnp.exp2(decay[d] * total[d, slot][None])
                        value = through * entering[way, slot, kind].astype(F32) + local[d, slot]
                        held[way, slot, kind] = value.astype(held.dtype)
                copy(way, s).start()

        return carry

    lax.fori_loop(0, waves + count - 1, wave, 0)

    def drain(s, carry):
        for way in range(2):

            @pl.when(ways[way][1])
            def _():
                copy(way, s).wait_send()

        return carry

    lax.fori_loop(0, waves, drain, 0)


def pass_states(end, pull, total, decay):
    _, slots, halves, rows, channels = end.shape
    run = RUN
    shape = (2, slots, 2, halves, rows, channels)
    return pl.pallas_call(
        functools.partial(chain, lax.axis_size("fsdp"), run),
        in_specs=[pl.BlockSpec(memory_space=pltpu.VMEM)] * 4,
        out_specs=pl.BlockSpec(memory_space=pltpu.VMEM),
        out_shape=jax.ShapeDtypeStruct(shape, BF16),
        scratch_shapes=[
            pltpu.VMEM(shape, BF16),
            pltpu.SemaphoreType.DMA((2, slots // run)),
            pltpu.SemaphoreType.DMA((2, slots // run)),
        ],
        compiler_params=pltpu.CompilerParams(
            collective_id=0, has_side_effects=True, vmem_limit_bytes=40 * MIB
        ),
        name="pass_states",
    )(end, pull, total, decay)


def partner(g, bit):
    return g + bit * (1 - 2 * lax.rem(g // bit, 2))


class Mail:
    def __init__(self, send_sem, recv_sem):
        self.send_sem, self.recv_sem, self.made = send_sem, recv_sem, []

    def post(self, src, dst, target, here=None, there=None, landing=None):
        n = len(self.made)
        copy = lambda into: pltpu.make_async_remote_copy(
            src_ref=src,
            dst_ref=into,
            send_sem=self.send_sem.at[n],
            recv_sem=self.recv_sem.at[n],
            device_id=target,
            device_id_type=pl.DeviceIdType.MESH,
        )
        when = lambda cond: (lambda body: body()) if cond is None else pl.when(cond)
        landing = dst if landing is None else landing
        entry = dict(got=False)

        @when(here)
        def _():
            copy(dst).start()

        def take():
            if not entry["got"]:
                entry["got"] = True

                @when(there)
                def _():
                    copy(landing).wait_recv()

        def sent():
            @when(here)
            def _():
                copy(dst).wait_send()

        self.made.append((take, sent))
        return take

    def finish(self):
        for take, _ in self.made:
            take()
        for _, sent in self.made:
            sent()


def collect(
    groups,
    parts,
    tokens,
    halo,
    in_own,
    xproj,
    small,
    facts,
    all_tokens,
    all_halo,
    in_matrix,
    all_xproj,
    all_small,
    all_facts,
    send_sem,
    recv_sem,
    own_sem,
):
    g, f = lax.axis_index("group"), lax.axis_index("fsdp")
    chips = parts // 2
    z, core = f // 2, lax.rem(f, 2)
    ways = groups.bit_length() - 1
    bits = [1 << i for i in range(ways)]
    barrier = pltpu.get_barrier_semaphore()
    for bit in bits:
        pl.semaphore_signal(
            barrier, inc=1, device_id={"group": partner(g, bit)}, device_id_type=pl.DeviceIdType.MESH
        )
    for k in range(1, parts):
        pl.semaphore_signal(
            barrier,
            inc=1,
            device_id={"fsdp": lax.rem(f + k, parts)},
            device_id_type=pl.DeviceIdType.MESH,
        )
    pl.semaphore_wait(barrier, ways + parts - 1)
    mail = Mail(send_sem, recv_sem)
    place = lambda part: lax.rem(part + 2 * parts, parts)
    sibling = {"fsdp": f + 1 - 2 * core}
    up, down = {"fsdp": f + 2}, {"fsdp": f - 2}

    fact_takes = []
    for k in range(1, parts):
        fact_takes.append(
            mail.post(
                facts,
                all_facts.at[0, f],
                {"fsdp": lax.rem(f + k, parts)},
                landing=all_facts.at[0, lax.rem(f + parts - k, parts)],
            )
        )

    def cuts(count):
        edges = [count * i // ways for i in range(ways + 1)]
        return [pl.ds(lo, hi - lo) for lo, hi in zip(edges[:-1], edges[1:])]

    def relative(own, every, count):
        pieces = cuts(count)
        held = [{0: None} for _ in range(ways)]
        steps = [[] for _ in range(ways)]
        for t in range(ways):
            for p in range(ways):
                bit = bits[(p + t) % ways]
                for r in list(held[p]):
                    held[p][r ^ bit] = None
                    steps[t].append((p, r, bit))
        takes = {}

        def run(chosen):
            for p, r, bit in chosen:
                if r:
                    takes[p, r]()
                src = own.at[pieces[p]] if r == 0 else every.at[r, pieces[p]]
                takes[p, r ^ bit] = mail.post(
                    src, every.at[r ^ bit, pieces[p]], {"group": partner(g, bit)}
                )

        run([move for step in steps for move in step if move[1] == 0])
        return [functools.partial(run, [move for move in step if move[1]]) for step in steps[1:]]

    token_steps = relative(tokens, all_tokens, tokens.shape[0])
    halo_steps = relative(halo, all_halo, halo.shape[0])

    line = []

    def hop(h):
        for sign, target, inside in ((1, up, z < chips - 1), (-1, down, z > 0)):
            shard = f - sign * 2 * (h - 1)
            src = in_own if h == 1 else in_matrix.at[place(shard)]
            far = z - sign * (h - 1)
            come = z - sign * h
            line.append(
                mail.post(
                    src,
                    in_matrix.at[place(shard)],
                    target,
                    here=inside & (far >= 0) & (far < chips),
                    there=(come >= 0) & (come < chips),
                    landing=in_matrix.at[place(f - sign * 2 * h)],
                )
            )

    def share(h):
        for sign in (1, -1):
            shard = place(f - sign * 2 * h)
            come = z - sign * h
            known = (come >= 0) & (come < chips)
            mail.post(
                in_own if h == 0 else in_matrix.at[shard],
                in_matrix.at[shard],
                sibling,
                here=known,
                there=known,
                landing=in_matrix.at[place(f + 1 - 2 * core - sign * 2 * h)],
            )
            if h == 0:
                break

    hop(1)
    share(0)

    own_fact = pltpu.make_async_copy(facts, all_facts.at[0, f], own_sem.at[0])
    own_fact.start()
    held_copies = [
        pltpu.make_async_copy(xproj, all_xproj.at[core], own_sem.at[1]),
        pltpu.make_async_copy(small, all_small.at[core], own_sem.at[2]),
    ]

    @pl.when(z == g)
    def _():
        for copy in held_copies:
            copy.start()

    own_fact.wait()
    for take in fact_takes:
        take()
    fact_steps = relative(all_facts.at[0], all_facts, parts)

    pairs = ((xproj, all_xproj), (small, all_small))
    for distance in range(1, chips):
        for sign, target in ((1, up), (-1, down)):
            source = g + sign * (distance - 1)
            here = (z == source) & (source + sign >= 0) & (source + sign < chips)
            there = z == source + sign
            for own, every in pairs:
                src = own if distance == 1 else every.at[core]
                take = mail.post(src, every.at[core], target, here=here, there=there)
                take()
        if distance == 1:
            for step in fact_steps:
                step()
    for own, every in pairs:
        for src, where in ((own, z == g), (every.at[core], z != g)):
            mail.post(
                src, every.at[core], sibling, here=where, there=where, landing=every.at[1 - core]
            )

    for h in range(1, chips):
        for take in line[-2:]:
            take()
        if h < chips - 1:
            hop(h + 1)
        share(h)
        if h == 1 or chips == 2:
            for step in halo_steps:
                step()
            for step in token_steps:
                step()
    @pl.when(z == g)
    def _():
        for copy in held_copies:
            copy.wait()

    mail.finish()


def collect_inputs(tokens, halo, in_own, xproj, small, facts):
    groups, parts = lax.axis_size("group"), lax.axis_size("fsdp")
    ins = (tokens, halo, in_own, xproj, small, facts)
    outs = [
        jax.ShapeDtypeStruct((groups,) + tokens.shape, tokens.dtype),
        jax.ShapeDtypeStruct((groups,) + halo.shape, halo.dtype),
        jax.ShapeDtypeStruct((parts,) + in_own.shape, in_own.dtype),
        jax.ShapeDtypeStruct((2,) + xproj.shape, xproj.dtype),
        jax.ShapeDtypeStruct((2,) + small.shape, small.dtype),
        jax.ShapeDtypeStruct((groups, parts) + facts.shape, facts.dtype),
    ]
    ways = groups.bit_length() - 1
    copies = 3 * ways * (groups - 1) + (parts - 1) + 4 * (parts // 2 - 1) + 1 + 4 * (parts // 2 - 1) + 4
    outs = pl.pallas_call(
        functools.partial(collect, groups, parts),
        in_specs=[pl.BlockSpec(memory_space=pl.ANY)] * len(ins),
        out_specs=[pl.BlockSpec(memory_space=pl.ANY)] * len(outs),
        out_shape=outs,
        scratch_shapes=[
            pltpu.SemaphoreType.DMA((copies,)),
            pltpu.SemaphoreType.DMA((copies,)),
            pltpu.SemaphoreType.DMA((3,)),
        ],
        compiler_params=pltpu.CompilerParams(collective_id=1, has_side_effects=True),
        name="collect_inputs",
    )(*ins)
    all_tokens, all_halo, in_matrix, all_xproj, all_small, all_facts = outs
    return (
        all_tokens.at[0].set(tokens),
        all_halo.at[0].set(halo),
        lax.dynamic_update_index_in_dim(in_matrix, in_own, lax.axis_index("fsdp"), 0),
        all_xproj,
        all_small,
        all_facts,
    )


def runs(count, ways):
    edges = [count * i // ways for i in range(ways + 1)]
    return [pl.ds(lo, hi - lo) for lo, hi in zip(edges[:-1], edges[1:])]


def greet(groups):
    g = lax.axis_index("group")
    bits = [1 << i for i in range(groups.bit_length() - 1)]
    barrier = pltpu.get_barrier_semaphore()
    for bit in bits:
        pl.semaphore_signal(
            barrier, inc=1, device_id={"group": partner(g, bit)}, device_id_type=pl.DeviceIdType.MESH
        )
    pl.semaphore_wait(barrier, len(bits))
    return g, bits


def total_blocks(groups, terms, out, sums, parcel, landed, gathered, send_sem, recv_sem):
    g, bits = greet(groups)
    ways = len(bits)
    pieces = runs(terms.shape[1], ways)
    mail = Mail(send_sem, recv_sem)
    sums[...] = terms[...]
    held = [set(range(groups)) for _ in range(ways)]
    for t in range(ways):
        coming = []
        for p in range(ways):
            bit = bits[(p + t) % ways]
            for r in sorted(r for r in held[p] if r & bit):
                parcel[r, pieces[p]] = sums[r, pieces[p]].astype(parcel.dtype)
                take = mail.post(
                    parcel.at[r, pieces[p]],
                    landed.at[t, r ^ bit, pieces[p]],
                    {"group": partner(g, bit)},
                )
                coming.append((take, p, r ^ bit))
                held[p].remove(r)
        for take, p, r in coming:
            take()
            sums[r, pieces[p]] = sums[r, pieces[p]] + landed[t, r, pieces[p]].astype(F32)
    gathered[0] = sums[0].astype(gathered.dtype)
    known = [{0: None} for _ in range(ways)]
    for t in range(ways):
        for p in range(ways):
            bit = bits[(p + t) % ways]
            for r, take in list(known[p].items()):
                if take is not None:
                    take()
                known[p][r ^ bit] = mail.post(
                    gathered.at[r, pieces[p]],
                    gathered.at[r ^ bit, pieces[p]],
                    {"group": partner(g, bit)},
                )
    mail.finish()
    out[...] = gathered[...].astype(out.dtype)


def sum_blocks(terms, sent, result, number):
    groups = lax.axis_size("group")
    ways = groups.bit_length() - 1
    shape = (groups, terms.shape[0] // groups, terms.shape[1] * terms.shape[2], terms.shape[3])
    copies = 2 * ways * (groups - 1)
    return pl.pallas_call(
        functools.partial(total_blocks, groups),
        in_specs=[pl.BlockSpec(memory_space=pltpu.VMEM)],
        out_specs=pl.BlockSpec(memory_space=pltpu.VMEM),
        out_shape=jax.ShapeDtypeStruct(shape, result),
        scratch_shapes=[
            pltpu.VMEM(shape, F32),
            pltpu.VMEM(shape, sent),
            pltpu.VMEM((ways,) + shape, sent),
            pltpu.VMEM(shape, BF16),
            pltpu.SemaphoreType.DMA((copies,)),
            pltpu.SemaphoreType.DMA((copies,)),
        ],
        compiler_params=pltpu.CompilerParams(
            collective_id=number, has_side_effects=True, vmem_limit_bytes=32 * MIB
        ),
        cost_estimate=pl.CostEstimate(flops=30000 * terms.size // 2, bytes_accessed=8 * terms.size, transcendentals=0),
        name="sum_blocks",
    )(terms.reshape(shape)).reshape(terms.shape)


def front(
    halo_rows,
    info,
    tokens,
    halo,
    modulation,
    in_matrix,
    taps,
    conv_shift,
    xproj,
    modulated,
    extended,
    gate_z,
    conv_out,
    projected,
):
    slot = pl.program_id(0)
    length, model_width = tokens.shape
    channels = gate_z.shape[1]
    count, base = info[slot], info[pl.num_programs(0)]
    outs = (modulated, extended, gate_z, conv_out, projected)

    @pl.when(count <= base)
    def _():
        for out in outs:
            out[...] = jnp.zeros_like(out)

    @pl.when(count > base)
    def _():
        values = jnp.concatenate([tokens[...].astype(F32), halo[...].astype(F32)], axis=0)
        row = lax.broadcasted_iota(jnp.int32, (length + ROWS, 1), 0)
        behind, ahead = row - length - halo_rows, row - halo_rows
        at = jnp.where(row < length, row, jnp.where(behind < 0, behind, ahead))
        at = at + base
        known = (row < length + 2 * halo_rows) & (at >= 0) & (at < count)
        mask = known.astype(F32)
        centered = values - jnp.mean(values, axis=1, keepdims=True)
        normed = centered * lax.rsqrt(
            jnp.mean(centered * centered, axis=1, keepdims=True) + EPSILON
        )
        shift = modulation[:, :model_width]
        scale = modulation[:, model_width : 2 * model_width]
        low = ((normed * (1.0 + scale) + shift) * mask).astype(BF16)
        modulated[...] = low[:length]
        inner = dot32(low, in_matrix[...], ((1,), (0,)))
        gate_z[...] = inner[:length, channels:]
        extended[...] = jnp.zeros_like(extended)
        extended[ROWS : ROWS + length, :] = inner[:length, :channels]
        extended[ROWS - halo_rows : ROWS, :] = inner[length : length + halo_rows, :channels]
        extended[ROWS + length : ROWS + length + halo_rows, :] = inner[
            length + halo_rows : length + 2 * halo_rows, :channels
        ]
        for d in range(2):
            pre = conv_rows(extended, taps, conv_shift, d, length)
            value = (pre * jax.nn.sigmoid(pre) * mask[:length]).astype(BF16)
            conv_out[d] = value
            projected[d] = dot32(value, xproj[d], ((1,), (0,)))


def tap_row(d, k, kernel):
    return ROWS - (kernel - 1) + k if d == 0 else ROWS + (kernel - 1) - k


def conv_rows(extended, taps, conv_shift, d, length):
    kernel = taps.shape[1]
    pre = conv_shift[d : d + 1, :]
    for k in range(kernel):
        row = tap_row(d, k, kernel)
        pre = pre + taps[d, k : k + 1, :] * extended[row : row + length, :]
    return pre


def project(info, tokens, halo, modulation, in_matrix, taps, conv_shift, xproj):
    slots, length, model_width = tokens.shape
    channels = taps.shape[2]
    width = xproj.shape[2]
    fixed = lambda array: pl.BlockSpec(array.shape, lambda s, i: (0,) * array.ndim)
    one = lambda *tail: pl.BlockSpec((None,) + tail, lambda s, i: (s,) + (0,) * len(tail))
    return pl.pallas_call(
        functools.partial(front, taps.shape[1] - 1),
        grid_spec=pltpu.PrefetchScalarGridSpec(
            num_scalar_prefetch=1,
            grid=(slots,),
            in_specs=[
                one(length, model_width),
                one(ROWS, model_width),
                one(1, modulation.shape[2]),
                fixed(in_matrix),
                fixed(taps),
                fixed(conv_shift),
                fixed(xproj),
            ],
            out_specs=[
                one(length, model_width),
                one(length + 2 * ROWS, channels),
                one(length, channels),
                pl.BlockSpec((2, None, length, channels), lambda s, i: (0, s, 0, 0)),
                one(2, length, width),
            ],
        ),
        out_shape=[
            jax.ShapeDtypeStruct((slots, length, model_width), BF16),
            jax.ShapeDtypeStruct((slots, length + 2 * ROWS, channels), F32),
            jax.ShapeDtypeStruct((slots, length, channels), F32),
            jax.ShapeDtypeStruct((2, slots, length, channels), BF16),
            jax.ShapeDtypeStruct((slots, 2, length, width), F32),
        ],
        compiler_params=pltpu.CompilerParams(vmem_limit_bytes=40 * MIB),
        cost_estimate=pl.CostEstimate(
            flops=18000 * slots * length * channels,
            bytes_accessed=20 * slots * length * channels,
            transcendentals=0,
        ),
        name="project",
    )(info, tokens, halo, modulation, in_matrix, taps, conv_shift, xproj)


def back(
    info,
    extended,
    conv_grad,
    proj_grad,
    conv_out,
    taps,
    conv_shift,
    xproj,
    grad_x,
    rim,
    sums,
    xproj_grad,
    rows,
):
    slot = pl.program_id(0)
    length, channels = grad_x.shape
    kernel = taps.shape[1]
    halo = kernel - 1
    count, base = info[slot], info[pl.num_programs(0)]

    @pl.when(slot == 0)
    def _():
        sums[...] = jnp.zeros_like(sums)
        xproj_grad[...] = jnp.zeros_like(xproj_grad)
        rows[...] = jnp.zeros_like(rows)

    @pl.when(count <= base)
    def _():
        grad_x[...] = jnp.zeros_like(grad_x)
        rim[...] = jnp.zeros_like(rim)

    @pl.when(count > base)
    def _():
        row = lax.broadcasted_iota(jnp.int32, (length, 1), 0)
        mask = (base + row < count).astype(F32)
        for d in range(2):
            pre = conv_rows(extended, taps, conv_shift, d, length)
            sigmoid = jax.nn.sigmoid(pre)
            slope = sigmoid * (1.0 + pre * (1.0 - sigmoid))
            into = conv_grad[d] + dot32(proj_grad[d], xproj[d], ((1,), (1,)))
            value = into * mask * slope
            rows[d, ROWS : ROWS + length, :] = value
            turned = jnp.transpose(proj_grad[d].astype(F32)).astype(BF16)
            xproj_grad[d] += dot32(turned, conv_out[d], ((1,), (0,)))
            for k in range(kernel):
                first = tap_row(d, k, kernel)
                at = d * kernel + k
                sums[at : at + 1, :] += jnp.sum(
                    value * extended[first : first + length, :], axis=0, keepdims=True
                )
            at = 2 * kernel + d
            sums[at : at + 1, :] += jnp.sum(value, axis=0, keepdims=True)
        total = jnp.zeros((length, channels), F32)
        for k in range(kernel):
            ahead, behind = ROWS + halo - k, ROWS - halo + k
            total = total + taps[0, k : k + 1, :] * rows[0, ahead : ahead + length, :]
            total = total + taps[1, k : k + 1, :] * rows[1, behind : behind + length, :]
        grad_x[...] = total
        rim[0] = rows[0, ROWS : 2 * ROWS, :]
        rim[1] = rows[1, length : length + ROWS, :]


def back_through(info, extended, conv_grad, proj_grad, conv_out, taps, conv_shift, xproj):
    slots = extended.shape[0]
    length, channels = conv_out.shape[2:]
    width = xproj.shape[2]
    kernel = taps.shape[1]
    sum_rows = 2 * ROWS * ((2 * kernel + 2 + 2 * ROWS - 1) // (2 * ROWS))
    fixed = lambda array: pl.BlockSpec(array.shape, lambda s, i: (0,) * len(array.shape))
    one = lambda *tail: pl.BlockSpec((None,) + tail, lambda s, i: (s,) + (0,) * len(tail))
    both = pl.BlockSpec((2, None, length, channels), lambda s, i: (0, s, 0, 0))
    sums = jax.ShapeDtypeStruct((sum_rows, channels), F32)
    xproj_grad = jax.ShapeDtypeStruct((2, width, channels), F32)
    return pl.pallas_call(
        back,
        grid_spec=pltpu.PrefetchScalarGridSpec(
            num_scalar_prefetch=1,
            grid=(slots,),
            in_specs=[
                one(length + 2 * ROWS, channels),
                both,
                one(2, length, width),
                both,
                fixed(taps),
                fixed(conv_shift),
                fixed(xproj),
            ],
            out_specs=[one(length, channels), one(2, ROWS, channels), fixed(sums), fixed(xproj_grad)],
            scratch_shapes=[pltpu.VMEM((2, length + 2 * ROWS, channels), F32)],
        ),
        out_shape=[
            jax.ShapeDtypeStruct((slots, length, channels), F32),
            jax.ShapeDtypeStruct((slots, 2, ROWS, channels), F32),
            sums,
            xproj_grad,
        ],
        compiler_params=pltpu.CompilerParams(vmem_limit_bytes=32 * MIB),
        cost_estimate=pl.CostEstimate(
            flops=24000 * slots * length * channels,
            bytes_accessed=30 * slots * length * channels,
            transcendentals=0,
        ),
        name="back_through",
    )(info, extended, conv_grad, proj_grad, conv_out, taps, conv_shift, xproj)


def scatter(groups, terms, out, parcel, landed, send_sem, recv_sem):
    g, bits = greet(groups)
    ways = len(bits)
    pieces = runs(terms.shape[1], ways)
    mail = Mail(send_sem, recv_sem)
    held = [set(range(groups)) for _ in range(ways)]
    came = [{r: [] for r in range(groups)} for _ in range(ways)]

    def summed(p, r):
        value = terms[r, pieces[p]].astype(F32)
        for t, take in came[p][r]:
            take()
            value = value + landed[t, r, pieces[p]].astype(F32)
        return value

    for t in range(ways):
        for p in range(ways):
            bit = bits[(p + t) % ways]
            for r in sorted(r for r in held[p] if r & bit):
                src = terms
                if t:
                    parcel[r, pieces[p]] = summed(p, r).astype(parcel.dtype)
                    src = parcel
                take = mail.post(
                    src.at[r, pieces[p]],
                    landed.at[t, r ^ bit, pieces[p]],
                    {"group": partner(g, bit)},
                )
                came[p][r ^ bit].append((t, take))
                held[p].remove(r)
    for p in range(ways):
        out[pieces[p]] = summed(p, 0)
    mail.finish()


def scatter_blocks(terms, number):
    groups = lax.axis_size("group")
    ways = groups.bit_length() - 1
    slots, length, model_width = terms.shape
    block = (slots // groups, length, model_width)
    copies = ways * (groups - 1)
    return pl.pallas_call(
        functools.partial(scatter, groups),
        in_specs=[pl.BlockSpec(memory_space=pltpu.VMEM)],
        out_specs=pl.BlockSpec(memory_space=pltpu.VMEM),
        out_shape=jax.ShapeDtypeStruct(block, F32),
        scratch_shapes=[
            pltpu.VMEM((groups,) + block, terms.dtype),
            pltpu.VMEM((ways, groups) + block, terms.dtype),
            pltpu.SemaphoreType.DMA((copies,)),
            pltpu.SemaphoreType.DMA((copies,)),
        ],
        compiler_params=pltpu.CompilerParams(
            collective_id=number, has_side_effects=True, vmem_limit_bytes=48 * MIB
        ),
        name="scatter_blocks",
    )(terms.reshape((groups,) + block))


def finish(
    groups,
    parts,
    terms,
    in_x,
    in_z,
    packed,
    modulation,
    in_grad,
    out_grad,
    rest,
    landed,
    every_x,
    every_z,
    every_p,
    send_sem,
    recv_sem,
):
    g, f = lax.axis_index("group"), lax.axis_index("fsdp")
    bits = [1 << i for i in range(groups.bit_length() - 1)]
    ways = len(bits)
    barrier = pltpu.get_barrier_semaphore()
    others = [{"group": partner(g, bit)} for bit in bits]
    others += [{"fsdp": lax.rem(f + k, parts)} for k in range(1, parts)]
    for other in others:
        pl.semaphore_signal(barrier, inc=1, device_id=other, device_id_type=pl.DeviceIdType.MESH)
    pl.semaphore_wait(barrier, len(others))
    mail = Mail(send_sem, recv_sem)
    takes = []
    for k in range(1, parts):
        there = lax.rem(f + k, parts)
        takes.append(mail.post(terms.at[there], landed.at[k - 1], {"fsdp": there}))

    def absolute(r):
        at = g
        for bit in bits:
            at = partner(at, bit) if r & bit else at
        return at

    shards = ((in_x, every_x), (in_z, every_z), (packed, every_p))
    known = {}
    forwards = [[] for _ in range(ways)]
    for own, every in shards:
        every[g] = own[...]
    for n, (own, every) in enumerate(shards):
        tiles = own.shape[1] // LANES
        for p in range(ways):
            lo, hi = (tiles * i // ways * LANES for i in (p, p + 1))
            held = [0]
            for t in range(ways):
                bit = bits[(p + t) % ways]
                for r in list(held):
                    move = (n, every, pl.ds(lo, hi - lo), p, r, bit)
                    forwards[t if r else 0].append(move)
                    held.append(r ^ bit)

    def run(moves):
        for n, every, cols, p, r, bit in moves:
            if r:
                known[n, p, r]()
            block = every.at[absolute(r), :, cols]
            known[n, p, r ^ bit] = mail.post(
                block,
                block,
                {"group": partner(g, bit)},
                landing=every.at[absolute(r ^ bit), :, cols],
            )

    run(forwards[0])
    total = terms[f]
    for k, take in enumerate(takes):
        take()
        total = total + landed[k]
    modulation[0] = total
    found = {0: None}
    for bit in bits:
        for r, take in list(found.items()):
            if take is not None:
                take()
            found[r ^ bit] = mail.post(
                modulation.at[r], modulation.at[r ^ bit], {"group": partner(g, bit)}
            )
    for moves in forwards[1:]:
        run(moves)
    mail.finish()
    channels = in_x.shape[1]
    piece, model_width = packed.shape[0], out_grad.shape[1]
    for j in range(groups):
        for h, every in enumerate((every_x, every_z)):
            at = (h * groups + j) * channels
            in_grad[:, at : at + channels] = every[j].astype(F32)
        out_grad[j * piece : (j + 1) * piece, :] = every_p[j, :, :model_width].astype(F32)
        rest[j * piece : (j + 1) * piece, :] = every_p[j, :, model_width:].astype(F32)


def finish_gradients(terms, in_x, in_z, packed, model_width, number):
    groups, parts = lax.axis_size("group"), lax.axis_size("fsdp")
    ways = groups.bit_length() - 1
    block = terms.shape[1:]
    copies = parts - 1 + groups - 1 + 3 * ways * (groups - 1)
    rows, channels = in_x.shape
    piece, wide = packed.shape
    return pl.pallas_call(
        functools.partial(finish, groups, parts),
        in_specs=[pl.BlockSpec(memory_space=pltpu.VMEM)] * 4,
        out_specs=[pl.BlockSpec(memory_space=pltpu.VMEM)] * 4,
        out_shape=[
            jax.ShapeDtypeStruct((groups,) + block, F32),
            jax.ShapeDtypeStruct((rows, 2 * groups * channels), F32),
            jax.ShapeDtypeStruct((groups * piece, model_width), F32),
            jax.ShapeDtypeStruct((groups * piece, wide - model_width), F32),
        ],
        scratch_shapes=[
            pltpu.VMEM((parts - 1,) + block, F32),
            pltpu.VMEM((groups, rows, channels), BF16),
            pltpu.VMEM((groups, rows, channels), BF16),
            pltpu.VMEM((groups, piece, wide), BF16),
            pltpu.SemaphoreType.DMA((copies,)),
            pltpu.SemaphoreType.DMA((copies,)),
        ],
        compiler_params=pltpu.CompilerParams(
            collective_id=number, has_side_effects=True, vmem_limit_bytes=32 * MIB
        ),
        name="finish_gradients",
    )(terms, in_x, in_z, packed)


def to_owner(groups, parts):
    ratio = parts // groups
    pairs = []
    for g in range(groups):
        for f in range(parts):
            pairs.append((g * parts + f, (f // ratio) * parts + groups * (f % ratio) + g))
    return pairs


def cut(array, pieces):
    slots = array.shape[0]
    edges = [slots * i // pieces for i in range(pieces + 1)]
    return [array[lo:hi] for lo, hi in zip(edges[:-1], edges[1:])]


def flip(array, groups, bit):
    return lax.ppermute(array, "group", [(i, i ^ bit) for i in range(groups)])


def bits_of(groups, first):
    count = groups.bit_length() - 1
    return [1 << ((first + i) % count) for i in range(count)]


def scatter_stage(pieces, groups, t):
    nexts = []
    for p, held in enumerate(pieces):
        bit = bits_of(groups, p)[t]
        sums = {r: value for r, value in held.items() if not r & bit}
        for r in [r for r in held if r & bit]:
            came = flip(held[r], groups, bit).astype(F32)
            sums[r ^ bit] = (sums[r ^ bit].astype(F32) + came).astype(BF16)
        nexts.append(sums)
    return nexts


def on_device(
    tokens,
    item_bucket,
    slot_item,
    slot_live,
    slot_tokens,
    ada_weight,
    ada_bias,
    in_weight,
    conv_weight,
    conv_bias,
    xproj_weight,
    dt_weight,
    dt_bias,
    a_log,
    skip_gain,
    out_weight,
    cotangent,
):
    own_slots, length, model_width = tokens.shape
    groups, parts = lax.axis_size("group"), lax.axis_size("fsdp")
    g, f = lax.axis_index("group"), lax.axis_index("fsdp")
    slots = own_slots * groups
    inner_width = in_weight.shape[1] // 2
    channels = inner_width // groups
    kernel = conv_weight.shape[1]
    halo = kernel - 1
    rank_width = dt_weight.shape[1]
    width = xproj_weight.shape[2]
    states = (width - rank_width) // 2

    matches = slot_item[:, None] == jnp.arange(item_bucket.shape[0], dtype=jnp.int32)[None, :]
    own_buckets = jnp.sum(jnp.where(matches, item_bucket[None, :], 0), axis=1)
    own_condition = jax.nn.silu(time_embed(own_buckets, model_width)).astype(BF16)
    own_modulation = jnp.dot(own_condition, ada_weight, preferred_element_type=F32)
    own_modulation = own_modulation + ada_bias.astype(F32)
    plain = jnp.stack([slot_tokens * slot_live, own_buckets], axis=1).astype(F32)
    facts = jnp.concatenate([own_modulation, jnp.repeat(plain, LANES // 2, axis=1)], axis=1)

    edges = [(i, i + 1) for i in range(parts - 1)]
    before = lax.ppermute(tokens[:, length - halo :], "fsdp", edges)
    after = lax.ppermute(tokens[:, :halo], "fsdp", [(j, i) for i, j in edges])
    padding = jnp.zeros((own_slots, ROWS - 2 * halo, model_width), tokens.dtype)
    in_own = jnp.concatenate(
        [
            lax.dynamic_slice_in_dim(in_weight, h * inner_width + g * channels, channels, 1)
            for h in range(2)
        ],
        axis=1,
    )
    shard = out_weight.shape[0]
    small = jnp.concatenate(
        [
            dt_weight.reshape(2 * rank_width, shard),
            a_log.reshape(2 * states, shard),
            conv_weight.reshape(2 * kernel, shard),
            conv_bias,
            dt_bias,
            skip_gain,
        ],
        axis=0,
    )
    small_rows = small.shape[0]
    small_pad = -small_rows % LANES
    small = jnp.pad(small, ((0, -small_rows % BLOCK), (0, 0)))
    all_tokens, all_halo, in_matrix, all_xproj, all_small, all_facts = collect_inputs(
        tokens,
        jnp.concatenate([before, after, padding], axis=1),
        in_own,
        xproj_weight,
        small,
        facts,
    )
    ways = groups.bit_length() - 1
    all_tokens, late = lax.optimization_barrier((all_tokens, cotangent))
    travelling = [{0: part} for part in cut(late, ways)]
    for p, held in enumerate(travelling):
        for bit in bits_of(groups, p):
            held[bit] = flip(held[0], groups, bit)
    all_tokens = all_tokens.reshape(slots, length, model_width)
    all_halo = all_halo.reshape(slots, ROWS, model_width)
    in_matrix = in_matrix.reshape(model_width, 2 * channels)

    piece = shard // groups
    sent = lax.ppermute(
        lax.dynamic_slice_in_dim(out_weight, g * piece, piece, 0),
        ("group", "fsdp"),
        to_owner(groups, parts),
    )
    out_matrix = lax.all_gather(sent, "fsdp", axis=0, tiled=True)
    xproj = jnp.concatenate([all_xproj[0], all_xproj[1]], axis=1)
    rest = jnp.concatenate([all_small[0], all_small[1]], axis=1)
    edge = 0

    def take(rows):
        nonlocal edge
        edge += rows
        return rest[edge - rows : edge]

    dt_matrix = jnp.pad(
        take(2 * rank_width).reshape(2, rank_width, channels), ((0, 0), (0, width - rank_width), (0, 0))
    )
    rate = -jnp.exp(take(2 * states).astype(F32)).reshape(2, states // ROWS, ROWS, channels)
    taps = take(2 * kernel).reshape(2, kernel, channels).astype(F32)
    conv_shift = take(2).astype(F32)
    dt_shift = take(2).astype(F32).reshape(2, 1, channels)
    skip = take(2).astype(F32).reshape(2, 1, channels)
    decay = rate * LOG2E

    columns = facts.shape[1] - LANES
    plain = all_facts[:, 0, :, columns:].reshape(slots, LANES).astype(jnp.int32)
    counts, buckets = plain[:, 0], plain[:, LANES // 2]
    modulation = all_facts[:, :, :, :columns].transpose(0, 2, 1, 3).reshape(slots, parts * columns)
    group_counts = jnp.sum(counts.reshape(groups, own_slots), axis=1).astype(F32)
    share = jnp.repeat(group_counts / jnp.sum(group_counts), own_slots)
    positions = f * length + jnp.arange(length, dtype=jnp.int32)
    mask = (positions[None, :] < counts[:, None]).astype(F32)
    active = (counts > f * length).astype(jnp.int32)
    own_mask = mask[:own_slots, :, None]
    own_share = share[:own_slots, None, None]
    condition = jax.nn.silu(time_embed(buckets, model_width)).astype(BF16)
    shift_mod = modulation[:, None, :model_width]
    scale_mod = modulation[:, None, model_width : 2 * model_width]
    gate_mod = modulation[:, None, 2 * model_width :]

    info = jnp.concatenate([counts, (f * length)[None]]).astype(jnp.int32)
    modulated, wide_x, gate_z, conv_out, projected = project(
        info, all_tokens, all_halo, modulation[:, None, :], in_matrix, taps, conv_shift, xproj
    )
    travelling, projected = lax.optimization_barrier((travelling, projected))
    for p, held in enumerate(travelling):
        order = bits_of(groups, p)
        for t in range(1, ways):
            for r in [r for r in held if r and r < groups and all(r & bit == 0 for bit in order[t:])]:
                held[r ^ order[t]] = flip(held[r], groups, order[t])
    proj = sum_blocks(projected, F32, F32, 2)
    proj, travelling = lax.optimization_barrier((proj, travelling))
    all_cotangent = jnp.concatenate([held[r] for r in range(groups) for held in travelling], axis=0)

    def normalise(values):
        inputs = values.astype(F32)
        centered = inputs - jnp.mean(inputs, axis=2, keepdims=True)
        inv_std = lax.rsqrt(jnp.mean(centered * centered, axis=2, keepdims=True) + EPSILON)
        return (inputs, centered * inv_std, inv_std)

    grad_in_all = all_cotangent.astype(F32) * (mask * share[:, None])[:, :, None]
    branch_gradient = (grad_in_all * gate_mod).astype(BF16)
    grad_gated = jnp.einsum("sld,cd->slc", branch_gradient, out_matrix, preferred_element_type=F32)
    grad_y = grad_gated * jax.nn.silu(gate_z)

    step, end, pull, total, mix_b, mix_c = scan_ends(active, conv_out, proj, grad_y, dt_matrix, dt_shift, decay)
    entering = pass_states(end, pull, total, decay)
    gated_output, grad_z, conv_grad, proj_part, dtw_grad, dtb_grad, decay_grad, skip_grad = scan_all(
        active,
        conv_out,
        proj,
        grad_y,
        step,
        mix_b,
        mix_c,
        entering,
        gate_z,
        grad_gated,
        dt_matrix,
        decay,
        skip,
    )
    proj_grad = sum_blocks(proj_part, BF16, BF16, 3)
    alog_grad = (decay_grad * rate).reshape(2 * states, channels)

    branch_part = jnp.einsum("slc,cd->sld", gated_output, out_matrix, preferred_element_type=F32)
    inward_z = jnp.einsum("sld,slc->dc", modulated, grad_z, preferred_element_type=F32)
    branch_part, inward_z, proj_grad = lax.optimization_barrier(
        (branch_part.astype(BF16), inward_z.astype(BF16), proj_grad)
    )
    inward_z = lax.psum_scatter(inward_z, "fsdp", scatter_dimension=0, tiled=True)
    ways = groups.bit_length() - 1
    cut_blocks = [cut(block, ways) for block in jnp.split(branch_part, groups, axis=0)]
    moving = [{r: cut_blocks[r][p] for r in range(groups)} for p in range(ways)]
    moving = scatter_stage(moving, groups, 0)
    outward = jnp.einsum("slc,sld->cd", gated_output, branch_gradient, preferred_element_type=F32)

    grad_x, rim, conv_sums, xproj_grads = back_through(
        info, wide_x, conv_grad, proj_grad, conv_out, taps, conv_shift, xproj
    )
    outward, moving, rim = lax.optimization_barrier((outward.astype(BF16), moving, rim))
    ahead = lax.ppermute(rim[:, 0, :halo], "fsdp", [(j, i) for i, j in edges])
    behind = lax.ppermute(rim[:, 1, ROWS - halo :], "fsdp", edges)
    zeros = jnp.zeros_like(ahead)
    ahead, behind = jnp.concatenate([zeros, ahead], 1), jnp.concatenate([behind, zeros], 1)
    last = sum(taps[0, k] * ahead[:, halo - k : 2 * halo - k] for k in range(kernel))
    first = sum(taps[1, k] * behind[:, k : k + halo] for k in range(kernel))
    grad_x = grad_x + jnp.concatenate(
        [first, jnp.zeros((slots, length - 2 * halo, channels), F32), last], axis=1
    )
    grad_x = grad_x.astype(BF16)
    inner_gradient = jnp.concatenate([grad_x, grad_z], axis=2)
    inward = jnp.einsum("sld,slc->dc", modulated, grad_x, preferred_element_type=F32)
    grad_mod_part = jnp.einsum(
        "slc,dc->sld", inner_gradient, in_matrix, preferred_element_type=F32
    ).astype(BF16)
    for t in range(1, ways):
        moving = scatter_stage(moving, groups, t)
    branch = jnp.concatenate([held[0] for held in moving], axis=0)
    small_grads = jnp.concatenate(
        [
            xproj_grads.reshape(2 * width, channels),
            dtw_grad[:, :rank_width].reshape(2 * rank_width, channels),
            alog_grad,
            conv_sums[: 2 * kernel + 2],
            dtb_grad.reshape(2, channels),
            skip_grad.reshape(2, channels),
            jnp.zeros((small_pad, channels), F32),
        ],
        axis=0,
    ).astype(BF16)
    packed_grads = jnp.concatenate([outward, small_grads.T], axis=1)
    packed_grads, inward_z = lax.optimization_barrier((packed_grads, inward_z))
    inward, grad_mod_part, branch, packed_grads = lax.optimization_barrier(
        (inward.astype(BF16), grad_mod_part, branch, packed_grads)
    )
    branch = branch.astype(F32)
    grad_mod = scatter_blocks(grad_mod_part, 4) * own_mask

    own_gate = gate_mod[:own_slots]
    own_scale = scale_mod[:own_slots]
    own_inputs, own_normed, own_inv = normalise(tokens)
    layer_out = ((own_inputs + own_gate * branch) * own_mask).astype(BF16)
    grad_in = cotangent.astype(F32) * own_mask * own_share
    grad_gate = jnp.sum(grad_in * branch, axis=1)

    grad_shift = jnp.sum(grad_mod, axis=1)
    grad_scale = jnp.sum(grad_mod * own_normed, axis=1)
    grad_normed = grad_mod * (1.0 + own_scale)
    grad_ln = own_inv * (
        grad_normed
        - jnp.mean(grad_normed, axis=2, keepdims=True)
        - own_normed * jnp.mean(grad_normed * own_normed, axis=2, keepdims=True)
    )
    tokens_grad = grad_in + grad_ln

    mod_part = jnp.concatenate([grad_shift, grad_scale, grad_gate], axis=1)
    packed_piece = lax.psum_scatter(packed_grads, "fsdp", scatter_dimension=0, tiled=True)
    packed_piece = lax.ppermute(
        packed_piece, ("group", "fsdp"), [(j, i) for i, j in to_owner(groups, parts)]
    )
    inward_x = lax.psum_scatter(inward, "fsdp", scatter_dimension=0, tiled=True)
    mod_terms = mod_part.reshape(own_slots, parts, -1).transpose(1, 0, 2)
    mod_all, in_grad, out_grad, packed_own = finish_gradients(
        mod_terms, inward_x, inward_z, packed_piece, model_width, 5
    )
    mod_all = mod_all.reshape(slots, -1)
    ada_grad = jnp.einsum("sd,sk->dk", condition, mod_all.astype(BF16), preferred_element_type=F32)
    adab_grad = jnp.sum(mod_all, axis=0)
    xproj_grad = jnp.stack(
        [packed_own[:, d * width : (d + 1) * width] for d in range(2)]
    )
    rest_grads = packed_own[:, 2 * width :].T
    sizes = [2 * rank_width, 2 * states, 2 * kernel, 2, 2, 2]
    cuts = [sum(sizes[:i]) for i in range(len(sizes) + 1)]
    dtw_out, alog_out, conv_w_out, conv_b_out, dtb_out, skip_out = [
        rest_grads[cuts[i] : cuts[i + 1]] for i in range(len(sizes))
    ]
    return (
        layer_out,
        tokens_grad,
        ada_grad,
        adab_grad,
        in_grad,
        conv_w_out.reshape(2, kernel, shard),
        conv_b_out,
        xproj_grad,
        dtw_out.reshape(2, rank_width, shard),
        dtb_out,
        alog_out.reshape(2, states, shard),
        skip_out,
        out_grad,
    )


def solution(mesh):
    in_specs = (
        P("group", "fsdp", None),
        P(),
        P("group"),
        P("group"),
        P("group"),
        P(None, "fsdp"),
        P("fsdp"),
        P("fsdp", None),
        P(None, None, "fsdp"),
        P(None, "fsdp"),
        P(None, "fsdp", None),
        P(None, None, "fsdp"),
        P(None, "fsdp"),
        P(None, None, "fsdp"),
        P(None, "fsdp"),
        P("fsdp", None),
        P("group", "fsdp", None),
    )
    out_specs = (
        P("group", "fsdp", None),
        P("group", "fsdp", None),
        P(None, "fsdp"),
        P("fsdp"),
        P("fsdp", None),
        P(None, None, "fsdp"),
        P(None, "fsdp"),
        P(None, "fsdp", None),
        P(None, None, "fsdp"),
        P(None, "fsdp"),
        P(None, None, "fsdp"),
        P(None, "fsdp"),
        P("fsdp", None),
    )
    return jax.shard_map(
        on_device, mesh=mesh, in_specs=in_specs, out_specs=out_specs, check_vma=False
    )
```

```python
import functools
import math

import jax
import jax.numpy as jnp
from jax import lax
from jax.experimental import pallas as pl
from jax.experimental.pallas import tpu as pltpu
from jax.sharding import PartitionSpec as P

EPSILON = 1e-06
LANES = 128
ROWS = 8
BLOCK = 16
WIDE = 256
LAG = 3
RUN = 2
LOG2E = math.log2(math.e)
LN2 = math.log(2.0)
F32 = jnp.float32
BF16 = jnp.bfloat16
MIB = 1 << 20


def time_embed(buckets, model_width):
    half_width = model_width // 2
    frequency = jnp.exp(-math.log(10000.0) * jnp.arange(half_width, dtype=F32) / half_width)
    angles = buckets.astype(F32)[:, None] * frequency[None, :]
    return jnp.concatenate([jnp.cos(angles), jnp.sin(angles)], axis=1)


def silu_slope(values):
    sigmoid = jax.nn.sigmoid(values)
    return sigmoid * (1.0 + values * (1.0 - sigmoid))


def dot32(left, right, dims):
    return lax.dot_general(left, right, (dims, ((), ())), preferred_element_type=F32)


def pass_one(
    states, active, conv, proj, grad_y, dt_w, dt_b, decay, step, end, pull, total, mix_b, mix_c, drive, turned
):
    slot, direction = pl.program_id(0), pl.program_id(1)
    length, channels = drive.shape
    chunks = channels // LANES
    halves = states // ROWS
    rank = proj.shape[1] - 2 * states

    @pl.when(active[slot] == 0)
    def _():
        end[...] = jnp.zeros_like(end)
        pull[...] = jnp.zeros_like(pull)
        total[...] = jnp.zeros_like(total)

    @pl.when(active[slot] != 0)
    def _():
        pre = dot32(proj[...].astype(BF16), dt_w[direction], ((1,), (0,))) + dt_b[direction]
        steps = jnp.maximum(pre, 0.0) + jnp.log(1.0 + jnp.exp(-jnp.abs(pre)))
        step[...] = steps
        drive[...] = steps * conv[...].astype(F32)
        total[...] = jnp.broadcast_to(jnp.sum(steps, axis=0, keepdims=True), total.shape)

        def turn(i, carry):
            at = pl.multiple_of(i * ROWS, ROWS)
            turned[i] = jnp.transpose(proj[pl.ds(at, ROWS), :])[rank : rank + 2 * states]
            return carry

        lax.fori_loop(0, length // ROWS, turn, 0, unroll=True)
        zero = jnp.zeros((halves, ROWS, LANES), F32)
        for backward in range(2):

            @pl.when(direction == backward)
            def _():
                carry = ((zero,) * chunks, (zero + 1.0,) * chunks, (zero,) * chunks)
                rates = [decay[direction, :, :, k : k + LANES] for k in range(0, channels, LANES)]

                def block(i, carry):
                    at = length // ROWS - 1 - i if backward else i
                    rows = pl.ds(pl.multiple_of(at * ROWS, ROWS), ROWS)
                    held = [ref[rows, :] for ref in (step, drive, grad_y)]
                    hidden, running, pulled = carry
                    columns = turned[at]
                    for j in list(range(ROWS))[:: -1 if backward else 1]:
                        t = at * ROWS + j
                        wide = jnp.broadcast_to(columns[:, j : j + 1], (2 * states, LANES))
                        b = wide[:states].reshape(halves, ROWS, LANES)
                        c = wide[states:].reshape(halves, ROWS, LANES)
                        mix_b[t] = b
                        mix_c[t] = c
                        rowed = [
                            [
                                jnp.broadcast_to(h[j : j + 1, k : k + LANES], (ROWS, LANES))[None]
                                for k in range(0, channels, LANES)
                            ]
                            for h in held
                        ]
                        new = ([], [], [])
                        for k in range(chunks):
                            factor = jnp.exp2(rowed[0][k] * rates[k])
                            new[0].append(factor * hidden[k] + rowed[1][k] * b)
                            run = running[k] * factor
                            new[1].append(run)
                            new[2].append(pulled[k] + run * (rowed[2][k] * c))
                        hidden, running, pulled = new
                    return (tuple(hidden), tuple(running), tuple(pulled))

                hidden, _, pulled = lax.fori_loop(0, length // ROWS, block, carry)
                for k in range(chunks):
                    lanes = slice(k * LANES, (k + 1) * LANES)
                    end[:, :, lanes] = hidden[k]
                    pull[:, :, lanes] = pulled[k]


def pass_two(
    states,
    active,
    conv,
    proj,
    grad_y,
    step,
    mix_b,
    mix_c,
    entry,
    arrive,
    gate_z,
    grad_gated,
    dt_w,
    decay,
    skip,
    tile_b,
    tile_c,
    sel,
    take_b,
    take_c,
    gated,
    grad_z,
    conv_grad,
    proj_grad,
    dtw_grad,
    dtb_grad,
    alog_grad,
    skip_grad,
    drive,
    hid_even,
    hid_odd,
    edge,
    gst_even,
    gst_odd,
    thd_even,
    thd_odd,
    mixed,
    sdec,
    scan_y,
    in_part,
    out_part,
    rows_b,
    rows_c,
    drive_low,
    grad_low,
    y,
):
    slot, direction = pl.program_id(0), pl.program_id(1)
    length, channels = drive.shape
    chunks = channels // LANES
    halves = states // ROWS
    wide = BLOCK * states
    pairs = length // (2 * BLOCK)
    hid, gst, thd = (hid_even, hid_odd), (gst_even, gst_odd), (thd_even, thd_odd)
    lanes = [slice(k * LANES, (k + 1) * LANES) for k in range(chunks)]

    @pl.when((slot == 0) & (direction == 0))
    def _():
        dtw_grad[...] = jnp.zeros_like(dtw_grad)
        dtb_grad[...] = jnp.zeros_like(dtb_grad)
        alog_grad[...] = jnp.zeros_like(alog_grad)
        skip_grad[...] = jnp.zeros_like(skip_grad)

    @pl.when(direction == 0)
    def _():
        y[...] = jnp.zeros_like(y)

    @pl.when(active[slot] == 0)
    def _():
        conv_grad[...] = jnp.zeros_like(conv_grad)
        proj_grad[...] = jnp.zeros_like(proj_grad)
        gated[...] = jnp.zeros_like(gated)
        grad_z[...] = jnp.zeros_like(grad_z)

    def low(value):
        return value.reshape(states, LANES).astype(BF16)

    def block_range(pair, odd):
        return pl.ds(pl.multiple_of((2 * pair + odd) * BLOCK, BLOCK), BLOCK)

    def sweep_blocks(backward, tokens, matmuls, start):
        first, second = (1, 0) if backward else (0, 1)

        def two(i, carry):
            pair = pairs - 1 - i if backward else i
            before = lax.rem(pair + (1 if backward else pairs - 1), pairs)
            carry = tokens(pair, first, backward, matmuls(before, second), carry)
            return tokens(pair, second, backward, matmuls(pair, first), carry)

        carry = lax.fori_loop(0, pairs, two, start)
        for issue, keep in matmuls(0 if backward else pairs - 1, second):
            keep(issue())
        return carry

    def pieces(out, rows, left, right, dims, width):
        made = []
        for n in range(0, width, WIDE):
            cols = slice(n, min(n + WIDE, width))
            picked = right[:, cols] if dims[1] == (0,) else right

            def issue(left=left, picked=picked):
                return dot32(left, picked, dims)

            def keep(product, cols=cols):
                out[rows, cols] = product

            made.append((issue, keep))
        return made

    def scan_rows(pair, odd, backward, refs, body, beside, carry):
        order = list(range(BLOCK))[:: -1 if backward else 1]
        waiting = []
        for at_step, j in enumerate(order):
            if j % ROWS == (ROWS - 1 if backward else 0):
                at = pl.multiple_of((2 * pair + odd) * BLOCK + j // ROWS * ROWS, ROWS)
                held = [ref[pl.ds(at, ROWS), :] for ref in refs]
            i = j % ROWS
            rows = [
                [jnp.broadcast_to(h[i : i + 1, c], (ROWS, LANES))[None] for c in lanes] for h in held
            ]
            for issue, keep in beside[at_step * len(beside) // BLOCK : (at_step + 1) * len(beside) // BLOCK]:
                waiting.append((at_step + LAG, keep, issue()))
            carry = body(j, rows, carry)
            while waiting and waiting[0][0] <= at_step:
                _, keep, product = waiting.pop(0)
                keep(product)
        for _, keep, product in waiting:
            keep(product)
        return carry

    def forward_tokens(pair, odd, backward, beside, hidden):
        for k in range(chunks):
            edge[2 * pair + odd, :, lanes[k]] = low(hidden[k])

        def token(j, rows, hidden):
            b = mix_b[(2 * pair + odd) * BLOCK + j]
            new = []
            for k in range(chunks):
                factor = jnp.exp2(rows[0][k] * decay[direction, :, :, lanes[k]])
                value = factor * hidden[k] + rows[1][k] * b
                hid[odd][pair, j, :, lanes[k]] = low(value)
                new.append(value)
            return tuple(new)

        return scan_rows(pair, odd, backward, (step, drive), token, beside, hidden)

    def forward_matmuls(pair, odd):
        rows = block_range(pair, odd)
        h_rows = hid[odd][pair].reshape(wide, channels)
        return pieces(scan_y, rows, rows_c[rows, :], h_rows, ((1,), (0,)), channels) + pieces(
            out_part, rows, grad_low[rows, :], h_rows, ((1,), (1,)), wide
        )

    def backward_tokens(pair, odd, backward, beside, carry):
        earlier = -1 if backward else 1

        def token(j, rows, carry):
            carried, total = carry
            c = mix_c[(2 * pair + odd) * BLOCK + j]
            news, sums = [], []
            p = j + earlier
            for k in range(chunks):
                rate = decay[direction, :, :, lanes[k]]
                factor = jnp.exp2(rows[0][k] * rate)
                grad_state = rows[1][k] * c + carried[k]
                gst[odd][j, :, lanes[k]] = low(grad_state)
                onward = factor * grad_state
                if 0 <= p < BLOCK:
                    before = hid[odd][pair, p, :, lanes[k]]
                else:
                    before = edge[2 * pair + odd, :, lanes[k]]
                through = onward * before.astype(F32).reshape(halves, ROWS, LANES)
                sums.append(total[k] + through * rows[0][k])
                thd[odd][j, :, lanes[k]] = low(through * rate)
                news.append(onward)
            return (tuple(news), tuple(sums))

        return scan_rows(pair, odd, backward, (step, grad_y), token, beside, carry)

    def backward_matmuls(pair, odd):
        rows = block_range(pair, odd)
        g_rows = gst[odd][...].reshape(wide, channels)
        t_rows = thd[odd][...].reshape(wide, channels)
        return (
            pieces(mixed, rows, rows_b[rows, :], g_rows, ((1,), (0,)), channels)
            + pieces(sdec, rows, sel[...].astype(BF16), t_rows, ((1,), (0,)), channels)
            + pieces(in_part, rows, drive_low[rows, :], g_rows, ((1,), (1,)), wide)
        )

    @pl.when(active[slot] != 0)
    def _():
        drive[...] = step[...] * conv[...].astype(F32)
        drive_low[...] = drive[...].astype(BF16)
        grad_low[...] = grad_y[...].astype(BF16)
        proj_low = proj[...].astype(BF16)
        picked = jnp.concatenate([sel[...]] * (length // BLOCK), axis=0)
        rows_b[...] = (dot32(proj_low, tile_b[...], ((1,), (0,))) * picked).astype(BF16)
        rows_c[...] = (dot32(proj_low, tile_c[...], ((1,), (0,))) * picked).astype(BF16)
        zero = jnp.zeros((halves, ROWS, LANES), F32)
        for reverse in (False, True):

            @pl.when(direction == int(reverse))
            def _():
                start = tuple(entry[:, :, c].astype(F32) for c in lanes)
                sweep_blocks(reverse, forward_tokens, forward_matmuls, start)
                start = (tuple(arrive[:, :, c].astype(F32) for c in lanes), (zero,) * chunks)
                _, sums = sweep_blocks(not reverse, backward_tokens, backward_matmuls, start)
                for k in range(chunks):
                    alog_grad[direction, :, :, lanes[k]] += sums[k]

        conv_values = conv[...].astype(F32)
        steps = step[...]
        grads = grad_y[...]
        step_grad = conv_values * mixed[...] + LN2 * sdec[...]
        pre_grad = step_grad * (1.0 - jnp.exp(-steps))
        dtb_grad[direction] += jnp.sum(pre_grad, axis=0, keepdims=True)
        pre_low = pre_grad.astype(BF16)
        proj_grad[...] = (
            dot32((in_part[...] * picked).astype(BF16), take_b[...], ((1,), (0,)))
            + dot32((out_part[...] * picked).astype(BF16), take_c[...], ((1,), (0,)))
            + dot32(pre_low, dt_w[direction], ((1,), (1,)))
        )
        dtw_grad[direction] += dot32(jnp.transpose(proj[...]).astype(BF16), pre_low, ((1,), (0,)))
        y[...] += scan_y[...] + skip[direction] * conv_values
        skip_grad[direction] += jnp.sum(grads * conv_values, axis=0, keepdims=True)
        conv_grad[...] = grads * skip[direction] + steps * mixed[...]

        @pl.when(direction == 1)
        def _():
            total = y[...]
            value = gate_z[...]
            sigmoid = jax.nn.sigmoid(value)
            gated[...] = (total * (value * sigmoid)).astype(BF16)
            slope = sigmoid * (1.0 + value * (1.0 - sigmoid))
            grad_z[...] = (grad_gated[...] * total * slope).astype(BF16)


def whole(array):
    zeros = (0,) * array.ndim
    return pl.BlockSpec(array.shape, lambda s, d, a: zeros)


def scan_ends(active, conv, proj, grad_y, dt_w, dt_b, decay):
    slots, length, channels = grad_y.shape
    halves = decay.shape[1]
    width = proj.shape[3]
    states = halves * ROWS
    turn = lambda *tail: pl.BlockSpec((None, None) + tail, lambda s, d, a: (s, d) + (0,) * len(tail))
    pair = lambda *tail: pl.BlockSpec((None, None) + tail, lambda s, d, a: (d, s) + (0,) * len(tail))
    state = (2, slots, halves, ROWS, channels)
    mixes = (length, halves, ROWS, LANES)
    spare = lambda s, a: jnp.where(a[s] != 0, s, slots)
    kept_pair = pl.BlockSpec(
        (None, None, length, channels), lambda s, d, a: (jnp.where(a[s] != 0, d, 0), spare(s, a), 0, 0)
    )
    kept_mix = pl.BlockSpec(
        (None, None) + mixes, lambda s, d, a: (spare(s, a), jnp.where(a[s] != 0, d, 0), 0, 0, 0, 0)
    )
    return pl.pallas_call(
        functools.partial(pass_one, states),
        grid_spec=pltpu.PrefetchScalarGridSpec(
            num_scalar_prefetch=1,
            grid=(slots, 2),
            in_specs=[
                pair(length, channels),
                turn(length, width),
                pl.BlockSpec((None, length, channels), lambda s, d, a: (s, 0, 0)),
                whole(dt_w),
                whole(dt_b),
                whole(decay),
            ],
            out_specs=[
                kept_pair,
                pair(halves, ROWS, channels),
                pair(halves, ROWS, channels),
                pair(ROWS, channels),
                kept_mix,
                kept_mix,
            ],
            scratch_shapes=[
                pltpu.VMEM((length, channels), F32),
                pltpu.VMEM((length // ROWS, 2 * states, ROWS), F32),
            ],
        ),
        out_shape=[
            jax.ShapeDtypeStruct((2, slots + 1, length, channels), F32),
            jax.ShapeDtypeStruct(state, F32),
            jax.ShapeDtypeStruct(state, F32),
            jax.ShapeDtypeStruct((2, slots, ROWS, channels), F32),
            jax.ShapeDtypeStruct((slots + 1, 2) + mixes, F32),
            jax.ShapeDtypeStruct((slots + 1, 2) + mixes, F32),
        ],
        compiler_params=pltpu.CompilerParams(vmem_limit_bytes=24 * MIB),
        name="scan_ends",
    )(active, conv, proj, grad_y, dt_w, dt_b, decay)


def scan_all(
    active, conv, proj, grad_y, step, mix_b, mix_c, entering, gate_z, grad_gated, dt_w, decay, skip
):
    slots, length, channels = grad_y.shape
    halves = decay.shape[1]
    width = proj.shape[3]
    states = halves * ROWS
    wide = BLOCK * states
    rank = width - 2 * states
    column = jnp.arange(width)[:, None]
    lane = jnp.arange(wide)[None, :]
    tile_b = (column == rank + lane % states).astype(BF16)
    tile_c = (column == rank + states + lane % states).astype(BF16)
    sel = (jnp.arange(BLOCK)[:, None] == lane // states).astype(F32)
    turn = lambda *tail: pl.BlockSpec((None, None) + tail, lambda s, d, a: (s, d) + (0,) * len(tail))
    pair = lambda *tail: pl.BlockSpec((None, None) + tail, lambda s, d, a: (d, s) + (0,) * len(tail))
    one = pl.BlockSpec((None, length, channels), lambda s, d, a: (s, 0, 0))
    constants = (dt_w, decay, skip, tile_b, tile_c, sel, tile_b.T, tile_c.T)
    sums = (
        jax.ShapeDtypeStruct((2, width, channels), F32),
        jax.ShapeDtypeStruct((2, 1, channels), F32),
        jax.ShapeDtypeStruct((2, halves, ROWS, channels), F32),
        jax.ShapeDtypeStruct((2, 1, channels), F32),
    )
    pairs = length // (2 * BLOCK)
    read_s = lambda s, a: jnp.where(a[s] != 0, s, 0)
    read_d = lambda s, d, a: jnp.where(a[s] != 0, d, 0)
    got_one = pl.BlockSpec((None, length, channels), lambda s, d, a: (read_s(s, a), 0, 0))

    def got_pair(*tail):
        return pl.BlockSpec(
            (None, None) + tail, lambda s, d, a: (read_d(s, d, a), read_s(s, a)) + (0,) * len(tail)
        )

    def got_turn(*tail):
        return pl.BlockSpec(
            (None, None) + tail, lambda s, d, a: (read_s(s, a), read_d(s, d, a)) + (0,) * len(tail)
        )

    def got_state(kind):
        def place(s, d, a):
            way = read_d(s, d, a)
            return (way + kind * (1 - 2 * way), read_s(s, a), kind, 0, 0, 0)

        return pl.BlockSpec((None, None, None, halves, ROWS, channels), place)

    return pl.pallas_call(
        functools.partial(pass_two, states),
        grid_spec=pltpu.PrefetchScalarGridSpec(
            num_scalar_prefetch=1,
            grid=(slots, 2),
            in_specs=[
                got_pair(length, channels),
                got_turn(length, width),
                got_one,
                got_pair(length, channels),
                got_turn(length, halves, ROWS, LANES),
                got_turn(length, halves, ROWS, LANES),
                got_state(0),
                got_state(1),
                got_one,
                got_one,
            ]
            + [whole(c) for c in constants],
            out_specs=[one, one, pair(length, channels), turn(length, width)] + [whole(c) for c in sums],
            scratch_shapes=[pltpu.VMEM((length, channels), F32)]
            + [pltpu.VMEM((pairs, BLOCK, states, channels), BF16)] * 2
            + [pltpu.VMEM((2 * pairs, states, channels), BF16)]
            + [pltpu.VMEM((BLOCK, states, channels), BF16)] * 4
            + [pltpu.VMEM((length, channels), F32)] * 3
            + [pltpu.VMEM((length, wide), F32)] * 2
            + [pltpu.VMEM((length, wide), BF16)] * 2
            + [pltpu.VMEM((length, channels), BF16)] * 2
            + [pltpu.VMEM((length, channels), F32)],
        ),
        out_shape=[
            jax.ShapeDtypeStruct((slots, length, channels), BF16),
            jax.ShapeDtypeStruct((slots, length, channels), BF16),
            jax.ShapeDtypeStruct((2, slots, length, channels), F32),
            jax.ShapeDtypeStruct((slots, 2, length, width), F32),
        ]
        + list(sums),
        compiler_params=pltpu.CompilerParams(vmem_limit_bytes=44 * MIB),
        name="scan_all",
    )(active, conv, proj, grad_y, step, mix_b, mix_c, entering, entering, gate_z, grad_gated, *constants)


def chain(count, run, end, pull, total, decay, entering, held, send_sem, recv_sem):
    mine = lax.axis_index("fsdp")
    waves = end.shape[1] // run
    mesh_id = pl.DeviceIdType.MESH
    after, before = lax.rem(mine + 1, count), lax.rem(mine + count - 1, count)
    barrier = pltpu.get_barrier_semaphore()
    for other in (after, before):
        pl.semaphore_signal(barrier, inc=1, device_id={"fsdp": other}, device_id_type=mesh_id)
    pl.semaphore_wait(barrier, 2)
    ways = ((mine > 0, mine < count - 1, after), (mine < count - 1, mine > 0, before))

    def copy(way, s):
        slots = pl.ds(s * run, run)
        return pltpu.make_async_remote_copy(
            src_ref=held.at[way, slots],
            dst_ref=entering.at[way, slots],
            send_sem=send_sem.at[way, s],
            recv_sem=recv_sem.at[way, s],
            device_id={"fsdp": ways[way][2]},
            device_id_type=mesh_id,
        )

    lags = (mine, count - 1 - mine)

    def wave(turn, carry):
        for way in range(2):
            gets, sends, _ = ways[way]
            s = turn - lags[way]
            here = (s >= 0) & (s < waves)

            @pl.when(here & gets)
            def _():
                copy(way, s).wait_recv()

            @pl.when(here & jnp.logical_not(gets))
            def _():
                entering[way, pl.ds(s * run, run)] = jnp.zeros((run,) + entering.shape[2:], entering.dtype)

            @pl.when(here & sends)
            def _():
                for i in range(run):
                    slot = s * run + i
                    for kind, local in enumerate((end, pull)):
                        d = (way + kind) % 2
                        through = jnp.exp2(decay[d] * total[d, slot][None])
                        value = through * entering[way, slot, kind].astype(F32) + local[d, slot]
                        held[way, slot, kind] = value.astype(held.dtype)
                copy(way, s).start()

        return carry

    lax.fori_loop(0, waves + count - 1, wave, 0)

    def drain(s, carry):
        for way in range(2):

            @pl.when(ways[way][1])
            def _():
                copy(way, s).wait_send()

        return carry

    lax.fori_loop(0, waves, drain, 0)


def pass_states(end, pull, total, decay):
    _, slots, halves, rows, channels = end.shape
    run = RUN
    shape = (2, slots, 2, halves, rows, channels)
    return pl.pallas_call(
        functools.partial(chain, lax.axis_size("fsdp"), run),
        in_specs=[pl.BlockSpec(memory_space=pltpu.VMEM)] * 4,
        out_specs=pl.BlockSpec(memory_space=pltpu.VMEM),
        out_shape=jax.ShapeDtypeStruct(shape, BF16),
        scratch_shapes=[
            pltpu.VMEM(shape, BF16),
            pltpu.SemaphoreType.DMA((2, slots // run)),
            pltpu.SemaphoreType.DMA((2, slots // run)),
        ],
        compiler_params=pltpu.CompilerParams(
            collective_id=0, has_side_effects=True, vmem_limit_bytes=40 * MIB
        ),
        name="pass_states",
    )(end, pull, total, decay)


def partner(g, bit):
    return g + bit * (1 - 2 * lax.rem(g // bit, 2))


class Mail:
    def __init__(self, send_sem, recv_sem):
        self.send_sem, self.recv_sem, self.made = send_sem, recv_sem, []

    def post(self, src, dst, target, here=None, there=None, landing=None):
        n = len(self.made)
        copy = lambda into: pltpu.make_async_remote_copy(
            src_ref=src,
            dst_ref=into,
            send_sem=self.send_sem.at[n],
            recv_sem=self.recv_sem.at[n],
            device_id=target,
            device_id_type=pl.DeviceIdType.MESH,
        )
        when = lambda cond: (lambda body: body()) if cond is None else pl.when(cond)
        landing = dst if landing is None else landing
        entry = dict(got=False)

        @when(here)
        def _():
            copy(dst).start()

        def take():
            if not entry["got"]:
                entry["got"] = True

                @when(there)
                def _():
                    copy(landing).wait_recv()

        def sent():
            @when(here)
            def _():
                copy(dst).wait_send()

        self.made.append((take, sent))
        return take

    def finish(self):
        for take, _ in self.made:
            take()
        for _, sent in self.made:
            sent()


def collect(
    groups,
    parts,
    tokens,
    halo,
    in_own,
    xproj,
    small,
    facts,
    all_tokens,
    all_halo,
    in_matrix,
    all_xproj,
    all_small,
    all_facts,
    send_sem,
    recv_sem,
    own_sem,
):
    g, f = lax.axis_index("group"), lax.axis_index("fsdp")
    chips = parts // 2
    z, core = f // 2, lax.rem(f, 2)
    ways = groups.bit_length() - 1
    bits = [1 << i for i in range(ways)]
    barrier = pltpu.get_barrier_semaphore()
    for bit in bits:
        pl.semaphore_signal(
            barrier, inc=1, device_id={"group": partner(g, bit)}, device_id_type=pl.DeviceIdType.MESH
        )
    for k in range(1, parts):
        pl.semaphore_signal(
            barrier,
            inc=1,
            device_id={"fsdp": lax.rem(f + k, parts)},
            device_id_type=pl.DeviceIdType.MESH,
        )
    pl.semaphore_wait(barrier, ways + parts - 1)
    mail = Mail(send_sem, recv_sem)
    place = lambda part: lax.rem(part + 2 * parts, parts)
    sibling = {"fsdp": f + 1 - 2 * core}
    up, down = {"fsdp": f + 2}, {"fsdp": f - 2}

    fact_takes = []
    for k in range(1, parts):
        fact_takes.append(
            mail.post(
                facts,
                all_facts.at[0, f],
                {"fsdp": lax.rem(f + k, parts)},
                landing=all_facts.at[0, lax.rem(f + parts - k, parts)],
            )
        )

    def cuts(count):
        edges = [count * i // ways for i in range(ways + 1)]
        return [pl.ds(lo, hi - lo) for lo, hi in zip(edges[:-1], edges[1:])]

    def relative(own, every, count):
        pieces = cuts(count)
        held = [{0: None} for _ in range(ways)]
        steps = [[] for _ in range(ways)]
        for t in range(ways):
            for p in range(ways):
                bit = bits[(p + t) % ways]
                for r in list(held[p]):
                    held[p][r ^ bit] = None
                    steps[t].append((p, r, bit))
        takes = {}

        def run(chosen):
            for p, r, bit in chosen:
                if r:
                    takes[p, r]()
                src = own.at[pieces[p]] if r == 0 else every.at[r, pieces[p]]
                takes[p, r ^ bit] = mail.post(
                    src, every.at[r ^ bit, pieces[p]], {"group": partner(g, bit)}
                )

        run([move for step in steps for move in step if move[1] == 0])
        return [functools.partial(run, [move for move in step if move[1]]) for step in steps[1:]]

    token_steps = relative(tokens, all_tokens, tokens.shape[0])
    halo_steps = relative(halo, all_halo, halo.shape[0])

    line = []

    def hop(h):
        for sign, target, inside in ((1, up, z < chips - 1), (-1, down, z > 0)):
            shard = f - sign * 2 * (h - 1)
            src = in_own if h == 1 else in_matrix.at[place(shard)]
            far = z - sign * (h - 1)
            come = z - sign * h
            line.append(
                mail.post(
                    src,
                    in_matrix.at[place(shard)],
                    target,
                    here=inside & (far >= 0) & (far < chips),
                    there=(come >= 0) & (come < chips),
                    landing=in_matrix.at[place(f - sign * 2 * h)],
                )
            )

    def share(h):
        for sign in (1, -1):
            shard = place(f - sign * 2 * h)
            come = z - sign * h
            known = (come >= 0) & (come < chips)
            mail.post(
                in_own if h == 0 else in_matrix.at[shard],
                in_matrix.at[shard],
                sibling,
                here=known,
                there=known,
                landing=in_matrix.at[place(f + 1 - 2 * core - sign * 2 * h)],
            )
            if h == 0:
                break

    hop(1)
    share(0)

    own_fact = pltpu.make_async_copy(facts, all_facts.at[0, f], own_sem.at[0])
    own_fact.start()
    held_copies = [
        pltpu.make_async_copy(xproj, all_xproj.at[core], own_sem.at[1]),
        pltpu.make_async_copy(small, all_small.at[core], own_sem.at[2]),
    ]

    @pl.when(z == g)
    def _():
        for copy in held_copies:
            copy.start()

    own_fact.wait()
    for take in fact_takes:
        take()
    fact_steps = relative(all_facts.at[0], all_facts, parts)

    pairs = ((xproj, all_xproj), (small, all_small))
    for distance in range(1, chips):
        for sign, target in ((1, up), (-1, down)):
            source = g + sign * (distance - 1)
            here = (z == source) & (source + sign >= 0) & (source + sign < chips)
            there = z == source + sign
            for own, every in pairs:
                src = own if distance == 1 else every.at[core]
                take = mail.post(src, every.at[core], target, here=here, there=there)
                take()
        if distance == 1:
            for step in fact_steps:
                step()
    for own, every in pairs:
        for src, where in ((own, z == g), (every.at[core], z != g)):
            mail.post(
                src, every.at[core], sibling, here=where, there=where, landing=every.at[1 - core]
            )

    for h in range(1, chips):
        for take in line[-2:]:
            take()
        if h < chips - 1:
            hop(h + 1)
        share(h)
        if h == 1 or chips == 2:
            for step in halo_steps:
                step()
            for step in token_steps:
                step()
    @pl.when(z == g)
    def _():
        for copy in held_copies:
            copy.wait()

    mail.finish()


def collect_inputs(tokens, halo, in_own, xproj, small, facts):
    groups, parts = lax.axis_size("group"), lax.axis_size("fsdp")
    ins = (tokens, halo, in_own, xproj, small, facts)
    outs = [
        jax.ShapeDtypeStruct((groups,) + tokens.shape, tokens.dtype),
        jax.ShapeDtypeStruct((groups,) + halo.shape, halo.dtype),
        jax.ShapeDtypeStruct((parts,) + in_own.shape, in_own.dtype),
        jax.ShapeDtypeStruct((2,) + xproj.shape, xproj.dtype),
        jax.ShapeDtypeStruct((2,) + small.shape, small.dtype),
        jax.ShapeDtypeStruct((groups, parts) + facts.shape, facts.dtype),
    ]
    ways = groups.bit_length() - 1
    copies = 3 * ways * (groups - 1) + (parts - 1) + 4 * (parts // 2 - 1) + 1 + 4 * (parts // 2 - 1) + 4
    outs = pl.pallas_call(
        functools.partial(collect, groups, parts),
        in_specs=[pl.BlockSpec(memory_space=pl.ANY)] * len(ins),
        out_specs=[pl.BlockSpec(memory_space=pl.ANY)] * len(outs),
        out_shape=outs,
        scratch_shapes=[
            pltpu.SemaphoreType.DMA((copies,)),
            pltpu.SemaphoreType.DMA((copies,)),
            pltpu.SemaphoreType.DMA((3,)),
        ],
        compiler_params=pltpu.CompilerParams(collective_id=1, has_side_effects=True),
        name="collect_inputs",
    )(*ins)
    all_tokens, all_halo, in_matrix, all_xproj, all_small, all_facts = outs
    return (
        all_tokens.at[0].set(tokens),
        all_halo.at[0].set(halo),
        lax.dynamic_update_index_in_dim(in_matrix, in_own, lax.axis_index("fsdp"), 0),
        all_xproj,
        all_small,
        all_facts,
    )


def runs(count, ways):
    edges = [count * i // ways for i in range(ways + 1)]
    return [pl.ds(lo, hi - lo) for lo, hi in zip(edges[:-1], edges[1:])]


def greet(groups):
    g = lax.axis_index("group")
    bits = [1 << i for i in range(groups.bit_length() - 1)]
    barrier = pltpu.get_barrier_semaphore()
    for bit in bits:
        pl.semaphore_signal(
            barrier, inc=1, device_id={"group": partner(g, bit)}, device_id_type=pl.DeviceIdType.MESH
        )
    pl.semaphore_wait(barrier, len(bits))
    return g, bits


def total_blocks(groups, terms, out, sums, parcel, landed, gathered, send_sem, recv_sem):
    g, bits = greet(groups)
    ways = len(bits)
    pieces = runs(terms.shape[1], ways)
    mail = Mail(send_sem, recv_sem)
    sums[...] = terms[...]
    held = [set(range(groups)) for _ in range(ways)]
    for t in range(ways):
        coming = []
        for p in range(ways):
            bit = bits[(p + t) % ways]
            for r in sorted(r for r in held[p] if r & bit):
                parcel[r, pieces[p]] = sums[r, pieces[p]].astype(parcel.dtype)
                take = mail.post(
                    parcel.at[r, pieces[p]],
                    landed.at[t, r ^ bit, pieces[p]],
                    {"group": partner(g, bit)},
                )
                coming.append((take, p, r ^ bit))
                held[p].remove(r)
        for take, p, r in coming:
            take()
            sums[r, pieces[p]] = sums[r, pieces[p]] + landed[t, r, pieces[p]].astype(F32)
    gathered[0] = sums[0].astype(gathered.dtype)
    known = [{0: None} for _ in range(ways)]
    for t in range(ways):
        for p in range(ways):
            bit = bits[(p + t) % ways]
            for r, take in list(known[p].items()):
                if take is not None:
                    take()
                known[p][r ^ bit] = mail.post(
                    gathered.at[r, pieces[p]],
                    gathered.at[r ^ bit, pieces[p]],
                    {"group": partner(g, bit)},
                )
    mail.finish()
    out[...] = gathered[...].astype(out.dtype)


def sum_blocks(terms, sent, result, number):
    groups = lax.axis_size("group")
    ways = groups.bit_length() - 1
    shape = (groups, terms.shape[0] // groups, terms.shape[1] * terms.shape[2], terms.shape[3])
    copies = 2 * ways * (groups - 1)
    return pl.pallas_call(
        functools.partial(total_blocks, groups),
        in_specs=[pl.BlockSpec(memory_space=pltpu.VMEM)],
        out_specs=pl.BlockSpec(memory_space=pltpu.VMEM),
        out_shape=jax.ShapeDtypeStruct(shape, result),
        scratch_shapes=[
            pltpu.VMEM(shape, F32),
            pltpu.VMEM(shape, sent),
            pltpu.VMEM((ways,) + shape, sent),
            pltpu.VMEM(shape, BF16),
            pltpu.SemaphoreType.DMA((copies,)),
            pltpu.SemaphoreType.DMA((copies,)),
        ],
        compiler_params=pltpu.CompilerParams(
            collective_id=number, has_side_effects=True, vmem_limit_bytes=32 * MIB
        ),
        cost_estimate=pl.CostEstimate(flops=30000 * terms.size // 2, bytes_accessed=8 * terms.size, transcendentals=0),
        name="sum_blocks",
    )(terms.reshape(shape)).reshape(terms.shape)


def front(
    halo_rows,
    info,
    tokens,
    halo,
    modulation,
    in_matrix,
    taps,
    conv_shift,
    xproj,
    modulated,
    extended,
    gate_z,
    conv_out,
    projected,
):
    slot = pl.program_id(0)
    length, model_width = tokens.shape
    channels = gate_z.shape[1]
    count, base = info[slot], info[pl.num_programs(0)]
    outs = (modulated, extended, gate_z, conv_out, projected)

    @pl.when(count <= base)
    def _():
        for out in outs:
            out[...] = jnp.zeros_like(out)

    @pl.when(count > base)
    def _():
        values = jnp.concatenate([tokens[...].astype(F32), halo[...].astype(F32)], axis=0)
        row = lax.broadcasted_iota(jnp.int32, (length + ROWS, 1), 0)
        behind, ahead = row - length - halo_rows, row - halo_rows
        at = jnp.where(row < length, row, jnp.where(behind < 0, behind, ahead))
        at = at + base
        known = (row < length + 2 * halo_rows) & (at >= 0) & (at < count)
        mask = known.astype(F32)
        centered = values - jnp.mean(values, axis=1, keepdims=True)
        normed = centered * lax.rsqrt(
            jnp.mean(centered * centered, axis=1, keepdims=True) + EPSILON
        )
        shift = modulation[:, :model_width]
        scale = modulation[:, model_width : 2 * model_width]
        low = ((normed * (1.0 + scale) + shift) * mask).astype(BF16)
        modulated[...] = low[:length]
        inner = dot32(low, in_matrix[...], ((1,), (0,)))
        gate_z[...] = inner[:length, channels:]
        extended[...] = jnp.zeros_like(extended)
        extended[ROWS : ROWS + length, :] = inner[:length, :channels]
        extended[ROWS - halo_rows : ROWS, :] = inner[length : length + halo_rows, :channels]
        extended[ROWS + length : ROWS + length + halo_rows, :] = inner[
            length + halo_rows : length + 2 * halo_rows, :channels
        ]
        for d in range(2):
            pre = conv_rows(extended, taps, conv_shift, d, length)
            value = (pre * jax.nn.sigmoid(pre) * mask[:length]).astype(BF16)
            conv_out[d] = value
            projected[d] = dot32(value, xproj[d], ((1,), (0,)))


def tap_row(d, k, kernel):
    return ROWS - (kernel - 1) + k if d == 0 else ROWS + (kernel - 1) - k


def conv_rows(extended, taps, conv_shift, d, length):
    kernel = taps.shape[1]
    pre = conv_shift[d : d + 1, :]
    for k in range(kernel):
        row = tap_row(d, k, kernel)
        pre = pre + taps[d, k : k + 1, :] * extended[row : row + length, :]
    return pre


def project(info, tokens, halo, modulation, in_matrix, taps, conv_shift, xproj):
    slots, length, model_width = tokens.shape
    channels = taps.shape[2]
    width = xproj.shape[2]
    fixed = lambda array: pl.BlockSpec(array.shape, lambda s, i: (0,) * array.ndim)
    one = lambda *tail: pl.BlockSpec((None,) + tail, lambda s, i: (s,) + (0,) * len(tail))
    return pl.pallas_call(
        functools.partial(front, taps.shape[1] - 1),
        grid_spec=pltpu.PrefetchScalarGridSpec(
            num_scalar_prefetch=1,
            grid=(slots,),
            in_specs=[
                one(length, model_width),
                one(ROWS, model_width),
                one(1, modulation.shape[2]),
                fixed(in_matrix),
                fixed(taps),
                fixed(conv_shift),
                fixed(xproj),
            ],
            out_specs=[
                one(length, model_width),
                one(length + 2 * ROWS, channels),
                one(length, channels),
                pl.BlockSpec((2, None, length, channels), lambda s, i: (0, s, 0, 0)),
                one(2, length, width),
            ],
        ),
        out_shape=[
            jax.ShapeDtypeStruct((slots, length, model_width), BF16),
            jax.ShapeDtypeStruct((slots, length + 2 * ROWS, channels), F32),
            jax.ShapeDtypeStruct((slots, length, channels), F32),
            jax.ShapeDtypeStruct((2, slots, length, channels), BF16),
            jax.ShapeDtypeStruct((slots, 2, length, width), F32),
        ],
        compiler_params=pltpu.CompilerParams(vmem_limit_bytes=40 * MIB),
        cost_estimate=pl.CostEstimate(
            flops=18000 * slots * length * channels,
            bytes_accessed=20 * slots * length * channels,
            transcendentals=0,
        ),
        name="project",
    )(info, tokens, halo, modulation, in_matrix, taps, conv_shift, xproj)


def back(
    info,
    extended,
    conv_grad,
    proj_grad,
    conv_out,
    taps,
    conv_shift,
    xproj,
    grad_x,
    rim,
    sums,
    xproj_grad,
    rows,
):
    slot = pl.program_id(0)
    length, channels = grad_x.shape
    kernel = taps.shape[1]
    halo = kernel - 1
    count, base = info[slot], info[pl.num_programs(0)]

    @pl.when(slot == 0)
    def _():
        sums[...] = jnp.zeros_like(sums)
        xproj_grad[...] = jnp.zeros_like(xproj_grad)
        rows[...] = jnp.zeros_like(rows)

    @pl.when(count <= base)
    def _():
        grad_x[...] = jnp.zeros_like(grad_x)
        rim[...] = jnp.zeros_like(rim)

    @pl.when(count > base)
    def _():
        row = lax.broadcasted_iota(jnp.int32, (length, 1), 0)
        mask = (base + row < count).astype(F32)
        for d in range(2):
            pre = conv_rows(extended, taps, conv_shift, d, length)
            sigmoid = jax.nn.sigmoid(pre)
            slope = sigmoid * (1.0 + pre * (1.0 - sigmoid))
            into = conv_grad[d] + dot32(proj_grad[d], xproj[d], ((1,), (1,)))
            value = into * mask * slope
            rows[d, ROWS : ROWS + length, :] = value
            turned = jnp.transpose(proj_grad[d].astype(F32)).astype(BF16)
            xproj_grad[d] += dot32(turned, conv_out[d], ((1,), (0,)))
            for k in range(kernel):
                first = tap_row(d, k, kernel)
                at = d * kernel + k
                sums[at : at + 1, :] += jnp.sum(
                    value * extended[first : first + length, :], axis=0, keepdims=True
                )
            at = 2 * kernel + d
            sums[at : at + 1, :] += jnp.sum(value, axis=0, keepdims=True)
        total = jnp.zeros((length, channels), F32)
        for k in range(kernel):
            ahead, behind = ROWS + halo - k, ROWS - halo + k
            total = total + taps[0, k : k + 1, :] * rows[0, ahead : ahead + length, :]
            total = total + taps[1, k : k + 1, :] * rows[1, behind : behind + length, :]
        grad_x[...] = total
        rim[0] = rows[0, ROWS : 2 * ROWS, :]
        rim[1] = rows[1, length : length + ROWS, :]


def back_through(info, extended, conv_grad, proj_grad, conv_out, taps, conv_shift, xproj):
    slots = extended.shape[0]
    length, channels = conv_out.shape[2:]
    width = xproj.shape[2]
    kernel = taps.shape[1]
    sum_rows = 2 * ROWS * ((2 * kernel + 2 + 2 * ROWS - 1) // (2 * ROWS))
    fixed = lambda array: pl.BlockSpec(array.shape, lambda s, i: (0,) * len(array.shape))
    one = lambda *tail: pl.BlockSpec((None,) + tail, lambda s, i: (s,) + (0,) * len(tail))
    both = pl.BlockSpec((2, None, length, channels), lambda s, i: (0, s, 0, 0))
    sums = jax.ShapeDtypeStruct((sum_rows, channels), F32)
    xproj_grad = jax.ShapeDtypeStruct((2, width, channels), F32)
    return pl.pallas_call(
        back,
        grid_spec=pltpu.PrefetchScalarGridSpec(
            num_scalar_prefetch=1,
            grid=(slots,),
            in_specs=[
                one(length + 2 * ROWS, channels),
                both,
                one(2, length, width),
                both,
                fixed(taps),
                fixed(conv_shift),
                fixed(xproj),
            ],
            out_specs=[one(length, channels), one(2, ROWS, channels), fixed(sums), fixed(xproj_grad)],
            scratch_shapes=[pltpu.VMEM((2, length + 2 * ROWS, channels), F32)],
        ),
        out_shape=[
            jax.ShapeDtypeStruct((slots, length, channels), F32),
            jax.ShapeDtypeStruct((slots, 2, ROWS, channels), F32),
            sums,
            xproj_grad,
        ],
        compiler_params=pltpu.CompilerParams(vmem_limit_bytes=32 * MIB),
        cost_estimate=pl.CostEstimate(
            flops=24000 * slots * length * channels,
            bytes_accessed=30 * slots * length * channels,
            transcendentals=0,
        ),
        name="back_through",
    )(info, extended, conv_grad, proj_grad, conv_out, taps, conv_shift, xproj)


def scatter(groups, parts, terms, packed, out, moved, parcel, landed, send_sem, recv_sem):
    g, f = lax.axis_index("group"), lax.axis_index("fsdp")
    ratio = parts // groups
    target = {"group": lax.rem(f, groups), "fsdp": ratio * g + f // groups}
    source = {"group": f // ratio, "fsdp": groups * lax.rem(f, ratio) + g}
    stays = (target["group"] == g) & (target["fsdp"] == f)

    bits = [1 << i for i in range(groups.bit_length() - 1)]
    barrier = pltpu.get_barrier_semaphore()
    for bit in bits:
        pl.semaphore_signal(
            barrier, inc=1, device_id={"group": partner(g, bit)}, device_id_type=pl.DeviceIdType.MESH
        )

    @pl.when(jnp.logical_not(stays))
    def _():
        pl.semaphore_signal(barrier, inc=1, device_id=source, device_id_type=pl.DeviceIdType.MESH)
        pl.semaphore_wait(barrier, len(bits) + 1)

    @pl.when(stays)
    def _():
        pl.semaphore_wait(barrier, len(bits))

    ways = len(bits)
    pieces = runs(terms.shape[1], ways)
    mail = Mail(send_sem, recv_sem)
    moves = jnp.logical_not(stays)
    mail.post(packed, moved, target, here=moves, there=moves)

    @pl.when(stays)
    def _():
        moved[...] = packed[...]

    held = [set(range(groups)) for _ in range(ways)]
    came = [{r: [] for r in range(groups)} for _ in range(ways)]

    def summed(p, r):
        value = terms[r, pieces[p]].astype(F32)
        for t, take in came[p][r]:
            take()
            value = value + landed[t, r, pieces[p]].astype(F32)
        return value

    for t in range(ways):
        for p in range(ways):
            bit = bits[(p + t) % ways]
            for r in sorted(r for r in held[p] if r & bit):
                src = terms
                if t:
                    parcel[r, pieces[p]] = summed(p, r).astype(parcel.dtype)
                    src = parcel
                take = mail.post(
                    src.at[r, pieces[p]],
                    landed.at[t, r ^ bit, pieces[p]],
                    {"group": partner(g, bit)},
                )
                came[p][r ^ bit].append((t, take))
                held[p].remove(r)
    for p in range(ways):
        out[pieces[p]] = summed(p, 0)
    mail.finish()


def scatter_blocks(terms, packed, number):
    groups, parts = lax.axis_size("group"), lax.axis_size("fsdp")
    ways = groups.bit_length() - 1
    slots, length, model_width = terms.shape
    block = (slots // groups, length, model_width)
    copies = ways * (groups - 1) + 1
    return pl.pallas_call(
        functools.partial(scatter, groups, parts),
        in_specs=[pl.BlockSpec(memory_space=pltpu.VMEM)] * 2,
        out_specs=[pl.BlockSpec(memory_space=pltpu.VMEM)] * 2,
        out_shape=[
            jax.ShapeDtypeStruct(block, F32),
            jax.ShapeDtypeStruct(packed.shape, packed.dtype),
        ],
        scratch_shapes=[
            pltpu.VMEM((groups,) + block, terms.dtype),
            pltpu.VMEM((ways, groups) + block, terms.dtype),
            pltpu.SemaphoreType.DMA((copies,)),
            pltpu.SemaphoreType.DMA((copies,)),
        ],
        compiler_params=pltpu.CompilerParams(
            collective_id=number, has_side_effects=True, vmem_limit_bytes=48 * MIB
        ),
        cost_estimate=pl.CostEstimate(
            flops=20000 * terms.size, bytes_accessed=4 * terms.size, transcendentals=0
        ),
        name="scatter_blocks",
    )(terms.reshape((groups,) + block), packed)


def finish(
    groups,
    parts,
    terms,
    in_x,
    in_z,
    packed,
    modulation,
    in_grad,
    out_grad,
    rest,
    landed,
    every_x,
    every_z,
    every_p,
    send_sem,
    recv_sem,
):
    g, f = lax.axis_index("group"), lax.axis_index("fsdp")
    bits = [1 << i for i in range(groups.bit_length() - 1)]
    ways = len(bits)
    barrier = pltpu.get_barrier_semaphore()
    others = [{"group": partner(g, bit)} for bit in bits]
    others += [{"fsdp": lax.rem(f + k, parts)} for k in range(1, parts)]
    for other in others:
        pl.semaphore_signal(barrier, inc=1, device_id=other, device_id_type=pl.DeviceIdType.MESH)
    pl.semaphore_wait(barrier, len(others))
    mail = Mail(send_sem, recv_sem)
    takes = []
    for k in range(1, parts):
        there = lax.rem(f + k, parts)
        takes.append(mail.post(terms.at[there], landed.at[k - 1], {"fsdp": there}))

    def absolute(r):
        at = g
        for bit in bits:
            at = partner(at, bit) if r & bit else at
        return at

    shards = ((in_x, every_x), (in_z, every_z), (packed, every_p))
    known = {}
    forwards = [[] for _ in range(ways)]
    for own, every in shards:
        every[g] = own[...]
    for n, (own, every) in enumerate(shards):
        tiles = own.shape[1] // LANES
        for p in range(ways):
            lo, hi = (tiles * i // ways * LANES for i in (p, p + 1))
            held = [0]
            for t in range(ways):
                bit = bits[(p + t) % ways]
                for r in list(held):
                    move = (n, every, pl.ds(lo, hi - lo), p, r, bit)
                    forwards[t if r else 0].append(move)
                    held.append(r ^ bit)

    def run(moves):
        for n, every, cols, p, r, bit in moves:
            if r:
                known[n, p, r]()
            block = every.at[absolute(r), :, cols]
            known[n, p, r ^ bit] = mail.post(
                block,
                block,
                {"group": partner(g, bit)},
                landing=every.at[absolute(r ^ bit), :, cols],
            )

    run(forwards[0])
    total = terms[f]
    for k, take in enumerate(takes):
        take()
        total = total + landed[k]
    modulation[0] = total
    found = {0: None}
    for bit in bits:
        for r, take in list(found.items()):
            if take is not None:
                take()
            found[r ^ bit] = mail.post(
                modulation.at[r], modulation.at[r ^ bit], {"group": partner(g, bit)}
            )
    for moves in forwards[1:]:
        run(moves)
    mail.finish()
    channels = in_x.shape[1]
    piece, model_width = packed.shape[0], out_grad.shape[1]
    for j in range(groups):
        for h, every in enumerate((every_x, every_z)):
            at = (h * groups + j) * channels
            in_grad[:, at : at + channels] = every[j]
        out_grad[j * piece : (j + 1) * piece, :] = every_p[j, :, :model_width].astype(F32)
        rest[j * piece : (j + 1) * piece, :] = every_p[j, :, model_width:].astype(F32)


def finish_gradients(terms, in_x, in_z, packed, model_width, number):
    groups, parts = lax.axis_size("group"), lax.axis_size("fsdp")
    ways = groups.bit_length() - 1
    block = terms.shape[1:]
    copies = parts - 1 + groups - 1 + 3 * ways * (groups - 1)
    rows, channels = in_x.shape
    piece, wide = packed.shape
    return pl.pallas_call(
        functools.partial(finish, groups, parts),
        in_specs=[pl.BlockSpec(memory_space=pltpu.VMEM)] * 4,
        out_specs=[pl.BlockSpec(memory_space=pltpu.VMEM)] * 4,
        out_shape=[
            jax.ShapeDtypeStruct((groups,) + block, F32),
            jax.ShapeDtypeStruct((rows, 2 * groups * channels), BF16),
            jax.ShapeDtypeStruct((groups * piece, model_width), F32),
            jax.ShapeDtypeStruct((groups * piece, wide - model_width), F32),
        ],
        scratch_shapes=[
            pltpu.VMEM((parts - 1,) + block, F32),
            pltpu.VMEM((groups, rows, channels), BF16),
            pltpu.VMEM((groups, rows, channels), BF16),
            pltpu.VMEM((groups, piece, wide), BF16),
            pltpu.SemaphoreType.DMA((copies,)),
            pltpu.SemaphoreType.DMA((copies,)),
        ],
        compiler_params=pltpu.CompilerParams(
            collective_id=number, has_side_effects=True, vmem_limit_bytes=32 * MIB
        ),
        name="finish_gradients",
    )(terms, in_x, in_z, packed)


def to_owner(groups, parts):
    ratio = parts // groups
    pairs = []
    for g in range(groups):
        for f in range(parts):
            pairs.append((g * parts + f, (f // ratio) * parts + groups * (f % ratio) + g))
    return pairs


def cut(array, pieces):
    slots = array.shape[0]
    edges = [slots * i // pieces for i in range(pieces + 1)]
    return [array[lo:hi] for lo, hi in zip(edges[:-1], edges[1:])]


def flip(array, groups, bit):
    return lax.ppermute(array, "group", [(i, i ^ bit) for i in range(groups)])


def bits_of(groups, first):
    count = groups.bit_length() - 1
    return [1 << ((first + i) % count) for i in range(count)]


def scatter_stage(pieces, groups, t):
    nexts = []
    for p, held in enumerate(pieces):
        bit = bits_of(groups, p)[t]
        sums = {r: value for r, value in held.items() if not r & bit}
        for r in [r for r in held if r & bit]:
            came = flip(held[r], groups, bit).astype(F32)
            sums[r ^ bit] = (sums[r ^ bit].astype(F32) + came).astype(BF16)
        nexts.append(sums)
    return nexts


def on_device(
    tokens,
    item_bucket,
    slot_item,
    slot_live,
    slot_tokens,
    ada_weight,
    ada_bias,
    in_weight,
    conv_weight,
    conv_bias,
    xproj_weight,
    dt_weight,
    dt_bias,
    a_log,
    skip_gain,
    out_weight,
    cotangent,
):
    own_slots, length, model_width = tokens.shape
    groups, parts = lax.axis_size("group"), lax.axis_size("fsdp")
    g, f = lax.axis_index("group"), lax.axis_index("fsdp")
    slots = own_slots * groups
    inner_width = in_weight.shape[1] // 2
    channels = inner_width // groups
    kernel = conv_weight.shape[1]
    halo = kernel - 1
    rank_width = dt_weight.shape[1]
    width = xproj_weight.shape[2]
    states = (width - rank_width) // 2

    matches = slot_item[:, None] == jnp.arange(item_bucket.shape[0], dtype=jnp.int32)[None, :]
    own_buckets = jnp.sum(jnp.where(matches, item_bucket[None, :], 0), axis=1)
    own_condition = jax.nn.silu(time_embed(own_buckets, model_width)).astype(BF16)
    own_modulation = jnp.dot(own_condition, ada_weight, preferred_element_type=F32)
    own_modulation = own_modulation + ada_bias.astype(F32)
    plain = jnp.stack([slot_tokens * slot_live, own_buckets], axis=1).astype(F32)
    facts = jnp.concatenate([own_modulation, jnp.repeat(plain, LANES // 2, axis=1)], axis=1)

    edges = [(i, i + 1) for i in range(parts - 1)]
    before = lax.ppermute(tokens[:, length - halo :], "fsdp", edges)
    after = lax.ppermute(tokens[:, :halo], "fsdp", [(j, i) for i, j in edges])
    padding = jnp.zeros((own_slots, ROWS - 2 * halo, model_width), tokens.dtype)
    in_own = jnp.concatenate(
        [
            lax.dynamic_slice_in_dim(in_weight, h * inner_width + g * channels, channels, 1)
            for h in range(2)
        ],
        axis=1,
    )
    shard = out_weight.shape[0]
    small = jnp.concatenate(
        [
            dt_weight.reshape(2 * rank_width, shard),
            a_log.reshape(2 * states, shard),
            conv_weight.reshape(2 * kernel, shard),
            conv_bias,
            dt_bias,
            skip_gain,
        ],
        axis=0,
    )
    small_rows = small.shape[0]
    small_pad = -small_rows % LANES
    small = jnp.pad(small, ((0, -small_rows % BLOCK), (0, 0)))
    all_tokens, all_halo, in_matrix, all_xproj, all_small, all_facts = collect_inputs(
        tokens,
        jnp.concatenate([before, after, padding], axis=1),
        in_own,
        xproj_weight,
        small,
        facts,
    )
    ways = groups.bit_length() - 1
    all_tokens, late = lax.optimization_barrier((all_tokens, cotangent))
    travelling = [{0: part} for part in cut(late, ways)]
    for p, held in enumerate(travelling):
        for bit in bits_of(groups, p):
            held[bit] = flip(held[0], groups, bit)
    all_tokens = all_tokens.reshape(slots, length, model_width)
    all_halo = all_halo.reshape(slots, ROWS, model_width)
    in_matrix = in_matrix.reshape(model_width, 2 * channels)

    piece = shard // groups
    sent = lax.ppermute(
        lax.dynamic_slice_in_dim(out_weight, g * piece, piece, 0),
        ("group", "fsdp"),
        to_owner(groups, parts),
    )
    out_matrix = lax.all_gather(sent, "fsdp", axis=0, tiled=True)
    xproj = jnp.concatenate([all_xproj[0], all_xproj[1]], axis=1)
    rest = jnp.concatenate([all_small[0], all_small[1]], axis=1)
    edge = 0

    def take(rows):
        nonlocal edge
        edge += rows
        return rest[edge - rows : edge]

    dt_matrix = jnp.pad(
        take(2 * rank_width).reshape(2, rank_width, channels), ((0, 0), (0, width - rank_width), (0, 0))
    )
    rate = -jnp.exp(take(2 * states).astype(F32)).reshape(2, states // ROWS, ROWS, channels)
    taps = take(2 * kernel).reshape(2, kernel, channels).astype(F32)
    conv_shift = take(2).astype(F32)
    dt_shift = take(2).astype(F32).reshape(2, 1, channels)
    skip = take(2).astype(F32).reshape(2, 1, channels)
    decay = rate * LOG2E

    columns = facts.shape[1] - LANES
    plain = all_facts[:, 0, :, columns:].reshape(slots, LANES).astype(jnp.int32)
    counts, buckets = plain[:, 0], plain[:, LANES // 2]
    modulation = all_facts[:, :, :, :columns].transpose(0, 2, 1, 3).reshape(slots, parts * columns)
    group_counts = jnp.sum(counts.reshape(groups, own_slots), axis=1).astype(F32)
    share = jnp.repeat(group_counts / jnp.sum(group_counts), own_slots)
    positions = f * length + jnp.arange(length, dtype=jnp.int32)
    mask = (positions[None, :] < counts[:, None]).astype(F32)
    active = (counts > f * length).astype(jnp.int32)
    own_mask = mask[:own_slots, :, None]
    own_share = share[:own_slots, None, None]
    condition = jax.nn.silu(time_embed(buckets, model_width)).astype(BF16)
    shift_mod = modulation[:, None, :model_width]
    scale_mod = modulation[:, None, model_width : 2 * model_width]
    gate_mod = modulation[:, None, 2 * model_width :]

    info = jnp.concatenate([counts, (f * length)[None]]).astype(jnp.int32)
    modulated, wide_x, gate_z, conv_out, projected = project(
        info, all_tokens, all_halo, modulation[:, None, :], in_matrix, taps, conv_shift, xproj
    )
    travelling, projected = lax.optimization_barrier((travelling, projected))
    for p, held in enumerate(travelling):
        order = bits_of(groups, p)
        for t in range(1, ways):
            for r in [r for r in held if r and r < groups and all(r & bit == 0 for bit in order[t:])]:
                held[r ^ order[t]] = flip(held[r], groups, order[t])
    proj = sum_blocks(projected, BF16, F32, 2)
    proj, travelling = lax.optimization_barrier((proj, travelling))
    all_cotangent = jnp.concatenate([held[r] for r in range(groups) for held in travelling], axis=0)

    def normalise(values):
        inputs = values.astype(F32)
        centered = inputs - jnp.mean(inputs, axis=2, keepdims=True)
        inv_std = lax.rsqrt(jnp.mean(centered * centered, axis=2, keepdims=True) + EPSILON)
        return (inputs, centered * inv_std, inv_std)

    grad_in_all = all_cotangent.astype(F32) * (mask * share[:, None])[:, :, None]
    branch_gradient = (grad_in_all * gate_mod).astype(BF16)
    grad_gated = jnp.einsum("sld,cd->slc", branch_gradient, out_matrix, preferred_element_type=F32)
    grad_y = grad_gated * jax.nn.silu(gate_z)

    step, end, pull, total, mix_b, mix_c = scan_ends(active, conv_out, proj, grad_y, dt_matrix, dt_shift, decay)
    entering = pass_states(end, pull, total, decay)
    gated_output, grad_z, conv_grad, proj_part, dtw_grad, dtb_grad, decay_grad, skip_grad = scan_all(
        active,
        conv_out,
        proj,
        grad_y,
        step,
        mix_b,
        mix_c,
        entering,
        gate_z,
        grad_gated,
        dt_matrix,
        decay,
        skip,
    )
    proj_grad = sum_blocks(proj_part, BF16, BF16, 3)
    alog_grad = (decay_grad * rate).reshape(2 * states, channels)

    branch_part = jnp.einsum("slc,cd->sld", gated_output, out_matrix, preferred_element_type=F32)
    inward_z = jnp.einsum("sld,slc->dc", modulated, grad_z, preferred_element_type=F32)
    branch_part, inward_z, proj_grad = lax.optimization_barrier(
        (branch_part.astype(BF16), inward_z.astype(BF16), proj_grad)
    )
    inward_z = lax.psum_scatter(inward_z, "fsdp", scatter_dimension=0, tiled=True)
    ways = groups.bit_length() - 1
    cut_blocks = [cut(block, ways) for block in jnp.split(branch_part, groups, axis=0)]
    moving = [{r: cut_blocks[r][p] for r in range(groups)} for p in range(ways)]
    moving = scatter_stage(moving, groups, 0)
    outward = jnp.einsum("slc,sld->cd", gated_output, branch_gradient, preferred_element_type=F32)

    grad_x, rim, conv_sums, xproj_grads = back_through(
        info, wide_x, conv_grad, proj_grad, conv_out, taps, conv_shift, xproj
    )
    outward, moving, rim, inward_z = lax.optimization_barrier(
        (outward.astype(BF16), moving, rim, inward_z)
    )
    ahead = lax.ppermute(rim[:, 0, :halo], "fsdp", [(j, i) for i, j in edges])
    behind = lax.ppermute(rim[:, 1, ROWS - halo :], "fsdp", edges)
    zeros = jnp.zeros_like(ahead)
    ahead, behind = jnp.concatenate([zeros, ahead], 1), jnp.concatenate([behind, zeros], 1)
    last = sum(taps[0, k] * ahead[:, halo - k : 2 * halo - k] for k in range(kernel))
    first = sum(taps[1, k] * behind[:, k : k + halo] for k in range(kernel))
    grad_x = grad_x + jnp.concatenate(
        [first, jnp.zeros((slots, length - 2 * halo, channels), F32), last], axis=1
    )
    grad_x = grad_x.astype(BF16)
    inner_gradient = jnp.concatenate([grad_x, grad_z], axis=2)
    inward = jnp.einsum("sld,slc->dc", modulated, grad_x, preferred_element_type=F32)
    grad_mod_part = jnp.einsum(
        "slc,dc->sld", inner_gradient, in_matrix, preferred_element_type=F32
    ).astype(BF16)
    for t in range(1, ways):
        moving = scatter_stage(moving, groups, t)
    branch = jnp.concatenate([held[0] for held in moving], axis=0)
    small_grads = jnp.concatenate(
        [
            xproj_grads.reshape(2 * width, channels),
            dtw_grad[:, :rank_width].reshape(2 * rank_width, channels),
            alog_grad,
            conv_sums[: 2 * kernel + 2],
            dtb_grad.reshape(2, channels),
            skip_grad.reshape(2, channels),
            jnp.zeros((small_pad, channels), F32),
        ],
        axis=0,
    ).astype(BF16)
    packed_grads = jnp.concatenate([outward, small_grads.T], axis=1)
    packed_piece = lax.psum_scatter(packed_grads, "fsdp", scatter_dimension=0, tiled=True)
    inward, grad_mod_part, branch, packed_piece = lax.optimization_barrier(
        (inward.astype(BF16), grad_mod_part, branch, packed_piece)
    )
    branch = branch.astype(F32)
    grad_mod, packed_piece = scatter_blocks(grad_mod_part, packed_piece, 4)
    grad_mod = grad_mod * own_mask

    own_gate = gate_mod[:own_slots]
    own_scale = scale_mod[:own_slots]
    own_inputs, own_normed, own_inv = normalise(tokens)
    layer_out = ((own_inputs + own_gate * branch) * own_mask).astype(BF16)
    grad_in = cotangent.astype(F32) * own_mask * own_share
    grad_gate = jnp.sum(grad_in * branch, axis=1)

    grad_shift = jnp.sum(grad_mod, axis=1)
    grad_scale = jnp.sum(grad_mod * own_normed, axis=1)
    grad_normed = grad_mod * (1.0 + own_scale)
    grad_ln = own_inv * (
        grad_normed
        - jnp.mean(grad_normed, axis=2, keepdims=True)
        - own_normed * jnp.mean(grad_normed * own_normed, axis=2, keepdims=True)
    )
    tokens_grad = grad_in + grad_ln

    mod_part = jnp.concatenate([grad_shift, grad_scale, grad_gate], axis=1)
    inward_x = lax.psum_scatter(inward, "fsdp", scatter_dimension=0, tiled=True)
    mod_terms = mod_part.reshape(own_slots, parts, -1).transpose(1, 0, 2)
    mod_all, in_grad, out_grad, packed_own = finish_gradients(
        mod_terms, inward_x, inward_z, packed_piece, model_width, 5
    )
    in_grad = in_grad.astype(F32)
    mod_all = mod_all.reshape(slots, -1)
    ada_grad = jnp.einsum("sd,sk->dk", condition, mod_all.astype(BF16), preferred_element_type=F32)
    adab_grad = jnp.sum(mod_all, axis=0)
    xproj_grad = jnp.stack(
        [packed_own[:, d * width : (d + 1) * width] for d in range(2)]
    )
    rest_grads = packed_own[:, 2 * width :].T
    sizes = [2 * rank_width, 2 * states, 2 * kernel, 2, 2, 2]
    cuts = [sum(sizes[:i]) for i in range(len(sizes) + 1)]
    dtw_out, alog_out, conv_w_out, conv_b_out, dtb_out, skip_out = [
        rest_grads[cuts[i] : cuts[i + 1]] for i in range(len(sizes))
    ]
    return (
        layer_out,
        tokens_grad,
        ada_grad,
        adab_grad,
        in_grad,
        conv_w_out.reshape(2, kernel, shard),
        conv_b_out,
        xproj_grad,
        dtw_out.reshape(2, rank_width, shard),
        dtb_out,
        alog_out.reshape(2, states, shard),
        skip_out,
        out_grad,
    )


def solution(mesh):
    in_specs = (
        P("group", "fsdp", None),
        P(),
        P("group"),
        P("group"),
        P("group"),
        P(None, "fsdp"),
        P("fsdp"),
        P("fsdp", None),
        P(None, None, "fsdp"),
        P(None, "fsdp"),
        P(None, "fsdp", None),
        P(None, None, "fsdp"),
        P(None, "fsdp"),
        P(None, None, "fsdp"),
        P(None, "fsdp"),
        P("fsdp", None),
        P("group", "fsdp", None),
    )
    out_specs = (
        P("group", "fsdp", None),
        P("group", "fsdp", None),
        P(None, "fsdp"),
        P("fsdp"),
        P("fsdp", None),
        P(None, None, "fsdp"),
        P(None, "fsdp"),
        P(None, "fsdp", None),
        P(None, None, "fsdp"),
        P(None, "fsdp"),
        P(None, None, "fsdp"),
        P(None, "fsdp"),
        P("fsdp", None),
    )
    return jax.shard_map(
        on_device, mesh=mesh, in_specs=in_specs, out_specs=out_specs, check_vma=False
    )
```

```python
import functools
import math

import jax
import jax.numpy as jnp
from jax import lax
from jax.experimental import pallas as pl
from jax.experimental.pallas import tpu as pltpu
from jax.sharding import PartitionSpec as P

EPSILON = 1e-06
LANES = 128
ROWS = 8
BLOCK = 16
WIDE = 256
LAG = 3
RUN = 2
LOG2E = math.log2(math.e)
LN2 = math.log(2.0)
F32 = jnp.float32
BF16 = jnp.bfloat16
MIB = 1 << 20


def time_embed(buckets, model_width):
    half_width = model_width // 2
    frequency = jnp.exp(-math.log(10000.0) * jnp.arange(half_width, dtype=F32) / half_width)
    angles = buckets.astype(F32)[:, None] * frequency[None, :]
    return jnp.concatenate([jnp.cos(angles), jnp.sin(angles)], axis=1)


def silu_slope(values):
    sigmoid = jax.nn.sigmoid(values)
    return sigmoid * (1.0 + values * (1.0 - sigmoid))


def dot32(left, right, dims):
    return lax.dot_general(left, right, (dims, ((), ())), preferred_element_type=F32)


def pass_one(
    states, active, conv, proj, grad_y, dt_w, dt_b, decay, step, end, pull, total, mix_b, mix_c, drive, turned
):
    slot, direction = pl.program_id(0), pl.program_id(1)
    length, channels = drive.shape
    chunks = channels // LANES
    halves = states // ROWS
    rank = proj.shape[1] - 2 * states

    @pl.when(active[slot] == 0)
    def _():
        end[...] = jnp.zeros_like(end)
        pull[...] = jnp.zeros_like(pull)
        total[...] = jnp.zeros_like(total)

    @pl.when(active[slot] != 0)
    def _():
        pre = dot32(proj[...].astype(BF16), dt_w[direction], ((1,), (0,))) + dt_b[direction]
        steps = jnp.maximum(pre, 0.0) + jnp.log(1.0 + jnp.exp(-jnp.abs(pre)))
        step[...] = steps
        drive[...] = steps * conv[...].astype(F32)
        total[...] = jnp.broadcast_to(jnp.sum(steps, axis=0, keepdims=True), total.shape)

        def turn(i, carry):
            at = pl.multiple_of(i * ROWS, ROWS)
            turned[i] = jnp.transpose(proj[pl.ds(at, ROWS), :])[rank : rank + 2 * states]
            return carry

        lax.fori_loop(0, length // ROWS, turn, 0, unroll=True)
        zero = jnp.zeros((halves, ROWS, LANES), F32)
        for backward in range(2):

            @pl.when(direction == backward)
            def _():
                carry = ((zero,) * chunks, (zero + 1.0,) * chunks, (zero,) * chunks)
                rates = [decay[direction, :, :, k : k + LANES] for k in range(0, channels, LANES)]

                def block(i, carry):
                    at = length // ROWS - 1 - i if backward else i
                    rows = pl.ds(pl.multiple_of(at * ROWS, ROWS), ROWS)
                    held = [ref[rows, :] for ref in (step, drive, grad_y)]
                    hidden, running, pulled = carry
                    columns = turned[at]
                    for j in list(range(ROWS))[:: -1 if backward else 1]:
                        t = at * ROWS + j
                        wide = jnp.broadcast_to(columns[:, j : j + 1], (2 * states, LANES))
                        b = wide[:states].reshape(halves, ROWS, LANES)
                        c = wide[states:].reshape(halves, ROWS, LANES)
                        mix_b[t] = b
                        mix_c[t] = c
                        rowed = [
                            [
                                jnp.broadcast_to(h[j : j + 1, k : k + LANES], (ROWS, LANES))[None]
                                for k in range(0, channels, LANES)
                            ]
                            for h in held
                        ]
                        new = ([], [], [])
                        for k in range(chunks):
                            factor = jnp.exp2(rowed[0][k] * rates[k])
                            new[0].append(factor * hidden[k] + rowed[1][k] * b)
                            run = running[k] * factor
                            new[1].append(run)
                            new[2].append(pulled[k] + run * (rowed[2][k] * c))
                        hidden, running, pulled = new
                    return (tuple(hidden), tuple(running), tuple(pulled))

                hidden, _, pulled = lax.fori_loop(0, length // ROWS, block, carry)
                for k in range(chunks):
                    lanes = slice(k * LANES, (k + 1) * LANES)
                    end[:, :, lanes] = hidden[k]
                    pull[:, :, lanes] = pulled[k]


def pass_two(
    states,
    active,
    conv,
    proj,
    grad_y,
    step,
    mix_b,
    mix_c,
    entry,
    arrive,
    gate_z,
    grad_gated,
    dt_w,
    decay,
    skip,
    tile_b,
    tile_c,
    sel,
    take_b,
    take_c,
    gated,
    grad_z,
    conv_grad,
    proj_grad,
    dtw_grad,
    dtb_grad,
    alog_grad,
    skip_grad,
    drive,
    hid_even,
    hid_odd,
    edge,
    gst_even,
    gst_odd,
    thd_even,
    thd_odd,
    mixed,
    sdec,
    scan_y,
    in_part,
    out_part,
    rows_b,
    rows_c,
    drive_low,
    grad_low,
    y,
):
    slot, direction = pl.program_id(0), pl.program_id(1)
    length, channels = drive.shape
    chunks = channels // LANES
    halves = states // ROWS
    wide = BLOCK * states
    pairs = length // (2 * BLOCK)
    hid, gst, thd = (hid_even, hid_odd), (gst_even, gst_odd), (thd_even, thd_odd)
    lanes = [slice(k * LANES, (k + 1) * LANES) for k in range(chunks)]

    @pl.when((slot == 0) & (direction == 0))
    def _():
        dtw_grad[...] = jnp.zeros_like(dtw_grad)
        dtb_grad[...] = jnp.zeros_like(dtb_grad)
        alog_grad[...] = jnp.zeros_like(alog_grad)
        skip_grad[...] = jnp.zeros_like(skip_grad)

    @pl.when(direction == 0)
    def _():
        y[...] = jnp.zeros_like(y)

    @pl.when(active[slot] == 0)
    def _():
        conv_grad[...] = jnp.zeros_like(conv_grad)
        proj_grad[...] = jnp.zeros_like(proj_grad)
        gated[...] = jnp.zeros_like(gated)
        grad_z[...] = jnp.zeros_like(grad_z)

    def low(value):
        return value.reshape(states, LANES).astype(BF16)

    def block_range(pair, odd):
        return pl.ds(pl.multiple_of((2 * pair + odd) * BLOCK, BLOCK), BLOCK)

    def sweep_blocks(backward, tokens, matmuls, start):
        first, second = (1, 0) if backward else (0, 1)

        def two(i, carry):
            pair = pairs - 1 - i if backward else i
            before = lax.rem(pair + (1 if backward else pairs - 1), pairs)
            carry = tokens(pair, first, backward, matmuls(before, second), carry)
            return tokens(pair, second, backward, matmuls(pair, first), carry)

        carry = lax.fori_loop(0, pairs, two, start)
        for issue, keep in matmuls(0 if backward else pairs - 1, second):
            keep(issue())
        return carry

    def pieces(out, rows, left, right, dims, width):
        made = []
        for n in range(0, width, WIDE):
            cols = slice(n, min(n + WIDE, width))
            picked = right[:, cols] if dims[1] == (0,) else right

            def issue(left=left, picked=picked):
                return dot32(left, picked, dims)

            def keep(product, cols=cols):
                out[rows, cols] = product

            made.append((issue, keep))
        return made

    def scan_rows(pair, odd, backward, refs, body, beside, carry):
        order = list(range(BLOCK))[:: -1 if backward else 1]
        waiting = []
        for at_step, j in enumerate(order):
            if j % ROWS == (ROWS - 1 if backward else 0):
                at = pl.multiple_of((2 * pair + odd) * BLOCK + j // ROWS * ROWS, ROWS)
                held = [ref[pl.ds(at, ROWS), :] for ref in refs]
            i = j % ROWS
            rows = [
                [jnp.broadcast_to(h[i : i + 1, c], (ROWS, LANES))[None] for c in lanes] for h in held
            ]
            for issue, keep in beside[at_step * len(beside) // BLOCK : (at_step + 1) * len(beside) // BLOCK]:
                waiting.append((at_step + LAG, keep, issue()))
            carry = body(j, rows, carry)
            while waiting and waiting[0][0] <= at_step:
                _, keep, product = waiting.pop(0)
                keep(product)
        for _, keep, product in waiting:
            keep(product)
        return carry

    def forward_tokens(pair, odd, backward, beside, hidden):
        for k in range(chunks):
            edge[2 * pair + odd, :, lanes[k]] = low(hidden[k])

        def token(j, rows, hidden):
            b = mix_b[(2 * pair + odd) * BLOCK + j]
            new = []
            for k in range(chunks):
                factor = jnp.exp2(rows[0][k] * decay[direction, :, :, lanes[k]])
                value = factor * hidden[k] + rows[1][k] * b
                hid[odd][pair, j, :, lanes[k]] = low(value)
                new.append(value)
            return tuple(new)

        return scan_rows(pair, odd, backward, (step, drive), token, beside, hidden)

    def forward_matmuls(pair, odd):
        rows = block_range(pair, odd)
        h_rows = hid[odd][pair].reshape(wide, channels)
        return pieces(scan_y, rows, rows_c[rows, :], h_rows, ((1,), (0,)), channels) + pieces(
            out_part, rows, grad_low[rows, :], h_rows, ((1,), (1,)), wide
        )

    def backward_tokens(pair, odd, backward, beside, carry):
        earlier = -1 if backward else 1

        def token(j, rows, carry):
            carried, total = carry
            c = mix_c[(2 * pair + odd) * BLOCK + j]
            news, sums = [], []
            p = j + earlier
            for k in range(chunks):
                rate = decay[direction, :, :, lanes[k]]
                factor = jnp.exp2(rows[0][k] * rate)
                grad_state = rows[1][k] * c + carried[k]
                gst[odd][j, :, lanes[k]] = low(grad_state)
                onward = factor * grad_state
                if 0 <= p < BLOCK:
                    before = hid[odd][pair, p, :, lanes[k]]
                else:
                    before = edge[2 * pair + odd, :, lanes[k]]
                through = onward * before.astype(F32).reshape(halves, ROWS, LANES)
                sums.append(total[k] + through * rows[0][k])
                thd[odd][j, :, lanes[k]] = low(through * rate)
                news.append(onward)
            return (tuple(news), tuple(sums))

        return scan_rows(pair, odd, backward, (step, grad_y), token, beside, carry)

    def backward_matmuls(pair, odd):
        rows = block_range(pair, odd)
        g_rows = gst[odd][...].reshape(wide, channels)
        t_rows = thd[odd][...].reshape(wide, channels)
        return (
            pieces(mixed, rows, rows_b[rows, :], g_rows, ((1,), (0,)), channels)
            + pieces(sdec, rows, sel[...].astype(BF16), t_rows, ((1,), (0,)), channels)
            + pieces(in_part, rows, drive_low[rows, :], g_rows, ((1,), (1,)), wide)
        )

    @pl.when(active[slot] != 0)
    def _():
        drive[...] = step[...] * conv[...].astype(F32)
        drive_low[...] = drive[...].astype(BF16)
        grad_low[...] = grad_y[...].astype(BF16)
        proj_low = proj[...].astype(BF16)
        picked = jnp.concatenate([sel[...]] * (length // BLOCK), axis=0)
        rows_b[...] = (dot32(proj_low, tile_b[...], ((1,), (0,))) * picked).astype(BF16)
        rows_c[...] = (dot32(proj_low, tile_c[...], ((1,), (0,))) * picked).astype(BF16)
        zero = jnp.zeros((halves, ROWS, LANES), F32)
        for reverse in (False, True):

            @pl.when(direction == int(reverse))
            def _():
                start = tuple(entry[:, :, c].astype(F32) for c in lanes)
                sweep_blocks(reverse, forward_tokens, forward_matmuls, start)
                start = (tuple(arrive[:, :, c].astype(F32) for c in lanes), (zero,) * chunks)
                _, sums = sweep_blocks(not reverse, backward_tokens, backward_matmuls, start)
                for k in range(chunks):
                    alog_grad[direction, :, :, lanes[k]] += sums[k]

        conv_values = conv[...].astype(F32)
        steps = step[...]
        grads = grad_y[...]
        step_grad = conv_values * mixed[...] + LN2 * sdec[...]
        pre_grad = step_grad * (1.0 - jnp.exp(-steps))
        dtb_grad[direction] += jnp.sum(pre_grad, axis=0, keepdims=True)
        pre_low = pre_grad.astype(BF16)
        proj_grad[...] = (
            dot32((in_part[...] * picked).astype(BF16), take_b[...], ((1,), (0,)))
            + dot32((out_part[...] * picked).astype(BF16), take_c[...], ((1,), (0,)))
            + dot32(pre_low, dt_w[direction], ((1,), (1,)))
        )
        dtw_grad[direction] += dot32(jnp.transpose(proj[...]).astype(BF16), pre_low, ((1,), (0,)))
        y[...] += scan_y[...] + skip[direction] * conv_values
        skip_grad[direction] += jnp.sum(grads * conv_values, axis=0, keepdims=True)
        conv_grad[...] = grads * skip[direction] + steps * mixed[...]

        @pl.when(direction == 1)
        def _():
            total = y[...]
            value = gate_z[...]
            sigmoid = jax.nn.sigmoid(value)
            gated[...] = (total * (value * sigmoid)).astype(BF16)
            slope = sigmoid * (1.0 + value * (1.0 - sigmoid))
            grad_z[...] = (grad_gated[...] * total * slope).astype(BF16)


def whole(array):
    zeros = (0,) * array.ndim
    return pl.BlockSpec(array.shape, lambda s, d, a: zeros)


def scan_ends(active, conv, proj, grad_y, dt_w, dt_b, decay):
    slots, length, channels = grad_y.shape
    halves = decay.shape[1]
    width = proj.shape[3]
    states = halves * ROWS
    turn = lambda *tail: pl.BlockSpec((None, None) + tail, lambda s, d, a: (s, d) + (0,) * len(tail))
    pair = lambda *tail: pl.BlockSpec((None, None) + tail, lambda s, d, a: (d, s) + (0,) * len(tail))
    state = (2, slots, halves, ROWS, channels)
    mixes = (length, halves, ROWS, LANES)
    spare = lambda s, a: jnp.where(a[s] != 0, s, slots)
    kept_pair = pl.BlockSpec(
        (None, None, length, channels), lambda s, d, a: (jnp.where(a[s] != 0, d, 0), spare(s, a), 0, 0)
    )
    kept_mix = pl.BlockSpec(
        (None, None) + mixes, lambda s, d, a: (spare(s, a), jnp.where(a[s] != 0, d, 0), 0, 0, 0, 0)
    )
    return pl.pallas_call(
        functools.partial(pass_one, states),
        grid_spec=pltpu.PrefetchScalarGridSpec(
            num_scalar_prefetch=1,
            grid=(slots, 2),
            in_specs=[
                pair(length, channels),
                turn(length, width),
                pl.BlockSpec((None, length, channels), lambda s, d, a: (s, 0, 0)),
                whole(dt_w),
                whole(dt_b),
                whole(decay),
            ],
            out_specs=[
                kept_pair,
                pair(halves, ROWS, channels),
                pair(halves, ROWS, channels),
                pair(ROWS, channels),
                kept_mix,
                kept_mix,
            ],
            scratch_shapes=[
                pltpu.VMEM((length, channels), F32),
                pltpu.VMEM((length // ROWS, 2 * states, ROWS), F32),
            ],
        ),
        out_shape=[
            jax.ShapeDtypeStruct((2, slots + 1, length, channels), F32),
            jax.ShapeDtypeStruct(state, F32),
            jax.ShapeDtypeStruct(state, F32),
            jax.ShapeDtypeStruct((2, slots, ROWS, channels), F32),
            jax.ShapeDtypeStruct((slots + 1, 2) + mixes, F32),
            jax.ShapeDtypeStruct((slots + 1, 2) + mixes, F32),
        ],
        compiler_params=pltpu.CompilerParams(vmem_limit_bytes=24 * MIB),
        name="scan_ends",
    )(active, conv, proj, grad_y, dt_w, dt_b, decay)


def scan_all(
    active, conv, proj, grad_y, step, mix_b, mix_c, entering, gate_z, grad_gated, dt_w, decay, skip
):
    slots, length, channels = grad_y.shape
    halves = decay.shape[1]
    width = proj.shape[3]
    states = halves * ROWS
    wide = BLOCK * states
    rank = width - 2 * states
    column = jnp.arange(width)[:, None]
    lane = jnp.arange(wide)[None, :]
    tile_b = (column == rank + lane % states).astype(BF16)
    tile_c = (column == rank + states + lane % states).astype(BF16)
    sel = (jnp.arange(BLOCK)[:, None] == lane // states).astype(F32)
    turn = lambda *tail: pl.BlockSpec((None, None) + tail, lambda s, d, a: (s, d) + (0,) * len(tail))
    pair = lambda *tail: pl.BlockSpec((None, None) + tail, lambda s, d, a: (d, s) + (0,) * len(tail))
    one = pl.BlockSpec((None, length, channels), lambda s, d, a: (s, 0, 0))
    constants = (dt_w, decay, skip, tile_b, tile_c, sel, tile_b.T, tile_c.T)
    sums = (
        jax.ShapeDtypeStruct((2, width, channels), F32),
        jax.ShapeDtypeStruct((2, 1, channels), F32),
        jax.ShapeDtypeStruct((2, halves, ROWS, channels), F32),
        jax.ShapeDtypeStruct((2, 1, channels), F32),
    )
    pairs = length // (2 * BLOCK)
    read_s = lambda s, a: jnp.where(a[s] != 0, s, 0)
    read_d = lambda s, d, a: jnp.where(a[s] != 0, d, 0)
    got_one = pl.BlockSpec((None, length, channels), lambda s, d, a: (read_s(s, a), 0, 0))

    def got_pair(*tail):
        return pl.BlockSpec(
            (None, None) + tail, lambda s, d, a: (read_d(s, d, a), read_s(s, a)) + (0,) * len(tail)
        )

    def got_turn(*tail):
        return pl.BlockSpec(
            (None, None) + tail, lambda s, d, a: (read_s(s, a), read_d(s, d, a)) + (0,) * len(tail)
        )

    def got_state(kind):
        def place(s, d, a):
            way = read_d(s, d, a)
            return (way + kind * (1 - 2 * way), read_s(s, a), kind, 0, 0, 0)

        return pl.BlockSpec((None, None, None, halves, ROWS, channels), place)

    return pl.pallas_call(
        functools.partial(pass_two, states),
        grid_spec=pltpu.PrefetchScalarGridSpec(
            num_scalar_prefetch=1,
            grid=(slots, 2),
            in_specs=[
                got_pair(length, channels),
                got_turn(length, width),
                got_one,
                got_pair(length, channels),
                got_turn(length, halves, ROWS, LANES),
                got_turn(length, halves, ROWS, LANES),
                got_state(0),
                got_state(1),
                got_one,
                got_one,
            ]
            + [whole(c) for c in constants],
            out_specs=[one, one, pair(length, channels), turn(length, width)] + [whole(c) for c in sums],
            scratch_shapes=[pltpu.VMEM((length, channels), F32)]
            + [pltpu.VMEM((pairs, BLOCK, states, channels), BF16)] * 2
            + [pltpu.VMEM((2 * pairs, states, channels), BF16)]
            + [pltpu.VMEM((BLOCK, states, channels), BF16)] * 4
            + [pltpu.VMEM((length, channels), F32)] * 3
            + [pltpu.VMEM((length, wide), F32)] * 2
            + [pltpu.VMEM((length, wide), BF16)] * 2
            + [pltpu.VMEM((length, channels), BF16)] * 2
            + [pltpu.VMEM((length, channels), F32)],
        ),
        out_shape=[
            jax.ShapeDtypeStruct((slots, length, channels), BF16),
            jax.ShapeDtypeStruct((slots, length, channels), BF16),
            jax.ShapeDtypeStruct((2, slots, length, channels), F32),
            jax.ShapeDtypeStruct((slots, 2, length, width), F32),
        ]
        + list(sums),
        compiler_params=pltpu.CompilerParams(vmem_limit_bytes=44 * MIB),
        name="scan_all",
    )(active, conv, proj, grad_y, step, mix_b, mix_c, entering, entering, gate_z, grad_gated, *constants)


def chain(count, run, end, pull, total, decay, entering, held, send_sem, recv_sem):
    mine = lax.axis_index("fsdp")
    waves = end.shape[1] // run
    mesh_id = pl.DeviceIdType.MESH
    after, before = lax.rem(mine + 1, count), lax.rem(mine + count - 1, count)
    barrier = pltpu.get_barrier_semaphore()
    for other in (after, before):
        pl.semaphore_signal(barrier, inc=1, device_id={"fsdp": other}, device_id_type=mesh_id)
    pl.semaphore_wait(barrier, 2)
    ways = ((mine > 0, mine < count - 1, after), (mine < count - 1, mine > 0, before))

    def copy(way, s):
        slots = pl.ds(s * run, run)
        return pltpu.make_async_remote_copy(
            src_ref=held.at[way, slots],
            dst_ref=entering.at[way, slots],
            send_sem=send_sem.at[way, s],
            recv_sem=recv_sem.at[way, s],
            device_id={"fsdp": ways[way][2]},
            device_id_type=mesh_id,
        )

    lags = (mine, count - 1 - mine)

    def wave(turn, carry):
        for way in range(2):
            gets, sends, _ = ways[way]
            s = turn - lags[way]
            here = (s >= 0) & (s < waves)

            @pl.when(here & gets)
            def _():
                copy(way, s).wait_recv()

            @pl.when(here & jnp.logical_not(gets))
            def _():
                entering[way, pl.ds(s * run, run)] = jnp.zeros((run,) + entering.shape[2:], entering.dtype)

            @pl.when(here & sends)
            def _():
                for i in range(run):
                    slot = s * run + i
                    for kind, local in enumerate((end, pull)):
                        d = (way + kind) % 2
                        through = jnp.exp2(decay[d] * total[d, slot][None])
                        value = through * entering[way, slot, kind].astype(F32) + local[d, slot]
                        held[way, slot, kind] = value.astype(held.dtype)
                copy(way, s).start()

        return carry

    lax.fori_loop(0, waves + count - 1, wave, 0)

    def drain(s, carry):
        for way in range(2):

            @pl.when(ways[way][1])
            def _():
                copy(way, s).wait_send()

        return carry

    lax.fori_loop(0, waves, drain, 0)


def pass_states(end, pull, total, decay):
    _, slots, halves, rows, channels = end.shape
    run = RUN
    shape = (2, slots, 2, halves, rows, channels)
    return pl.pallas_call(
        functools.partial(chain, lax.axis_size("fsdp"), run),
        in_specs=[pl.BlockSpec(memory_space=pltpu.VMEM)] * 4,
        out_specs=pl.BlockSpec(memory_space=pltpu.VMEM),
        out_shape=jax.ShapeDtypeStruct(shape, BF16),
        scratch_shapes=[
            pltpu.VMEM(shape, BF16),
            pltpu.SemaphoreType.DMA((2, slots // run)),
            pltpu.SemaphoreType.DMA((2, slots // run)),
        ],
        compiler_params=pltpu.CompilerParams(
            collective_id=0, has_side_effects=True, vmem_limit_bytes=40 * MIB
        ),
        name="pass_states",
    )(end, pull, total, decay)


def partner(g, bit):
    return g + bit * (1 - 2 * lax.rem(g // bit, 2))


class Mail:
    def __init__(self, send_sem, recv_sem):
        self.send_sem, self.recv_sem, self.made = send_sem, recv_sem, []

    def post(self, src, dst, target, here=None, there=None, landing=None):
        n = len(self.made)
        copy = lambda into: pltpu.make_async_remote_copy(
            src_ref=src,
            dst_ref=into,
            send_sem=self.send_sem.at[n],
            recv_sem=self.recv_sem.at[n],
            device_id=target,
            device_id_type=pl.DeviceIdType.MESH,
        )
        when = lambda cond: (lambda body: body()) if cond is None else pl.when(cond)
        landing = dst if landing is None else landing
        entry = dict(got=False)

        @when(here)
        def _():
            copy(dst).start()

        def take():
            if not entry["got"]:
                entry["got"] = True

                @when(there)
                def _():
                    copy(landing).wait_recv()

        def sent():
            @when(here)
            def _():
                copy(dst).wait_send()

        self.made.append((take, sent))
        return take

    def finish(self):
        for take, _ in self.made:
            take()
        for _, sent in self.made:
            sent()


def collect(
    groups,
    parts,
    tokens,
    halo,
    in_own,
    xproj,
    small,
    facts,
    all_tokens,
    all_halo,
    in_matrix,
    all_xproj,
    all_small,
    all_facts,
    send_sem,
    recv_sem,
    own_sem,
):
    g, f = lax.axis_index("group"), lax.axis_index("fsdp")
    chips = parts // 2
    z, core = f // 2, lax.rem(f, 2)
    ways = groups.bit_length() - 1
    bits = [1 << i for i in range(ways)]
    barrier = pltpu.get_barrier_semaphore()
    for bit in bits:
        pl.semaphore_signal(
            barrier, inc=1, device_id={"group": partner(g, bit)}, device_id_type=pl.DeviceIdType.MESH
        )
    for k in range(1, parts):
        pl.semaphore_signal(
            barrier,
            inc=1,
            device_id={"fsdp": lax.rem(f + k, parts)},
            device_id_type=pl.DeviceIdType.MESH,
        )
    pl.semaphore_wait(barrier, ways + parts - 1)
    mail = Mail(send_sem, recv_sem)
    place = lambda part: lax.rem(part + 2 * parts, parts)
    sibling = {"fsdp": f + 1 - 2 * core}
    up, down = {"fsdp": f + 2}, {"fsdp": f - 2}

    fact_takes = []
    for k in range(1, parts):
        fact_takes.append(
            mail.post(
                facts,
                all_facts.at[0, f],
                {"fsdp": lax.rem(f + k, parts)},
                landing=all_facts.at[0, lax.rem(f + parts - k, parts)],
            )
        )

    def cuts(count):
        edges = [count * i // ways for i in range(ways + 1)]
        return [pl.ds(lo, hi - lo) for lo, hi in zip(edges[:-1], edges[1:])]

    def relative(own, every, count):
        pieces = cuts(count)
        held = [{0: None} for _ in range(ways)]
        steps = [[] for _ in range(ways)]
        for t in range(ways):
            for p in range(ways):
                bit = bits[(p + t) % ways]
                for r in list(held[p]):
                    held[p][r ^ bit] = None
                    steps[t].append((p, r, bit))
        takes = {}

        def run(chosen):
            for p, r, bit in chosen:
                if r:
                    takes[p, r]()
                src = own.at[pieces[p]] if r == 0 else every.at[r, pieces[p]]
                takes[p, r ^ bit] = mail.post(
                    src, every.at[r ^ bit, pieces[p]], {"group": partner(g, bit)}
                )

        run([move for step in steps for move in step if move[1] == 0])
        return [functools.partial(run, [move for move in step if move[1]]) for step in steps[1:]]

    token_steps = relative(tokens, all_tokens, tokens.shape[0])
    halo_steps = relative(halo, all_halo, halo.shape[0])

    line = []

    def hop(h):
        for sign, target, inside in ((1, up, z < chips - 1), (-1, down, z > 0)):
            shard = f - sign * 2 * (h - 1)
            src = in_own if h == 1 else in_matrix.at[place(shard)]
            far = z - sign * (h - 1)
            come = z - sign * h
            line.append(
                mail.post(
                    src,
                    in_matrix.at[place(shard)],
                    target,
                    here=inside & (far >= 0) & (far < chips),
                    there=(come >= 0) & (come < chips),
                    landing=in_matrix.at[place(f - sign * 2 * h)],
                )
            )

    def share(h):
        for sign in (1, -1):
            shard = place(f - sign * 2 * h)
            come = z - sign * h
            known = (come >= 0) & (come < chips)
            mail.post(
                in_own if h == 0 else in_matrix.at[shard],
                in_matrix.at[shard],
                sibling,
                here=known,
                there=known,
                landing=in_matrix.at[place(f + 1 - 2 * core - sign * 2 * h)],
            )
            if h == 0:
                break

    hop(1)
    share(0)

    own_fact = pltpu.make_async_copy(facts, all_facts.at[0, f], own_sem.at[0])
    own_fact.start()
    held_copies = [
        pltpu.make_async_copy(xproj, all_xproj.at[core], own_sem.at[1]),
        pltpu.make_async_copy(small, all_small.at[core], own_sem.at[2]),
    ]

    @pl.when(z == g)
    def _():
        for copy in held_copies:
            copy.start()

    own_fact.wait()
    for take in fact_takes:
        take()
    fact_steps = relative(all_facts.at[0], all_facts, parts)

    pairs = ((xproj, all_xproj), (small, all_small))
    for distance in range(1, chips):
        for sign, target in ((1, up), (-1, down)):
            source = g + sign * (distance - 1)
            here = (z == source) & (source + sign >= 0) & (source + sign < chips)
            there = z == source + sign
            for own, every in pairs:
                src = own if distance == 1 else every.at[core]
                take = mail.post(src, every.at[core], target, here=here, there=there)
                take()
        if distance == 1:
            for step in fact_steps:
                step()
    for own, every in pairs:
        for src, where in ((own, z == g), (every.at[core], z != g)):
            mail.post(
                src, every.at[core], sibling, here=where, there=where, landing=every.at[1 - core]
            )

    for h in range(1, chips):
        for take in line[-2:]:
            take()
        if h < chips - 1:
            hop(h + 1)
        share(h)
        if h == 1 or chips == 2:
            for step in halo_steps:
                step()
            for step in token_steps:
                step()
    @pl.when(z == g)
    def _():
        for copy in held_copies:
            copy.wait()

    mail.finish()


def collect_inputs(tokens, halo, in_own, xproj, small, facts):
    groups, parts = lax.axis_size("group"), lax.axis_size("fsdp")
    ins = (tokens, halo, in_own, xproj, small, facts)
    outs = [
        jax.ShapeDtypeStruct((groups,) + tokens.shape, tokens.dtype),
        jax.ShapeDtypeStruct((groups,) + halo.shape, halo.dtype),
        jax.ShapeDtypeStruct((parts,) + in_own.shape, in_own.dtype),
        jax.ShapeDtypeStruct((2,) + xproj.shape, xproj.dtype),
        jax.ShapeDtypeStruct((2,) + small.shape, small.dtype),
        jax.ShapeDtypeStruct((groups, parts) + facts.shape, facts.dtype),
    ]
    ways = groups.bit_length() - 1
    copies = 3 * ways * (groups - 1) + (parts - 1) + 4 * (parts // 2 - 1) + 1 + 4 * (parts // 2 - 1) + 4
    outs = pl.pallas_call(
        functools.partial(collect, groups, parts),
        in_specs=[pl.BlockSpec(memory_space=pl.ANY)] * len(ins),
        out_specs=[pl.BlockSpec(memory_space=pl.ANY)] * len(outs),
        out_shape=outs,
        scratch_shapes=[
            pltpu.SemaphoreType.DMA((copies,)),
            pltpu.SemaphoreType.DMA((copies,)),
            pltpu.SemaphoreType.DMA((3,)),
        ],
        compiler_params=pltpu.CompilerParams(collective_id=1, has_side_effects=True),
        name="collect_inputs",
    )(*ins)
    all_tokens, all_halo, in_matrix, all_xproj, all_small, all_facts = outs
    return (
        all_tokens.at[0].set(tokens),
        all_halo.at[0].set(halo),
        lax.dynamic_update_index_in_dim(in_matrix, in_own, lax.axis_index("fsdp"), 0),
        all_xproj,
        all_small,
        all_facts,
    )


def runs(count, ways):
    edges = [count * i // ways for i in range(ways + 1)]
    return [pl.ds(lo, hi - lo) for lo, hi in zip(edges[:-1], edges[1:])]


def greet(groups):
    g = lax.axis_index("group")
    bits = [1 << i for i in range(groups.bit_length() - 1)]
    barrier = pltpu.get_barrier_semaphore()
    for bit in bits:
        pl.semaphore_signal(
            barrier, inc=1, device_id={"group": partner(g, bit)}, device_id_type=pl.DeviceIdType.MESH
        )
    pl.semaphore_wait(barrier, len(bits))
    return g, bits


def total_blocks(groups, terms, out, sums, parcel, landed, gathered, send_sem, recv_sem):
    g, bits = greet(groups)
    ways = len(bits)
    pieces = runs(terms.shape[1], ways)
    mail = Mail(send_sem, recv_sem)
    sums[...] = terms[...]
    held = [set(range(groups)) for _ in range(ways)]
    for t in range(ways):
        coming = []
        for p in range(ways):
            bit = bits[(p + t) % ways]
            for r in sorted(r for r in held[p] if r & bit):
                parcel[r, pieces[p]] = sums[r, pieces[p]].astype(parcel.dtype)
                take = mail.post(
                    parcel.at[r, pieces[p]],
                    landed.at[t, r ^ bit, pieces[p]],
                    {"group": partner(g, bit)},
                )
                coming.append((take, p, r ^ bit))
                held[p].remove(r)
        for take, p, r in coming:
            take()
            sums[r, pieces[p]] = sums[r, pieces[p]] + landed[t, r, pieces[p]].astype(F32)
    gathered[0] = sums[0].astype(gathered.dtype)
    known = [{0: None} for _ in range(ways)]
    for t in range(ways):
        for p in range(ways):
            bit = bits[(p + t) % ways]
            for r, take in list(known[p].items()):
                if take is not None:
                    take()
                known[p][r ^ bit] = mail.post(
                    gathered.at[r, pieces[p]],
                    gathered.at[r ^ bit, pieces[p]],
                    {"group": partner(g, bit)},
                )
    mail.finish()
    out[...] = gathered[...].astype(out.dtype)


def sum_blocks(terms, sent, result, number):
    groups = lax.axis_size("group")
    ways = groups.bit_length() - 1
    shape = (groups, terms.shape[0] // groups, terms.shape[1] * terms.shape[2], terms.shape[3])
    copies = 2 * ways * (groups - 1)
    return pl.pallas_call(
        functools.partial(total_blocks, groups),
        in_specs=[pl.BlockSpec(memory_space=pltpu.VMEM)],
        out_specs=pl.BlockSpec(memory_space=pltpu.VMEM),
        out_shape=jax.ShapeDtypeStruct(shape, result),
        scratch_shapes=[
            pltpu.VMEM(shape, F32),
            pltpu.VMEM(shape, sent),
            pltpu.VMEM((ways,) + shape, sent),
            pltpu.VMEM(shape, BF16),
            pltpu.SemaphoreType.DMA((copies,)),
            pltpu.SemaphoreType.DMA((copies,)),
        ],
        compiler_params=pltpu.CompilerParams(
            collective_id=number, has_side_effects=True, vmem_limit_bytes=32 * MIB
        ),
        cost_estimate=pl.CostEstimate(flops=30000 * terms.size // 2, bytes_accessed=8 * terms.size, transcendentals=0),
        name="sum_blocks",
    )(terms.reshape(shape)).reshape(terms.shape)


def front(
    halo_rows,
    info,
    tokens,
    halo,
    modulation,
    in_matrix,
    taps,
    conv_shift,
    xproj,
    modulated,
    extended,
    gate_z,
    conv_out,
    projected,
):
    slot = pl.program_id(0)
    length, model_width = tokens.shape
    channels = gate_z.shape[1]
    count, base = info[slot], info[pl.num_programs(0)]
    outs = (modulated, extended, gate_z, conv_out, projected)

    @pl.when(count <= base)
    def _():
        for out in outs:
            out[...] = jnp.zeros_like(out)

    @pl.when(count > base)
    def _():
        values = jnp.concatenate([tokens[...].astype(F32), halo[...].astype(F32)], axis=0)
        row = lax.broadcasted_iota(jnp.int32, (length + ROWS, 1), 0)
        behind, ahead = row - length - halo_rows, row - halo_rows
        at = jnp.where(row < length, row, jnp.where(behind < 0, behind, ahead))
        at = at + base
        known = (row < length + 2 * halo_rows) & (at >= 0) & (at < count)
        mask = known.astype(F32)
        centered = values - jnp.mean(values, axis=1, keepdims=True)
        normed = centered * lax.rsqrt(
            jnp.mean(centered * centered, axis=1, keepdims=True) + EPSILON
        )
        shift = modulation[:, :model_width]
        scale = modulation[:, model_width : 2 * model_width]
        low = ((normed * (1.0 + scale) + shift) * mask).astype(BF16)
        modulated[...] = low[:length]
        inner = dot32(low, in_matrix[...], ((1,), (0,)))
        gate_z[...] = inner[:length, channels:]
        extended[...] = jnp.zeros_like(extended)
        extended[ROWS : ROWS + length, :] = inner[:length, :channels]
        extended[ROWS - halo_rows : ROWS, :] = inner[length : length + halo_rows, :channels]
        extended[ROWS + length : ROWS + length + halo_rows, :] = inner[
            length + halo_rows : length + 2 * halo_rows, :channels
        ]
        for d in range(2):
            pre = conv_rows(extended, taps, conv_shift, d, length)
            value = (pre * jax.nn.sigmoid(pre) * mask[:length]).astype(BF16)
            conv_out[d] = value
            projected[d] = dot32(value, xproj[d], ((1,), (0,)))


def tap_row(d, k, kernel):
    return ROWS - (kernel - 1) + k if d == 0 else ROWS + (kernel - 1) - k


def conv_rows(extended, taps, conv_shift, d, length):
    kernel = taps.shape[1]
    pre = conv_shift[d : d + 1, :]
    for k in range(kernel):
        row = tap_row(d, k, kernel)
        pre = pre + taps[d, k : k + 1, :] * extended[row : row + length, :]
    return pre


def project(info, tokens, halo, modulation, in_matrix, taps, conv_shift, xproj):
    slots, length, model_width = tokens.shape
    channels = taps.shape[2]
    width = xproj.shape[2]
    fixed = lambda array: pl.BlockSpec(array.shape, lambda s, i: (0,) * array.ndim)
    one = lambda *tail: pl.BlockSpec((None,) + tail, lambda s, i: (s,) + (0,) * len(tail))
    return pl.pallas_call(
        functools.partial(front, taps.shape[1] - 1),
        grid_spec=pltpu.PrefetchScalarGridSpec(
            num_scalar_prefetch=1,
            grid=(slots,),
            in_specs=[
                one(length, model_width),
                one(ROWS, model_width),
                one(1, modulation.shape[2]),
                fixed(in_matrix),
                fixed(taps),
                fixed(conv_shift),
                fixed(xproj),
            ],
            out_specs=[
                one(length, model_width),
                one(length + 2 * ROWS, channels),
                one(length, channels),
                pl.BlockSpec((2, None, length, channels), lambda s, i: (0, s, 0, 0)),
                one(2, length, width),
            ],
        ),
        out_shape=[
            jax.ShapeDtypeStruct((slots, length, model_width), BF16),
            jax.ShapeDtypeStruct((slots, length + 2 * ROWS, channels), F32),
            jax.ShapeDtypeStruct((slots, length, channels), F32),
            jax.ShapeDtypeStruct((2, slots, length, channels), BF16),
            jax.ShapeDtypeStruct((slots, 2, length, width), F32),
        ],
        compiler_params=pltpu.CompilerParams(vmem_limit_bytes=40 * MIB),
        cost_estimate=pl.CostEstimate(
            flops=18000 * slots * length * channels,
            bytes_accessed=20 * slots * length * channels,
            transcendentals=0,
        ),
        name="project",
    )(info, tokens, halo, modulation, in_matrix, taps, conv_shift, xproj)


def back(
    info,
    extended,
    conv_grad,
    proj_grad,
    conv_out,
    taps,
    conv_shift,
    xproj,
    grad_x,
    rim,
    sums,
    xproj_grad,
    rows,
):
    slot = pl.program_id(0)
    length, channels = grad_x.shape
    kernel = taps.shape[1]
    halo = kernel - 1
    count, base = info[slot], info[pl.num_programs(0)]

    @pl.when(slot == 0)
    def _():
        sums[...] = jnp.zeros_like(sums)
        xproj_grad[...] = jnp.zeros_like(xproj_grad)
        rows[...] = jnp.zeros_like(rows)

    @pl.when(count <= base)
    def _():
        grad_x[...] = jnp.zeros_like(grad_x)
        rim[...] = jnp.zeros_like(rim)

    @pl.when(count > base)
    def _():
        row = lax.broadcasted_iota(jnp.int32, (length, 1), 0)
        mask = (base + row < count).astype(F32)
        for d in range(2):
            pre = conv_rows(extended, taps, conv_shift, d, length)
            sigmoid = jax.nn.sigmoid(pre)
            slope = sigmoid * (1.0 + pre * (1.0 - sigmoid))
            into = conv_grad[d] + dot32(proj_grad[d], xproj[d], ((1,), (1,)))
            value = into * mask * slope
            rows[d, ROWS : ROWS + length, :] = value
            turned = jnp.transpose(proj_grad[d].astype(F32)).astype(BF16)
            xproj_grad[d] += dot32(turned, conv_out[d], ((1,), (0,)))
            for k in range(kernel):
                first = tap_row(d, k, kernel)
                at = d * kernel + k
                sums[at : at + 1, :] += jnp.sum(
                    value * extended[first : first + length, :], axis=0, keepdims=True
                )
            at = 2 * kernel + d
            sums[at : at + 1, :] += jnp.sum(value, axis=0, keepdims=True)
        total = jnp.zeros((length, channels), F32)
        for k in range(kernel):
            ahead, behind = ROWS + halo - k, ROWS - halo + k
            total = total + taps[0, k : k + 1, :] * rows[0, ahead : ahead + length, :]
            total = total + taps[1, k : k + 1, :] * rows[1, behind : behind + length, :]
        grad_x[...] = total
        rim[0] = rows[0, ROWS : 2 * ROWS, :]
        rim[1] = rows[1, length : length + ROWS, :]


def back_through(info, extended, conv_grad, proj_grad, conv_out, taps, conv_shift, xproj):
    slots = extended.shape[0]
    length, channels = conv_out.shape[2:]
    width = xproj.shape[2]
    kernel = taps.shape[1]
    sum_rows = 2 * ROWS * ((2 * kernel + 2 + 2 * ROWS - 1) // (2 * ROWS))
    fixed = lambda array: pl.BlockSpec(array.shape, lambda s, i: (0,) * len(array.shape))
    one = lambda *tail: pl.BlockSpec((None,) + tail, lambda s, i: (s,) + (0,) * len(tail))
    both = pl.BlockSpec((2, None, length, channels), lambda s, i: (0, s, 0, 0))
    sums = jax.ShapeDtypeStruct((sum_rows, channels), F32)
    xproj_grad = jax.ShapeDtypeStruct((2, width, channels), F32)
    return pl.pallas_call(
        back,
        grid_spec=pltpu.PrefetchScalarGridSpec(
            num_scalar_prefetch=1,
            grid=(slots,),
            in_specs=[
                one(length + 2 * ROWS, channels),
                both,
                one(2, length, width),
                both,
                fixed(taps),
                fixed(conv_shift),
                fixed(xproj),
            ],
            out_specs=[one(length, channels), one(2, ROWS, channels), fixed(sums), fixed(xproj_grad)],
            scratch_shapes=[pltpu.VMEM((2, length + 2 * ROWS, channels), F32)],
        ),
        out_shape=[
            jax.ShapeDtypeStruct((slots, length, channels), F32),
            jax.ShapeDtypeStruct((slots, 2, ROWS, channels), F32),
            sums,
            xproj_grad,
        ],
        compiler_params=pltpu.CompilerParams(vmem_limit_bytes=32 * MIB),
        cost_estimate=pl.CostEstimate(
            flops=24000 * slots * length * channels,
            bytes_accessed=30 * slots * length * channels,
            transcendentals=0,
        ),
        name="back_through",
    )(info, extended, conv_grad, proj_grad, conv_out, taps, conv_shift, xproj)


def scatter(groups, terms, out, parcel, landed, send_sem, recv_sem):
    g, bits = greet(groups)
    ways = len(bits)
    pieces = runs(terms.shape[1], ways)
    mail = Mail(send_sem, recv_sem)
    held = [set(range(groups)) for _ in range(ways)]
    came = [{r: [] for r in range(groups)} for _ in range(ways)]

    def summed(p, r):
        value = terms[r, pieces[p]].astype(F32)
        for t, take in came[p][r]:
            take()
            value = value + landed[t, r, pieces[p]].astype(F32)
        return value

    for t in range(ways):
        for p in range(ways):
            bit = bits[(p + t) % ways]
            for r in sorted(r for r in held[p] if r & bit):
                src = terms
                if t:
                    parcel[r, pieces[p]] = summed(p, r).astype(parcel.dtype)
                    src = parcel
                take = mail.post(
                    src.at[r, pieces[p]],
                    landed.at[t, r ^ bit, pieces[p]],
                    {"group": partner(g, bit)},
                )
                came[p][r ^ bit].append((t, take))
                held[p].remove(r)
    for p in range(ways):
        out[pieces[p]] = summed(p, 0)
    mail.finish()


def scatter_blocks(terms, number):
    groups = lax.axis_size("group")
    ways = groups.bit_length() - 1
    slots, length, model_width = terms.shape
    block = (slots // groups, length, model_width)
    copies = ways * (groups - 1)
    return pl.pallas_call(
        functools.partial(scatter, groups),
        in_specs=[pl.BlockSpec(memory_space=pltpu.VMEM)],
        out_specs=pl.BlockSpec(memory_space=pltpu.VMEM),
        out_shape=jax.ShapeDtypeStruct(block, F32),
        scratch_shapes=[
            pltpu.VMEM((groups,) + block, terms.dtype),
            pltpu.VMEM((ways, groups) + block, terms.dtype),
            pltpu.SemaphoreType.DMA((copies,)),
            pltpu.SemaphoreType.DMA((copies,)),
        ],
        compiler_params=pltpu.CompilerParams(
            collective_id=number, has_side_effects=True, vmem_limit_bytes=48 * MIB
        ),
        cost_estimate=pl.CostEstimate(
            flops=20000 * terms.size, bytes_accessed=4 * terms.size, transcendentals=0
        ),
        name="scatter_blocks",
    )(terms.reshape((groups,) + block))


def finish(
    groups,
    parts,
    terms,
    in_x,
    in_z,
    packed,
    modulation,
    in_grad,
    out_grad,
    rest,
    landed,
    every_x,
    every_z,
    every_p,
    moved,
    send_sem,
    recv_sem,
):
    g, f = lax.axis_index("group"), lax.axis_index("fsdp")
    bits = [1 << i for i in range(groups.bit_length() - 1)]
    ways = len(bits)
    barrier = pltpu.get_barrier_semaphore()
    others = [{"group": partner(g, bit)} for bit in bits]
    others += [{"fsdp": lax.rem(f + k, parts)} for k in range(1, parts)]
    for other in others:
        pl.semaphore_signal(barrier, inc=1, device_id=other, device_id_type=pl.DeviceIdType.MESH)
    ratio = parts // groups
    target = {"group": lax.rem(f, groups), "fsdp": ratio * g + f // groups}
    source = {"group": f // ratio, "fsdp": groups * lax.rem(f, ratio) + g}
    stays = (target["group"] == g) & (target["fsdp"] == f)
    leaves = jnp.logical_not(stays)

    @pl.when(leaves)
    def _():
        pl.semaphore_signal(barrier, inc=1, device_id=source, device_id_type=pl.DeviceIdType.MESH)
        pl.semaphore_wait(barrier, len(others) + 1)

    @pl.when(stays)
    def _():
        pl.semaphore_wait(barrier, len(others))
        moved[...] = packed[...]

    mail = Mail(send_sem, recv_sem)
    arrived = mail.post(packed, moved, target, here=leaves, there=leaves)
    takes = []
    for k in range(1, parts):
        there = lax.rem(f + k, parts)
        takes.append(mail.post(terms.at[there], landed.at[k - 1], {"fsdp": there}))

    def absolute(r):
        at = g
        for bit in bits:
            at = partner(at, bit) if r & bit else at
        return at

    shards = ((in_x, every_x), (in_z, every_z), (moved, every_p))
    known = {}
    forwards = [[] for _ in range(ways)]
    later = [[] for _ in range(ways)]
    for own, every in shards[:2]:
        every[g] = own[...]
    for n, (own, every) in enumerate(shards):
        tiles = own.shape[1] // LANES
        for p in range(ways):
            lo, hi = (tiles * i // ways * LANES for i in (p, p + 1))
            held = [0]
            for t in range(ways):
                bit = bits[(p + t) % ways]
                for r in list(held):
                    move = (n, every, pl.ds(lo, hi - lo), p, r, bit)
                    (forwards if n < 2 else later)[t if r else 0].append(move)
                    held.append(r ^ bit)

    def run(moves):
        for n, every, cols, p, r, bit in moves:
            if r:
                known[n, p, r]()
            block = every.at[absolute(r), :, cols]
            known[n, p, r ^ bit] = mail.post(
                block,
                block,
                {"group": partner(g, bit)},
                landing=every.at[absolute(r ^ bit), :, cols],
            )

    run(forwards[0])
    total = terms[f]
    for k, take in enumerate(takes):
        take()
        total = total + landed[k]
    modulation[0] = total
    found = {0: None}
    for bit in bits:
        for r, take in list(found.items()):
            if take is not None:
                take()
            found[r ^ bit] = mail.post(
                modulation.at[r], modulation.at[r ^ bit], {"group": partner(g, bit)}
            )
    arrived()
    every_p[g] = moved[...]
    run(later[0])
    for moves in forwards[1:] + later[1:]:
        run(moves)
    mail.finish()
    channels = in_x.shape[1]
    piece, model_width = packed.shape[0], out_grad.shape[1]
    for j in range(groups):
        for h, every in enumerate((every_x, every_z)):
            at = (h * groups + j) * channels
            in_grad[:, at : at + channels] = every[j]
        out_grad[j * piece : (j + 1) * piece, :] = every_p[j, :, :model_width].astype(F32)
        rest[j * piece : (j + 1) * piece, :] = every_p[j, :, model_width:].astype(F32)


def finish_gradients(terms, in_x, in_z, packed, model_width, number):
    groups, parts = lax.axis_size("group"), lax.axis_size("fsdp")
    ways = groups.bit_length() - 1
    block = terms.shape[1:]
    copies = parts + groups - 1 + 3 * ways * (groups - 1)
    rows, channels = in_x.shape
    piece, wide = packed.shape
    return pl.pallas_call(
        functools.partial(finish, groups, parts),
        in_specs=[pl.BlockSpec(memory_space=pltpu.VMEM)] * 4,
        out_specs=[pl.BlockSpec(memory_space=pltpu.VMEM)] * 4,
        out_shape=[
            jax.ShapeDtypeStruct((groups,) + block, F32),
            jax.ShapeDtypeStruct((rows, 2 * groups * channels), BF16),
            jax.ShapeDtypeStruct((groups * piece, model_width), F32),
            jax.ShapeDtypeStruct((groups * piece, wide - model_width), F32),
        ],
        scratch_shapes=[
            pltpu.VMEM((parts - 1,) + block, F32),
            pltpu.VMEM((groups, rows, channels), BF16),
            pltpu.VMEM((groups, rows, channels), BF16),
            pltpu.VMEM((groups, piece, wide), BF16),
            pltpu.VMEM((piece, wide), BF16),
            pltpu.SemaphoreType.DMA((copies,)),
            pltpu.SemaphoreType.DMA((copies,)),
        ],
        compiler_params=pltpu.CompilerParams(
            collective_id=number, has_side_effects=True, vmem_limit_bytes=32 * MIB
        ),
        name="finish_gradients",
    )(terms, in_x, in_z, packed)


def to_owner(groups, parts):
    ratio = parts // groups
    pairs = []
    for g in range(groups):
        for f in range(parts):
            pairs.append((g * parts + f, (f // ratio) * parts + groups * (f % ratio) + g))
    return pairs


def cut(array, pieces):
    slots = array.shape[0]
    edges = [slots * i // pieces for i in range(pieces + 1)]
    return [array[lo:hi] for lo, hi in zip(edges[:-1], edges[1:])]


def flip(array, groups, bit):
    return lax.ppermute(array, "group", [(i, i ^ bit) for i in range(groups)])


def bits_of(groups, first):
    count = groups.bit_length() - 1
    return [1 << ((first + i) % count) for i in range(count)]


def scatter_stage(pieces, groups, t):
    nexts = []
    for p, held in enumerate(pieces):
        bit = bits_of(groups, p)[t]
        sums = {r: value for r, value in held.items() if not r & bit}
        for r in [r for r in held if r & bit]:
            came = flip(held[r], groups, bit).astype(F32)
            sums[r ^ bit] = (sums[r ^ bit].astype(F32) + came).astype(BF16)
        nexts.append(sums)
    return nexts


def on_device(
    tokens,
    item_bucket,
    slot_item,
    slot_live,
    slot_tokens,
    ada_weight,
    ada_bias,
    in_weight,
    conv_weight,
    conv_bias,
    xproj_weight,
    dt_weight,
    dt_bias,
    a_log,
    skip_gain,
    out_weight,
    cotangent,
):
    own_slots, length, model_width = tokens.shape
    groups, parts = lax.axis_size("group"), lax.axis_size("fsdp")
    g, f = lax.axis_index("group"), lax.axis_index("fsdp")
    slots = own_slots * groups
    inner_width = in_weight.shape[1] // 2
    channels = inner_width // groups
    kernel = conv_weight.shape[1]
    halo = kernel - 1
    rank_width = dt_weight.shape[1]
    width = xproj_weight.shape[2]
    states = (width - rank_width) // 2

    matches = slot_item[:, None] == jnp.arange(item_bucket.shape[0], dtype=jnp.int32)[None, :]
    own_buckets = jnp.sum(jnp.where(matches, item_bucket[None, :], 0), axis=1)
    own_condition = jax.nn.silu(time_embed(own_buckets, model_width)).astype(BF16)
    own_modulation = jnp.dot(own_condition, ada_weight, preferred_element_type=F32)
    own_modulation = own_modulation + ada_bias.astype(F32)
    plain = jnp.stack([slot_tokens * slot_live, own_buckets], axis=1).astype(F32)
    facts = jnp.concatenate([own_modulation, jnp.repeat(plain, LANES // 2, axis=1)], axis=1)

    edges = [(i, i + 1) for i in range(parts - 1)]
    before = lax.ppermute(tokens[:, length - halo :], "fsdp", edges)
    after = lax.ppermute(tokens[:, :halo], "fsdp", [(j, i) for i, j in edges])
    padding = jnp.zeros((own_slots, ROWS - 2 * halo, model_width), tokens.dtype)
    in_own = jnp.concatenate(
        [
            lax.dynamic_slice_in_dim(in_weight, h * inner_width + g * channels, channels, 1)
            for h in range(2)
        ],
        axis=1,
    )
    shard = out_weight.shape[0]
    small = jnp.concatenate(
        [
            dt_weight.reshape(2 * rank_width, shard),
            a_log.reshape(2 * states, shard),
            conv_weight.reshape(2 * kernel, shard),
            conv_bias,
            dt_bias,
            skip_gain,
        ],
        axis=0,
    )
    small_rows = small.shape[0]
    small_pad = -small_rows % LANES
    small = jnp.pad(small, ((0, -small_rows % BLOCK), (0, 0)))
    all_tokens, all_halo, in_matrix, all_xproj, all_small, all_facts = collect_inputs(
        tokens,
        jnp.concatenate([before, after, padding], axis=1),
        in_own,
        xproj_weight,
        small,
        facts,
    )
    ways = groups.bit_length() - 1
    all_tokens, late = lax.optimization_barrier((all_tokens, cotangent))
    travelling = [{0: part} for part in cut(late, ways)]
    for p, held in enumerate(travelling):
        for bit in bits_of(groups, p):
            held[bit] = flip(held[0], groups, bit)
    all_tokens = all_tokens.reshape(slots, length, model_width)
    all_halo = all_halo.reshape(slots, ROWS, model_width)
    in_matrix = in_matrix.reshape(model_width, 2 * channels)

    piece = shard // groups
    sent = lax.ppermute(
        lax.dynamic_slice_in_dim(out_weight, g * piece, piece, 0),
        ("group", "fsdp"),
        to_owner(groups, parts),
    )
    out_matrix = lax.all_gather(sent, "fsdp", axis=0, tiled=True)
    xproj = jnp.concatenate([all_xproj[0], all_xproj[1]], axis=1)
    rest = jnp.concatenate([all_small[0], all_small[1]], axis=1)
    edge = 0

    def take(rows):
        nonlocal edge
        edge += rows
        return rest[edge - rows : edge]

    dt_matrix = jnp.pad(
        take(2 * rank_width).reshape(2, rank_width, channels), ((0, 0), (0, width - rank_width), (0, 0))
    )
    rate = -jnp.exp(take(2 * states).astype(F32)).reshape(2, states // ROWS, ROWS, channels)
    taps = take(2 * kernel).reshape(2, kernel, channels).astype(F32)
    conv_shift = take(2).astype(F32)
    dt_shift = take(2).astype(F32).reshape(2, 1, channels)
    skip = take(2).astype(F32).reshape(2, 1, channels)
    decay = rate * LOG2E

    columns = facts.shape[1] - LANES
    plain = all_facts[:, 0, :, columns:].reshape(slots, LANES).astype(jnp.int32)
    counts, buckets = plain[:, 0], plain[:, LANES // 2]
    modulation = all_facts[:, :, :, :columns].transpose(0, 2, 1, 3).reshape(slots, parts * columns)
    group_counts = jnp.sum(counts.reshape(groups, own_slots), axis=1).astype(F32)
    share = jnp.repeat(group_counts / jnp.sum(group_counts), own_slots)
    positions = f * length + jnp.arange(length, dtype=jnp.int32)
    mask = (positions[None, :] < counts[:, None]).astype(F32)
    active = (counts > f * length).astype(jnp.int32)
    own_mask = mask[:own_slots, :, None]
    own_share = share[:own_slots, None, None]
    condition = jax.nn.silu(time_embed(buckets, model_width)).astype(BF16)
    shift_mod = modulation[:, None, :model_width]
    scale_mod = modulation[:, None, model_width : 2 * model_width]
    gate_mod = modulation[:, None, 2 * model_width :]

    info = jnp.concatenate([counts, (f * length)[None]]).astype(jnp.int32)
    modulated, wide_x, gate_z, conv_out, projected = project(
        info, all_tokens, all_halo, modulation[:, None, :], in_matrix, taps, conv_shift, xproj
    )
    travelling, projected = lax.optimization_barrier((travelling, projected))
    for p, held in enumerate(travelling):
        order = bits_of(groups, p)
        for t in range(1, ways):
            for r in [r for r in held if r and r < groups and all(r & bit == 0 for bit in order[t:])]:
                held[r ^ order[t]] = flip(held[r], groups, order[t])
    proj = sum_blocks(projected, BF16, F32, 2)
    proj, travelling = lax.optimization_barrier((proj, travelling))
    all_cotangent = jnp.concatenate([held[r] for r in range(groups) for held in travelling], axis=0)

    def normalise(values):
        inputs = values.astype(F32)
        centered = inputs - jnp.mean(inputs, axis=2, keepdims=True)
        inv_std = lax.rsqrt(jnp.mean(centered * centered, axis=2, keepdims=True) + EPSILON)
        return (inputs, centered * inv_std, inv_std)

    grad_in_all = all_cotangent.astype(F32) * (mask * share[:, None])[:, :, None]
    branch_gradient = (grad_in_all * gate_mod).astype(BF16)
    grad_gated = jnp.einsum("sld,cd->slc", branch_gradient, out_matrix, preferred_element_type=F32)
    grad_y = grad_gated * jax.nn.silu(gate_z)

    step, end, pull, total, mix_b, mix_c = scan_ends(active, conv_out, proj, grad_y, dt_matrix, dt_shift, decay)
    entering = pass_states(end, pull, total, decay)
    gated_output, grad_z, conv_grad, proj_part, dtw_grad, dtb_grad, decay_grad, skip_grad = scan_all(
        active,
        conv_out,
        proj,
        grad_y,
        step,
        mix_b,
        mix_c,
        entering,
        gate_z,
        grad_gated,
        dt_matrix,
        decay,
        skip,
    )
    proj_grad = sum_blocks(proj_part, BF16, BF16, 3)
    alog_grad = (decay_grad * rate).reshape(2 * states, channels)

    branch_part = jnp.einsum("slc,cd->sld", gated_output, out_matrix, preferred_element_type=F32)
    inward_z = jnp.einsum("sld,slc->dc", modulated, grad_z, preferred_element_type=F32)
    branch_part, inward_z, proj_grad = lax.optimization_barrier(
        (branch_part.astype(BF16), inward_z.astype(BF16), proj_grad)
    )
    inward_z = lax.psum_scatter(inward_z, "fsdp", scatter_dimension=0, tiled=True)
    ways = groups.bit_length() - 1
    cut_blocks = [cut(block, ways) for block in jnp.split(branch_part, groups, axis=0)]
    moving = [{r: cut_blocks[r][p] for r in range(groups)} for p in range(ways)]
    moving = scatter_stage(moving, groups, 0)
    outward = jnp.einsum("slc,sld->cd", gated_output, branch_gradient, preferred_element_type=F32)

    grad_x, rim, conv_sums, xproj_grads = back_through(
        info, wide_x, conv_grad, proj_grad, conv_out, taps, conv_shift, xproj
    )
    outward, moving, rim, inward_z = lax.optimization_barrier(
        (outward.astype(BF16), moving, rim, inward_z)
    )
    ahead = lax.ppermute(rim[:, 0, :halo], "fsdp", [(j, i) for i, j in edges])
    behind = lax.ppermute(rim[:, 1, ROWS - halo :], "fsdp", edges)
    zeros = jnp.zeros_like(ahead)
    ahead, behind = jnp.concatenate([zeros, ahead], 1), jnp.concatenate([behind, zeros], 1)
    last = sum(taps[0, k] * ahead[:, halo - k : 2 * halo - k] for k in range(kernel))
    first = sum(taps[1, k] * behind[:, k : k + halo] for k in range(kernel))
    grad_x = grad_x + jnp.concatenate(
        [first, jnp.zeros((slots, length - 2 * halo, channels), F32), last], axis=1
    )
    grad_x = grad_x.astype(BF16)
    inner_gradient = jnp.concatenate([grad_x, grad_z], axis=2)
    inward = jnp.einsum("sld,slc->dc", modulated, grad_x, preferred_element_type=F32)
    grad_mod_part = jnp.einsum(
        "slc,dc->sld", inner_gradient, in_matrix, preferred_element_type=F32
    ).astype(BF16)
    for t in range(1, ways):
        moving = scatter_stage(moving, groups, t)
    branch = jnp.concatenate([held[0] for held in moving], axis=0)
    small_grads = jnp.concatenate(
        [
            xproj_grads.reshape(2 * width, channels),
            dtw_grad[:, :rank_width].reshape(2 * rank_width, channels),
            alog_grad,
            conv_sums[: 2 * kernel + 2],
            dtb_grad.reshape(2, channels),
            skip_grad.reshape(2, channels),
            jnp.zeros((small_pad, channels), F32),
        ],
        axis=0,
    ).astype(BF16)
    packed_grads = jnp.concatenate([outward, small_grads.T], axis=1)
    packed_piece = lax.psum_scatter(packed_grads, "fsdp", scatter_dimension=0, tiled=True)
    inward, grad_mod_part, branch, packed_piece = lax.optimization_barrier(
        (inward.astype(BF16), grad_mod_part, branch, packed_piece)
    )
    branch = branch.astype(F32)
    grad_mod = scatter_blocks(grad_mod_part, 4) * own_mask

    own_gate = gate_mod[:own_slots]
    own_scale = scale_mod[:own_slots]
    own_inputs, own_normed, own_inv = normalise(tokens)
    layer_out = ((own_inputs + own_gate * branch) * own_mask).astype(BF16)
    grad_in = cotangent.astype(F32) * own_mask * own_share
    grad_gate = jnp.sum(grad_in * branch, axis=1)

    grad_shift = jnp.sum(grad_mod, axis=1)
    grad_scale = jnp.sum(grad_mod * own_normed, axis=1)
    grad_normed = grad_mod * (1.0 + own_scale)
    grad_ln = own_inv * (
        grad_normed
        - jnp.mean(grad_normed, axis=2, keepdims=True)
        - own_normed * jnp.mean(grad_normed * own_normed, axis=2, keepdims=True)
    )
    tokens_grad = grad_in + grad_ln

    mod_part = jnp.concatenate([grad_shift, grad_scale, grad_gate], axis=1)
    inward_x = lax.psum_scatter(inward, "fsdp", scatter_dimension=0, tiled=True)
    mod_terms = mod_part.reshape(own_slots, parts, -1).transpose(1, 0, 2)
    mod_all, in_grad, out_grad, packed_own = finish_gradients(
        mod_terms, inward_x, inward_z, packed_piece, model_width, 5
    )
    in_grad = in_grad.astype(F32)
    mod_all = mod_all.reshape(slots, -1)
    ada_grad = jnp.einsum("sd,sk->dk", condition, mod_all.astype(BF16), preferred_element_type=F32)
    adab_grad = jnp.sum(mod_all, axis=0)
    xproj_grad = jnp.stack(
        [packed_own[:, d * width : (d + 1) * width] for d in range(2)]
    )
    rest_grads = packed_own[:, 2 * width :].T
    sizes = [2 * rank_width, 2 * states, 2 * kernel, 2, 2, 2]
    cuts = [sum(sizes[:i]) for i in range(len(sizes) + 1)]
    dtw_out, alog_out, conv_w_out, conv_b_out, dtb_out, skip_out = [
        rest_grads[cuts[i] : cuts[i + 1]] for i in range(len(sizes))
    ]
    return (
        layer_out,
        tokens_grad,
        ada_grad,
        adab_grad,
        in_grad,
        conv_w_out.reshape(2, kernel, shard),
        conv_b_out,
        xproj_grad,
        dtw_out.reshape(2, rank_width, shard),
        dtb_out,
        alog_out.reshape(2, states, shard),
        skip_out,
        out_grad,
    )


def solution(mesh):
    in_specs = (
        P("group", "fsdp", None),
        P(),
        P("group"),
        P("group"),
        P("group"),
        P(None, "fsdp"),
        P("fsdp"),
        P("fsdp", None),
        P(None, None, "fsdp"),
        P(None, "fsdp"),
        P(None, "fsdp", None),
        P(None, None, "fsdp"),
        P(None, "fsdp"),
        P(None, None, "fsdp"),
        P(None, "fsdp"),
        P("fsdp", None),
        P("group", "fsdp", None),
    )
    out_specs = (
        P("group", "fsdp", None),
        P("group", "fsdp", None),
        P(None, "fsdp"),
        P("fsdp"),
        P("fsdp", None),
        P(None, None, "fsdp"),
        P(None, "fsdp"),
        P(None, "fsdp", None),
        P(None, None, "fsdp"),
        P(None, "fsdp"),
        P(None, None, "fsdp"),
        P(None, "fsdp"),
        P("fsdp", None),
    )
    return jax.shard_map(
        on_device, mesh=mesh, in_specs=in_specs, out_specs=out_specs, check_vma=False
    )
```

```python
import functools
import math

import jax
import jax.numpy as jnp
from jax import lax
from jax.experimental import pallas as pl
from jax.experimental.pallas import tpu as pltpu
from jax.sharding import PartitionSpec as P

EPSILON = 1e-06
LANES = 128
ROWS = 8
BLOCK = 16
WIDE = 256
LAG = 3
RUN = 2
LOG2E = math.log2(math.e)
LN2 = math.log(2.0)
F32 = jnp.float32
BF16 = jnp.bfloat16
MIB = 1 << 20


def time_embed(buckets, model_width):
    half_width = model_width // 2
    frequency = jnp.exp(-math.log(10000.0) * jnp.arange(half_width, dtype=F32) / half_width)
    angles = buckets.astype(F32)[:, None] * frequency[None, :]
    return jnp.concatenate([jnp.cos(angles), jnp.sin(angles)], axis=1)


def silu_slope(values):
    sigmoid = jax.nn.sigmoid(values)
    return sigmoid * (1.0 + values * (1.0 - sigmoid))


def dot32(left, right, dims):
    return lax.dot_general(left, right, (dims, ((), ())), preferred_element_type=F32)


def pass_one(
    states, active, conv, proj, grad_y, dt_w, dt_b, decay, step, end, pull, total, mix_b, mix_c, drive, turned
):
    slot, direction = pl.program_id(0), pl.program_id(1)
    length, channels = drive.shape
    chunks = channels // LANES
    halves = states // ROWS
    rank = proj.shape[1] - 2 * states

    @pl.when(active[slot] == 0)
    def _():
        end[...] = jnp.zeros_like(end)
        pull[...] = jnp.zeros_like(pull)
        total[...] = jnp.zeros_like(total)

    @pl.when(active[slot] != 0)
    def _():
        pre = dot32(proj[...].astype(BF16), dt_w[direction], ((1,), (0,))) + dt_b[direction]
        steps = jnp.maximum(pre, 0.0) + jnp.log(1.0 + jnp.exp(-jnp.abs(pre)))
        step[...] = steps
        drive[...] = steps * conv[...].astype(F32)
        total[...] = jnp.broadcast_to(jnp.sum(steps, axis=0, keepdims=True), total.shape)

        def turn(i, carry):
            at = pl.multiple_of(i * ROWS, ROWS)
            turned[i] = jnp.transpose(proj[pl.ds(at, ROWS), :])[rank : rank + 2 * states]
            return carry

        lax.fori_loop(0, length // ROWS, turn, 0, unroll=True)
        zero = jnp.zeros((halves, ROWS, LANES), F32)
        for backward in range(2):

            @pl.when(direction == backward)
            def _():
                carry = ((zero,) * chunks, (zero + 1.0,) * chunks, (zero,) * chunks)
                rates = [decay[direction, :, :, k : k + LANES] for k in range(0, channels, LANES)]

                def block(i, carry):
                    at = length // ROWS - 1 - i if backward else i
                    rows = pl.ds(pl.multiple_of(at * ROWS, ROWS), ROWS)
                    held = [ref[rows, :] for ref in (step, drive, grad_y)]
                    hidden, running, pulled = carry
                    columns = turned[at]
                    for j in list(range(ROWS))[:: -1 if backward else 1]:
                        t = at * ROWS + j
                        wide = jnp.broadcast_to(columns[:, j : j + 1], (2 * states, LANES))
                        b = wide[:states].reshape(halves, ROWS, LANES)
                        c = wide[states:].reshape(halves, ROWS, LANES)
                        mix_b[t] = b
                        mix_c[t] = c
                        rowed = [
                            [
                                jnp.broadcast_to(h[j : j + 1, k : k + LANES], (ROWS, LANES))[None]
                                for k in range(0, channels, LANES)
                            ]
                            for h in held
                        ]
                        new = ([], [], [])
                        for k in range(chunks):
                            factor = jnp.exp2(rowed[0][k] * rates[k])
                            new[0].append(factor * hidden[k] + rowed[1][k] * b)
                            run = running[k] * factor
                            new[1].append(run)
                            new[2].append(pulled[k] + run * (rowed[2][k] * c))
                        hidden, running, pulled = new
                    return (tuple(hidden), tuple(running), tuple(pulled))

                hidden, _, pulled = lax.fori_loop(0, length // ROWS, block, carry)
                for k in range(chunks):
                    lanes = slice(k * LANES, (k + 1) * LANES)
                    end[:, :, lanes] = hidden[k]
                    pull[:, :, lanes] = pulled[k]


def pass_two(
    states,
    active,
    conv,
    proj,
    grad_y,
    step,
    mix_b,
    mix_c,
    entry,
    arrive,
    gate_z,
    grad_gated,
    dt_w,
    decay,
    skip,
    tile_b,
    tile_c,
    sel,
    take_b,
    take_c,
    gated,
    grad_z,
    conv_grad,
    proj_grad,
    dtw_grad,
    dtb_grad,
    alog_grad,
    skip_grad,
    drive,
    hid_even,
    hid_odd,
    edge,
    gst_even,
    gst_odd,
    thd_even,
    thd_odd,
    mixed,
    sdec,
    scan_y,
    in_part,
    out_part,
    rows_b,
    rows_c,
    drive_low,
    grad_low,
    y,
):
    slot, direction = pl.program_id(0), pl.program_id(1)
    length, channels = drive.shape
    chunks = channels // LANES
    halves = states // ROWS
    wide = BLOCK * states
    pairs = length // (2 * BLOCK)
    hid, gst, thd = (hid_even, hid_odd), (gst_even, gst_odd), (thd_even, thd_odd)
    lanes = [slice(k * LANES, (k + 1) * LANES) for k in range(chunks)]

    @pl.when((slot == 0) & (direction == 0))
    def _():
        dtw_grad[...] = jnp.zeros_like(dtw_grad)
        dtb_grad[...] = jnp.zeros_like(dtb_grad)
        alog_grad[...] = jnp.zeros_like(alog_grad)
        skip_grad[...] = jnp.zeros_like(skip_grad)

    @pl.when(direction == 0)
    def _():
        y[...] = jnp.zeros_like(y)

    @pl.when(active[slot] == 0)
    def _():
        conv_grad[...] = jnp.zeros_like(conv_grad)
        proj_grad[...] = jnp.zeros_like(proj_grad)
        gated[...] = jnp.zeros_like(gated)
        grad_z[...] = jnp.zeros_like(grad_z)

    def low(value):
        return value.reshape(states, LANES).astype(BF16)

    def block_range(pair, odd):
        return pl.ds(pl.multiple_of((2 * pair + odd) * BLOCK, BLOCK), BLOCK)

    def sweep_blocks(backward, tokens, matmuls, start):
        first, second = (1, 0) if backward else (0, 1)

        def two(i, carry):
            pair = pairs - 1 - i if backward else i
            before = lax.rem(pair + (1 if backward else pairs - 1), pairs)
            carry = tokens(pair, first, backward, matmuls(before, second), carry)
            return tokens(pair, second, backward, matmuls(pair, first), carry)

        carry = lax.fori_loop(0, pairs, two, start)
        for issue, keep in matmuls(0 if backward else pairs - 1, second):
            keep(issue())
        return carry

    def pieces(out, rows, left, right, dims, width):
        made = []
        for n in range(0, width, WIDE):
            cols = slice(n, min(n + WIDE, width))
            picked = right[:, cols] if dims[1] == (0,) else right

            def issue(left=left, picked=picked):
                return dot32(left, picked, dims)

            def keep(product, cols=cols):
                out[rows, cols] = product

            made.append((issue, keep))
        return made

    def scan_rows(pair, odd, backward, refs, body, beside, carry):
        order = list(range(BLOCK))[:: -1 if backward else 1]
        waiting = []
        for at_step, j in enumerate(order):
            if j % ROWS == (ROWS - 1 if backward else 0):
                at = pl.multiple_of((2 * pair + odd) * BLOCK + j // ROWS * ROWS, ROWS)
                held = [ref[pl.ds(at, ROWS), :] for ref in refs]
            i = j % ROWS
            rows = [
                [jnp.broadcast_to(h[i : i + 1, c], (ROWS, LANES))[None] for c in lanes] for h in held
            ]
            for issue, keep in beside[at_step * len(beside) // BLOCK : (at_step + 1) * len(beside) // BLOCK]:
                waiting.append((at_step + LAG, keep, issue()))
            carry = body(j, rows, carry)
            while waiting and waiting[0][0] <= at_step:
                _, keep, product = waiting.pop(0)
                keep(product)
        for _, keep, product in waiting:
            keep(product)
        return carry

    def forward_tokens(pair, odd, backward, beside, hidden):
        for k in range(chunks):
            edge[2 * pair + odd, :, lanes[k]] = low(hidden[k])

        def token(j, rows, hidden):
            b = mix_b[(2 * pair + odd) * BLOCK + j]
            new = []
            for k in range(chunks):
                factor = jnp.exp2(rows[0][k] * decay[direction, :, :, lanes[k]])
                value = factor * hidden[k] + rows[1][k] * b
                hid[odd][pair, j, :, lanes[k]] = low(value)
                new.append(value)
            return tuple(new)

        return scan_rows(pair, odd, backward, (step, drive), token, beside, hidden)

    def forward_matmuls(pair, odd):
        rows = block_range(pair, odd)
        h_rows = hid[odd][pair].reshape(wide, channels)
        return pieces(scan_y, rows, rows_c[rows, :], h_rows, ((1,), (0,)), channels) + pieces(
            out_part, rows, grad_low[rows, :], h_rows, ((1,), (1,)), wide
        )

    def backward_tokens(pair, odd, backward, beside, carry):
        earlier = -1 if backward else 1

        def token(j, rows, carry):
            carried, total = carry
            c = mix_c[(2 * pair + odd) * BLOCK + j]
            news, sums = [], []
            p = j + earlier
            for k in range(chunks):
                rate = decay[direction, :, :, lanes[k]]
                factor = jnp.exp2(rows[0][k] * rate)
                grad_state = rows[1][k] * c + carried[k]
                gst[odd][j, :, lanes[k]] = low(grad_state)
                onward = factor * grad_state
                if 0 <= p < BLOCK:
                    before = hid[odd][pair, p, :, lanes[k]]
                else:
                    before = edge[2 * pair + odd, :, lanes[k]]
                through = onward * before.astype(F32).reshape(halves, ROWS, LANES)
                sums.append(total[k] + through * rows[0][k])
                thd[odd][j, :, lanes[k]] = low(through * rate)
                news.append(onward)
            return (tuple(news), tuple(sums))

        return scan_rows(pair, odd, backward, (step, grad_y), token, beside, carry)

    def backward_matmuls(pair, odd):
        rows = block_range(pair, odd)
        g_rows = gst[odd][...].reshape(wide, channels)
        t_rows = thd[odd][...].reshape(wide, channels)
        return (
            pieces(mixed, rows, rows_b[rows, :], g_rows, ((1,), (0,)), channels)
            + pieces(sdec, rows, sel[...].astype(BF16), t_rows, ((1,), (0,)), channels)
            + pieces(in_part, rows, drive_low[rows, :], g_rows, ((1,), (1,)), wide)
        )

    @pl.when(active[slot] != 0)
    def _():
        drive[...] = step[...] * conv[...].astype(F32)
        drive_low[...] = drive[...].astype(BF16)
        grad_low[...] = grad_y[...].astype(BF16)
        proj_low = proj[...].astype(BF16)
        picked = jnp.concatenate([sel[...]] * (length // BLOCK), axis=0)
        rows_b[...] = (dot32(proj_low, tile_b[...], ((1,), (0,))) * picked).astype(BF16)
        rows_c[...] = (dot32(proj_low, tile_c[...], ((1,), (0,))) * picked).astype(BF16)
        zero = jnp.zeros((halves, ROWS, LANES), F32)
        for reverse in (False, True):

            @pl.when(direction == int(reverse))
            def _():
                start = tuple(entry[:, :, c].astype(F32) for c in lanes)
                sweep_blocks(reverse, forward_tokens, forward_matmuls, start)
                start = (tuple(arrive[:, :, c].astype(F32) for c in lanes), (zero,) * chunks)
                _, sums = sweep_blocks(not reverse, backward_tokens, backward_matmuls, start)
                for k in range(chunks):
                    alog_grad[direction, :, :, lanes[k]] += sums[k]

        conv_values = conv[...].astype(F32)
        steps = step[...]
        grads = grad_y[...]
        step_grad = conv_values * mixed[...] + LN2 * sdec[...]
        pre_grad = step_grad * (1.0 - jnp.exp(-steps))
        dtb_grad[direction] += jnp.sum(pre_grad, axis=0, keepdims=True)
        pre_low = pre_grad.astype(BF16)
        proj_grad[...] = (
            dot32((in_part[...] * picked).astype(BF16), take_b[...], ((1,), (0,)))
            + dot32((out_part[...] * picked).astype(BF16), take_c[...], ((1,), (0,)))
            + dot32(pre_low, dt_w[direction], ((1,), (1,)))
        )
        dtw_grad[direction] += dot32(jnp.transpose(proj[...]).astype(BF16), pre_low, ((1,), (0,)))
        y[...] += scan_y[...] + skip[direction] * conv_values
        skip_grad[direction] += jnp.sum(grads * conv_values, axis=0, keepdims=True)
        conv_grad[...] = grads * skip[direction] + steps * mixed[...]

        @pl.when(direction == 1)
        def _():
            total = y[...]
            value = gate_z[...]
            sigmoid = jax.nn.sigmoid(value)
            gated[...] = (total * (value * sigmoid)).astype(BF16)
            slope = sigmoid * (1.0 + value * (1.0 - sigmoid))
            grad_z[...] = (grad_gated[...] * total * slope).astype(BF16)


def whole(array):
    zeros = (0,) * array.ndim
    return pl.BlockSpec(array.shape, lambda s, d, a: zeros)


def scan_ends(active, conv, proj, grad_y, dt_w, dt_b, decay):
    slots, length, channels = grad_y.shape
    halves = decay.shape[1]
    width = proj.shape[3]
    states = halves * ROWS
    turn = lambda *tail: pl.BlockSpec((None, None) + tail, lambda s, d, a: (s, d) + (0,) * len(tail))
    pair = lambda *tail: pl.BlockSpec((None, None) + tail, lambda s, d, a: (d, s) + (0,) * len(tail))
    state = (2, slots, halves, ROWS, channels)
    mixes = (length, halves, ROWS, LANES)
    spare = lambda s, a: jnp.where(a[s] != 0, s, slots)
    kept_pair = pl.BlockSpec(
        (None, None, length, channels), lambda s, d, a: (jnp.where(a[s] != 0, d, 0), spare(s, a), 0, 0)
    )
    kept_mix = pl.BlockSpec(
        (None, None) + mixes, lambda s, d, a: (spare(s, a), jnp.where(a[s] != 0, d, 0), 0, 0, 0, 0)
    )
    return pl.pallas_call(
        functools.partial(pass_one, states),
        grid_spec=pltpu.PrefetchScalarGridSpec(
            num_scalar_prefetch=1,
            grid=(slots, 2),
            in_specs=[
                pair(length, channels),
                turn(length, width),
                pl.BlockSpec((None, length, channels), lambda s, d, a: (s, 0, 0)),
                whole(dt_w),
                whole(dt_b),
                whole(decay),
            ],
            out_specs=[
                kept_pair,
                pair(halves, ROWS, channels),
                pair(halves, ROWS, channels),
                pair(ROWS, channels),
                kept_mix,
                kept_mix,
            ],
            scratch_shapes=[
                pltpu.VMEM((length, channels), F32),
                pltpu.VMEM((length // ROWS, 2 * states, ROWS), F32),
            ],
        ),
        out_shape=[
            jax.ShapeDtypeStruct((2, slots + 1, length, channels), F32),
            jax.ShapeDtypeStruct(state, F32),
            jax.ShapeDtypeStruct(state, F32),
            jax.ShapeDtypeStruct((2, slots, ROWS, channels), F32),
            jax.ShapeDtypeStruct((slots + 1, 2) + mixes, F32),
            jax.ShapeDtypeStruct((slots + 1, 2) + mixes, F32),
        ],
        compiler_params=pltpu.CompilerParams(vmem_limit_bytes=24 * MIB),
        name="scan_ends",
    )(active, conv, proj, grad_y, dt_w, dt_b, decay)


def scan_all(
    active, conv, proj, grad_y, step, mix_b, mix_c, entering, gate_z, grad_gated, dt_w, decay, skip
):
    slots, length, channels = grad_y.shape
    halves = decay.shape[1]
    width = proj.shape[3]
    states = halves * ROWS
    wide = BLOCK * states
    rank = width - 2 * states
    column = jnp.arange(width)[:, None]
    lane = jnp.arange(wide)[None, :]
    tile_b = (column == rank + lane % states).astype(BF16)
    tile_c = (column == rank + states + lane % states).astype(BF16)
    sel = (jnp.arange(BLOCK)[:, None] == lane // states).astype(F32)
    turn = lambda *tail: pl.BlockSpec((None, None) + tail, lambda s, d, a: (s, d) + (0,) * len(tail))
    pair = lambda *tail: pl.BlockSpec((None, None) + tail, lambda s, d, a: (d, s) + (0,) * len(tail))
    one = pl.BlockSpec((None, length, channels), lambda s, d, a: (s, 0, 0))
    constants = (dt_w, decay, skip, tile_b, tile_c, sel, tile_b.T, tile_c.T)
    sums = (
        jax.ShapeDtypeStruct((2, width, channels), F32),
        jax.ShapeDtypeStruct((2, 1, channels), F32),
        jax.ShapeDtypeStruct((2, halves, ROWS, channels), F32),
        jax.ShapeDtypeStruct((2, 1, channels), F32),
    )
    pairs = length // (2 * BLOCK)
    read_s = lambda s, a: jnp.where(a[s] != 0, s, 0)
    read_d = lambda s, d, a: jnp.where(a[s] != 0, d, 0)
    got_one = pl.BlockSpec((None, length, channels), lambda s, d, a: (read_s(s, a), 0, 0))

    def got_pair(*tail):
        return pl.BlockSpec(
            (None, None) + tail, lambda s, d, a: (read_d(s, d, a), read_s(s, a)) + (0,) * len(tail)
        )

    def got_turn(*tail):
        return pl.BlockSpec(
            (None, None) + tail, lambda s, d, a: (read_s(s, a), read_d(s, d, a)) + (0,) * len(tail)
        )

    def got_state(kind):
        def place(s, d, a):
            way = read_d(s, d, a)
            return (way + kind * (1 - 2 * way), read_s(s, a), kind, 0, 0, 0)

        return pl.BlockSpec((None, None, None, halves, ROWS, channels), place)

    return pl.pallas_call(
        functools.partial(pass_two, states),
        grid_spec=pltpu.PrefetchScalarGridSpec(
            num_scalar_prefetch=1,
            grid=(slots, 2),
            in_specs=[
                got_pair(length, channels),
                got_turn(length, width),
                got_one,
                got_pair(length, channels),
                got_turn(length, halves, ROWS, LANES),
                got_turn(length, halves, ROWS, LANES),
                got_state(0),
                got_state(1),
                got_one,
                got_one,
            ]
            + [whole(c) for c in constants],
            out_specs=[one, one, pair(length, channels), turn(length, width)] + [whole(c) for c in sums],
            scratch_shapes=[pltpu.VMEM((length, channels), F32)]
            + [pltpu.VMEM((pairs, BLOCK, states, channels), BF16)] * 2
            + [pltpu.VMEM((2 * pairs, states, channels), BF16)]
            + [pltpu.VMEM((BLOCK, states, channels), BF16)] * 4
            + [pltpu.VMEM((length, channels), F32)] * 3
            + [pltpu.VMEM((length, wide), F32)] * 2
            + [pltpu.VMEM((length, wide), BF16)] * 2
            + [pltpu.VMEM((length, channels), BF16)] * 2
            + [pltpu.VMEM((length, channels), F32)],
        ),
        out_shape=[
            jax.ShapeDtypeStruct((slots, length, channels), BF16),
            jax.ShapeDtypeStruct((slots, length, channels), BF16),
            jax.ShapeDtypeStruct((2, slots, length, channels), F32),
            jax.ShapeDtypeStruct((slots, 2, length, width), F32),
        ]
        + list(sums),
        compiler_params=pltpu.CompilerParams(vmem_limit_bytes=44 * MIB),
        name="scan_all",
    )(active, conv, proj, grad_y, step, mix_b, mix_c, entering, entering, gate_z, grad_gated, *constants)


def chain(count, run, end, pull, total, decay, entering, held, send_sem, recv_sem):
    mine = lax.axis_index("fsdp")
    waves = end.shape[1] // run
    mesh_id = pl.DeviceIdType.MESH
    after, before = lax.rem(mine + 1, count), lax.rem(mine + count - 1, count)
    barrier = pltpu.get_barrier_semaphore()
    for other in (after, before):
        pl.semaphore_signal(barrier, inc=1, device_id={"fsdp": other}, device_id_type=mesh_id)
    pl.semaphore_wait(barrier, 2)
    ways = ((mine > 0, mine < count - 1, after), (mine < count - 1, mine > 0, before))

    def copy(way, s):
        slots = pl.ds(s * run, run)
        return pltpu.make_async_remote_copy(
            src_ref=held.at[way, slots],
            dst_ref=entering.at[way, slots],
            send_sem=send_sem.at[way, s],
            recv_sem=recv_sem.at[way, s],
            device_id={"fsdp": ways[way][2]},
            device_id_type=mesh_id,
        )

    lags = (mine, count - 1 - mine)

    def wave(turn, carry):
        for way in range(2):
            gets, sends, _ = ways[way]
            s = turn - lags[way]
            here = (s >= 0) & (s < waves)

            @pl.when(here & gets)
            def _():
                copy(way, s).wait_recv()

            @pl.when(here & jnp.logical_not(gets))
            def _():
                entering[way, pl.ds(s * run, run)] = jnp.zeros((run,) + entering.shape[2:], entering.dtype)

            @pl.when(here & sends)
            def _():
                for i in range(run):
                    slot = s * run + i
                    for kind, local in enumerate((end, pull)):
                        d = (way + kind) % 2
                        through = jnp.exp2(decay[d] * total[d, slot][None])
                        value = through * entering[way, slot, kind].astype(F32) + local[d, slot]
                        held[way, slot, kind] = value.astype(held.dtype)
                copy(way, s).start()

        return carry

    lax.fori_loop(0, waves + count - 1, wave, 0)

    def drain(s, carry):
        for way in range(2):

            @pl.when(ways[way][1])
            def _():
                copy(way, s).wait_send()

        return carry

    lax.fori_loop(0, waves, drain, 0)


def pass_states(end, pull, total, decay):
    _, slots, halves, rows, channels = end.shape
    run = RUN
    shape = (2, slots, 2, halves, rows, channels)
    return pl.pallas_call(
        functools.partial(chain, lax.axis_size("fsdp"), run),
        in_specs=[pl.BlockSpec(memory_space=pltpu.VMEM)] * 4,
        out_specs=pl.BlockSpec(memory_space=pltpu.VMEM),
        out_shape=jax.ShapeDtypeStruct(shape, BF16),
        scratch_shapes=[
            pltpu.VMEM(shape, BF16),
            pltpu.SemaphoreType.DMA((2, slots // run)),
            pltpu.SemaphoreType.DMA((2, slots // run)),
        ],
        compiler_params=pltpu.CompilerParams(
            collective_id=0, has_side_effects=True, vmem_limit_bytes=40 * MIB
        ),
        name="pass_states",
    )(end, pull, total, decay)


def partner(g, bit):
    return g + bit * (1 - 2 * lax.rem(g // bit, 2))


class Mail:
    def __init__(self, send_sem, recv_sem):
        self.send_sem, self.recv_sem, self.made = send_sem, recv_sem, []

    def post(self, src, dst, target, here=None, there=None, landing=None):
        n = len(self.made)
        copy = lambda into: pltpu.make_async_remote_copy(
            src_ref=src,
            dst_ref=into,
            send_sem=self.send_sem.at[n],
            recv_sem=self.recv_sem.at[n],
            device_id=target,
            device_id_type=pl.DeviceIdType.MESH,
        )
        when = lambda cond: (lambda body: body()) if cond is None else pl.when(cond)
        landing = dst if landing is None else landing
        entry = dict(got=False)

        @when(here)
        def _():
            copy(dst).start()

        def take():
            if not entry["got"]:
                entry["got"] = True

                @when(there)
                def _():
                    copy(landing).wait_recv()

        def sent():
            @when(here)
            def _():
                copy(dst).wait_send()

        self.made.append((take, sent))
        return take

    def finish(self):
        for take, _ in self.made:
            take()
        for _, sent in self.made:
            sent()


def collect(
    groups,
    parts,
    tokens,
    halo,
    in_own,
    xproj,
    small,
    facts,
    all_tokens,
    all_halo,
    in_matrix,
    all_xproj,
    all_small,
    all_facts,
    send_sem,
    recv_sem,
    own_sem,
):
    g, f = lax.axis_index("group"), lax.axis_index("fsdp")
    chips = parts // 2
    z, core = f // 2, lax.rem(f, 2)
    ways = groups.bit_length() - 1
    bits = [1 << i for i in range(ways)]
    barrier = pltpu.get_barrier_semaphore()
    for bit in bits:
        pl.semaphore_signal(
            barrier, inc=1, device_id={"group": partner(g, bit)}, device_id_type=pl.DeviceIdType.MESH
        )
    for k in range(1, parts):
        pl.semaphore_signal(
            barrier,
            inc=1,
            device_id={"fsdp": lax.rem(f + k, parts)},
            device_id_type=pl.DeviceIdType.MESH,
        )
    pl.semaphore_wait(barrier, ways + parts - 1)
    mail = Mail(send_sem, recv_sem)
    place = lambda part: lax.rem(part + 2 * parts, parts)
    sibling = {"fsdp": f + 1 - 2 * core}
    up, down = {"fsdp": f + 2}, {"fsdp": f - 2}

    fact_takes = []
    for k in range(1, parts):
        fact_takes.append(
            mail.post(
                facts,
                all_facts.at[0, f],
                {"fsdp": lax.rem(f + k, parts)},
                landing=all_facts.at[0, lax.rem(f + parts - k, parts)],
            )
        )

    def cuts(count):
        edges = [count * i // ways for i in range(ways + 1)]
        return [pl.ds(lo, hi - lo) for lo, hi in zip(edges[:-1], edges[1:])]

    def relative(own, every, count):
        pieces = cuts(count)
        held = [{0: None} for _ in range(ways)]
        steps = [[] for _ in range(ways)]
        for t in range(ways):
            for p in range(ways):
                bit = bits[(p + t) % ways]
                for r in list(held[p]):
                    held[p][r ^ bit] = None
                    steps[t].append((p, r, bit))
        takes = {}

        def run(chosen):
            for p, r, bit in chosen:
                if r:
                    takes[p, r]()
                src = own.at[pieces[p]] if r == 0 else every.at[r, pieces[p]]
                takes[p, r ^ bit] = mail.post(
                    src, every.at[r ^ bit, pieces[p]], {"group": partner(g, bit)}
                )

        run([move for step in steps for move in step if move[1] == 0])
        return [functools.partial(run, [move for move in step if move[1]]) for step in steps[1:]]

    token_steps = relative(tokens, all_tokens, tokens.shape[0])
    halo_steps = relative(halo, all_halo, halo.shape[0])

    line = []

    def hop(h):
        for sign, target, inside in ((1, up, z < chips - 1), (-1, down, z > 0)):
            shard = f - sign * 2 * (h - 1)
            src = in_own if h == 1 else in_matrix.at[place(shard)]
            far = z - sign * (h - 1)
            come = z - sign * h
            line.append(
                mail.post(
                    src,
                    in_matrix.at[place(shard)],
                    target,
                    here=inside & (far >= 0) & (far < chips),
                    there=(come >= 0) & (come < chips),
                    landing=in_matrix.at[place(f - sign * 2 * h)],
                )
            )

    def share(h):
        for sign in (1, -1):
            shard = place(f - sign * 2 * h)
            come = z - sign * h
            known = (come >= 0) & (come < chips)
            mail.post(
                in_own if h == 0 else in_matrix.at[shard],
                in_matrix.at[shard],
                sibling,
                here=known,
                there=known,
                landing=in_matrix.at[place(f + 1 - 2 * core - sign * 2 * h)],
            )
            if h == 0:
                break

    hop(1)
    share(0)

    own_fact = pltpu.make_async_copy(facts, all_facts.at[0, f], own_sem.at[0])
    own_fact.start()
    held_copies = [
        pltpu.make_async_copy(xproj, all_xproj.at[core], own_sem.at[1]),
        pltpu.make_async_copy(small, all_small.at[core], own_sem.at[2]),
    ]

    @pl.when(z == g)
    def _():
        for copy in held_copies:
            copy.start()

    own_fact.wait()
    for take in fact_takes:
        take()
    fact_steps = relative(all_facts.at[0], all_facts, parts)

    for step in fact_steps:
        step()

    pairs = ((xproj, all_xproj), (small, all_small))

    def pass_on(distance):
        takes = []
        for sign, target in ((1, up), (-1, down)):
            sender = g + sign * (distance - 1)
            here = (z == sender) & (sender + sign >= 0) & (sender + sign < chips)
            there = z == sender + sign
            for own, every in pairs:
                src = own if distance == 1 else every.at[core]
                takes.append(mail.post(src, every.at[core], target, here=here, there=there))
        return takes

    passing = pass_on(1)
    for h in range(1, chips):
        for take in line[-2:]:
            take()
        if h < chips - 1:
            hop(h + 1)
        share(h)
        if h == 1:
            for step in halo_steps:
                step()
            for step in token_steps:
                step()
        for take in passing:
            take()
        if h < chips - 1:
            passing = pass_on(h + 1)
    for own, every in pairs:
        for src, where in ((own, z == g), (every.at[core], z != g)):
            mail.post(
                src, every.at[core], sibling, here=where, there=where, landing=every.at[1 - core]
            )

    @pl.when(z == g)
    def _():
        for copy in held_copies:
            copy.wait()

    mail.finish()


def collect_inputs(tokens, halo, in_own, xproj, small, facts):
    groups, parts = lax.axis_size("group"), lax.axis_size("fsdp")
    ins = (tokens, halo, in_own, xproj, small, facts)
    outs = [
        jax.ShapeDtypeStruct((groups,) + tokens.shape, tokens.dtype),
        jax.ShapeDtypeStruct((groups,) + halo.shape, halo.dtype),
        jax.ShapeDtypeStruct((parts,) + in_own.shape, in_own.dtype),
        jax.ShapeDtypeStruct((2,) + xproj.shape, xproj.dtype),
        jax.ShapeDtypeStruct((2,) + small.shape, small.dtype),
        jax.ShapeDtypeStruct((groups, parts) + facts.shape, facts.dtype),
    ]
    ways = groups.bit_length() - 1
    copies = 3 * ways * (groups - 1) + (parts - 1) + 4 * (parts // 2 - 1) + 1 + 4 * (parts // 2 - 1) + 4
    outs = pl.pallas_call(
        functools.partial(collect, groups, parts),
        in_specs=[pl.BlockSpec(memory_space=pl.ANY)] * len(ins),
        out_specs=[pl.BlockSpec(memory_space=pl.ANY)] * len(outs),
        out_shape=outs,
        scratch_shapes=[
            pltpu.SemaphoreType.DMA((copies,)),
            pltpu.SemaphoreType.DMA((copies,)),
            pltpu.SemaphoreType.DMA((3,)),
        ],
        compiler_params=pltpu.CompilerParams(collective_id=1, has_side_effects=True),
        name="collect_inputs",
    )(*ins)
    all_tokens, all_halo, in_matrix, all_xproj, all_small, all_facts = outs
    return (
        all_tokens.at[0].set(tokens),
        all_halo.at[0].set(halo),
        lax.dynamic_update_index_in_dim(in_matrix, in_own, lax.axis_index("fsdp"), 0),
        all_xproj,
        all_small,
        all_facts,
    )


def runs(count, ways):
    edges = [count * i // ways for i in range(ways + 1)]
    return [pl.ds(lo, hi - lo) for lo, hi in zip(edges[:-1], edges[1:])]


def greet(groups):
    g = lax.axis_index("group")
    bits = [1 << i for i in range(groups.bit_length() - 1)]
    barrier = pltpu.get_barrier_semaphore()
    for bit in bits:
        pl.semaphore_signal(
            barrier, inc=1, device_id={"group": partner(g, bit)}, device_id_type=pl.DeviceIdType.MESH
        )
    pl.semaphore_wait(barrier, len(bits))
    return g, bits


def total_blocks(groups, terms, out, sums, parcel, landed, gathered, send_sem, recv_sem):
    g, bits = greet(groups)
    ways = len(bits)
    pieces = runs(terms.shape[1], ways)
    mail = Mail(send_sem, recv_sem)
    sums[...] = terms[...]
    held = [set(range(groups)) for _ in range(ways)]
    for t in range(ways):
        coming = []
        for p in range(ways):
            bit = bits[(p + t) % ways]
            for r in sorted(r for r in held[p] if r & bit):
                parcel[r, pieces[p]] = sums[r, pieces[p]].astype(parcel.dtype)
                take = mail.post(
                    parcel.at[r, pieces[p]],
                    landed.at[t, r ^ bit, pieces[p]],
                    {"group": partner(g, bit)},
                )
                coming.append((take, p, r ^ bit))
                held[p].remove(r)
        for take, p, r in coming:
            take()
            sums[r, pieces[p]] = sums[r, pieces[p]] + landed[t, r, pieces[p]].astype(F32)
    gathered[0] = sums[0].astype(gathered.dtype)
    known = [{0: None} for _ in range(ways)]
    for t in range(ways):
        for p in range(ways):
            bit = bits[(p + t) % ways]
            for r, take in list(known[p].items()):
                if take is not None:
                    take()
                known[p][r ^ bit] = mail.post(
                    gathered.at[r, pieces[p]],
                    gathered.at[r ^ bit, pieces[p]],
                    {"group": partner(g, bit)},
                )
    mail.finish()
    out[...] = gathered[...].astype(out.dtype)


def sum_blocks(terms, sent, result, number):
    groups = lax.axis_size("group")
    ways = groups.bit_length() - 1
    shape = (groups, terms.shape[0] // groups, terms.shape[1] * terms.shape[2], terms.shape[3])
    copies = 2 * ways * (groups - 1)
    return pl.pallas_call(
        functools.partial(total_blocks, groups),
        in_specs=[pl.BlockSpec(memory_space=pltpu.VMEM)],
        out_specs=pl.BlockSpec(memory_space=pltpu.VMEM),
        out_shape=jax.ShapeDtypeStruct(shape, result),
        scratch_shapes=[
            pltpu.VMEM(shape, F32),
            pltpu.VMEM(shape, sent),
            pltpu.VMEM((ways,) + shape, sent),
            pltpu.VMEM(shape, BF16),
            pltpu.SemaphoreType.DMA((copies,)),
            pltpu.SemaphoreType.DMA((copies,)),
        ],
        compiler_params=pltpu.CompilerParams(
            collective_id=number, has_side_effects=True, vmem_limit_bytes=32 * MIB
        ),
        cost_estimate=pl.CostEstimate(flops=30000 * terms.size // 2, bytes_accessed=8 * terms.size, transcendentals=0),
        name="sum_blocks",
    )(terms.reshape(shape)).reshape(terms.shape)


def front(
    halo_rows,
    info,
    tokens,
    halo,
    modulation,
    in_matrix,
    taps,
    conv_shift,
    xproj,
    modulated,
    extended,
    gate_z,
    conv_out,
    projected,
):
    slot = pl.program_id(0)
    length, model_width = tokens.shape
    channels = gate_z.shape[1]
    count, base = info[slot], info[pl.num_programs(0)]
    outs = (modulated, extended, gate_z, conv_out, projected)

    @pl.when(count <= base)
    def _():
        for out in outs:
            out[...] = jnp.zeros_like(out)

    @pl.when(count > base)
    def _():
        values = jnp.concatenate([tokens[...].astype(F32), halo[...].astype(F32)], axis=0)
        row = lax.broadcasted_iota(jnp.int32, (length + ROWS, 1), 0)
        behind, ahead = row - length - halo_rows, row - halo_rows
        at = jnp.where(row < length, row, jnp.where(behind < 0, behind, ahead))
        at = at + base
        known = (row < length + 2 * halo_rows) & (at >= 0) & (at < count)
        mask = known.astype(F32)
        centered = values - jnp.mean(values, axis=1, keepdims=True)
        normed = centered * lax.rsqrt(
            jnp.mean(centered * centered, axis=1, keepdims=True) + EPSILON
        )
        shift = modulation[:, :model_width]
        scale = modulation[:, model_width : 2 * model_width]
        low = ((normed * (1.0 + scale) + shift) * mask).astype(BF16)
        modulated[...] = low[:length]
        inner = dot32(low, in_matrix[...], ((1,), (0,)))
        gate_z[...] = inner[:length, channels:]
        extended[...] = jnp.zeros_like(extended)
        extended[ROWS : ROWS + length, :] = inner[:length, :channels]
        extended[ROWS - halo_rows : ROWS, :] = inner[length : length + halo_rows, :channels]
        extended[ROWS + length : ROWS + length + halo_rows, :] = inner[
            length + halo_rows : length + 2 * halo_rows, :channels
        ]
        for d in range(2):
            pre = conv_rows(extended, taps, conv_shift, d, length)
            value = (pre * jax.nn.sigmoid(pre) * mask[:length]).astype(BF16)
            conv_out[d] = value
            projected[d] = dot32(value, xproj[d], ((1,), (0,)))


def tap_row(d, k, kernel):
    return ROWS - (kernel - 1) + k if d == 0 else ROWS + (kernel - 1) - k


def conv_rows(extended, taps, conv_shift, d, length):
    kernel = taps.shape[1]
    pre = conv_shift[d : d + 1, :]
    for k in range(kernel):
        row = tap_row(d, k, kernel)
        pre = pre + taps[d, k : k + 1, :] * extended[row : row + length, :]
    return pre


def project(info, tokens, halo, modulation, in_matrix, taps, conv_shift, xproj):
    slots, length, model_width = tokens.shape
    channels = taps.shape[2]
    width = xproj.shape[2]
    fixed = lambda array: pl.BlockSpec(array.shape, lambda s, i: (0,) * array.ndim)
    one = lambda *tail: pl.BlockSpec((None,) + tail, lambda s, i: (s,) + (0,) * len(tail))
    return pl.pallas_call(
        functools.partial(front, taps.shape[1] - 1),
        grid_spec=pltpu.PrefetchScalarGridSpec(
            num_scalar_prefetch=1,
            grid=(slots,),
            in_specs=[
                one(length, model_width),
                one(ROWS, model_width),
                one(1, modulation.shape[2]),
                fixed(in_matrix),
                fixed(taps),
                fixed(conv_shift),
                fixed(xproj),
            ],
            out_specs=[
                one(length, model_width),
                one(length + 2 * ROWS, channels),
                one(length, channels),
                pl.BlockSpec((2, None, length, channels), lambda s, i: (0, s, 0, 0)),
                one(2, length, width),
            ],
        ),
        out_shape=[
            jax.ShapeDtypeStruct((slots, length, model_width), BF16),
            jax.ShapeDtypeStruct((slots, length + 2 * ROWS, channels), F32),
            jax.ShapeDtypeStruct((slots, length, channels), F32),
            jax.ShapeDtypeStruct((2, slots, length, channels), BF16),
            jax.ShapeDtypeStruct((slots, 2, length, width), F32),
        ],
        compiler_params=pltpu.CompilerParams(vmem_limit_bytes=40 * MIB),
        cost_estimate=pl.CostEstimate(
            flops=18000 * slots * length * channels,
            bytes_accessed=20 * slots * length * channels,
            transcendentals=0,
        ),
        name="project",
    )(info, tokens, halo, modulation, in_matrix, taps, conv_shift, xproj)


def back(
    info,
    extended,
    conv_grad,
    proj_grad,
    conv_out,
    taps,
    conv_shift,
    xproj,
    grad_x,
    rim,
    sums,
    xproj_grad,
    rows,
):
    slot = pl.program_id(0)
    length, channels = grad_x.shape
    kernel = taps.shape[1]
    halo = kernel - 1
    count, base = info[slot], info[pl.num_programs(0)]

    @pl.when(slot == 0)
    def _():
        sums[...] = jnp.zeros_like(sums)
        xproj_grad[...] = jnp.zeros_like(xproj_grad)
        rows[...] = jnp.zeros_like(rows)

    @pl.when(count <= base)
    def _():
        grad_x[...] = jnp.zeros_like(grad_x)
        rim[...] = jnp.zeros_like(rim)

    @pl.when(count > base)
    def _():
        row = lax.broadcasted_iota(jnp.int32, (length, 1), 0)
        mask = (base + row < count).astype(F32)
        for d in range(2):
            pre = conv_rows(extended, taps, conv_shift, d, length)
            sigmoid = jax.nn.sigmoid(pre)
            slope = sigmoid * (1.0 + pre * (1.0 - sigmoid))
            into = conv_grad[d] + dot32(proj_grad[d], xproj[d], ((1,), (1,)))
            value = into * mask * slope
            rows[d, ROWS : ROWS + length, :] = value
            turned = jnp.transpose(proj_grad[d].astype(F32)).astype(BF16)
            xproj_grad[d] += dot32(turned, conv_out[d], ((1,), (0,)))
            for k in range(kernel):
                first = tap_row(d, k, kernel)
                at = d * kernel + k
                sums[at : at + 1, :] += jnp.sum(
                    value * extended[first : first + length, :], axis=0, keepdims=True
                )
            at = 2 * kernel + d
            sums[at : at + 1, :] += jnp.sum(value, axis=0, keepdims=True)
        total = jnp.zeros((length, channels), F32)
        for k in range(kernel):
            ahead, behind = ROWS + halo - k, ROWS - halo + k
            total = total + taps[0, k : k + 1, :] * rows[0, ahead : ahead + length, :]
            total = total + taps[1, k : k + 1, :] * rows[1, behind : behind + length, :]
        grad_x[...] = total
        rim[0] = rows[0, ROWS : 2 * ROWS, :]
        rim[1] = rows[1, length : length + ROWS, :]


def back_through(info, extended, conv_grad, proj_grad, conv_out, taps, conv_shift, xproj):
    slots = extended.shape[0]
    length, channels = conv_out.shape[2:]
    width = xproj.shape[2]
    kernel = taps.shape[1]
    sum_rows = 2 * ROWS * ((2 * kernel + 2 + 2 * ROWS - 1) // (2 * ROWS))
    fixed = lambda array: pl.BlockSpec(array.shape, lambda s, i: (0,) * len(array.shape))
    one = lambda *tail: pl.BlockSpec((None,) + tail, lambda s, i: (s,) + (0,) * len(tail))
    both = pl.BlockSpec((2, None, length, channels), lambda s, i: (0, s, 0, 0))
    sums = jax.ShapeDtypeStruct((sum_rows, channels), F32)
    xproj_grad = jax.ShapeDtypeStruct((2, width, channels), F32)
    return pl.pallas_call(
        back,
        grid_spec=pltpu.PrefetchScalarGridSpec(
            num_scalar_prefetch=1,
            grid=(slots,),
            in_specs=[
                one(length + 2 * ROWS, channels),
                both,
                one(2, length, width),
                both,
                fixed(taps),
                fixed(conv_shift),
                fixed(xproj),
            ],
            out_specs=[one(length, channels), one(2, ROWS, channels), fixed(sums), fixed(xproj_grad)],
            scratch_shapes=[pltpu.VMEM((2, length + 2 * ROWS, channels), F32)],
        ),
        out_shape=[
            jax.ShapeDtypeStruct((slots, length, channels), F32),
            jax.ShapeDtypeStruct((slots, 2, ROWS, channels), F32),
            sums,
            xproj_grad,
        ],
        compiler_params=pltpu.CompilerParams(vmem_limit_bytes=32 * MIB),
        cost_estimate=pl.CostEstimate(
            flops=24000 * slots * length * channels,
            bytes_accessed=30 * slots * length * channels,
            transcendentals=0,
        ),
        name="back_through",
    )(info, extended, conv_grad, proj_grad, conv_out, taps, conv_shift, xproj)


def scatter(groups, terms, out, parcel, landed, send_sem, recv_sem):
    g, bits = greet(groups)
    ways = len(bits)
    pieces = runs(terms.shape[1], ways)
    mail = Mail(send_sem, recv_sem)
    held = [set(range(groups)) for _ in range(ways)]
    came = [{r: [] for r in range(groups)} for _ in range(ways)]

    def summed(p, r):
        value = terms[r, pieces[p]].astype(F32)
        for t, take in came[p][r]:
            take()
            value = value + landed[t, r, pieces[p]].astype(F32)
        return value

    for t in range(ways):
        for p in range(ways):
            bit = bits[(p + t) % ways]
            for r in sorted(r for r in held[p] if r & bit):
                src = terms
                if t:
                    parcel[r, pieces[p]] = summed(p, r).astype(parcel.dtype)
                    src = parcel
                take = mail.post(
                    src.at[r, pieces[p]],
                    landed.at[t, r ^ bit, pieces[p]],
                    {"group": partner(g, bit)},
                )
                came[p][r ^ bit].append((t, take))
                held[p].remove(r)
    for p in range(ways):
        out[pieces[p]] = summed(p, 0)
    mail.finish()


def scatter_blocks(terms, number):
    groups = lax.axis_size("group")
    ways = groups.bit_length() - 1
    slots, length, model_width = terms.shape
    block = (slots // groups, length, model_width)
    copies = ways * (groups - 1)
    return pl.pallas_call(
        functools.partial(scatter, groups),
        in_specs=[pl.BlockSpec(memory_space=pltpu.VMEM)],
        out_specs=pl.BlockSpec(memory_space=pltpu.VMEM),
        out_shape=jax.ShapeDtypeStruct(block, F32),
        scratch_shapes=[
            pltpu.VMEM((groups,) + block, terms.dtype),
            pltpu.VMEM((ways, groups) + block, terms.dtype),
            pltpu.SemaphoreType.DMA((copies,)),
            pltpu.SemaphoreType.DMA((copies,)),
        ],
        compiler_params=pltpu.CompilerParams(
            collective_id=number, has_side_effects=True, vmem_limit_bytes=48 * MIB
        ),
        cost_estimate=pl.CostEstimate(
            flops=20000 * terms.size, bytes_accessed=4 * terms.size, transcendentals=0
        ),
        name="scatter_blocks",
    )(terms.reshape((groups,) + block))


def finish(
    groups,
    parts,
    terms,
    in_x,
    in_z,
    packed,
    modulation,
    in_grad,
    out_grad,
    rest,
    landed,
    every_x,
    every_z,
    every_p,
    moved,
    send_sem,
    recv_sem,
):
    g, f = lax.axis_index("group"), lax.axis_index("fsdp")
    bits = [1 << i for i in range(groups.bit_length() - 1)]
    ways = len(bits)
    barrier = pltpu.get_barrier_semaphore()
    others = [{"group": partner(g, bit)} for bit in bits]
    others += [{"fsdp": lax.rem(f + k, parts)} for k in range(1, parts)]
    for other in others:
        pl.semaphore_signal(barrier, inc=1, device_id=other, device_id_type=pl.DeviceIdType.MESH)
    ratio = parts // groups
    target = {"group": lax.rem(f, groups), "fsdp": ratio * g + f // groups}
    source = {"group": f // ratio, "fsdp": groups * lax.rem(f, ratio) + g}
    stays = (target["group"] == g) & (target["fsdp"] == f)
    leaves = jnp.logical_not(stays)

    @pl.when(leaves)
    def _():
        pl.semaphore_signal(barrier, inc=1, device_id=source, device_id_type=pl.DeviceIdType.MESH)
        pl.semaphore_wait(barrier, len(others) + 1)

    @pl.when(stays)
    def _():
        pl.semaphore_wait(barrier, len(others))
        moved[...] = packed[...]

    mail = Mail(send_sem, recv_sem)
    arrived = mail.post(packed, moved, target, here=leaves, there=leaves)
    takes = []
    for k in range(1, parts):
        there = lax.rem(f + k, parts)
        takes.append(mail.post(terms.at[there], landed.at[k - 1], {"fsdp": there}))

    def absolute(r):
        at = g
        for bit in bits:
            at = partner(at, bit) if r & bit else at
        return at

    shards = ((in_x, every_x), (in_z, every_z), (moved, every_p))
    known = {}
    forwards = [[] for _ in range(ways)]
    later = [[] for _ in range(ways)]
    for own, every in shards[:2]:
        every[g] = own[...]
    for n, (own, every) in enumerate(shards):
        tiles = own.shape[1] // LANES
        for p in range(ways):
            lo, hi = (tiles * i // ways * LANES for i in (p, p + 1))
            held = [0]
            for t in range(ways):
                bit = bits[(p + t) % ways]
                for r in list(held):
                    move = (n, every, pl.ds(lo, hi - lo), p, r, bit)
                    (forwards if n < 2 else later)[t if r else 0].append(move)
                    held.append(r ^ bit)

    def run(moves):
        for n, every, cols, p, r, bit in moves:
            if r:
                known[n, p, r]()
            block = every.at[absolute(r), :, cols]
            known[n, p, r ^ bit] = mail.post(
                block,
                block,
                {"group": partner(g, bit)},
                landing=every.at[absolute(r ^ bit), :, cols],
            )

    run(forwards[0])
    total = terms[f]
    for k, take in enumerate(takes):
        take()
        total = total + landed[k]
    modulation[0] = total
    found = {0: None}
    for bit in bits:
        for r, take in list(found.items()):
            if take is not None:
                take()
            found[r ^ bit] = mail.post(
                modulation.at[r], modulation.at[r ^ bit], {"group": partner(g, bit)}
            )
    arrived()
    every_p[g] = moved[...]
    run(later[0])
    for moves in forwards[1:] + later[1:]:
        run(moves)
    mail.finish()
    channels = in_x.shape[1]
    piece, model_width = packed.shape[0], out_grad.shape[1]
    for j in range(groups):
        for h, every in enumerate((every_x, every_z)):
            at = (h * groups + j) * channels
            in_grad[:, at : at + channels] = every[j]
        out_grad[j * piece : (j + 1) * piece, :] = every_p[j, :, :model_width].astype(F32)
        rest[j * piece : (j + 1) * piece, :] = every_p[j, :, model_width:].astype(F32)


def finish_gradients(terms, in_x, in_z, packed, model_width, number):
    groups, parts = lax.axis_size("group"), lax.axis_size("fsdp")
    ways = groups.bit_length() - 1
    block = terms.shape[1:]
    copies = parts + groups - 1 + 3 * ways * (groups - 1)
    rows, channels = in_x.shape
    piece, wide = packed.shape
    return pl.pallas_call(
        functools.partial(finish, groups, parts),
        in_specs=[pl.BlockSpec(memory_space=pltpu.VMEM)] * 4,
        out_specs=[pl.BlockSpec(memory_space=pltpu.VMEM)] * 4,
        out_shape=[
            jax.ShapeDtypeStruct((groups,) + block, F32),
            jax.ShapeDtypeStruct((rows, 2 * groups * channels), BF16),
            jax.ShapeDtypeStruct((groups * piece, model_width), F32),
            jax.ShapeDtypeStruct((groups * piece, wide - model_width), F32),
        ],
        scratch_shapes=[
            pltpu.VMEM((parts - 1,) + block, F32),
            pltpu.VMEM((groups, rows, channels), BF16),
            pltpu.VMEM((groups, rows, channels), BF16),
            pltpu.VMEM((groups, piece, wide), BF16),
            pltpu.VMEM((piece, wide), BF16),
            pltpu.SemaphoreType.DMA((copies,)),
            pltpu.SemaphoreType.DMA((copies,)),
        ],
        compiler_params=pltpu.CompilerParams(
            collective_id=number, has_side_effects=True, vmem_limit_bytes=32 * MIB
        ),
        name="finish_gradients",
    )(terms, in_x, in_z, packed)


def to_owner(groups, parts):
    ratio = parts // groups
    pairs = []
    for g in range(groups):
        for f in range(parts):
            pairs.append((g * parts + f, (f // ratio) * parts + groups * (f % ratio) + g))
    return pairs


def cut(array, pieces):
    slots = array.shape[0]
    edges = [slots * i // pieces for i in range(pieces + 1)]
    return [array[lo:hi] for lo, hi in zip(edges[:-1], edges[1:])]


def flip(array, groups, bit):
    return lax.ppermute(array, "group", [(i, i ^ bit) for i in range(groups)])


def bits_of(groups, first):
    count = groups.bit_length() - 1
    return [1 << ((first + i) % count) for i in range(count)]


def scatter_stage(pieces, groups, t):
    nexts = []
    for p, held in enumerate(pieces):
        bit = bits_of(groups, p)[t]
        sums = {r: value for r, value in held.items() if not r & bit}
        for r in [r for r in held if r & bit]:
            came = flip(held[r], groups, bit).astype(F32)
            sums[r ^ bit] = (sums[r ^ bit].astype(F32) + came).astype(BF16)
        nexts.append(sums)
    return nexts


def on_device(
    tokens,
    item_bucket,
    slot_item,
    slot_live,
    slot_tokens,
    ada_weight,
    ada_bias,
    in_weight,
    conv_weight,
    conv_bias,
    xproj_weight,
    dt_weight,
    dt_bias,
    a_log,
    skip_gain,
    out_weight,
    cotangent,
):
    own_slots, length, model_width = tokens.shape
    groups, parts = lax.axis_size("group"), lax.axis_size("fsdp")
    g, f = lax.axis_index("group"), lax.axis_index("fsdp")
    slots = own_slots * groups
    inner_width = in_weight.shape[1] // 2
    channels = inner_width // groups
    kernel = conv_weight.shape[1]
    halo = kernel - 1
    rank_width = dt_weight.shape[1]
    width = xproj_weight.shape[2]
    states = (width - rank_width) // 2

    matches = slot_item[:, None] == jnp.arange(item_bucket.shape[0], dtype=jnp.int32)[None, :]
    own_buckets = jnp.sum(jnp.where(matches, item_bucket[None, :], 0), axis=1)
    own_condition = jax.nn.silu(time_embed(own_buckets, model_width)).astype(BF16)
    own_modulation = jnp.dot(own_condition, ada_weight, preferred_element_type=F32)
    own_modulation = own_modulation + ada_bias.astype(F32)
    plain = jnp.stack([slot_tokens * slot_live, own_buckets], axis=1).astype(F32)
    facts = jnp.concatenate([own_modulation, jnp.repeat(plain, LANES // 2, axis=1)], axis=1)

    edges = [(i, i + 1) for i in range(parts - 1)]
    before = lax.ppermute(tokens[:, length - halo :], "fsdp", edges)
    after = lax.ppermute(tokens[:, :halo], "fsdp", [(j, i) for i, j in edges])
    padding = jnp.zeros((own_slots, ROWS - 2 * halo, model_width), tokens.dtype)
    in_own = jnp.concatenate(
        [
            lax.dynamic_slice_in_dim(in_weight, h * inner_width + g * channels, channels, 1)
            for h in range(2)
        ],
        axis=1,
    )
    shard = out_weight.shape[0]
    small = jnp.concatenate(
        [
            dt_weight.reshape(2 * rank_width, shard),
            a_log.reshape(2 * states, shard),
            conv_weight.reshape(2 * kernel, shard),
            conv_bias,
            dt_bias,
            skip_gain,
        ],
        axis=0,
    )
    small_rows = small.shape[0]
    small_pad = -small_rows % LANES
    small = jnp.pad(small, ((0, -small_rows % BLOCK), (0, 0)))
    all_tokens, all_halo, in_matrix, all_xproj, all_small, all_facts = collect_inputs(
        tokens,
        jnp.concatenate([before, after, padding], axis=1),
        in_own,
        xproj_weight,
        small,
        facts,
    )
    ways = groups.bit_length() - 1
    all_tokens, late = lax.optimization_barrier((all_tokens, cotangent))
    travelling = [{0: part} for part in cut(late, ways)]
    for p, held in enumerate(travelling):
        for bit in bits_of(groups, p):
            held[bit] = flip(held[0], groups, bit)
    all_tokens = all_tokens.reshape(slots, length, model_width)
    all_halo = all_halo.reshape(slots, ROWS, model_width)
    in_matrix = in_matrix.reshape(model_width, 2 * channels)

    piece = shard // groups
    sent = lax.ppermute(
        lax.dynamic_slice_in_dim(out_weight, g * piece, piece, 0),
        ("group", "fsdp"),
        to_owner(groups, parts),
    )
    out_matrix = lax.all_gather(sent, "fsdp", axis=0, tiled=True)
    xproj = jnp.concatenate([all_xproj[0], all_xproj[1]], axis=1)
    rest = jnp.concatenate([all_small[0], all_small[1]], axis=1)
    edge = 0

    def take(rows):
        nonlocal edge
        edge += rows
        return rest[edge - rows : edge]

    dt_matrix = jnp.pad(
        take(2 * rank_width).reshape(2, rank_width, channels), ((0, 0), (0, width - rank_width), (0, 0))
    )
    rate = -jnp.exp(take(2 * states).astype(F32)).reshape(2, states // ROWS, ROWS, channels)
    taps = take(2 * kernel).reshape(2, kernel, channels).astype(F32)
    conv_shift = take(2).astype(F32)
    dt_shift = take(2).astype(F32).reshape(2, 1, channels)
    skip = take(2).astype(F32).reshape(2, 1, channels)
    decay = rate * LOG2E

    columns = facts.shape[1] - LANES
    plain = all_facts[:, 0, :, columns:].reshape(slots, LANES).astype(jnp.int32)
    counts, buckets = plain[:, 0], plain[:, LANES // 2]
    modulation = all_facts[:, :, :, :columns].transpose(0, 2, 1, 3).reshape(slots, parts * columns)
    group_counts = jnp.sum(counts.reshape(groups, own_slots), axis=1).astype(F32)
    share = jnp.repeat(group_counts / jnp.sum(group_counts), own_slots)
    positions = f * length + jnp.arange(length, dtype=jnp.int32)
    mask = (positions[None, :] < counts[:, None]).astype(F32)
    active = (counts > f * length).astype(jnp.int32)
    own_mask = mask[:own_slots, :, None]
    own_share = share[:own_slots, None, None]
    condition = jax.nn.silu(time_embed(buckets, model_width)).astype(BF16)
    shift_mod = modulation[:, None, :model_width]
    scale_mod = modulation[:, None, model_width : 2 * model_width]
    gate_mod = modulation[:, None, 2 * model_width :]

    info = jnp.concatenate([counts, (f * length)[None]]).astype(jnp.int32)
    modulated, wide_x, gate_z, conv_out, projected = project(
        info, all_tokens, all_halo, modulation[:, None, :], in_matrix, taps, conv_shift, xproj
    )
    travelling, projected = lax.optimization_barrier((travelling, projected))
    for p, held in enumerate(travelling):
        order = bits_of(groups, p)
        for t in range(1, ways):
            for r in [r for r in held if r and r < groups and all(r & bit == 0 for bit in order[t:])]:
                held[r ^ order[t]] = flip(held[r], groups, order[t])
    proj = sum_blocks(projected, BF16, F32, 2)
    proj, travelling = lax.optimization_barrier((proj, travelling))
    all_cotangent = jnp.concatenate([held[r] for r in range(groups) for held in travelling], axis=0)

    def normalise(values):
        inputs = values.astype(F32)
        centered = inputs - jnp.mean(inputs, axis=2, keepdims=True)
        inv_std = lax.rsqrt(jnp.mean(centered * centered, axis=2, keepdims=True) + EPSILON)
        return (inputs, centered * inv_std, inv_std)

    grad_in_all = all_cotangent.astype(F32) * (mask * share[:, None])[:, :, None]
    branch_gradient = (grad_in_all * gate_mod).astype(BF16)
    grad_gated = jnp.einsum("sld,cd->slc", branch_gradient, out_matrix, preferred_element_type=F32)
    grad_y = grad_gated * jax.nn.silu(gate_z)

    step, end, pull, total, mix_b, mix_c = scan_ends(active, conv_out, proj, grad_y, dt_matrix, dt_shift, decay)
    entering = pass_states(end, pull, total, decay)
    gated_output, grad_z, conv_grad, proj_part, dtw_grad, dtb_grad, decay_grad, skip_grad = scan_all(
        active,
        conv_out,
        proj,
        grad_y,
        step,
        mix_b,
        mix_c,
        entering,
        gate_z,
        grad_gated,
        dt_matrix,
        decay,
        skip,
    )
    proj_grad = sum_blocks(proj_part, BF16, BF16, 3)
    alog_grad = (decay_grad * rate).reshape(2 * states, channels)

    branch_part = jnp.einsum("slc,cd->sld", gated_output, out_matrix, preferred_element_type=F32)
    inward_z = jnp.einsum("sld,slc->dc", modulated, grad_z, preferred_element_type=F32)
    branch_part, inward_z, proj_grad = lax.optimization_barrier(
        (branch_part.astype(BF16), inward_z.astype(BF16), proj_grad)
    )
    inward_z = lax.psum_scatter(inward_z, "fsdp", scatter_dimension=0, tiled=True)
    ways = groups.bit_length() - 1
    cut_blocks = [cut(block, ways) for block in jnp.split(branch_part, groups, axis=0)]
    moving = [{r: cut_blocks[r][p] for r in range(groups)} for p in range(ways)]
    moving = scatter_stage(moving, groups, 0)
    outward = jnp.einsum("slc,sld->cd", gated_output, branch_gradient, preferred_element_type=F32)

    grad_x, rim, conv_sums, xproj_grads = back_through(
        info, wide_x, conv_grad, proj_grad, conv_out, taps, conv_shift, xproj
    )
    outward, moving, rim, inward_z = lax.optimization_barrier(
        (outward.astype(BF16), moving, rim, inward_z)
    )
    ahead = lax.ppermute(rim[:, 0, :halo], "fsdp", [(j, i) for i, j in edges])
    behind = lax.ppermute(rim[:, 1, ROWS - halo :], "fsdp", edges)
    zeros = jnp.zeros_like(ahead)
    ahead, behind = jnp.concatenate([zeros, ahead], 1), jnp.concatenate([behind, zeros], 1)
    last = sum(taps[0, k] * ahead[:, halo - k : 2 * halo - k] for k in range(kernel))
    first = sum(taps[1, k] * behind[:, k : k + halo] for k in range(kernel))
    grad_x = grad_x + jnp.concatenate(
        [first, jnp.zeros((slots, length - 2 * halo, channels), F32), last], axis=1
    )
    grad_x = grad_x.astype(BF16)
    inner_gradient = jnp.concatenate([grad_x, grad_z], axis=2)
    inward = jnp.einsum("sld,slc->dc", modulated, grad_x, preferred_element_type=F32)
    grad_mod_part = jnp.einsum(
        "slc,dc->sld", inner_gradient, in_matrix, preferred_element_type=F32
    ).astype(BF16)
    for t in range(1, ways):
        moving = scatter_stage(moving, groups, t)
    branch = jnp.concatenate([held[0] for held in moving], axis=0)
    small_grads = jnp.concatenate(
        [
            xproj_grads.reshape(2 * width, channels),
            dtw_grad[:, :rank_width].reshape(2 * rank_width, channels),
            alog_grad,
            conv_sums[: 2 * kernel + 2],
            dtb_grad.reshape(2, channels),
            skip_grad.reshape(2, channels),
            jnp.zeros((small_pad, channels), F32),
        ],
        axis=0,
    ).astype(BF16)
    packed_grads = jnp.concatenate([outward, small_grads.T], axis=1)
    packed_piece = lax.psum_scatter(packed_grads, "fsdp", scatter_dimension=0, tiled=True)
    inward, grad_mod_part, branch, packed_piece = lax.optimization_barrier(
        (inward.astype(BF16), grad_mod_part, branch, packed_piece)
    )
    branch = branch.astype(F32)
    grad_mod = scatter_blocks(grad_mod_part, 4) * own_mask

    own_gate = gate_mod[:own_slots]
    own_scale = scale_mod[:own_slots]
    own_inputs, own_normed, own_inv = normalise(tokens)
    layer_out = ((own_inputs + own_gate * branch) * own_mask).astype(BF16)
    grad_in = cotangent.astype(F32) * own_mask * own_share
    grad_gate = jnp.sum(grad_in * branch, axis=1)

    grad_shift = jnp.sum(grad_mod, axis=1)
    grad_scale = jnp.sum(grad_mod * own_normed, axis=1)
    grad_normed = grad_mod * (1.0 + own_scale)
    grad_ln = own_inv * (
        grad_normed
        - jnp.mean(grad_normed, axis=2, keepdims=True)
        - own_normed * jnp.mean(grad_normed * own_normed, axis=2, keepdims=True)
    )
    tokens_grad = grad_in + grad_ln

    mod_part = jnp.concatenate([grad_shift, grad_scale, grad_gate], axis=1)
    inward_x = lax.psum_scatter(inward, "fsdp", scatter_dimension=0, tiled=True)
    mod_terms = mod_part.reshape(own_slots, parts, -1).transpose(1, 0, 2)
    mod_all, in_grad, out_grad, packed_own = finish_gradients(
        mod_terms, inward_x, inward_z, packed_piece, model_width, 5
    )
    in_grad = in_grad.astype(F32)
    mod_all = mod_all.reshape(slots, -1)
    ada_grad = jnp.einsum("sd,sk->dk", condition, mod_all.astype(BF16), preferred_element_type=F32)
    adab_grad = jnp.sum(mod_all, axis=0)
    xproj_grad = jnp.stack(
        [packed_own[:, d * width : (d + 1) * width] for d in range(2)]
    )
    rest_grads = packed_own[:, 2 * width :].T
    sizes = [2 * rank_width, 2 * states, 2 * kernel, 2, 2, 2]
    cuts = [sum(sizes[:i]) for i in range(len(sizes) + 1)]
    dtw_out, alog_out, conv_w_out, conv_b_out, dtb_out, skip_out = [
        rest_grads[cuts[i] : cuts[i + 1]] for i in range(len(sizes))
    ]
    return (
        layer_out,
        tokens_grad,
        ada_grad,
        adab_grad,
        in_grad,
        conv_w_out.reshape(2, kernel, shard),
        conv_b_out,
        xproj_grad,
        dtw_out.reshape(2, rank_width, shard),
        dtb_out,
        alog_out.reshape(2, states, shard),
        skip_out,
        out_grad,
    )


def solution(mesh):
    in_specs = (
        P("group", "fsdp", None),
        P(),
        P("group"),
        P("group"),
        P("group"),
        P(None, "fsdp"),
        P("fsdp"),
        P("fsdp", None),
        P(None, None, "fsdp"),
        P(None, "fsdp"),
        P(None, "fsdp", None),
        P(None, None, "fsdp"),
        P(None, "fsdp"),
        P(None, None, "fsdp"),
        P(None, "fsdp"),
        P("fsdp", None),
        P("group", "fsdp", None),
    )
    out_specs = (
        P("group", "fsdp", None),
        P("group", "fsdp", None),
        P(None, "fsdp"),
        P("fsdp"),
        P("fsdp", None),
        P(None, None, "fsdp"),
        P(None, "fsdp"),
        P(None, "fsdp", None),
        P(None, None, "fsdp"),
        P(None, "fsdp"),
        P(None, None, "fsdp"),
        P(None, "fsdp"),
        P("fsdp", None),
    )
    return jax.shard_map(
        on_device, mesh=mesh, in_specs=in_specs, out_specs=out_specs, check_vma=False
    )
```

```python
import functools
import math

import jax
import jax.numpy as jnp
from jax import lax
from jax.experimental import pallas as pl
from jax.experimental.pallas import tpu as pltpu
from jax.sharding import PartitionSpec as P

EPSILON = 1e-06
LANES = 128
ROWS = 8
BLOCK = 16
WIDE = 256
LAG = 3
RUN = 2
LOG2E = math.log2(math.e)
LN2 = math.log(2.0)
F32 = jnp.float32
BF16 = jnp.bfloat16
MIB = 1 << 20


def time_embed(buckets, model_width):
    half_width = model_width // 2
    frequency = jnp.exp(-math.log(10000.0) * jnp.arange(half_width, dtype=F32) / half_width)
    angles = buckets.astype(F32)[:, None] * frequency[None, :]
    return jnp.concatenate([jnp.cos(angles), jnp.sin(angles)], axis=1)


def silu_slope(values):
    sigmoid = jax.nn.sigmoid(values)
    return sigmoid * (1.0 + values * (1.0 - sigmoid))


def dot32(left, right, dims):
    return lax.dot_general(left, right, (dims, ((), ())), preferred_element_type=F32)


def pass_one(
    states, active, conv, proj, grad_y, dt_w, dt_b, decay, step, end, pull, total, mix_b, mix_c, drive, turned
):
    slot, direction = pl.program_id(0), pl.program_id(1)
    length, channels = drive.shape
    chunks = channels // LANES
    halves = states // ROWS
    rank = proj.shape[1] - 2 * states

    @pl.when(active[slot] == 0)
    def _():
        end[...] = jnp.zeros_like(end)
        pull[...] = jnp.zeros_like(pull)
        total[...] = jnp.zeros_like(total)

    @pl.when(active[slot] != 0)
    def _():
        pre = dot32(proj[...].astype(BF16), dt_w[direction], ((1,), (0,))) + dt_b[direction]
        steps = jnp.maximum(pre, 0.0) + jnp.log(1.0 + jnp.exp(-jnp.abs(pre)))
        step[...] = steps
        drive[...] = steps * conv[...].astype(F32)
        total[...] = jnp.broadcast_to(jnp.sum(steps, axis=0, keepdims=True), total.shape)

        def turn(i, carry):
            at = pl.multiple_of(i * ROWS, ROWS)
            turned[i] = jnp.transpose(proj[pl.ds(at, ROWS), :])[rank : rank + 2 * states]
            return carry

        lax.fori_loop(0, length // ROWS, turn, 0, unroll=True)
        zero = jnp.zeros((halves, ROWS, LANES), F32)
        for backward in range(2):

            @pl.when(direction == backward)
            def _():
                carry = ((zero,) * chunks, (zero + 1.0,) * chunks, (zero,) * chunks)
                rates = [decay[direction, :, :, k : k + LANES] for k in range(0, channels, LANES)]

                def block(i, carry):
                    at = length // ROWS - 1 - i if backward else i
                    rows = pl.ds(pl.multiple_of(at * ROWS, ROWS), ROWS)
                    held = [ref[rows, :] for ref in (step, drive, grad_y)]
                    hidden, running, pulled = carry
                    columns = turned[at]
                    for j in list(range(ROWS))[:: -1 if backward else 1]:
                        t = at * ROWS + j
                        wide = jnp.broadcast_to(columns[:, j : j + 1], (2 * states, LANES))
                        b = wide[:states].reshape(halves, ROWS, LANES)
                        c = wide[states:].reshape(halves, ROWS, LANES)
                        mix_b[t] = b
                        mix_c[t] = c
                        rowed = [
                            [
                                jnp.broadcast_to(h[j : j + 1, k : k + LANES], (ROWS, LANES))[None]
                                for k in range(0, channels, LANES)
                            ]
                            for h in held
                        ]
                        new = ([], [], [])
                        for k in range(chunks):
                            factor = jnp.exp2(rowed[0][k] * rates[k])
                            new[0].append(factor * hidden[k] + rowed[1][k] * b)
                            run = running[k] * factor
                            new[1].append(run)
                            new[2].append(pulled[k] + run * (rowed[2][k] * c))
                        hidden, running, pulled = new
                    return (tuple(hidden), tuple(running), tuple(pulled))

                hidden, _, pulled = lax.fori_loop(0, length // ROWS, block, carry)
                for k in range(chunks):
                    lanes = slice(k * LANES, (k + 1) * LANES)
                    end[:, :, lanes] = hidden[k]
                    pull[:, :, lanes] = pulled[k]


def pass_two(
    states,
    active,
    conv,
    proj,
    grad_y,
    step,
    mix_b,
    mix_c,
    entry,
    arrive,
    gate_z,
    grad_gated,
    dt_w,
    decay,
    skip,
    tile_b,
    tile_c,
    sel,
    take_b,
    take_c,
    gated,
    grad_z,
    conv_grad,
    proj_grad,
    dtw_grad,
    dtb_grad,
    alog_grad,
    skip_grad,
    drive,
    hid_even,
    hid_odd,
    edge,
    gst_even,
    gst_odd,
    thd_even,
    thd_odd,
    mixed,
    sdec,
    scan_y,
    in_part,
    out_part,
    rows_b,
    rows_c,
    drive_low,
    grad_low,
    y,
):
    slot, direction = pl.program_id(0), pl.program_id(1)
    length, channels = drive.shape
    chunks = channels // LANES
    halves = states // ROWS
    wide = BLOCK * states
    pairs = length // (2 * BLOCK)
    hid, gst, thd = (hid_even, hid_odd), (gst_even, gst_odd), (thd_even, thd_odd)
    lanes = [slice(k * LANES, (k + 1) * LANES) for k in range(chunks)]

    @pl.when((slot == 0) & (direction == 0))
    def _():
        dtw_grad[...] = jnp.zeros_like(dtw_grad)
        dtb_grad[...] = jnp.zeros_like(dtb_grad)
        alog_grad[...] = jnp.zeros_like(alog_grad)
        skip_grad[...] = jnp.zeros_like(skip_grad)

    @pl.when(direction == 0)
    def _():
        y[...] = jnp.zeros_like(y)

    @pl.when(active[slot] == 0)
    def _():
        conv_grad[...] = jnp.zeros_like(conv_grad)
        proj_grad[...] = jnp.zeros_like(proj_grad)
        gated[...] = jnp.zeros_like(gated)
        grad_z[...] = jnp.zeros_like(grad_z)

    def low(value):
        return value.reshape(states, LANES).astype(BF16)

    def block_range(pair, odd):
        return pl.ds(pl.multiple_of((2 * pair + odd) * BLOCK, BLOCK), BLOCK)

    def sweep_blocks(backward, tokens, matmuls, start):
        first, second = (1, 0) if backward else (0, 1)

        def two(i, carry):
            pair = pairs - 1 - i if backward else i
            before = lax.rem(pair + (1 if backward else pairs - 1), pairs)
            carry = tokens(pair, first, backward, matmuls(before, second), carry)
            return tokens(pair, second, backward, matmuls(pair, first), carry)

        carry = lax.fori_loop(0, pairs, two, start)
        for issue, keep in matmuls(0 if backward else pairs - 1, second):
            keep(issue())
        return carry

    def pieces(out, rows, left, right, dims, width):
        made = []
        for n in range(0, width, WIDE):
            cols = slice(n, min(n + WIDE, width))
            picked = right[:, cols] if dims[1] == (0,) else right

            def issue(left=left, picked=picked):
                return dot32(left, picked, dims)

            def keep(product, cols=cols):
                out[rows, cols] = product

            made.append((issue, keep))
        return made

    def scan_rows(pair, odd, backward, refs, body, beside, carry):
        order = list(range(BLOCK))[:: -1 if backward else 1]
        waiting = []
        for at_step, j in enumerate(order):
            if j % ROWS == (ROWS - 1 if backward else 0):
                at = pl.multiple_of((2 * pair + odd) * BLOCK + j // ROWS * ROWS, ROWS)
                held = [ref[pl.ds(at, ROWS), :] for ref in refs]
            i = j % ROWS
            rows = [
                [jnp.broadcast_to(h[i : i + 1, c], (ROWS, LANES))[None] for c in lanes] for h in held
            ]
            for issue, keep in beside[at_step * len(beside) // BLOCK : (at_step + 1) * len(beside) // BLOCK]:
                waiting.append((at_step + LAG, keep, issue()))
            carry = body(j, rows, carry)
            while waiting and waiting[0][0] <= at_step:
                _, keep, product = waiting.pop(0)
                keep(product)
        for _, keep, product in waiting:
            keep(product)
        return carry

    def forward_tokens(pair, odd, backward, beside, hidden):
        for k in range(chunks):
            edge[2 * pair + odd, :, lanes[k]] = low(hidden[k])

        def token(j, rows, hidden):
            b = mix_b[(2 * pair + odd) * BLOCK + j]
            new = []
            for k in range(chunks):
                factor = jnp.exp2(rows[0][k] * decay[direction, :, :, lanes[k]])
                value = factor * hidden[k] + rows[1][k] * b
                hid[odd][pair, j, :, lanes[k]] = low(value)
                new.append(value)
            return tuple(new)

        return scan_rows(pair, odd, backward, (step, drive), token, beside, hidden)

    def forward_matmuls(pair, odd):
        rows = block_range(pair, odd)
        h_rows = hid[odd][pair].reshape(wide, channels)
        return pieces(scan_y, rows, rows_c[rows, :], h_rows, ((1,), (0,)), channels) + pieces(
            out_part, rows, grad_low[rows, :], h_rows, ((1,), (1,)), wide
        )

    def backward_tokens(pair, odd, backward, beside, carry):
        earlier = -1 if backward else 1

        def token(j, rows, carry):
            carried, total = carry
            c = mix_c[(2 * pair + odd) * BLOCK + j]
            news, sums = [], []
            p = j + earlier
            for k in range(chunks):
                rate = decay[direction, :, :, lanes[k]]
                factor = jnp.exp2(rows[0][k] * rate)
                grad_state = rows[1][k] * c + carried[k]
                gst[odd][j, :, lanes[k]] = low(grad_state)
                onward = factor * grad_state
                if 0 <= p < BLOCK:
                    before = hid[odd][pair, p, :, lanes[k]]
                else:
                    before = edge[2 * pair + odd, :, lanes[k]]
                through = onward * before.astype(F32).reshape(halves, ROWS, LANES)
                sums.append(total[k] + through * rows[0][k])
                thd[odd][j, :, lanes[k]] = low(through * rate)
                news.append(onward)
            return (tuple(news), tuple(sums))

        return scan_rows(pair, odd, backward, (step, grad_y), token, beside, carry)

    def backward_matmuls(pair, odd):
        rows = block_range(pair, odd)
        g_rows = gst[odd][...].reshape(wide, channels)
        t_rows = thd[odd][...].reshape(wide, channels)
        return (
            pieces(mixed, rows, rows_b[rows, :], g_rows, ((1,), (0,)), channels)
            + pieces(sdec, rows, sel[...].astype(BF16), t_rows, ((1,), (0,)), channels)
            + pieces(in_part, rows, drive_low[rows, :], g_rows, ((1,), (1,)), wide)
        )

    @pl.when(active[slot] != 0)
    def _():
        drive[...] = step[...] * conv[...].astype(F32)
        drive_low[...] = drive[...].astype(BF16)
        grad_low[...] = grad_y[...].astype(BF16)
        proj_low = proj[...].astype(BF16)
        picked = jnp.concatenate([sel[...]] * (length // BLOCK), axis=0)
        rows_b[...] = (dot32(proj_low, tile_b[...], ((1,), (0,))) * picked).astype(BF16)
        rows_c[...] = (dot32(proj_low, tile_c[...], ((1,), (0,))) * picked).astype(BF16)
        zero = jnp.zeros((halves, ROWS, LANES), F32)
        for reverse in (False, True):

            @pl.when(direction == int(reverse))
            def _():
                start = tuple(entry[:, :, c].astype(F32) for c in lanes)
                sweep_blocks(reverse, forward_tokens, forward_matmuls, start)
                start = (tuple(arrive[:, :, c].astype(F32) for c in lanes), (zero,) * chunks)
                _, sums = sweep_blocks(not reverse, backward_tokens, backward_matmuls, start)
                for k in range(chunks):
                    alog_grad[direction, :, :, lanes[k]] += sums[k]

        conv_values = conv[...].astype(F32)
        steps = step[...]
        grads = grad_y[...]
        step_grad = conv_values * mixed[...] + LN2 * sdec[...]
        pre_grad = step_grad * (1.0 - jnp.exp(-steps))
        dtb_grad[direction] += jnp.sum(pre_grad, axis=0, keepdims=True)
        pre_low = pre_grad.astype(BF16)
        proj_grad[...] = (
            dot32((in_part[...] * picked).astype(BF16), take_b[...], ((1,), (0,)))
            + dot32((out_part[...] * picked).astype(BF16), take_c[...], ((1,), (0,)))
            + dot32(pre_low, dt_w[direction], ((1,), (1,)))
        )
        dtw_grad[direction] += dot32(jnp.transpose(proj[...]).astype(BF16), pre_low, ((1,), (0,)))
        y[...] += scan_y[...] + skip[direction] * conv_values
        skip_grad[direction] += jnp.sum(grads * conv_values, axis=0, keepdims=True)
        conv_grad[...] = grads * skip[direction] + steps * mixed[...]

        @pl.when(direction == 1)
        def _():
            total = y[...]
            value = gate_z[...]
            sigmoid = jax.nn.sigmoid(value)
            gated[...] = (total * (value * sigmoid)).astype(BF16)
            slope = sigmoid * (1.0 + value * (1.0 - sigmoid))
            grad_z[...] = (grad_gated[...] * total * slope).astype(BF16)


def whole(array):
    zeros = (0,) * array.ndim
    return pl.BlockSpec(array.shape, lambda s, d, a: zeros)


def scan_ends(active, conv, proj, grad_y, dt_w, dt_b, decay):
    slots, length, channels = grad_y.shape
    halves = decay.shape[1]
    width = proj.shape[3]
    states = halves * ROWS
    turn = lambda *tail: pl.BlockSpec((None, None) + tail, lambda s, d, a: (s, d) + (0,) * len(tail))
    pair = lambda *tail: pl.BlockSpec((None, None) + tail, lambda s, d, a: (d, s) + (0,) * len(tail))
    state = (2, slots, halves, ROWS, channels)
    mixes = (length, halves, ROWS, LANES)
    spare = lambda s, a: jnp.where(a[s] != 0, s, slots)
    kept_pair = pl.BlockSpec(
        (None, None, length, channels), lambda s, d, a: (jnp.where(a[s] != 0, d, 0), spare(s, a), 0, 0)
    )
    kept_mix = pl.BlockSpec(
        (None, None) + mixes, lambda s, d, a: (spare(s, a), jnp.where(a[s] != 0, d, 0), 0, 0, 0, 0)
    )
    return pl.pallas_call(
        functools.partial(pass_one, states),
        grid_spec=pltpu.PrefetchScalarGridSpec(
            num_scalar_prefetch=1,
            grid=(slots, 2),
            in_specs=[
                pair(length, channels),
                turn(length, width),
                pl.BlockSpec((None, length, channels), lambda s, d, a: (s, 0, 0)),
                whole(dt_w),
                whole(dt_b),
                whole(decay),
            ],
            out_specs=[
                kept_pair,
                pair(halves, ROWS, channels),
                pair(halves, ROWS, channels),
                pair(ROWS, channels),
                kept_mix,
                kept_mix,
            ],
            scratch_shapes=[
                pltpu.VMEM((length, channels), F32),
                pltpu.VMEM((length // ROWS, 2 * states, ROWS), F32),
            ],
        ),
        out_shape=[
            jax.ShapeDtypeStruct((2, slots + 1, length, channels), F32),
            jax.ShapeDtypeStruct(state, F32),
            jax.ShapeDtypeStruct(state, F32),
            jax.ShapeDtypeStruct((2, slots, ROWS, channels), F32),
            jax.ShapeDtypeStruct((slots + 1, 2) + mixes, F32),
            jax.ShapeDtypeStruct((slots + 1, 2) + mixes, F32),
        ],
        compiler_params=pltpu.CompilerParams(vmem_limit_bytes=24 * MIB),
        name="scan_ends",
    )(active, conv, proj, grad_y, dt_w, dt_b, decay)


def scan_all(
    active, conv, proj, grad_y, step, mix_b, mix_c, entering, gate_z, grad_gated, dt_w, decay, skip
):
    slots, length, channels = grad_y.shape
    halves = decay.shape[1]
    width = proj.shape[3]
    states = halves * ROWS
    wide = BLOCK * states
    rank = width - 2 * states
    column = jnp.arange(width)[:, None]
    lane = jnp.arange(wide)[None, :]
    tile_b = (column == rank + lane % states).astype(BF16)
    tile_c = (column == rank + states + lane % states).astype(BF16)
    sel = (jnp.arange(BLOCK)[:, None] == lane // states).astype(F32)
    turn = lambda *tail: pl.BlockSpec((None, None) + tail, lambda s, d, a: (s, d) + (0,) * len(tail))
    pair = lambda *tail: pl.BlockSpec((None, None) + tail, lambda s, d, a: (d, s) + (0,) * len(tail))
    one = pl.BlockSpec((None, length, channels), lambda s, d, a: (s, 0, 0))
    constants = (dt_w, decay, skip, tile_b, tile_c, sel, tile_b.T, tile_c.T)
    sums = (
        jax.ShapeDtypeStruct((2, width, channels), F32),
        jax.ShapeDtypeStruct((2, 1, channels), F32),
        jax.ShapeDtypeStruct((2, halves, ROWS, channels), F32),
        jax.ShapeDtypeStruct((2, 1, channels), F32),
    )
    pairs = length // (2 * BLOCK)
    read_s = lambda s, a: jnp.where(a[s] != 0, s, 0)
    read_d = lambda s, d, a: jnp.where(a[s] != 0, d, 0)
    got_one = pl.BlockSpec((None, length, channels), lambda s, d, a: (read_s(s, a), 0, 0))

    def got_pair(*tail):
        return pl.BlockSpec(
            (None, None) + tail, lambda s, d, a: (read_d(s, d, a), read_s(s, a)) + (0,) * len(tail)
        )

    def got_turn(*tail):
        return pl.BlockSpec(
            (None, None) + tail, lambda s, d, a: (read_s(s, a), read_d(s, d, a)) + (0,) * len(tail)
        )

    def got_state(kind):
        def place(s, d, a):
            way = read_d(s, d, a)
            return (way + kind * (1 - 2 * way), read_s(s, a), kind, 0, 0, 0)

        return pl.BlockSpec((None, None, None, halves, ROWS, channels), place)

    return pl.pallas_call(
        functools.partial(pass_two, states),
        grid_spec=pltpu.PrefetchScalarGridSpec(
            num_scalar_prefetch=1,
            grid=(slots, 2),
            in_specs=[
                got_pair(length, channels),
                got_turn(length, width),
                got_one,
                got_pair(length, channels),
                got_turn(length, halves, ROWS, LANES),
                got_turn(length, halves, ROWS, LANES),
                got_state(0),
                got_state(1),
                got_one,
                got_one,
            ]
            + [whole(c) for c in constants],
            out_specs=[one, one, pair(length, channels), turn(length, width)] + [whole(c) for c in sums],
            scratch_shapes=[pltpu.VMEM((length, channels), F32)]
            + [pltpu.VMEM((pairs, BLOCK, states, channels), BF16)] * 2
            + [pltpu.VMEM((2 * pairs, states, channels), BF16)]
            + [pltpu.VMEM((BLOCK, states, channels), BF16)] * 4
            + [pltpu.VMEM((length, channels), F32)] * 3
            + [pltpu.VMEM((length, wide), F32)] * 2
            + [pltpu.VMEM((length, wide), BF16)] * 2
            + [pltpu.VMEM((length, channels), BF16)] * 2
            + [pltpu.VMEM((length, channels), F32)],
        ),
        out_shape=[
            jax.ShapeDtypeStruct((slots, length, channels), BF16),
            jax.ShapeDtypeStruct((slots, length, channels), BF16),
            jax.ShapeDtypeStruct((2, slots, length, channels), F32),
            jax.ShapeDtypeStruct((slots, 2, length, width), F32),
        ]
        + list(sums),
        compiler_params=pltpu.CompilerParams(vmem_limit_bytes=44 * MIB),
        name="scan_all",
    )(active, conv, proj, grad_y, step, mix_b, mix_c, entering, entering, gate_z, grad_gated, *constants)


def chain(count, run, end, pull, total, decay, entering, held, send_sem, recv_sem):
    mine = lax.axis_index("fsdp")
    waves = end.shape[1] // run
    mesh_id = pl.DeviceIdType.MESH
    after, before = lax.rem(mine + 1, count), lax.rem(mine + count - 1, count)
    barrier = pltpu.get_barrier_semaphore()
    for other in (after, before):
        pl.semaphore_signal(barrier, inc=1, device_id={"fsdp": other}, device_id_type=mesh_id)
    pl.semaphore_wait(barrier, 2)
    ways = ((mine > 0, mine < count - 1, after), (mine < count - 1, mine > 0, before))

    def copy(way, s):
        slots = pl.ds(s * run, run)
        return pltpu.make_async_remote_copy(
            src_ref=held.at[way, slots],
            dst_ref=entering.at[way, slots],
            send_sem=send_sem.at[way, s],
            recv_sem=recv_sem.at[way, s],
            device_id={"fsdp": ways[way][2]},
            device_id_type=mesh_id,
        )

    lags = (mine, count - 1 - mine)

    def wave(turn, carry):
        for way in range(2):
            gets, sends, _ = ways[way]
            s = turn - lags[way]
            here = (s >= 0) & (s < waves)

            @pl.when(here & gets)
            def _():
                copy(way, s).wait_recv()

            @pl.when(here & jnp.logical_not(gets))
            def _():
                entering[way, pl.ds(s * run, run)] = jnp.zeros((run,) + entering.shape[2:], entering.dtype)

            @pl.when(here & sends)
            def _():
                for i in range(run):
                    slot = s * run + i
                    for kind, local in enumerate((end, pull)):
                        d = (way + kind) % 2
                        through = jnp.exp2(decay[d] * total[d, slot][None])
                        value = through * entering[way, slot, kind].astype(F32) + local[d, slot]
                        held[way, slot, kind] = value.astype(held.dtype)
                copy(way, s).start()

        return carry

    lax.fori_loop(0, waves + count - 1, wave, 0)

    def drain(s, carry):
        for way in range(2):

            @pl.when(ways[way][1])
            def _():
                copy(way, s).wait_send()

        return carry

    lax.fori_loop(0, waves, drain, 0)


def pass_states(end, pull, total, decay):
    _, slots, halves, rows, channels = end.shape
    run = RUN
    shape = (2, slots, 2, halves, rows, channels)
    return pl.pallas_call(
        functools.partial(chain, lax.axis_size("fsdp"), run),
        in_specs=[pl.BlockSpec(memory_space=pltpu.VMEM)] * 4,
        out_specs=pl.BlockSpec(memory_space=pltpu.VMEM),
        out_shape=jax.ShapeDtypeStruct(shape, BF16),
        scratch_shapes=[
            pltpu.VMEM(shape, BF16),
            pltpu.SemaphoreType.DMA((2, slots // run)),
            pltpu.SemaphoreType.DMA((2, slots // run)),
        ],
        compiler_params=pltpu.CompilerParams(
            collective_id=0, has_side_effects=True, vmem_limit_bytes=40 * MIB
        ),
        name="pass_states",
    )(end, pull, total, decay)


def partner(g, bit):
    return g + bit * (1 - 2 * lax.rem(g // bit, 2))


class Mail:
    def __init__(self, send_sem, recv_sem):
        self.send_sem, self.recv_sem, self.made = send_sem, recv_sem, []

    def post(self, src, dst, target, here=None, there=None, landing=None):
        n = len(self.made)
        copy = lambda into: pltpu.make_async_remote_copy(
            src_ref=src,
            dst_ref=into,
            send_sem=self.send_sem.at[n],
            recv_sem=self.recv_sem.at[n],
            device_id=target,
            device_id_type=pl.DeviceIdType.MESH,
        )
        when = lambda cond: (lambda body: body()) if cond is None else pl.when(cond)
        landing = dst if landing is None else landing
        entry = dict(got=False)

        @when(here)
        def _():
            copy(dst).start()

        def take():
            if not entry["got"]:
                entry["got"] = True

                @when(there)
                def _():
                    copy(landing).wait_recv()

        def sent():
            @when(here)
            def _():
                copy(dst).wait_send()

        self.made.append((take, sent))
        return take

    def finish(self):
        for take, _ in self.made:
            take()
        for _, sent in self.made:
            sent()


def collect(
    groups,
    parts,
    tokens,
    halo,
    in_own,
    xproj,
    small,
    facts,
    all_tokens,
    all_halo,
    in_matrix,
    all_xproj,
    all_small,
    all_facts,
    send_sem,
    recv_sem,
    own_sem,
):
    g, f = lax.axis_index("group"), lax.axis_index("fsdp")
    chips = parts // 2
    z, core = f // 2, lax.rem(f, 2)
    ways = groups.bit_length() - 1
    bits = [1 << i for i in range(ways)]
    barrier = pltpu.get_barrier_semaphore()
    for bit in bits:
        pl.semaphore_signal(
            barrier, inc=1, device_id={"group": partner(g, bit)}, device_id_type=pl.DeviceIdType.MESH
        )
    for k in range(1, parts):
        pl.semaphore_signal(
            barrier,
            inc=1,
            device_id={"fsdp": lax.rem(f + k, parts)},
            device_id_type=pl.DeviceIdType.MESH,
        )
    pl.semaphore_wait(barrier, ways + parts - 1)
    mail = Mail(send_sem, recv_sem)
    place = lambda part: lax.rem(part + 2 * parts, parts)
    sibling = {"fsdp": f + 1 - 2 * core}
    up, down = {"fsdp": f + 2}, {"fsdp": f - 2}

    fact_takes = []
    for k in range(1, parts):
        fact_takes.append(
            mail.post(
                facts,
                all_facts.at[0, f],
                {"fsdp": lax.rem(f + k, parts)},
                landing=all_facts.at[0, lax.rem(f + parts - k, parts)],
            )
        )

    def cuts(count):
        edges = [count * i // ways for i in range(ways + 1)]
        return [pl.ds(lo, hi - lo) for lo, hi in zip(edges[:-1], edges[1:])]

    def relative(own, every, count):
        pieces = cuts(count)
        held = [{0: None} for _ in range(ways)]
        steps = [[] for _ in range(ways)]
        for t in range(ways):
            for p in range(ways):
                bit = bits[(p + t) % ways]
                for r in list(held[p]):
                    held[p][r ^ bit] = None
                    steps[t].append((p, r, bit))
        takes = {}

        def run(chosen):
            for p, r, bit in chosen:
                if r:
                    takes[p, r]()
                src = own.at[pieces[p]] if r == 0 else every.at[r, pieces[p]]
                takes[p, r ^ bit] = mail.post(
                    src, every.at[r ^ bit, pieces[p]], {"group": partner(g, bit)}
                )

        run([move for step in steps for move in step if move[1] == 0])
        return [functools.partial(run, [move for move in step if move[1]]) for step in steps[1:]]

    token_steps = relative(tokens, all_tokens, tokens.shape[0])
    halo_steps = relative(halo, all_halo, halo.shape[0])

    line = []

    def hop(h):
        for sign, target, inside in ((1, up, z < chips - 1), (-1, down, z > 0)):
            shard = f - sign * 2 * (h - 1)
            src = in_own if h == 1 else in_matrix.at[place(shard)]
            far = z - sign * (h - 1)
            come = z - sign * h
            line.append(
                mail.post(
                    src,
                    in_matrix.at[place(shard)],
                    target,
                    here=inside & (far >= 0) & (far < chips),
                    there=(come >= 0) & (come < chips),
                    landing=in_matrix.at[place(f - sign * 2 * h)],
                )
            )

    def share(h):
        for sign in (1, -1):
            shard = place(f - sign * 2 * h)
            come = z - sign * h
            known = (come >= 0) & (come < chips)
            mail.post(
                in_own if h == 0 else in_matrix.at[shard],
                in_matrix.at[shard],
                sibling,
                here=known,
                there=known,
                landing=in_matrix.at[place(f + 1 - 2 * core - sign * 2 * h)],
            )
            if h == 0:
                break

    hop(1)
    share(0)

    own_fact = pltpu.make_async_copy(facts, all_facts.at[0, f], own_sem.at[0])
    own_fact.start()
    held_copies = [
        pltpu.make_async_copy(xproj, all_xproj.at[core], own_sem.at[1]),
        pltpu.make_async_copy(small, all_small.at[core], own_sem.at[2]),
    ]

    @pl.when(z == g)
    def _():
        for copy in held_copies:
            copy.start()

    own_fact.wait()
    for take in fact_takes:
        take()
    fact_steps = relative(all_facts.at[0], all_facts, parts)

    for step in fact_steps:
        step()

    pairs = ((xproj, all_xproj), (small, all_small))

    def pass_on(distance):
        takes = []
        for sign, target in ((1, up), (-1, down)):
            sender = g + sign * (distance - 1)
            here = (z == sender) & (sender + sign >= 0) & (sender + sign < chips)
            there = z == sender + sign
            for own, every in pairs:
                src = own if distance == 1 else every.at[core]
                takes.append(mail.post(src, every.at[core], target, here=here, there=there))
        return takes

    passing = pass_on(1)
    for h in range(1, chips):
        for take in line[-2:]:
            take()
        if h < chips - 1:
            hop(h + 1)
        share(h)
        if h == 1:
            for step in halo_steps:
                step()
            for step in token_steps:
                step()
        for take in passing:
            take()
        if h < chips - 1:
            passing = pass_on(h + 1)
    for own, every in pairs:
        for src, where in ((own, z == g), (every.at[core], z != g)):
            mail.post(
                src, every.at[core], sibling, here=where, there=where, landing=every.at[1 - core]
            )

    @pl.when(z == g)
    def _():
        for copy in held_copies:
            copy.wait()

    mail.finish()


def collect_inputs(tokens, halo, in_own, xproj, small, facts):
    groups, parts = lax.axis_size("group"), lax.axis_size("fsdp")
    ins = (tokens, halo, in_own, xproj, small, facts)
    outs = [
        jax.ShapeDtypeStruct((groups,) + tokens.shape, tokens.dtype),
        jax.ShapeDtypeStruct((groups,) + halo.shape, halo.dtype),
        jax.ShapeDtypeStruct((parts,) + in_own.shape, in_own.dtype),
        jax.ShapeDtypeStruct((2,) + xproj.shape, xproj.dtype),
        jax.ShapeDtypeStruct((2,) + small.shape, small.dtype),
        jax.ShapeDtypeStruct((groups, parts) + facts.shape, facts.dtype),
    ]
    ways = groups.bit_length() - 1
    copies = 3 * ways * (groups - 1) + (parts - 1) + 4 * (parts // 2 - 1) + 1 + 4 * (parts // 2 - 1) + 4
    outs = pl.pallas_call(
        functools.partial(collect, groups, parts),
        in_specs=[pl.BlockSpec(memory_space=pl.ANY)] * len(ins),
        out_specs=[pl.BlockSpec(memory_space=pl.ANY)] * len(outs),
        out_shape=outs,
        scratch_shapes=[
            pltpu.SemaphoreType.DMA((copies,)),
            pltpu.SemaphoreType.DMA((copies,)),
            pltpu.SemaphoreType.DMA((3,)),
        ],
        compiler_params=pltpu.CompilerParams(collective_id=1, has_side_effects=True),
        name="collect_inputs",
    )(*ins)
    all_tokens, all_halo, in_matrix, all_xproj, all_small, all_facts = outs
    return (
        all_tokens.at[0].set(tokens),
        all_halo.at[0].set(halo),
        lax.dynamic_update_index_in_dim(in_matrix, in_own, lax.axis_index("fsdp"), 0),
        all_xproj,
        all_small,
        all_facts,
    )


def runs(count, ways):
    edges = [count * i // ways for i in range(ways + 1)]
    return [pl.ds(lo, hi - lo) for lo, hi in zip(edges[:-1], edges[1:])]


def greet(groups):
    g = lax.axis_index("group")
    bits = [1 << i for i in range(groups.bit_length() - 1)]
    barrier = pltpu.get_barrier_semaphore()
    for bit in bits:
        pl.semaphore_signal(
            barrier, inc=1, device_id={"group": partner(g, bit)}, device_id_type=pl.DeviceIdType.MESH
        )
    pl.semaphore_wait(barrier, len(bits))
    return g, bits


def total_blocks(groups, terms, out, sums, parcel, landed, gathered, send_sem, recv_sem):
    g, bits = greet(groups)
    ways = len(bits)
    pieces = runs(terms.shape[1], ways)
    mail = Mail(send_sem, recv_sem)
    sums[...] = terms[...]
    held = [set(range(groups)) for _ in range(ways)]
    for t in range(ways):
        coming = []
        for p in range(ways):
            bit = bits[(p + t) % ways]
            for r in sorted(r for r in held[p] if r & bit):
                parcel[r, pieces[p]] = sums[r, pieces[p]].astype(parcel.dtype)
                take = mail.post(
                    parcel.at[r, pieces[p]],
                    landed.at[t, r ^ bit, pieces[p]],
                    {"group": partner(g, bit)},
                )
                coming.append((take, p, r ^ bit))
                held[p].remove(r)
        for take, p, r in coming:
            take()
            sums[r, pieces[p]] = sums[r, pieces[p]] + landed[t, r, pieces[p]].astype(F32)
    gathered[0] = sums[0].astype(gathered.dtype)
    known = [{0: None} for _ in range(ways)]
    for t in range(ways):
        for p in range(ways):
            bit = bits[(p + t) % ways]
            for r, take in list(known[p].items()):
                if take is not None:
                    take()
                known[p][r ^ bit] = mail.post(
                    gathered.at[r, pieces[p]],
                    gathered.at[r ^ bit, pieces[p]],
                    {"group": partner(g, bit)},
                )
    mail.finish()
    out[...] = gathered[...].astype(out.dtype)


def sum_blocks(terms, sent, result, number):
    groups = lax.axis_size("group")
    ways = groups.bit_length() - 1
    shape = (groups, terms.shape[0] // groups, terms.shape[1] * terms.shape[2], terms.shape[3])
    copies = 2 * ways * (groups - 1)
    return pl.pallas_call(
        functools.partial(total_blocks, groups),
        in_specs=[pl.BlockSpec(memory_space=pltpu.VMEM)],
        out_specs=pl.BlockSpec(memory_space=pltpu.VMEM),
        out_shape=jax.ShapeDtypeStruct(shape, result),
        scratch_shapes=[
            pltpu.VMEM(shape, F32),
            pltpu.VMEM(shape, sent),
            pltpu.VMEM((ways,) + shape, sent),
            pltpu.VMEM(shape, BF16),
            pltpu.SemaphoreType.DMA((copies,)),
            pltpu.SemaphoreType.DMA((copies,)),
        ],
        compiler_params=pltpu.CompilerParams(
            collective_id=number, has_side_effects=True, vmem_limit_bytes=32 * MIB
        ),
        cost_estimate=pl.CostEstimate(flops=30000 * terms.size // 2, bytes_accessed=8 * terms.size, transcendentals=0),
        name="sum_blocks",
    )(terms.reshape(shape)).reshape(terms.shape)


def front(
    halo_rows,
    info,
    tokens,
    halo,
    modulation,
    in_matrix,
    taps,
    conv_shift,
    xproj,
    modulated,
    extended,
    gate_z,
    conv_out,
    projected,
):
    slot = pl.program_id(0)
    length, model_width = tokens.shape
    channels = gate_z.shape[1]
    count, base = info[slot], info[pl.num_programs(0)]
    outs = (modulated, extended, gate_z, conv_out, projected)

    @pl.when(count <= base)
    def _():
        for out in outs:
            out[...] = jnp.zeros_like(out)

    @pl.when(count > base)
    def _():
        values = jnp.concatenate([tokens[...].astype(F32), halo[...].astype(F32)], axis=0)
        row = lax.broadcasted_iota(jnp.int32, (length + ROWS, 1), 0)
        behind, ahead = row - length - halo_rows, row - halo_rows
        at = jnp.where(row < length, row, jnp.where(behind < 0, behind, ahead))
        at = at + base
        known = (row < length + 2 * halo_rows) & (at >= 0) & (at < count)
        mask = known.astype(F32)
        centered = values - jnp.mean(values, axis=1, keepdims=True)
        normed = centered * lax.rsqrt(
            jnp.mean(centered * centered, axis=1, keepdims=True) + EPSILON
        )
        shift = modulation[:, :model_width]
        scale = modulation[:, model_width : 2 * model_width]
        low = ((normed * (1.0 + scale) + shift) * mask).astype(BF16)
        modulated[...] = low[:length]
        inner = dot32(low, in_matrix[...], ((1,), (0,)))
        gate_z[...] = inner[:length, channels:]
        extended[...] = jnp.zeros_like(extended)
        extended[ROWS : ROWS + length, :] = inner[:length, :channels]
        extended[ROWS - halo_rows : ROWS, :] = inner[length : length + halo_rows, :channels]
        extended[ROWS + length : ROWS + length + halo_rows, :] = inner[
            length + halo_rows : length + 2 * halo_rows, :channels
        ]
        for d in range(2):
            pre = conv_rows(extended, taps, conv_shift, d, length)
            value = (pre * jax.nn.sigmoid(pre) * mask[:length]).astype(BF16)
            conv_out[d] = value
            projected[d] = dot32(value, xproj[d], ((1,), (0,)))


def tap_row(d, k, kernel):
    return ROWS - (kernel - 1) + k if d == 0 else ROWS + (kernel - 1) - k


def conv_rows(extended, taps, conv_shift, d, length):
    kernel = taps.shape[1]
    pre = conv_shift[d : d + 1, :]
    for k in range(kernel):
        row = tap_row(d, k, kernel)
        pre = pre + taps[d, k : k + 1, :] * extended[row : row + length, :]
    return pre


def project(info, tokens, halo, modulation, in_matrix, taps, conv_shift, xproj):
    slots, length, model_width = tokens.shape
    channels = taps.shape[2]
    width = xproj.shape[2]
    fixed = lambda array: pl.BlockSpec(array.shape, lambda s, i: (0,) * array.ndim)
    one = lambda *tail: pl.BlockSpec((None,) + tail, lambda s, i: (s,) + (0,) * len(tail))
    return pl.pallas_call(
        functools.partial(front, taps.shape[1] - 1),
        grid_spec=pltpu.PrefetchScalarGridSpec(
            num_scalar_prefetch=1,
            grid=(slots,),
            in_specs=[
                one(length, model_width),
                one(ROWS, model_width),
                one(1, modulation.shape[2]),
                fixed(in_matrix),
                fixed(taps),
                fixed(conv_shift),
                fixed(xproj),
            ],
            out_specs=[
                one(length, model_width),
                one(length + 2 * ROWS, channels),
                one(length, channels),
                pl.BlockSpec((2, None, length, channels), lambda s, i: (0, s, 0, 0)),
                one(2, length, width),
            ],
        ),
        out_shape=[
            jax.ShapeDtypeStruct((slots, length, model_width), BF16),
            jax.ShapeDtypeStruct((slots, length + 2 * ROWS, channels), F32),
            jax.ShapeDtypeStruct((slots, length, channels), F32),
            jax.ShapeDtypeStruct((2, slots, length, channels), BF16),
            jax.ShapeDtypeStruct((slots, 2, length, width), F32),
        ],
        compiler_params=pltpu.CompilerParams(vmem_limit_bytes=40 * MIB),
        cost_estimate=pl.CostEstimate(
            flops=18000 * slots * length * channels,
            bytes_accessed=20 * slots * length * channels,
            transcendentals=0,
        ),
        name="project",
    )(info, tokens, halo, modulation, in_matrix, taps, conv_shift, xproj)


def back(
    info,
    extended,
    conv_grad,
    proj_grad,
    conv_out,
    taps,
    conv_shift,
    xproj,
    grad_x,
    rim,
    sums,
    xproj_grad,
    rows,
):
    slot = pl.program_id(0)
    length, channels = grad_x.shape
    kernel = taps.shape[1]
    halo = kernel - 1
    count, base = info[slot], info[pl.num_programs(0)]

    @pl.when(slot == 0)
    def _():
        sums[...] = jnp.zeros_like(sums)
        xproj_grad[...] = jnp.zeros_like(xproj_grad)
        rows[...] = jnp.zeros_like(rows)

    @pl.when(count <= base)
    def _():
        grad_x[...] = jnp.zeros_like(grad_x)
        rim[...] = jnp.zeros_like(rim)

    @pl.when(count > base)
    def _():
        row = lax.broadcasted_iota(jnp.int32, (length, 1), 0)
        mask = (base + row < count).astype(F32)
        for d in range(2):
            pre = conv_rows(extended, taps, conv_shift, d, length)
            sigmoid = jax.nn.sigmoid(pre)
            slope = sigmoid * (1.0 + pre * (1.0 - sigmoid))
            into = conv_grad[d] + dot32(proj_grad[d], xproj[d], ((1,), (1,)))
            value = into * mask * slope
            rows[d, ROWS : ROWS + length, :] = value
            turned = jnp.transpose(proj_grad[d].astype(F32)).astype(BF16)
            xproj_grad[d] += dot32(turned, conv_out[d], ((1,), (0,)))
            for k in range(kernel):
                first = tap_row(d, k, kernel)
                at = d * kernel + k
                sums[at : at + 1, :] += jnp.sum(
                    value * extended[first : first + length, :], axis=0, keepdims=True
                )
            at = 2 * kernel + d
            sums[at : at + 1, :] += jnp.sum(value, axis=0, keepdims=True)
        total = jnp.zeros((length, channels), F32)
        for k in range(kernel):
            ahead, behind = ROWS + halo - k, ROWS - halo + k
            total = total + taps[0, k : k + 1, :] * rows[0, ahead : ahead + length, :]
            total = total + taps[1, k : k + 1, :] * rows[1, behind : behind + length, :]
        grad_x[...] = total
        rim[0] = rows[0, ROWS : 2 * ROWS, :]
        rim[1] = rows[1, length : length + ROWS, :]


def back_through(info, extended, conv_grad, proj_grad, conv_out, taps, conv_shift, xproj):
    slots = extended.shape[0]
    length, channels = conv_out.shape[2:]
    width = xproj.shape[2]
    kernel = taps.shape[1]
    sum_rows = 2 * ROWS * ((2 * kernel + 2 + 2 * ROWS - 1) // (2 * ROWS))
    fixed = lambda array: pl.BlockSpec(array.shape, lambda s, i: (0,) * len(array.shape))
    one = lambda *tail: pl.BlockSpec((None,) + tail, lambda s, i: (s,) + (0,) * len(tail))
    both = pl.BlockSpec((2, None, length, channels), lambda s, i: (0, s, 0, 0))
    sums = jax.ShapeDtypeStruct((sum_rows, channels), F32)
    xproj_grad = jax.ShapeDtypeStruct((2, width, channels), F32)
    return pl.pallas_call(
        back,
        grid_spec=pltpu.PrefetchScalarGridSpec(
            num_scalar_prefetch=1,
            grid=(slots,),
            in_specs=[
                one(length + 2 * ROWS, channels),
                both,
                one(2, length, width),
                both,
                fixed(taps),
                fixed(conv_shift),
                fixed(xproj),
            ],
            out_specs=[one(length, channels), one(2, ROWS, channels), fixed(sums), fixed(xproj_grad)],
            scratch_shapes=[pltpu.VMEM((2, length + 2 * ROWS, channels), F32)],
        ),
        out_shape=[
            jax.ShapeDtypeStruct((slots, length, channels), F32),
            jax.ShapeDtypeStruct((slots, 2, ROWS, channels), F32),
            sums,
            xproj_grad,
        ],
        compiler_params=pltpu.CompilerParams(vmem_limit_bytes=32 * MIB),
        cost_estimate=pl.CostEstimate(
            flops=24000 * slots * length * channels,
            bytes_accessed=30 * slots * length * channels,
            transcendentals=0,
        ),
        name="back_through",
    )(info, extended, conv_grad, proj_grad, conv_out, taps, conv_shift, xproj)


def scatter(groups, terms, out, parcel, landed, send_sem, recv_sem):
    g, bits = greet(groups)
    ways = len(bits)
    pieces = runs(terms.shape[1], ways)
    mail = Mail(send_sem, recv_sem)
    held = [set(range(groups)) for _ in range(ways)]
    came = [{r: [] for r in range(groups)} for _ in range(ways)]

    def summed(p, r):
        value = terms[r, pieces[p]].astype(F32)
        for t, take in came[p][r]:
            take()
            value = value + landed[t, r, pieces[p]].astype(F32)
        return value

    for t in range(ways):
        for p in range(ways):
            bit = bits[(p + t) % ways]
            for r in sorted(r for r in held[p] if r & bit):
                src = terms
                if t:
                    parcel[r, pieces[p]] = summed(p, r).astype(parcel.dtype)
                    src = parcel
                take = mail.post(
                    src.at[r, pieces[p]],
                    landed.at[t, r ^ bit, pieces[p]],
                    {"group": partner(g, bit)},
                )
                came[p][r ^ bit].append((t, take))
                held[p].remove(r)
    for p in range(ways):
        out[pieces[p]] = summed(p, 0)
    mail.finish()


def scatter_blocks(terms, number):
    groups = lax.axis_size("group")
    ways = groups.bit_length() - 1
    slots, length, model_width = terms.shape
    block = (slots // groups, length, model_width)
    copies = ways * (groups - 1)
    return pl.pallas_call(
        functools.partial(scatter, groups),
        in_specs=[pl.BlockSpec(memory_space=pltpu.VMEM)],
        out_specs=pl.BlockSpec(memory_space=pltpu.VMEM),
        out_shape=jax.ShapeDtypeStruct(block, F32),
        scratch_shapes=[
            pltpu.VMEM((groups,) + block, terms.dtype),
            pltpu.VMEM((ways, groups) + block, terms.dtype),
            pltpu.SemaphoreType.DMA((copies,)),
            pltpu.SemaphoreType.DMA((copies,)),
        ],
        compiler_params=pltpu.CompilerParams(
            collective_id=number, has_side_effects=True, vmem_limit_bytes=48 * MIB
        ),
        cost_estimate=pl.CostEstimate(
            flops=20000 * terms.size, bytes_accessed=4 * terms.size, transcendentals=0
        ),
        name="scatter_blocks",
    )(terms.reshape((groups,) + block))


def finish(
    groups,
    parts,
    terms,
    in_x,
    in_z,
    packed,
    modulation,
    in_grad,
    out_grad,
    rest,
    landed,
    every_x,
    every_z,
    every_p,
    moved,
    send_sem,
    recv_sem,
):
    g, f = lax.axis_index("group"), lax.axis_index("fsdp")
    bits = [1 << i for i in range(groups.bit_length() - 1)]
    ways = len(bits)
    barrier = pltpu.get_barrier_semaphore()
    others = [{"group": partner(g, bit)} for bit in bits]
    others += [{"fsdp": lax.rem(f + k, parts)} for k in range(1, parts)]
    for other in others:
        pl.semaphore_signal(barrier, inc=1, device_id=other, device_id_type=pl.DeviceIdType.MESH)
    ratio = parts // groups
    target = {"group": lax.rem(f, groups), "fsdp": ratio * g + f // groups}
    source = {"group": f // ratio, "fsdp": groups * lax.rem(f, ratio) + g}
    stays = (target["group"] == g) & (target["fsdp"] == f)
    leaves = jnp.logical_not(stays)

    @pl.when(leaves)
    def _():
        pl.semaphore_signal(barrier, inc=1, device_id=source, device_id_type=pl.DeviceIdType.MESH)
        pl.semaphore_wait(barrier, len(others) + 1)

    @pl.when(stays)
    def _():
        pl.semaphore_wait(barrier, len(others))
        moved[...] = packed[...]

    mail = Mail(send_sem, recv_sem)
    arrived = mail.post(packed, moved, target, here=leaves, there=leaves)
    takes = []
    for k in range(1, parts):
        there = lax.rem(f + k, parts)
        takes.append(mail.post(terms.at[there], landed.at[k - 1], {"fsdp": there}))

    def absolute(r):
        at = g
        for bit in bits:
            at = partner(at, bit) if r & bit else at
        return at

    shards = ((in_x, every_x), (in_z, every_z), (moved, every_p))
    known = {}
    forwards = [[] for _ in range(ways)]
    later = [[] for _ in range(ways)]
    for own, every in shards[:2]:
        every[g] = own[...]
    for n, (own, every) in enumerate(shards):
        tiles = own.shape[1] // LANES
        for p in range(ways):
            lo, hi = (tiles * i // ways * LANES for i in (p, p + 1))
            held = [0]
            for t in range(ways):
                bit = bits[(p + t) % ways]
                for r in list(held):
                    move = (n, every, pl.ds(lo, hi - lo), p, r, bit)
                    (forwards if n < 2 else later)[t if r else 0].append(move)
                    held.append(r ^ bit)

    def run(moves):
        for n, every, cols, p, r, bit in moves:
            if r:
                known[n, p, r]()
            block = every.at[absolute(r), :, cols]
            known[n, p, r ^ bit] = mail.post(
                block,
                block,
                {"group": partner(g, bit)},
                landing=every.at[absolute(r ^ bit), :, cols],
            )

    run(forwards[0])
    total = terms[f]
    for k, take in enumerate(takes):
        take()
        total = total + landed[k]
    modulation[0] = total
    found = {0: None}
    for bit in bits:
        for r, take in list(found.items()):
            if take is not None:
                take()
            found[r ^ bit] = mail.post(
                modulation.at[r], modulation.at[r ^ bit], {"group": partner(g, bit)}
            )
    arrived()
    every_p[g] = moved[...]
    run(later[0])
    for moves in forwards[1:] + later[1:]:
        run(moves)
    mail.finish()
    channels = in_x.shape[1]
    piece, model_width = packed.shape[0], out_grad.shape[1]
    for j in range(groups):
        for h, every in enumerate((every_x, every_z)):
            at = (h * groups + j) * channels
            in_grad[:, at : at + channels] = every[j]
        out_grad[j * piece : (j + 1) * piece, :] = every_p[j, :, :model_width].astype(F32)
        rest[j * piece : (j + 1) * piece, :] = every_p[j, :, model_width:].astype(F32)


def finish_gradients(terms, in_x, in_z, packed, model_width, number):
    groups, parts = lax.axis_size("group"), lax.axis_size("fsdp")
    ways = groups.bit_length() - 1
    block = terms.shape[1:]
    copies = parts + groups - 1 + 3 * ways * (groups - 1)
    rows, channels = in_x.shape
    piece, wide = packed.shape
    return pl.pallas_call(
        functools.partial(finish, groups, parts),
        in_specs=[pl.BlockSpec(memory_space=pltpu.VMEM)] * 4,
        out_specs=[pl.BlockSpec(memory_space=pltpu.VMEM)] * 4,
        out_shape=[
            jax.ShapeDtypeStruct((groups,) + block, F32),
            jax.ShapeDtypeStruct((rows, 2 * groups * channels), BF16),
            jax.ShapeDtypeStruct((groups * piece, model_width), F32),
            jax.ShapeDtypeStruct((groups * piece, wide - model_width), F32),
        ],
        scratch_shapes=[
            pltpu.VMEM((parts - 1,) + block, F32),
            pltpu.VMEM((groups, rows, channels), BF16),
            pltpu.VMEM((groups, rows, channels), BF16),
            pltpu.VMEM((groups, piece, wide), BF16),
            pltpu.VMEM((piece, wide), BF16),
            pltpu.SemaphoreType.DMA((copies,)),
            pltpu.SemaphoreType.DMA((copies,)),
        ],
        compiler_params=pltpu.CompilerParams(
            collective_id=number, has_side_effects=True, vmem_limit_bytes=32 * MIB
        ),
        name="finish_gradients",
    )(terms, in_x, in_z, packed)


def to_owner(groups, parts):
    ratio = parts // groups
    pairs = []
    for g in range(groups):
        for f in range(parts):
            pairs.append((g * parts + f, (f // ratio) * parts + groups * (f % ratio) + g))
    return pairs


def cut(array, pieces):
    slots = array.shape[0]
    edges = [slots * i // pieces for i in range(pieces + 1)]
    return [array[lo:hi] for lo, hi in zip(edges[:-1], edges[1:])]


def flip(array, groups, bit):
    return lax.ppermute(array, "group", [(i, i ^ bit) for i in range(groups)])


def bits_of(groups, first):
    count = groups.bit_length() - 1
    return [1 << ((first + i) % count) for i in range(count)]


def scatter_stage(pieces, groups, t):
    nexts = []
    for p, held in enumerate(pieces):
        bit = bits_of(groups, p)[t]
        sums = {r: value for r, value in held.items() if not r & bit}
        for r in [r for r in held if r & bit]:
            came = flip(held[r], groups, bit).astype(F32)
            sums[r ^ bit] = (sums[r ^ bit].astype(F32) + came).astype(BF16)
        nexts.append(sums)
    return nexts


def on_device(
    tokens,
    item_bucket,
    slot_item,
    slot_live,
    slot_tokens,
    ada_weight,
    ada_bias,
    in_weight,
    conv_weight,
    conv_bias,
    xproj_weight,
    dt_weight,
    dt_bias,
    a_log,
    skip_gain,
    out_weight,
    cotangent,
):
    own_slots, length, model_width = tokens.shape
    groups, parts = lax.axis_size("group"), lax.axis_size("fsdp")
    g, f = lax.axis_index("group"), lax.axis_index("fsdp")
    slots = own_slots * groups
    inner_width = in_weight.shape[1] // 2
    channels = inner_width // groups
    kernel = conv_weight.shape[1]
    halo = kernel - 1
    rank_width = dt_weight.shape[1]
    width = xproj_weight.shape[2]
    states = (width - rank_width) // 2

    matches = slot_item[:, None] == jnp.arange(item_bucket.shape[0], dtype=jnp.int32)[None, :]
    own_buckets = jnp.sum(jnp.where(matches, item_bucket[None, :], 0), axis=1)
    own_condition = jax.nn.silu(time_embed(own_buckets, model_width)).astype(BF16)
    own_modulation = jnp.dot(own_condition, ada_weight, preferred_element_type=F32)
    own_modulation = own_modulation + ada_bias.astype(F32)
    plain = jnp.stack([slot_tokens * slot_live, own_buckets], axis=1).astype(F32)
    facts = jnp.concatenate([own_modulation, jnp.repeat(plain, LANES // 2, axis=1)], axis=1)

    edges = [(i, i + 1) for i in range(parts - 1)]
    before = lax.ppermute(tokens[:, length - halo :], "fsdp", edges)
    after = lax.ppermute(tokens[:, :halo], "fsdp", [(j, i) for i, j in edges])
    padding = jnp.zeros((own_slots, ROWS - 2 * halo, model_width), tokens.dtype)
    in_own = jnp.concatenate(
        [
            lax.dynamic_slice_in_dim(in_weight, h * inner_width + g * channels, channels, 1)
            for h in range(2)
        ],
        axis=1,
    )
    shard = out_weight.shape[0]
    small = jnp.concatenate(
        [
            dt_weight.reshape(2 * rank_width, shard),
            a_log.reshape(2 * states, shard),
            conv_weight.reshape(2 * kernel, shard),
            conv_bias,
            dt_bias,
            skip_gain,
        ],
        axis=0,
    )
    small_rows = small.shape[0]
    small_pad = -small_rows % LANES
    small = jnp.pad(small, ((0, -small_rows % BLOCK), (0, 0)))
    all_tokens, all_halo, in_matrix, all_xproj, all_small, all_facts = collect_inputs(
        tokens,
        jnp.concatenate([before, after, padding], axis=1),
        in_own,
        xproj_weight,
        small,
        facts,
    )
    ways = groups.bit_length() - 1
    all_tokens, late = lax.optimization_barrier((all_tokens, cotangent))
    travelling = [{0: part} for part in cut(late, ways)]
    for p, held in enumerate(travelling):
        for bit in bits_of(groups, p):
            held[bit] = flip(held[0], groups, bit)
    all_tokens = all_tokens.reshape(slots, length, model_width)
    all_halo = all_halo.reshape(slots, ROWS, model_width)
    in_matrix = in_matrix.reshape(model_width, 2 * channels)

    piece = shard // groups
    sent = lax.ppermute(
        lax.dynamic_slice_in_dim(out_weight, g * piece, piece, 0),
        ("group", "fsdp"),
        to_owner(groups, parts),
    )
    out_matrix = lax.all_gather(sent, "fsdp", axis=0, tiled=True)
    xproj = jnp.concatenate([all_xproj[0], all_xproj[1]], axis=1)
    rest = jnp.concatenate([all_small[0], all_small[1]], axis=1)
    edge = 0

    def take(rows):
        nonlocal edge
        edge += rows
        return rest[edge - rows : edge]

    dt_matrix = jnp.pad(
        take(2 * rank_width).reshape(2, rank_width, channels), ((0, 0), (0, width - rank_width), (0, 0))
    )
    rate = -jnp.exp(take(2 * states).astype(F32)).reshape(2, states // ROWS, ROWS, channels)
    taps = take(2 * kernel).reshape(2, kernel, channels).astype(F32)
    conv_shift = take(2).astype(F32)
    dt_shift = take(2).astype(F32).reshape(2, 1, channels)
    skip = take(2).astype(F32).reshape(2, 1, channels)
    decay = rate * LOG2E

    columns = facts.shape[1] - LANES
    plain = all_facts[:, 0, :, columns:].reshape(slots, LANES).astype(jnp.int32)
    counts, buckets = plain[:, 0], plain[:, LANES // 2]
    modulation = all_facts[:, :, :, :columns].transpose(0, 2, 1, 3).reshape(slots, parts * columns)
    group_counts = jnp.sum(counts.reshape(groups, own_slots), axis=1).astype(F32)
    share = jnp.repeat(group_counts / jnp.sum(group_counts), own_slots)
    positions = f * length + jnp.arange(length, dtype=jnp.int32)
    mask = (positions[None, :] < counts[:, None]).astype(F32)
    active = (counts > f * length).astype(jnp.int32)
    own_mask = mask[:own_slots, :, None]
    own_share = share[:own_slots, None, None]
    condition = jax.nn.silu(time_embed(buckets, model_width)).astype(BF16)
    shift_mod = modulation[:, None, :model_width]
    scale_mod = modulation[:, None, model_width : 2 * model_width]
    gate_mod = modulation[:, None, 2 * model_width :]

    info = jnp.concatenate([counts, (f * length)[None]]).astype(jnp.int32)
    modulated, wide_x, gate_z, conv_out, projected = project(
        info, all_tokens, all_halo, modulation[:, None, :], in_matrix, taps, conv_shift, xproj
    )
    travelling, projected = lax.optimization_barrier((travelling, projected))
    for p, held in enumerate(travelling):
        order = bits_of(groups, p)
        for t in range(1, ways):
            for r in [r for r in held if r and r < groups and all(r & bit == 0 for bit in order[t:])]:
                held[r ^ order[t]] = flip(held[r], groups, order[t])
    proj = sum_blocks(projected, BF16, F32, 2)
    proj, travelling = lax.optimization_barrier((proj, travelling))
    all_cotangent = jnp.concatenate([held[r] for r in range(groups) for held in travelling], axis=0)

    def normalise(values):
        inputs = values.astype(F32)
        centered = inputs - jnp.mean(inputs, axis=2, keepdims=True)
        inv_std = lax.rsqrt(jnp.mean(centered * centered, axis=2, keepdims=True) + EPSILON)
        return (inputs, centered * inv_std, inv_std)

    grad_in_all = all_cotangent.astype(F32) * (mask * share[:, None])[:, :, None]
    branch_gradient = (grad_in_all * gate_mod).astype(BF16)
    grad_gated = jnp.einsum("sld,cd->slc", branch_gradient, out_matrix, preferred_element_type=F32)
    grad_y = grad_gated * jax.nn.silu(gate_z)

    step, end, pull, total, mix_b, mix_c = scan_ends(active, conv_out, proj, grad_y, dt_matrix, dt_shift, decay)
    entering = pass_states(end, pull, total, decay)
    gated_output, grad_z, conv_grad, proj_part, dtw_grad, dtb_grad, decay_grad, skip_grad = scan_all(
        active,
        conv_out,
        proj,
        grad_y,
        step,
        mix_b,
        mix_c,
        entering,
        gate_z,
        grad_gated,
        dt_matrix,
        decay,
        skip,
    )
    proj_grad = sum_blocks(proj_part, BF16, BF16, 3)
    alog_grad = (decay_grad * rate).reshape(2 * states, channels)

    branch_part = jnp.einsum("slc,cd->sld", gated_output, out_matrix, preferred_element_type=F32)
    inward_z = jnp.einsum("sld,slc->dc", modulated, grad_z, preferred_element_type=F32)
    branch_part, inward_z, proj_grad = lax.optimization_barrier(
        (branch_part.astype(BF16), inward_z.astype(BF16), proj_grad)
    )
    inward_z = lax.psum_scatter(inward_z, "fsdp", scatter_dimension=0, tiled=True)
    ways = groups.bit_length() - 1
    cut_blocks = [cut(block, ways) for block in jnp.split(branch_part, groups, axis=0)]
    moving = [{r: cut_blocks[r][p] for r in range(groups)} for p in range(ways)]
    moving = scatter_stage(moving, groups, 0)
    outward = jnp.einsum("slc,sld->cd", gated_output, branch_gradient, preferred_element_type=F32)

    grad_x, rim, conv_sums, xproj_grads = back_through(
        info, wide_x, conv_grad, proj_grad, conv_out, taps, conv_shift, xproj
    )
    outward, moving, rim, inward_z, own_tokens = lax.optimization_barrier(
        (outward.astype(BF16), moving, rim, inward_z, tokens)
    )
    ahead = lax.ppermute(rim[:, 0, :halo], "fsdp", [(j, i) for i, j in edges])
    behind = lax.ppermute(rim[:, 1, ROWS - halo :], "fsdp", edges)
    zeros = jnp.zeros_like(ahead)
    ahead, behind = jnp.concatenate([zeros, ahead], 1), jnp.concatenate([behind, zeros], 1)
    last = sum(taps[0, k] * ahead[:, halo - k : 2 * halo - k] for k in range(kernel))
    first = sum(taps[1, k] * behind[:, k : k + halo] for k in range(kernel))
    grad_x = grad_x + jnp.concatenate(
        [first, jnp.zeros((slots, length - 2 * halo, channels), F32), last], axis=1
    )
    grad_x = grad_x.astype(BF16)
    inner_gradient = jnp.concatenate([grad_x, grad_z], axis=2)
    inward = jnp.einsum("sld,slc->dc", modulated, grad_x, preferred_element_type=F32)
    grad_mod_part = jnp.einsum(
        "slc,dc->sld", inner_gradient, in_matrix, preferred_element_type=F32
    ).astype(BF16)
    for t in range(1, ways):
        moving = scatter_stage(moving, groups, t)
    branch = jnp.concatenate([held[0] for held in moving], axis=0)
    small_grads = jnp.concatenate(
        [
            xproj_grads.reshape(2 * width, channels),
            dtw_grad[:, :rank_width].reshape(2 * rank_width, channels),
            alog_grad,
            conv_sums[: 2 * kernel + 2],
            dtb_grad.reshape(2, channels),
            skip_grad.reshape(2, channels),
            jnp.zeros((small_pad, channels), F32),
        ],
        axis=0,
    ).astype(BF16)
    packed_grads = jnp.concatenate([outward, small_grads.T], axis=1)
    packed_piece = lax.psum_scatter(packed_grads, "fsdp", scatter_dimension=0, tiled=True)
    inward, grad_mod_part, branch, packed_piece = lax.optimization_barrier(
        (inward.astype(BF16), grad_mod_part, branch, packed_piece)
    )
    branch = branch.astype(F32)
    grad_mod = scatter_blocks(grad_mod_part, 4) * own_mask

    own_gate = gate_mod[:own_slots]
    own_scale = scale_mod[:own_slots]
    own_inputs, own_normed, own_inv = normalise(own_tokens)
    layer_out = ((own_inputs + own_gate * branch) * own_mask).astype(BF16)
    grad_in = cotangent.astype(F32) * own_mask * own_share
    grad_gate = jnp.sum(grad_in * branch, axis=1)

    grad_shift = jnp.sum(grad_mod, axis=1)
    grad_scale = jnp.sum(grad_mod * own_normed, axis=1)
    grad_normed = grad_mod * (1.0 + own_scale)
    grad_ln = own_inv * (
        grad_normed
        - jnp.mean(grad_normed, axis=2, keepdims=True)
        - own_normed * jnp.mean(grad_normed * own_normed, axis=2, keepdims=True)
    )
    tokens_grad = grad_in + grad_ln

    mod_part = jnp.concatenate([grad_shift, grad_scale, grad_gate], axis=1)
    inward_x = lax.psum_scatter(inward, "fsdp", scatter_dimension=0, tiled=True)
    mod_terms = mod_part.reshape(own_slots, parts, -1).transpose(1, 0, 2)
    mod_all, in_grad, out_grad, packed_own = finish_gradients(
        mod_terms, inward_x, inward_z, packed_piece, model_width, 5
    )
    in_grad = in_grad.astype(F32)
    mod_all = mod_all.reshape(slots, -1)
    ada_grad = jnp.einsum("sd,sk->dk", condition, mod_all.astype(BF16), preferred_element_type=F32)
    adab_grad = jnp.sum(mod_all, axis=0)
    xproj_grad = jnp.stack(
        [packed_own[:, d * width : (d + 1) * width] for d in range(2)]
    )
    rest_grads = packed_own[:, 2 * width :].T
    sizes = [2 * rank_width, 2 * states, 2 * kernel, 2, 2, 2]
    cuts = [sum(sizes[:i]) for i in range(len(sizes) + 1)]
    dtw_out, alog_out, conv_w_out, conv_b_out, dtb_out, skip_out = [
        rest_grads[cuts[i] : cuts[i + 1]] for i in range(len(sizes))
    ]
    return (
        layer_out,
        tokens_grad,
        ada_grad,
        adab_grad,
        in_grad,
        conv_w_out.reshape(2, kernel, shard),
        conv_b_out,
        xproj_grad,
        dtw_out.reshape(2, rank_width, shard),
        dtb_out,
        alog_out.reshape(2, states, shard),
        skip_out,
        out_grad,
    )


def solution(mesh):
    in_specs = (
        P("group", "fsdp", None),
        P(),
        P("group"),
        P("group"),
        P("group"),
        P(None, "fsdp"),
        P("fsdp"),
        P("fsdp", None),
        P(None, None, "fsdp"),
        P(None, "fsdp"),
        P(None, "fsdp", None),
        P(None, None, "fsdp"),
        P(None, "fsdp"),
        P(None, None, "fsdp"),
        P(None, "fsdp"),
        P("fsdp", None),
        P("group", "fsdp", None),
    )
    out_specs = (
        P("group", "fsdp", None),
        P("group", "fsdp", None),
        P(None, "fsdp"),
        P("fsdp"),
        P("fsdp", None),
        P(None, None, "fsdp"),
        P(None, "fsdp"),
        P(None, "fsdp", None),
        P(None, None, "fsdp"),
        P(None, "fsdp"),
        P(None, None, "fsdp"),
        P(None, "fsdp"),
        P("fsdp", None),
    )
    return jax.shard_map(
        on_device, mesh=mesh, in_specs=in_specs, out_specs=out_specs, check_vma=False
    )
```
